32 devices in a mesh: dp: 32 (over z, y, x, core).
Axes of the slice: x: 2, y: 2, z: 4, core: 2. Of those that a mesh axis runs over, the one named last changes fastest.
Arguments:
- text_input: bfloat16 [256, 77, 384], P('dp'), may hold values from -6 to 6
- eot_index: int32 [256], P('dp'), may hold values from 4 to 76
- image_input: bfloat16 [256, 50, 384], P('dp'), may hold values from -6 to 6
- ln1_gain: float32 [1, 384], replicated, may hold values from 0.25 to 1.75
- ln1_bias: float32 [1, 384], replicated, may hold values from -1.75 to 1.75
- w_qkv: bfloat16 [1, 384, 1152], replicated, may hold values from -0.4375 to 0.4375
- w_attn_out: bfloat16 [1, 384, 384], replicated, may hold values from -0.875 to 0.875
- ln2_gain: float32 [1, 384], replicated, may hold values from 0.25 to 1.75
- ln2_bias: float32 [1, 384], replicated, may hold values from -1.75 to 1.75
- w_fc: bfloat16 [1, 384, 1536], replicated, may hold values from -0.3125 to 0.3125
- w_fc_out: bfloat16 [1, 1536, 384], replicated, may hold values from -0.15625 to 0.15625
- img_ln1_gain: float32 [1, 384], replicated, may hold values from 0.25 to 1.75
- img_ln1_bias: float32 [1, 384], replicated, may hold values from -1.75 to 1.75
- img_w_qkv: bfloat16 [1, 384, 1152], replicated, may hold values from -0.4375 to 0.4375
- img_w_attn_out: bfloat16 [1, 384, 384], replicated, may hold values from -0.875 to 0.875
- img_ln2_gain: float32 [1, 384], replicated, may hold values from 0.25 to 1.75
- img_ln2_bias: float32 [1, 384], replicated, may hold values from -1.75 to 1.75
- img_w_fc: bfloat16 [1, 384, 1536], replicated, may hold values from -0.3125 to 0.3125
- img_w_fc_out: bfloat16 [1, 1536, 384], replicated, may hold values from -0.15625 to 0.15625
- final_gain: float32 [384], replicated, may hold values from 0.25 to 1.75
- final_bias: float32 [384], replicated, may hold values from -1.75 to 1.75
- text_proj: bfloat16 [384, 384], replicated, may hold values from -0.3125 to 0.3125
- image_gain: float32 [384], replicated, may hold values from 0.25 to 1.75
- image_bias: float32 [384], replicated, may hold values from -1.75 to 1.75
- image_proj: bfloat16 [384, 384], replicated, may hold values from -0.3125 to 0.3125
- logit_scale: float32 [1], replicated, may hold values from 3.4 to 4.1
Outputs:
- loss: float32 [1], replicated
- text_input_grad: float32 [256, 77, 384], P('dp')
- image_input_grad: float32 [256, 50, 384], P('dp')
- text_layer_grads: float32 [1, 1771008], P(None, 'dp')
- image_layer_grads: float32 [1, 1771008], P(None, 'dp')
- head_grads: float32 [296448], P('dp')
- logit_scale_grad: float32 [1], replicated
The draws below stay inside these ranges and needn't reach their ends.
Inputs may be any that keep to these rules, and one draw needn't show every extreme that they name: `eot_index`: the end token's position of each caption; slots after it are padding.
All inputs are finite; a program needn't handle non-finite values.
Results may differ from the reference program's by a relative error of at most 0.019.
Values may be sent and summed in bfloat16 or wider, within the bound.
No kernel may reach another device: no remote copies, remote signals or barrier semaphores. Data moves between devices by JAX's collectives and lax.ppermute only.
A program may use at most 128 MiB of HBM per device.

```python
import jax
import jax.numpy as jnp
from jax import lax

D = 384
HEAD_DIM = 64
FF = 1536
SEQ = 77
IMG_D = 384
IMG_FF = 1536
IMG_SEQ = 50
EMBED = 384
LAYERS = 1
CAP_DEV = 8
CAPTIONS = 256
TEXT_FLAT = 1771008
IMAGE_FLAT = 1771008
HEAD_FLAT = 296448
N_DP = 32


def place_ends(values, stream_key, low, top_value):
    spot = [jax.random.randint(jax.random.fold_in(stream_key, axis), (), 0, length) for axis, length in enumerate(values.shape)]
    widest = values.shape.index(max(values.shape))
    next_to = spot[:widest] + [(spot[widest] + 1) % values.shape[widest]] + spot[widest + 1:]
    return values.at[tuple(spot)].set(low).at[tuple(next_to)].set(top_value)


def shard_levels(stream_key, shape, cuts, least, largest):
    level, own = 1.0, jax.random.fold_in(stream_key, 6)
    for dim, shards_of in cuts:
        draws = jnp.exp(jax.random.uniform(jax.random.fold_in(own, dim), (shards_of,), jnp.float32, least / len(cuts), largest / len(cuts)))
        level = level * jnp.repeat(draws, shape[dim] // shards_of).reshape([-1 if axis == dim else 1 for axis in range(len(shape))])
    return level


def centred(rng, extent, scale, reach, split=(), kind=jnp.bfloat16):
    values = jax.random.normal(rng, extent, jnp.float32) * scale
    if len(split) > 0:
        values = shard_levels(rng, extent, split, -0.22, 0.18) * values
    return jnp.clip(values, min=-reach, max=reach).astype(kind)


def setup_inputs(seed: int = 0) -> dict:
    seeds = jax.random.split(jax.random.key(seed), 27)
    return {
        "text_input": centred(seeds[0], (CAPTIONS, SEQ, D), 1.0, 6.0, ((0, 32),)),
        "eot_index": place_ends(jax.random.randint(seeds[1], (CAPTIONS,), 4, SEQ), jax.random.fold_in(seeds[1], 1), 4, SEQ - 1).astype(jnp.int32),
        "image_input": centred(seeds[2], (CAPTIONS, IMG_SEQ, IMG_D), 1.0, 6.0, ((0, 32),)),
        "ln1_gain": jnp.clip(1.0 + 0.15 * jax.random.normal(seeds[3], (LAYERS, D), jnp.float32), 0.25, 1.75),
        "ln1_bias": centred(seeds[4], (LAYERS, D), 0.3, 1.75, (), jnp.float32),
        "w_qkv": centred(seeds[5], (LAYERS, D, 3 * D), (D // 2) ** -0.5, 0.4375),
        "w_attn_out": centred(seeds[6], (LAYERS, D, D), (D // 8) ** -0.5, 0.875),
        "ln2_gain": jnp.clip(1.0 + 0.15 * jax.random.normal(seeds[7], (LAYERS, D), jnp.float32), 0.25, 1.75),
        "ln2_bias": centred(seeds[8], (LAYERS, D), 0.3, 1.75, (), jnp.float32),
        "w_fc": centred(seeds[9], (LAYERS, D, FF), D ** -0.5, 0.3125),
        "w_fc_out": centred(seeds[10], (LAYERS, FF, D), FF ** -0.5, 0.15625),
        "img_ln1_gain": jnp.clip(1.0 + 0.15 * jax.random.normal(seeds[11], (LAYERS, IMG_D), jnp.float32), 0.25, 1.75),
        "img_ln1_bias": centred(seeds[12], (LAYERS, IMG_D), 0.3, 1.75, (), jnp.float32),
        "img_w_qkv": centred(seeds[13], (LAYERS, IMG_D, 3 * IMG_D), (IMG_D // 2) ** -0.5, 0.4375),
        "img_w_attn_out": centred(seeds[14], (LAYERS, IMG_D, IMG_D), (IMG_D // 8) ** -0.5, 0.875),
        "img_ln2_gain": jnp.clip(1.0 + 0.15 * jax.random.normal(seeds[15], (LAYERS, IMG_D), jnp.float32), 0.25, 1.75),
        "img_ln2_bias": centred(seeds[16], (LAYERS, IMG_D), 0.3, 1.75, (), jnp.float32),
        "img_w_fc": centred(seeds[17], (LAYERS, IMG_D, IMG_FF), IMG_D ** -0.5, 0.3125),
        "img_w_fc_out": centred(seeds[18], (LAYERS, IMG_FF, IMG_D), IMG_FF ** -0.5, 0.15625),
        "final_gain": jnp.clip(1.0 + 0.15 * jax.random.normal(seeds[19], (D,), jnp.float32), 0.25, 1.75),
        "final_bias": centred(seeds[20], (D,), 0.3, 1.75, (), jnp.float32),
        "text_proj": centred(seeds[21], (D, EMBED), D ** -0.5, 0.3125),
        "image_gain": jnp.clip(1.0 + 0.15 * jax.random.normal(seeds[22], (IMG_D,), jnp.float32), 0.25, 1.75),
        "image_bias": centred(seeds[23], (IMG_D,), 0.3, 1.75, (), jnp.float32),
        "image_proj": centred(seeds[24], (IMG_D, EMBED), IMG_D ** -0.5, 0.3125),
        "logit_scale": jnp.clip(jax.random.uniform(seeds[25], (1,), jnp.float32, 3.4, 4.1), 3.4, 4.1),
    }


EPS = 1e-05
UNIT_EPS = 1e-06
MASKED = -1000000000.0
HIGH = lax.Precision.HIGHEST

@jax.custom_vjp
def low(v):
    return lax.optimization_barrier(v.astype(jnp.bfloat16)).astype(jnp.float32)

@jax.custom_vjp
def low_back(v):
    return v

def low_keep(v):
    return (low(v), None)

def low_pass(kept, grad):
    return (grad,)

def back_keep(v):
    return (v, None)

def back_low(kept, grad):
    return (low(grad),)
low.defvjp(low_keep, low_pass)
low_back.defvjp(back_keep, back_low)

def both_ways(values):
    return low_back(low(values))

def matmul(left, right):
    return jnp.dot(left, right, precision=HIGH, preferred_element_type=jnp.float32)

def norm_apply(values, gain, bias):
    center = values - lax.optimization_barrier(jnp.mean(values, -1, keepdims=True))
    spread = lax.optimization_barrier(jnp.mean(center * center, -1, keepdims=True))
    return center * lax.rsqrt(spread + EPS) * gain + bias

def quick_gelu(values):
    return values * jax.nn.sigmoid(1.702 * values)

def unit_rows(values):
    return values * lax.rsqrt(lax.optimization_barrier(jnp.sum(values * values, -1, keepdims=True)) + UNIT_EPS)

def causal_mask(seq_len):
    row_pos = lax.broadcasted_iota(jnp.int32, (seq_len, seq_len), 0)
    col_pos = lax.broadcasted_iota(jnp.int32, (seq_len, seq_len), 1)
    return col_pos <= row_pos

def tower_block(stream, weights, causal):
    gain_one, bias_one, w_qkv, w_out, gain_two, bias_two, w_fc, w_fc_out = weights
    num_caps, seq_len, feat_dim = stream.shape
    num_heads = feat_dim // HEAD_DIM
    num_rows = num_caps * seq_len
    normed_one = low(norm_apply(stream, gain_one, bias_one)).reshape(num_rows, feat_dim)
    packed = both_ways(matmul(normed_one, w_qkv)).reshape(num_caps, seq_len, 3, num_heads, HEAD_DIM)
    queries = packed[:, :, 0]
    key_rows = packed[:, :, 1]
    value_rows = packed[:, :, 2]
    raw_score = low_back(jnp.einsum('bqhd,bkhd->bhqk', queries, key_rows, precision=HIGH))
    scores = raw_score * HEAD_DIM ** (-0.5)
    if causal:
        scores = jnp.where(causal_mask(seq_len), scores, MASKED)
    row_peak = lax.optimization_barrier(jnp.max(scores, -1, keepdims=True))
    log_total = row_peak + jnp.log(lax.optimization_barrier(jnp.sum(jnp.exp(scores - row_peak), -1, keepdims=True)))
    attn_probs = low(jnp.exp(scores - log_total))
    mixed_rows = both_ways(jnp.einsum('bhqk,bkhd->bqhd', attn_probs, value_rows, precision=HIGH)).reshape(num_rows, feat_dim)
    middle = stream + low_back(matmul(mixed_rows, w_out)).reshape(num_caps, seq_len, feat_dim)
    normed_two = low(norm_apply(middle, gain_two, bias_two)).reshape(num_rows, feat_dim)
    hidden = low_back(matmul(normed_two, w_fc))
    active = low(quick_gelu(hidden))
    return middle + low_back(matmul(active, w_fc_out)).reshape(num_caps, seq_len, feat_dim)

def head_unit(features, gain, bias, proj):
    normed = low(norm_apply(features, gain, bias))
    return unit_rows(low_back(matmul(normed, proj)))

def contrast_sum(logits):
    row_peak = lax.optimization_barrier(jnp.max(logits, -1, keepdims=True))
    log_total = row_peak[:, 0] + jnp.log(lax.optimization_barrier(jnp.sum(jnp.exp(logits - row_peak), -1)))
    return jnp.sum(log_total) - jnp.sum(jnp.diagonal(logits))

def flatten_padded(arrays, width):
    flat = jnp.concatenate([array.reshape(-1) for array in arrays])
    return jnp.pad(flat, (0, width - flat.shape[0]))

def reference(text_input, eot_index, image_input, ln1_gain, ln1_bias, w_qkv, w_attn_out, ln2_gain, ln2_bias, w_fc, w_fc_out, img_ln1_gain, img_ln1_bias, img_w_qkv, img_w_attn_out, img_ln2_gain, img_ln2_bias, img_w_fc, img_w_fc_out, final_gain, final_bias, text_proj, image_gain, image_bias, image_proj, logit_scale):
    text_params = tuple((array.astype(jnp.float32) for array in (ln1_gain, ln1_bias, w_qkv, w_attn_out, ln2_gain, ln2_bias, w_fc, w_fc_out)))
    image_params = tuple((array.astype(jnp.float32) for array in (img_ln1_gain, img_ln1_bias, img_w_qkv, img_w_attn_out, img_ln2_gain, img_ln2_bias, img_w_fc, img_w_fc_out)))
    heads_in = tuple((array.astype(jnp.float32) for array in (final_gain, final_bias, text_proj, image_gain, image_bias, image_proj, logit_scale)))
    eot_groups = eot_index.astype(jnp.int32).reshape(N_DP, CAP_DEV)

    def forward(text_layers, image_layers, head_params, text_x, image_x):
        fin_gain, fin_bias, txt_proj, img_gain, img_bias, img_proj, scale_log = head_params

        def text_group(pair):
            stream, eot_here = pair
            for layer_num in range(LAYERS):
                stream = tower_block(stream, tuple((array[layer_num] for array in text_layers)), True)
            pooled = jnp.take_along_axis(stream, eot_here[:, None, None], axis=1)[:, 0]
            return head_unit(pooled, fin_gain, fin_bias, txt_proj)

        def image_group(stream):
            for layer_num in range(LAYERS):
                stream = tower_block(stream, tuple((array[layer_num] for array in image_layers)), False)
            return head_unit(stream[:, 0], img_gain, img_bias, img_proj)
        text_groups = text_x.reshape(N_DP, CAP_DEV, SEQ, D)
        text_unit = lax.map(jax.checkpoint(text_group), (text_groups, eot_groups)).reshape(CAPTIONS, EMBED)
        image_groups = image_x.reshape(N_DP, CAP_DEV, IMG_SEQ, IMG_D)
        image_unit = lax.map(jax.checkpoint(image_group), image_groups).reshape(CAPTIONS, EMBED)
        image_low = low(image_unit)
        text_low = low(text_unit)
        raw_it = low_back(matmul(image_low, text_low.T))
        raw_ti = low_back(matmul(text_low, image_low.T))
        multiplier = jnp.exp(scale_log[0])
        return 0.5 * (contrast_sum(multiplier * raw_it) + contrast_sum(multiplier * raw_ti))
    total, pullback = jax.vjp(forward, text_params, image_params, heads_in, text_input.astype(jnp.float32), image_input.astype(jnp.float32))
    text_grads, image_grads, head_grads, text_grad, image_grad = pullback(jnp.ones_like(total))
    loss = (total / CAPTIONS).reshape(1)
    text_flat = jnp.stack([flatten_padded([grad[layer_num] for grad in text_grads], TEXT_FLAT) for layer_num in range(LAYERS)])
    image_flat = jnp.stack([flatten_padded([grad[layer_num] for grad in image_grads], IMAGE_FLAT) for layer_num in range(LAYERS)])
    head_flat = flatten_padded(list(head_grads[:6]), HEAD_FLAT)
    return (loss, text_grad, image_grad, text_flat, image_flat, head_flat, head_grads[6])
```

```python
import jax
import jax.numpy as jnp
from jax import lax
from jax.experimental import pallas as pl
from jax.experimental.pallas import tpu as pltpu
from jax.sharding import PartitionSpec as P

HEAD_DIM = 64
LANES = 128
WINDOW = 64

EPS = 1e-05
UNIT_EPS = 1e-06
MASKED = -1000000000.0
F32 = jnp.float32
BF16 = jnp.bfloat16


def dot(left, right):
    return jnp.dot(left, right, preferred_element_type=F32)


def dot_nt(left, right):
    return lax.dot_general(left, right, (((1,), (1,)), ((), ())), preferred_element_type=F32)


def dot_tn(left, right):
    return lax.dot_general(left, right, (((0,), (0,)), ((), ())), preferred_element_type=F32)


def standard(values):
    center = values - jnp.mean(values, -1, keepdims=True)
    scale = lax.rsqrt(jnp.mean(center * center, -1, keepdims=True) + EPS)
    return center * scale, scale


def norm_back(grad, unit, scale, gain):
    scaled = grad * gain
    return scale * (
        scaled
        - jnp.mean(scaled, -1, keepdims=True)
        - unit * jnp.mean(scaled * unit, -1, keepdims=True)
    )


def head_masks(width):
    lane = lax.broadcasted_iota(jnp.int32, (1, width), 1)
    return [
        ((lane >= h * HEAD_DIM) & (lane < (h + 1) * HEAD_DIM)).astype(F32)
        for h in range(width // HEAD_DIM)
    ]


def spread(rows):
    return jnp.concatenate([rows * mask for mask in head_masks(rows.shape[1])], 0)


def collect(rows, caps):
    masks = head_masks(rows.shape[1])
    return sum(rows[h * caps : (h + 1) * caps] * mask for h, mask in enumerate(masks))


def slot_of(seq):
    return -(-seq // 16) * 16


class Plan:
    def __init__(self, dim, hidden, devices):
        self.dim, self.hidden, self.devices = dim, hidden, devices
        self.row = 3 * dim
        self.qkv_at = 2 * dim
        self.out_at = self.qkv_at + dim * self.row
        self.norm_at = self.out_at + dim * dim
        self.fc_at = self.norm_at + 2 * dim
        self.fc_out_at = self.fc_at + dim * hidden
        self.total = self.fc_out_at + hidden * dim
        self.share = -(-self.total // devices)
        self.head_total = 2 * (2 * dim + dim * dim)
        self.head_share = -(-self.head_total // devices)
        self.roots = -(-self.out_at // self.share)
        self.rows_out = -(-(self.share // LANES + 2) // 8) * 8
        self.head_rows_out = -(-(self.head_share // LANES + 2) // 8) * 8
        assert self.share // self.row + 2 <= WINDOW
        assert self.total % devices == 0 and self.head_total % devices == 0

    def column(self, device):
        return jnp.maximum(device * self.share - self.qkv_at, 0) // self.row


def window_tiles(plan, text, image, device, caps):
    dim = text.shape[1]
    first = plan.column(device)
    lane = lax.broadcasted_iota(jnp.int32, (text.shape[0], LANES), 1)
    left = pltpu.roll(text, lax.rem(dim - first, dim), 1)[:, :LANES]
    right = pltpu.roll(image, lax.rem(dim - first + WINDOW, dim), 1)[:, :LANES]
    both = jnp.where(lane < WINDOW, left, right).astype(BF16)
    heads = text.shape[0] // caps
    return jnp.concatenate([both[h * caps : (h + 1) * caps] for h in range(heads)], 1)


def take_rows(source, at, count):
    row, lane_at = at // LANES, at % LANES
    lane = lax.broadcasted_iota(jnp.int32, (count, LANES), 1)
    mixed = jnp.where(
        lane >= lane_at, source[pl.ds(row, count), :], source[pl.ds(row + 1, count), :]
    )
    return pltpu.roll(mixed, lax.rem(LANES - lane_at, LANES), 1)


def put_tile(target, row, block):
    count, width = block.shape
    step = width // LANES
    for j in range(step):
        piece = block[:, j * LANES : (j + 1) * LANES]
        if count == 1:
            target[row + j : row + j + 1, :] = piece
        else:
            target[pl.ds(row + j, count, stride=step), :] = piece


def pad_rows(x_ref, wide_ref):
    caps, seq, dim = x_ref.shape
    slot = slot_of(seq)
    for b in range(caps):
        wide_ref[b * slot : b * slot + seq, :] = x_ref[b].astype(F32)
        if slot > seq:
            wide_ref[b * slot + seq : (b + 1) * slot, :] = jnp.zeros((slot - seq, dim), F32)
    return wide_ref[...]


def front_tower(x_ref, wide_ref, gain, bias, w_ref, picked, last):
    caps, seq, dim = x_ref.shape
    slot = slot_of(seq)
    heads = dim // HEAD_DIM
    stream = pad_rows(x_ref, wide_ref)
    total = stream.shape[0]
    unit, unused = standard(stream)
    normed = (unit * gain + bias).astype(BF16)
    key_value = dot(normed, w_ref[0, :, dim:]).astype(BF16)
    cap = lax.broadcasted_iota(jnp.int32, (caps, 1), 0)
    first = cap * slot
    pick_at, last_at = first, first
    for b in range(caps):
        pick_at = jnp.where(cap == b, first + picked[b], pick_at)
        last_at = jnp.where(cap == b, first + last[b], last_at)
    column = lax.broadcasted_iota(jnp.int32, (caps, total), 1)
    chosen = jnp.where(column == pick_at, 1.0, 0.0).astype(BF16)
    pooled = dot(chosen, stream.astype(BF16))
    pooled_unit, unused = standard(pooled)
    query = dot((pooled_unit * gain + bias).astype(BF16), w_ref[0, :, :dim]).astype(BF16)
    query = query.astype(F32)
    scores = dot_nt(spread(query).astype(BF16), key_value[:, :dim]) * HEAD_DIM ** (-0.5)
    seen = jnp.where((column >= first) & (column <= last_at), 1.0, 0.0)
    seen = jnp.concatenate([seen] * heads, 0) > 0.5
    peak = jnp.max(jnp.where(seen, scores, MASKED), -1, keepdims=True)
    sums = jnp.sum(jnp.where(seen, jnp.exp(scores - peak), 0.0), -1, keepdims=True)
    probs = jnp.where(seen, jnp.exp(scores - (peak + jnp.log(sums))), 0.0)
    probs_low = probs.astype(BF16)
    mixed = collect(dot(probs_low, key_value[:, dim:]), caps).astype(BF16)
    spread_values = dot(probs_low, normed)
    return pooled, mixed, spread_values, (normed, unit.astype(BF16), key_value, probs, query)


def front_kernel(plan):
    def kernel(
        eot_ref, xt_ref, xi_ref, gt_ref, bt_ref, wt_ref, gi_ref, bi_ref, wi_ref,
        rows_ref, spread_ref, *rest,
    ):
        kept_text, kept_image, (wide_t, wide_i) = rest[:5], rest[5:10], rest[10:]
        caps, seq, dim = xt_ref.shape
        img_seq = xi_ref.shape[1]
        ends = [eot_ref[b] for b in range(caps)]
        pooled_t, mixed_t, values_t, saved_t = front_tower(
            xt_ref, wide_t, gt_ref[...], bt_ref[...], wt_ref, ends, ends
        )
        pooled_i, mixed_i, values_i, saved_i = front_tower(
            xi_ref, wide_i, gi_ref[...], bi_ref[...], wi_ref, [0] * caps, [img_seq - 1] * caps
        )
        payload = jnp.concatenate(
            [pooled_t.astype(BF16), mixed_t, pooled_i.astype(BF16), mixed_i], 1
        )

        @pl.loop(0, plan.devices)
        def _(device):
            rows_ref[device] = payload

        for saved, refs in ((saved_t, kept_text), (saved_i, kept_image)):
            for value, ref in zip(saved, refs):
                ref[...] = value

        @pl.loop(0, plan.roots)
        def _(device):
            spread_ref[device] = window_tiles(plan, values_t, values_i, device, caps)

        @pl.loop(plan.roots, plan.devices)
        def _(device):
            spread_ref[device] = jnp.zeros(spread_ref.shape[1:], BF16)

    return kernel


def tower_forward(pooled, mixed, weights, active_ref, slope_ref, normed_ref, head_in_ref):
    w_out, gain, bias, w_fc, w_fc_out, head_gain, head_bias, proj = weights
    middle = pooled + dot(mixed, w_out[0])
    unit, scale = standard(middle)
    normed = (unit * gain[...] + bias[...]).astype(BF16)
    normed_ref[...] = normed
    result = middle
    hidden_dim = w_fc.shape[2]
    step = 512 if hidden_dim % 512 == 0 else hidden_dim
    for at in range(0, hidden_dim, step):
        hidden = dot(normed, w_fc[0, :, at : at + step])
        gate = jax.nn.sigmoid(1.702 * hidden)
        active = (hidden * gate).astype(BF16)
        active_ref[:, at : at + step] = active
        slope_ref[:, at : at + step] = gate + 1.702 * hidden * gate * (1.0 - gate)
        result = result + dot(active, w_fc_out[0, at : at + step, :])
    head_unit, head_scale = standard(result)
    head_in = (head_unit * head_gain[...] + head_bias[...]).astype(BF16)
    head_in_ref[...] = head_in
    embed = dot(head_in, proj[...])
    length = lax.rsqrt(jnp.sum(embed * embed, -1, keepdims=True) + UNIT_EPS)
    unit_embed = embed * length
    kept = (unit, scale, head_unit, head_scale, unit_embed, length)
    return unit_embed.astype(BF16), kept


def contrast(own, other, multiplier):
    logits = multiplier * dot_nt(own, other)
    peak = jnp.max(logits, -1, keepdims=True)
    log_total = peak + jnp.log(jnp.sum(jnp.exp(logits - peak), -1, keepdims=True))
    matched = lax.broadcasted_iota(jnp.int32, logits.shape, 1) == lax.broadcasted_iota(
        jnp.int32, logits.shape, 0
    )
    loss = jnp.sum(log_total) - jnp.sum(jnp.where(matched, logits, 0.0))
    grads = 0.5 * (jnp.exp(logits - log_total) - jnp.where(matched, 1.0, 0.0))
    return loss, jnp.sum(grads * logits), (multiplier * grads).astype(BF16)


def tower_backward(grad_unit, kept, weights, slope_ref, outs):
    w_out, gain, bias, w_fc, w_fc_out, head_gain, head_bias, proj = weights
    grad_embed_ref, grad_out_ref, grad_hidden_ref, middle_ref, small_ref = outs
    unit, scale, head_unit, head_scale, unit_embed, length = kept
    along = jnp.sum(unit_embed * grad_unit, -1, keepdims=True)
    grad_embed = (length * (grad_unit - unit_embed * along)).astype(BF16)
    grad_embed_ref[...] = grad_embed
    grad_head = dot_nt(grad_embed, proj[...])
    small_ref[2:3, :] = jnp.sum(grad_head * head_unit, 0, keepdims=True)
    small_ref[3:4, :] = jnp.sum(grad_head, 0, keepdims=True)
    grad_result = norm_back(grad_head, head_unit, head_scale, head_gain[...])
    grad_out = grad_result.astype(BF16)
    grad_out_ref[...] = grad_out
    hidden_dim = w_fc.shape[2]
    step = 512 if hidden_dim % 512 == 0 else hidden_dim
    grad_normed = 0.0
    for at in range(0, hidden_dim, step):
        grad_active = dot_nt(grad_out, w_fc_out[0, at : at + step, :])
        grad_hidden = (grad_active * slope_ref[:, at : at + step]).astype(BF16)
        grad_hidden_ref[:, at : at + step] = grad_hidden
        grad_normed = grad_normed + dot_nt(grad_hidden, w_fc[0, :, at : at + step])
    small_ref[0:1, :] = jnp.sum(grad_normed * unit, 0, keepdims=True)
    small_ref[1:2, :] = jnp.sum(grad_normed, 0, keepdims=True)
    grad_middle = grad_result + norm_back(grad_normed, unit, scale, gain[...])
    middle = grad_middle.astype(BF16)
    middle_ref[...] = middle
    return grad_middle, dot_nt(middle, w_out[0]).astype(BF16)


def attention_backward(grad_mixed, saved, w_ref, picked):
    normed, unit, key_value, probs, query = saved
    caps, dim = grad_mixed.shape
    heads = dim // HEAD_DIM
    grad_rows = spread(grad_mixed).astype(BF16)
    grad_probs = dot_nt(grad_rows, key_value[:, dim:])
    inner = jnp.sum(probs * grad_probs, -1, keepdims=True)
    grad_scores = (probs * (grad_probs - inner) * HEAD_DIM ** (-0.5)).astype(BF16)
    spread_keys = dot(grad_scores, normed)
    grad_query = collect(dot(grad_scores, key_value[:, :dim]), caps).astype(BF16)
    through_keys = dot_nt(spread(query).astype(BF16), w_ref[0, :, dim : 2 * dim])
    through_values = dot_nt(grad_rows, w_ref[0, :, 2 * dim :])
    through_query = dot_nt(grad_query, w_ref[0, :, :dim])
    units = through_keys * dot(grad_scores, unit) + through_values * dot(probs.astype(BF16), unit)
    total = unit.shape[0]
    slot = total // caps
    cap = lax.broadcasted_iota(jnp.int32, (caps, 1), 0)
    pick_at = cap * slot
    for b in range(caps):
        pick_at = jnp.where(cap == b, cap * slot + picked[b], pick_at)
    column = lax.broadcasted_iota(jnp.int32, (caps, total), 1)
    chosen = jnp.where(column == pick_at, 1.0, 0.0).astype(BF16)
    gain_part = jnp.sum(units, 0, keepdims=True) + jnp.sum(
        through_query * dot(chosen, unit), 0, keepdims=True
    )
    return grad_scores, spread_keys, grad_query, gain_part


def middle_kernel(plan):
    def kernel(at_ref, eot_ref, scale_ref, rows_ref, *refs):
        dim = plan.dim
        text_w, image_w = refs[0:8], refs[8:16]
        text_saved, image_saved = refs[16:21], refs[21:26]
        text_qkv, image_qkv = refs[26:28]
        loss_ref, scale_grad_ref, send_ref = refs[28:31]
        text_out, image_out = refs[31:42], refs[42:53]
        slope_t, slope_i, own_ref = refs[53:56]
        caps = eot_ref.shape[0]
        count = rows_ref.shape[0]
        zt, kept_t = tower_forward(
            rows_ref[:, :dim].astype(F32), rows_ref[:, dim : 2 * dim], text_w,
            text_out[1], slope_t, text_out[0], text_out[2],
        )
        zi, kept_i = tower_forward(
            rows_ref[:, 2 * dim : 3 * dim].astype(F32), rows_ref[:, 3 * dim :], image_w,
            image_out[1], slope_i, image_out[0], image_out[2],
        )
        multiplier = jnp.exp(jnp.full((1, 1), scale_ref[0], F32))
        loss_it, scale_it, raw_it = contrast(zi, zt, multiplier)
        loss_ti, scale_ti, raw_ti = contrast(zt, zi, multiplier)
        loss_ref[0] = (loss_it + loss_ti) / (2 * count)
        scale_grad_ref[0] = scale_it + scale_ti
        grad_iu = dot(raw_it, zt) + dot_tn(raw_ti, zt)
        grad_tu = dot(raw_ti, zi) + dot_tn(raw_it, zi)
        own_at = pl.multiple_of(at_ref[0] * caps, caps)
        ends = [eot_ref[b] for b in range(caps)]
        parts = []
        for grad_unit, kept, weights, slope, outs, saved, qkv, picked in (
            (grad_tu, kept_t, text_w, slope_t, text_out, text_saved, text_qkv, ends),
            (grad_iu, kept_i, image_w, slope_i, image_out, image_saved, image_qkv, [0] * caps),
        ):
            grad_middle, grad_mixed = tower_backward(grad_unit, kept, weights, slope, outs[3:8])
            outs[8][...] = grad_mixed
            own_ref[0] = grad_mixed.astype(F32)
            own_ref[1] = grad_middle
            own_mixed = own_ref[0, pl.ds(own_at, caps), :]
            outs[9][0] = own_mixed
            outs[9][1] = own_ref[1, pl.ds(own_at, caps), :]
            scores, keys, grad_query, gain_part = attention_backward(
                own_mixed, [ref[...] for ref in saved], qkv, picked
            )
            outs[10][...] = scores
            parts.append((keys, grad_query, gain_part))
        (keys_t, query_t, gain_t), (keys_i, query_i, gain_i) = parts
        tiles = dim // LANES
        small = jnp.concatenate(
            [g[:, j * LANES : (j + 1) * LANES] for g in (gain_t, gain_i) for j in range(tiles)]
            + [jnp.zeros((caps - 2 * tiles, LANES), F32)],
            0,
        )
        common = jnp.concatenate([query_t, query_i, small.astype(BF16)], 1)
        heads = dim // HEAD_DIM

        @pl.loop(0, plan.roots)
        def _(device):
            send_ref[device, :, : heads * LANES] = window_tiles(plan, keys_t, keys_i, device, caps)
            send_ref[device, :, heads * LANES :] = common

        @pl.loop(plan.roots, plan.devices)
        def _(device):
            send_ref[device] = jnp.zeros(send_ref.shape[1:], BF16)

    return kernel


def tail_kernel(plan):
    def kernel(at_ref, eot_ref, rows_ref, *refs):
        dim = plan.dim
        xt_ref, xi_ref, gt_ref, bt_ref, wt_ref, gi_ref, bi_ref, wi_ref = refs[:8]
        text_saved, image_saved = refs[8:10], refs[10:12]
        text_in, image_in = refs[12:24], refs[24:36]
        grad_t_ref, grad_i_ref, share_t, share_i, share_h, windows, queries = refs[36:43]
        wide_t, wide_i, flat, flat_head = refs[43:]
        device = at_ref[0]
        caps = eot_ref.shape[0]
        ends = [eot_ref[b] for b in range(caps)]
        for x_ref, wide, gain, w_ref, saved, values, picked, out_ref in (
            (xt_ref, wide_t, gt_ref, wt_ref, text_saved, text_in, ends, grad_t_ref),
            (xi_ref, wide_i, gi_ref, wi_ref, image_saved, image_in, [0] * caps, grad_i_ref),
        ):
            seq = x_ref.shape[1]
            slot = slot_of(seq)
            own = values[9]
            probs, query = saved
            unit, scale = standard(pad_rows(x_ref, wide))
            grad_keys = dot_tn(values[10][...], spread(query[...]).astype(BF16)).astype(BF16)
            grad_values = dot_tn(
                probs[...].astype(BF16), spread(own[0]).astype(BF16)
            ).astype(BF16)
            grad_normed = dot_nt(grad_keys, w_ref[0, :, dim : 2 * dim])
            grad_normed = grad_normed + dot_nt(grad_values, w_ref[0, :, 2 * dim :])
            through_query = dot_nt(values[11][...], w_ref[0, :, :dim])
            wide[...] = grad_normed
            for b in range(caps):
                at = b * slot + picked[b]
                wide[pl.ds(at, 1), :] = wide[pl.ds(at, 1), :] + through_query[b : b + 1]
            wide[...] = norm_back(wide[...], unit, scale, gain[...])
            for b in range(caps):
                at = b * slot + picked[b]
                wide[pl.ds(at, 1), :] = wide[pl.ds(at, 1), :] + own[1][b : b + 1]
            for b in range(caps):
                out_ref[b] = wide[b * slot : b * slot + seq, :]

        start = device * plan.share
        front = plan.rows_out
        for tower, (values, share_ref) in enumerate(((text_in, share_t), (image_in, share_i))):
            mixed_at = (2 * tower + 1) * dim

            def when_held(at, size, store):
                @pl.when((at < start + plan.share) & (at + size > start))
                def _():
                    store(front + (at - plan.out_at) // LANES)

            def product(at, left, left_at, right):
                def store(row):
                    put_tile(flat, row, dot_tn(left[:, left_at : left_at + LANES], right[...]))

                when_held(at, LANES * right.shape[1], store)

            def row_of(at, source, index):
                when_held(at, dim, lambda row: put_tile(flat, row, source[index : index + 1, :]))

            for t in range(dim // LANES):
                product(plan.out_at + t * LANES * dim, rows_ref, mixed_at + t * LANES, values[6])
            row_of(plan.norm_at, values[7], 0)
            row_of(plan.norm_at + dim, values[7], 1)
            for t in range(dim // LANES):
                product(plan.fc_at + t * LANES * plan.hidden, values[0], t * LANES, values[5])
            for t in range(plan.hidden // LANES):
                product(plan.fc_out_at + t * LANES * dim, values[1], t * LANES, values[4])
            at = jnp.maximum(start - plan.out_at + front * LANES, 0)
            share_ref[...] = take_rows(flat, at, plan.rows_out)

        half = plan.head_total // 2
        head_start = device * plan.head_share
        for tower, values in enumerate((text_in, image_in)):
            base = tower * half

            def when_kept(at, size, store):
                @pl.when((at < head_start + plan.head_share) & (at + size > head_start))
                def _():
                    store(at // LANES)

            for index in range(2):
                when_kept(
                    base + index * dim,
                    dim,
                    lambda row: put_tile(flat_head, row, values[7][2 + index : 3 + index, :]),
                )
            for t in range(dim // LANES):
                when_kept(
                    base + 2 * dim + t * LANES * dim,
                    LANES * dim,
                    lambda row: put_tile(
                        flat_head,
                        row,
                        dot_tn(values[2][:, t * LANES : (t + 1) * LANES], values[3][...]),
                    ),
                )
        share_h[...] = take_rows(flat_head, head_start, plan.head_rows_out)

        @pl.when(device < plan.roots)
        def _():
            first = plan.column(device)
            lane = lax.broadcasted_iota(jnp.int32, (rows_ref.shape[0], LANES), 1)
            normed = []
            for tower, (gain, bias, w_ref) in enumerate(
                ((gt_ref, bt_ref, wt_ref), (gi_ref, bi_ref, wi_ref))
            ):
                pooled = rows_ref[:, 2 * tower * dim : (2 * tower + 1) * dim].astype(F32)
                unit, unused = standard(pooled)
                rows = unit * gain[...] + bias[...]
                queries[:, tower * dim : (tower + 1) * dim] = dot(
                    rows.astype(BF16), w_ref[0, :, :dim]
                ).astype(BF16)
                shift = lax.rem(dim - first + tower * WINDOW, dim)
                normed.append(pltpu.roll(rows, shift, 1)[:, :LANES])
            windows[...] = jnp.where(lane < WINDOW, normed[0], normed[1]).astype(BF16)

    return kernel


def last_kernel(plan):
    def kernel(
        at_ref, sent_ref, values_ref, windows, queries, mixed_t, mixed_i, wq_t, wq_i,
        part_t, part_i, share_t, share_i, flat,
    ):
        dim = plan.dim
        heads = dim // HEAD_DIM
        tiles = dim // LANES
        device = at_ref[0]

        @pl.when(device >= plan.roots)
        def _():
            share_t[...] = part_t[...]
            share_i[...] = part_i[...]

        @pl.when(device < plan.roots)
        def _():
            at_query = heads * LANES
            at_small = at_query + 2 * dim
            count = sent_ref.shape[0]
            grad_query = sent_ref[:, at_query:at_small]
            small = sent_ref[:, at_small:].astype(F32)
            small = jnp.sum(small.reshape(count // 8, 8, LANES), 0)
            query_part = dot_tn(windows[...], grad_query)
            lane = lax.broadcasted_iota(jnp.int32, (1, LANES), 1)
            halves = [(lane < HEAD_DIM).astype(F32), (lane >= HEAD_DIM).astype(F32)]
            for j in range(tiles):
                put = []
                for source, factors in ((sent_ref, None), (values_ref, (mixed_t, mixed_i))):
                    cols = slice(j * LANES, (j + 1) * LANES)
                    if factors is None:
                        pair = [queries[:, cols], queries[:, dim + j * LANES : dim + (j + 1) * LANES]]
                    else:
                        pair = [factor[:, cols] for factor in factors]
                    right = jnp.concatenate(pair, 1).astype(F32)
                    total = 0.0
                    for odd in range(2):
                        h = 2 * j + odd
                        left = source[:, h * LANES : (h + 1) * LANES]
                        mask = jnp.concatenate([halves[odd]] * 2, 1)
                        total = total + dot_tn(left, (right * mask).astype(BF16))
                    put.append(total)
                for tower in range(2):
                    rows = slice(tower * WINDOW, (tower + 1) * WINDOW)
                    own = slice(tower * LANES, (tower + 1) * LANES)
                    q_at = tower * dim + j * LANES
                    for part, block in enumerate(
                        (query_part[rows, q_at : q_at + LANES], put[0][rows, own], put[1][rows, own])
                    ):
                        flat[
                            tower,
                            pl.ds(2 * tiles + part * tiles + j, WINDOW, stride=3 * tiles),
                            :,
                        ] = block
            for tower in range(2):
                flat[tower, 0:tiles, :] = small[tower * tiles : (tower + 1) * tiles]

            @pl.when(device == 0)
            def _():
                for tower, (w_ref, mixed) in enumerate(((wq_t, mixed_t), (wq_i, mixed_i))):
                    grads = grad_query[:, tower * dim : (tower + 1) * dim]
                    row = jnp.sum(dot_nt(grads, w_ref[0, :, :dim]), 0, keepdims=True)
                    row = row + jnp.sum(dot_nt(mixed[...], w_ref[0, :, 2 * dim :]), 0, keepdims=True)
                    for j in range(tiles):
                        flat[tower, tiles + j : tiles + j + 1, :] = row[
                            :, j * LANES : (j + 1) * LANES
                        ]

            start = device * plan.share
            at = start - plan.column(device) * plan.row
            shape = share_t.shape
            index = (
                start
                + lax.broadcasted_iota(jnp.int32, shape, 0) * LANES
                + lax.broadcasted_iota(jnp.int32, shape, 1)
            )
            for tower, (part, share) in enumerate(((part_t, share_t), (part_i, share_i))):
                own = take_rows(flat.at[tower], at, plan.rows_out)
                share[...] = jnp.where(index < plan.out_at, own, part[...])

    return kernel


def run(kernel, name, outs, scratch, scalars, arrays, limit):
    smem = pl.BlockSpec(memory_space=pltpu.SMEM)
    vmem = pl.BlockSpec(memory_space=pltpu.VMEM)
    out_specs = [smem if shape == (1,) else vmem for shape, unused in outs]
    return pl.pallas_call(
        kernel,
        name=name,
        out_shape=[jax.ShapeDtypeStruct(shape, kind) for shape, kind in outs],
        in_specs=[smem] * len(scalars) + [vmem] * len(arrays),
        out_specs=out_specs,
        scratch_shapes=[pltpu.VMEM(shape, kind) for shape, kind in scratch],
        compiler_params=pltpu.CompilerParams(vmem_limit_bytes=limit << 20),
    )(*scalars, *arrays)


def exchange(array):
    return lax.all_to_all(array, "dp", split_axis=0, concat_axis=0, tiled=True)


def compact(
    text_input, eot_index, image_input, ln1_gain, ln1_bias, w_qkv, w_attn_out, ln2_gain, ln2_bias,
    w_fc, w_fc_out, img_ln1_gain, img_ln1_bias, img_w_qkv, img_w_attn_out, img_ln2_gain,
    img_ln2_bias, img_w_fc, img_w_fc_out, final_gain, final_bias, text_proj, image_gain,
    image_bias, image_proj, logit_scale,
):
    caps, seq, dim = text_input.shape
    img_seq = image_input.shape[1]
    devices = lax.axis_size("dp")
    plan = Plan(dim, w_fc.shape[2], devices)
    heads = dim // HEAD_DIM
    count = devices * caps
    hidden = plan.hidden
    device = lax.axis_index("dp").astype(jnp.int32).reshape(1)
    text_rows, image_rows = caps * slot_of(seq), caps * slot_of(img_seq)

    def kept(total):
        return [
            ((total, dim), BF16),
            ((total, dim), BF16),
            ((total, 2 * dim), BF16),
            ((heads * caps, total), F32),
            ((caps, dim), F32),
        ]

    first = (
        text_input, image_input, ln1_gain, ln1_bias, w_qkv, img_ln1_gain, img_ln1_bias, img_w_qkv,
    )
    rows, spread_values, *saved = run(
        front_kernel(plan),
        "front",
        [((devices, caps, 4 * dim), BF16), ((devices, caps, heads * LANES), BF16)]
        + kept(text_rows)
        + kept(image_rows),
        [((text_rows, dim), F32), ((image_rows, dim), F32)],
        [eot_index],
        first,
        48,
    )
    rows = exchange(rows).reshape(count, 4 * dim)
    spread_values = exchange(spread_values).reshape(count, heads * LANES)

    def middle_outs(total):
        return [
            ((count, dim), BF16),
            ((count, hidden), BF16),
            ((count, dim), BF16),
            ((count, dim), BF16),
            ((count, dim), BF16),
            ((count, hidden), BF16),
            ((count, dim), BF16),
            ((8, dim), F32),
            ((count, dim), BF16),
            ((2, caps, dim), F32),
            ((heads * caps, total), BF16),
        ]

    text_w = (
        w_attn_out, ln2_gain, ln2_bias, w_fc, w_fc_out,
        final_gain.reshape(1, dim), final_bias.reshape(1, dim), text_proj,
    )
    image_w = (
        img_w_attn_out, img_ln2_gain, img_ln2_bias, img_w_fc, img_w_fc_out,
        image_gain.reshape(1, dim), image_bias.reshape(1, dim), image_proj,
    )
    width = heads * LANES + 2 * dim + LANES
    loss, scale_grad, send, *middle = run(
        middle_kernel(plan),
        "middle",
        [((1,), F32), ((1,), F32), ((devices, caps, width), BF16)]
        + middle_outs(text_rows)
        + middle_outs(image_rows),
        [((count, hidden), F32), ((count, hidden), F32), ((2, count, dim), F32)],
        [device, eot_index, logit_scale],
        [rows, *text_w, *image_w, *saved, w_qkv, img_w_qkv],
        56,
    )
    sent = exchange(send).reshape(count, width)
    text_mid, image_mid = middle[:11], middle[11:]
    at_query = heads * LANES
    text_query = lax.dynamic_index_in_dim(send, 0, 0, False)[:, at_query : at_query + dim]
    image_query = lax.dynamic_index_in_dim(send, 0, 0, False)[:, at_query + dim : at_query + 2 * dim]
    share_rows, head_rows = plan.rows_out, plan.head_rows_out
    region = (plan.total - plan.out_at) // LANES
    head_region = plan.head_total // LANES
    text_grad, image_grad, part_t, part_i, share_h, windows, queries = run(
        tail_kernel(plan),
        "tail",
        [
            ((caps, seq, dim), F32),
            ((caps, img_seq, dim), F32),
            ((share_rows, LANES), F32),
            ((share_rows, LANES), F32),
            ((head_rows, LANES), F32),
            ((count, LANES), BF16),
            ((count, 2 * dim), BF16),
        ],
        [
            ((text_rows, dim), F32),
            ((image_rows, dim), F32),
            ((region + 2 * share_rows + 8, LANES), F32),
            ((head_region + head_rows + 8, LANES), F32),
        ],
        [device, eot_index],
        [rows, *first, saved[3], saved[4], saved[8], saved[9], *text_mid, text_query, *image_mid, image_query],
        56,
    )
    flat_rows = -(-(2 * dim + 2 * plan.row + share_rows * LANES) // LANES // 8) * 8 + 8
    flat_rows = max(flat_rows, 2 * dim // LANES + WINDOW * plan.row // LANES)
    flat_rows = -(-flat_rows // 8) * 8
    share_t, share_i = run(
        last_kernel(plan),
        "last",
        [((share_rows, LANES), F32), ((share_rows, LANES), F32)],
        [((2, flat_rows, LANES), F32)],
        [device],
        [sent, spread_values, windows, queries, text_mid[8], image_mid[8], w_qkv, img_w_qkv, part_t, part_i],
        40,
    )

    def cut(array, size):
        return array.reshape(-1)[:size]

    return (
        loss,
        text_grad,
        image_grad,
        cut(share_t, plan.share)[None],
        cut(share_i, plan.share)[None],
        cut(share_h, plan.head_share),
        scale_grad,
    )


def norm_apply(values, gain, bias):
    center = values - jnp.mean(values, -1, keepdims=True)
    spread = jnp.mean(center * center, -1, keepdims=True)
    return center * lax.rsqrt(spread + EPS) * gain + bias


def quick_gelu(values):
    return values * jax.nn.sigmoid(1.702 * values)


def unit_rows(values):
    return values * lax.rsqrt(jnp.sum(values * values, -1, keepdims=True) + UNIT_EPS)


def causal_mask(seq_len):
    row_pos = lax.broadcasted_iota(jnp.int32, (seq_len, seq_len), 0)
    col_pos = lax.broadcasted_iota(jnp.int32, (seq_len, seq_len), 1)
    return col_pos <= row_pos


def matmul(left, right):
    return jnp.dot(left, right, preferred_element_type=jnp.float32)


def inner_rows(left, right):
    return lax.dot_general(
        left, right, (((0,), (0,)), ((), ())), preferred_element_type=jnp.float32
    )


def outer_cols(left, right):
    return lax.dot_general(
        left, right, (((1,), (1,)), ((), ())), preferred_element_type=jnp.float32
    )


def layer_forward(stream, weights, causal):
    gain_one, bias_one, w_qkv, w_out, gain_two, bias_two, w_fc, w_fc_out = weights
    num_caps, seq_len, feat_dim = stream.shape
    num_heads = feat_dim // HEAD_DIM
    num_rows = num_caps * seq_len
    normed_one = (
        norm_apply(stream, gain_one, bias_one).astype(jnp.bfloat16).reshape(num_rows, feat_dim)
    )
    packed = (
        matmul(normed_one, w_qkv)
        .astype(jnp.bfloat16)
        .reshape(num_caps, seq_len, 3, num_heads, HEAD_DIM)
    )
    queries = packed[:, :, 0]
    key_rows = packed[:, :, 1]
    value_rows = packed[:, :, 2]
    raw_score = jnp.einsum("bqhd,bkhd->bhqk", queries, key_rows, preferred_element_type=jnp.float32)
    scores = raw_score * HEAD_DIM ** (-0.5)
    if causal:
        scores = jnp.where(causal_mask(seq_len), scores, MASKED)
    row_peak = jnp.max(scores, -1, keepdims=True)
    log_total = row_peak + jnp.log(jnp.sum(jnp.exp(scores - row_peak), -1, keepdims=True))
    attn_probs = jnp.exp(scores - log_total)
    probs_low = attn_probs.astype(jnp.bfloat16)
    mixed_rows = jnp.einsum(
        "bhqk,bkhd->bqhd", probs_low, value_rows, preferred_element_type=jnp.float32
    )
    mixed_rows = mixed_rows.astype(jnp.bfloat16).reshape(num_rows, feat_dim)
    middle = stream + matmul(mixed_rows, w_out).reshape(num_caps, seq_len, feat_dim)
    normed_two = (
        norm_apply(middle, gain_two, bias_two).astype(jnp.bfloat16).reshape(num_rows, feat_dim)
    )
    hidden = matmul(normed_two, w_fc)
    active = quick_gelu(hidden).astype(jnp.bfloat16)
    result = middle + matmul(active, w_fc_out).reshape(num_caps, seq_len, feat_dim)
    return (
        result,
        (normed_one, packed, attn_probs, probs_low, mixed_rows, middle, normed_two, hidden, active),
    )


def layer_backward(stream, weights, grad_out, causal):
    gain_one, bias_one, w_qkv, w_out, gain_two, bias_two, w_fc, w_fc_out = weights
    num_caps, seq_len, feat_dim = stream.shape
    num_heads = feat_dim // HEAD_DIM
    num_rows = num_caps * seq_len
    unused, kept = layer_forward(stream, weights, causal)
    normed_one, packed, attn_probs, probs_low, mixed_rows, middle, normed_two, hidden, active = kept
    grad_low = grad_out.reshape(num_rows, feat_dim).astype(jnp.bfloat16)
    grad_fc_out = inner_rows(active, grad_low)
    grad_active = outer_cols(grad_low, w_fc_out)
    unused_gelu, gelu_back = jax.vjp(quick_gelu, hidden)
    grad_hidden = gelu_back(grad_active)[0].astype(jnp.bfloat16)
    grad_fc = inner_rows(normed_two, grad_hidden)
    grad_normed_two = outer_cols(grad_hidden, w_fc)
    unused_two, norm_back_two = jax.vjp(norm_apply, middle, gain_two, bias_two)
    grad_mid_norm, grad_gain_two, grad_bias_two = norm_back_two(
        grad_normed_two.reshape(num_caps, seq_len, feat_dim)
    )
    grad_middle = grad_out + grad_mid_norm
    middle_low = grad_middle.reshape(num_rows, feat_dim).astype(jnp.bfloat16)
    grad_w_out = inner_rows(mixed_rows, middle_low)
    grad_mixed = (
        outer_cols(middle_low, w_out)
        .astype(jnp.bfloat16)
        .reshape(num_caps, seq_len, num_heads, HEAD_DIM)
    )
    queries = packed[:, :, 0]
    key_rows = packed[:, :, 1]
    value_rows = packed[:, :, 2]
    grad_values = jnp.einsum(
        "bhqk,bqhd->bkhd", probs_low, grad_mixed, preferred_element_type=jnp.float32
    )
    grad_probs = jnp.einsum(
        "bqhd,bkhd->bhqk", grad_mixed, value_rows, preferred_element_type=jnp.float32
    )
    row_inner = jnp.sum(attn_probs * grad_probs, -1, keepdims=True)
    grad_raw = (attn_probs * (grad_probs - row_inner) * HEAD_DIM ** (-0.5)).astype(jnp.bfloat16)
    grad_queries = jnp.einsum(
        "bhqk,bkhd->bqhd", grad_raw, key_rows, preferred_element_type=jnp.float32
    )
    grad_keys = jnp.einsum("bhqk,bqhd->bkhd", grad_raw, queries, preferred_element_type=jnp.float32)
    grad_packed = (
        jnp.stack([grad_queries, grad_keys, grad_values], 2)
        .astype(jnp.bfloat16)
        .reshape(num_rows, 3 * feat_dim)
    )
    grad_qkv = inner_rows(normed_one, grad_packed)
    grad_normed_one = outer_cols(grad_packed, w_qkv)
    unused_one, norm_back_one = jax.vjp(norm_apply, stream, gain_one, bias_one)
    grad_in_norm, grad_gain_one, grad_bias_one = norm_back_one(
        grad_normed_one.reshape(num_caps, seq_len, feat_dim)
    )
    grads_here = [
        grad_gain_one,
        grad_bias_one,
        grad_qkv,
        grad_w_out,
        grad_gain_two,
        grad_bias_two,
        grad_fc,
        grad_fc_out,
    ]
    return (grad_middle + grad_in_norm, grads_here)


def head_forward(features, gain, bias, proj):
    normed = norm_apply(features, gain, bias).astype(jnp.bfloat16)
    embedded = matmul(normed, proj)
    return (unit_rows(embedded), (normed, embedded))


def head_backward(features, gain, bias, proj, kept, grad_unit):
    normed, embedded = kept
    unused_unit, unit_back = jax.vjp(unit_rows, embedded)
    grad_embed = unit_back(grad_unit)[0].astype(jnp.bfloat16)
    grad_proj = inner_rows(normed, grad_embed)
    grad_normed = outer_cols(grad_embed, proj)
    unused_norm, norm_back = jax.vjp(norm_apply, features, gain, bias)
    grad_feat, grad_gain, grad_bias = norm_back(grad_normed)
    return (grad_feat, [grad_gain, grad_bias, grad_proj])


def plain_contrast(own_rows, other_rows, multiplier, start):
    logits = multiplier * outer_cols(own_rows, other_rows)
    row_peak = jnp.max(logits, -1, keepdims=True)
    log_total = row_peak + jnp.log(jnp.sum(jnp.exp(logits - row_peak), -1, keepdims=True))
    col_pos = lax.broadcasted_iota(jnp.int32, logits.shape, 1)
    target_pos = lax.broadcasted_iota(jnp.int32, logits.shape, 0) + start
    matched = (col_pos == target_pos).astype(jnp.float32)
    loss_sum = jnp.sum(log_total) - jnp.sum(matched * logits)
    grad_logits = 0.5 * (jnp.exp(logits - log_total) - matched)
    scale_part = jnp.sum(grad_logits * logits)
    return (loss_sum, scale_part, (multiplier * grad_logits).astype(jnp.bfloat16), log_total[:, 0])


def pack_flat(arrays, devices):
    flat = jnp.concatenate([array.reshape(-1) for array in arrays])
    padding = -flat.shape[0] % devices
    return jnp.concatenate([flat, jnp.zeros((padding,), jnp.float32)])


def plain(
    text_input,
    eot_index,
    image_input,
    ln1_gain,
    ln1_bias,
    w_qkv,
    w_attn_out,
    ln2_gain,
    ln2_bias,
    w_fc,
    w_fc_out,
    img_ln1_gain,
    img_ln1_bias,
    img_w_qkv,
    img_w_attn_out,
    img_ln2_gain,
    img_ln2_bias,
    img_w_fc,
    img_w_fc_out,
    final_gain,
    final_bias,
    text_proj,
    image_gain,
    image_bias,
    image_proj,
    logit_scale,
):
    num_caps, seq_len, feat_dim = text_input.shape
    devices = lax.axis_size("dp")
    all_caps = num_caps * devices
    start = lax.axis_index("dp") * num_caps
    depth = ln1_gain.shape[0]
    text_stack = (ln1_gain, ln1_bias, w_qkv, w_attn_out, ln2_gain, ln2_bias, w_fc, w_fc_out)
    image_stack = (
        img_ln1_gain,
        img_ln1_bias,
        img_w_qkv,
        img_w_attn_out,
        img_ln2_gain,
        img_ln2_bias,
        img_w_fc,
        img_w_fc_out,
    )

    def text_weights(layer_num):
        return tuple((array[layer_num] for array in text_stack))

    def image_weights(layer_num):
        return tuple((array[layer_num] for array in image_stack))

    stream = text_input.astype(jnp.float32)
    layer_num = 0
    text_saved = [stream]
    stream, unused = layer_forward(stream, text_weights(layer_num), True)
    pooled = jnp.take_along_axis(stream, eot_index[:, None, None], axis=1)[:, 0]
    picture = image_input.astype(jnp.float32)
    layer_num = 0
    image_saved = [picture]
    picture, unused = layer_forward(picture, image_weights(layer_num), False)
    image_pooled = picture[:, 0]
    text_unit, text_kept = head_forward(pooled, final_gain, final_bias, text_proj)
    image_unit, image_kept = head_forward(image_pooled, image_gain, image_bias, image_proj)
    image_low = image_unit.astype(jnp.bfloat16)
    text_low = text_unit.astype(jnp.bfloat16)
    image_all, text_all = (
        lax.all_gather(image_low, "dp", axis=0, tiled=True),
        lax.all_gather(text_low, "dp", axis=0, tiled=True),
    )
    multiplier = jnp.exp(logit_scale[0])
    loss_image, scale_image, grad_raw_it, unused_it = plain_contrast(
        image_low, text_all, multiplier, start
    )
    loss_text, scale_text, grad_raw_ti, unused_ti = plain_contrast(text_low, image_all, multiplier, start)
    spread_text = inner_rows(grad_raw_it, image_low)
    spread_image = inner_rows(grad_raw_ti, text_low)
    back_text, back_image = (
        lax.psum_scatter(spread_text, "dp", scatter_dimension=0, tiled=True),
        lax.psum_scatter(spread_image, "dp", scatter_dimension=0, tiled=True),
    )
    total, grad_scale = lax.psum((loss_image + loss_text, scale_image + scale_text), "dp")
    grad_image_unit = matmul(grad_raw_it, text_all) + back_image
    grad_text_unit = matmul(grad_raw_ti, image_all) + back_text
    grad_pooled, text_head_grads = head_backward(
        pooled, final_gain, final_bias, text_proj, text_kept, grad_text_unit
    )
    grad_image_pooled, image_head_grads = head_backward(
        image_pooled, image_gain, image_bias, image_proj, image_kept, grad_image_unit
    )
    head_flat = pack_flat(text_head_grads + image_head_grads, devices)
    image_flat = [None] * depth
    img_seq = image_input.shape[1]
    img_dim = image_input.shape[2]
    grad_picture = jnp.concatenate(
        [grad_image_pooled[:, None, :], jnp.zeros((num_caps, img_seq - 1, img_dim), jnp.float32)], 1
    )
    for layer_num in reversed(range(depth)):
        grad_picture, grads_here = layer_backward(
            image_saved[layer_num], image_weights(layer_num), grad_picture, False
        )
        image_flat[layer_num] = pack_flat(grads_here, devices)
    text_flat = [None] * depth
    selected = (
        lax.broadcasted_iota(jnp.int32, (num_caps, seq_len), 1) == eot_index[:, None]
    ).astype(jnp.float32)
    grad_stream = selected[:, :, None] * grad_pooled[:, None, :]
    for layer_num in reversed(range(depth)):
        grad_stream, grads_here = layer_backward(
            text_saved[layer_num], text_weights(layer_num), grad_stream, True
        )
        text_flat[layer_num] = pack_flat(grads_here, devices)
    text_share, image_share, head_share = (
        lax.psum_scatter(jnp.stack(text_flat), "dp", scatter_dimension=1, tiled=True),
        lax.psum_scatter(jnp.stack(image_flat), "dp", scatter_dimension=1, tiled=True),
        lax.psum_scatter(head_flat, "dp", scatter_dimension=0, tiled=True),
    )
    loss = (total / (2 * all_caps)).reshape(1)
    return (
        loss,
        grad_stream,
        grad_picture,
        text_share,
        image_share,
        head_share,
        grad_scale.reshape(1),
    )


def shards(*args):
    caps = args[0].shape[0] * lax.axis_size("dp")
    return compact(*args) if caps <= 512 else plain(*args)


def solution(mesh):
    return jax.shard_map(
        shards,
        mesh=mesh,
        in_specs=(
            P("dp", None, None),
            P("dp"),
            P("dp", None, None),
            P(),
            P(),
            P(),
            P(),
            P(),
            P(),
            P(),
            P(),
            P(),
            P(),
            P(),
            P(),
            P(),
            P(),
            P(),
            P(),
            P(),
            P(),
            P(),
            P(),
            P(),
            P(),
            P(),
        ),
        out_specs=(
            P(),
            P("dp", None, None),
            P("dp", None, None),
            P(None, "dp"),
            P(None, "dp"),
            P("dp"),
            P(),
        ),
        check_vma=False,
    )
```

```python
import enum

import jax
import jax.numpy as jnp
from jax import lax
from jax.experimental import pallas as pl
from jax.experimental.pallas import tpu as pltpu
from jax.sharding import PartitionSpec as P

HEAD_DIM = 64
LANES = 128
WINDOW = 64

EPS = 1e-05
UNIT_EPS = 1e-06
MASKED = -1000000000.0
LIMIT = 44 * 2**20
IN_FLIGHT = 64 * 2**20
F32 = jnp.float32
BF16 = jnp.bfloat16


class Place(enum.Enum):
    FAR = enum.auto()
    FEW = enum.auto()
    RAW = enum.auto()
    AUTO = enum.auto()
    SCALAR = enum.auto()


class K(enum.Enum):
    BIAS = enum.auto()
    BIAS2 = enum.auto()
    EOT = enum.auto()
    GAIN = enum.auto()
    GAIN2 = enum.auto()
    HEAD = enum.auto()
    HEAD_BIAS = enum.auto()
    HEAD_GAIN = enum.auto()
    INPUT = enum.auto()
    LOSS = enum.auto()
    MINE = enum.auto()
    MIXED = enum.auto()
    NORMED = enum.auto()
    OTHERS = enum.auto()
    OWN = enum.auto()
    PACK = enum.auto()
    PART = enum.auto()
    PROBS = enum.auto()
    PROJ = enum.auto()
    QUERIES = enum.auto()
    QUERY = enum.auto()
    ROWS = enum.auto()
    SCALE = enum.auto()
    SCORES = enum.auto()
    SEND = enum.auto()
    SENT = enum.auto()
    SWAPPED = enum.auto()
    SHARE = enum.auto()
    UNIT = enum.auto()
    VALUES = enum.auto()
    W_FC = enum.auto()
    W_FC_OUT = enum.auto()
    W_OUT = enum.auto()
    W_QKV = enum.auto()
    WINDOWS = enum.auto()
    X = enum.auto()


def dot(left, right):
    return jnp.dot(left, right, preferred_element_type=F32)


def dot_nt(left, right):
    return lax.dot_general(left, right, (((1,), (1,)), ((), ())), preferred_element_type=F32)


def dot_tn(left, right):
    return lax.dot_general(left, right, (((0,), (0,)), ((), ())), preferred_element_type=F32)


def standard(values):
    center = values - jnp.mean(values, -1, keepdims=True)
    scale = lax.rsqrt(jnp.mean(center * center, -1, keepdims=True) + EPS)
    return center * scale, scale


def norm_back(grad, unit, scale, gain):
    scaled = grad * gain
    return scale * (
        scaled
        - jnp.mean(scaled, -1, keepdims=True)
        - unit * jnp.mean(scaled * unit, -1, keepdims=True)
    )


def head_masks(width):
    lane = lax.broadcasted_iota(jnp.int32, (1, width), 1)
    return [
        ((lane >= h * HEAD_DIM) & (lane < (h + 1) * HEAD_DIM)).astype(F32)
        for h in range(width // HEAD_DIM)
    ]


def spread(rows):
    return jnp.concatenate([rows * mask for mask in head_masks(rows.shape[1])], 0)


def collect(rows, caps):
    masks = head_masks(rows.shape[1])
    return sum(rows[h * caps : (h + 1) * caps] * mask for h, mask in enumerate(masks))


def picked_columns(caps, total, ends):
    cap = lax.broadcasted_iota(jnp.int32, (caps, 1), 0)
    at = cap
    for b in range(caps):
        at = jnp.where(cap == b, ends[b] * caps + b, at)
    column = lax.broadcasted_iota(jnp.int32, (caps, total), 1)
    chosen = jnp.where(column == at, 1.0, 0.0).astype(BF16)
    return chosen, column, at


class Plan:
    def __init__(self, dim, hidden, devices):
        self.dim, self.hidden, self.devices = dim, hidden, devices
        self.row = 3 * dim
        self.qkv_at = 2 * dim
        self.out_at = self.qkv_at + dim * self.row
        self.norm_at = self.out_at + dim * dim
        self.fc_at = self.norm_at + 2 * dim
        self.fc_out_at = self.fc_at + dim * hidden
        self.total = self.fc_out_at + hidden * dim
        self.share = -(-self.total // devices)
        self.head_total = 2 * (2 * dim + dim * dim)
        self.head_share = -(-self.head_total // devices)
        self.roots = -(-self.out_at // self.share)
        self.rows_out = -(-(self.share // LANES + 2) // 8) * 8
        self.head_rows_out = -(-(self.head_share // LANES + 2) // 8) * 8
        assert self.share // self.row + 2 <= WINDOW
        assert self.total % devices == 0 and self.head_total % devices == 0

    def column(self, device):
        if isinstance(device, int):
            return min(max(device * self.share - self.qkv_at, 0) // self.row, self.dim - 1)
        return jnp.minimum(jnp.maximum(device * self.share - self.qkv_at, 0) // self.row, self.dim - 1)


def window_tiles(plan, text, image, device, caps):
    dim = text.shape[1]
    first = plan.column(device)
    lane = lax.broadcasted_iota(jnp.int32, (text.shape[0], LANES), 1)
    left = pltpu.roll(text, (dim - first) % dim, 1)[:, :LANES]
    right = pltpu.roll(image, (dim - first + WINDOW) % dim, 1)[:, :LANES]
    both = jnp.where(lane < WINDOW, left, right).astype(BF16)
    heads = text.shape[0] // caps
    return jnp.concatenate([both[h * caps : (h + 1) * caps] for h in range(heads)], 1)


def pack_windows(plan, target, text, image, caps, common):
    width = text.shape[0] // caps * LANES
    held = plan.roots + plan.roots % 2

    def fill(device, core):
        target[device, :, :width] = window_tiles(plan, text, image, device, caps)
        if common is not None:
            target[device, :, width:] = common[core]

    if held <= 16:
        for device in range(held):
            fill(device, device % 2)
    else:

        @pl.loop(0, held // 2)
        def _(chip):
            for core in range(2):
                fill(2 * chip + core, core)

    @pl.loop(held, target.shape[0])
    def _(device):
        target[device] = jnp.zeros(target.shape[1:], BF16)


def take_rows(source, at, count):
    row, lane_at = at // LANES, at % LANES
    lane = lax.broadcasted_iota(jnp.int32, (count, LANES), 1)
    mixed = jnp.where(
        lane >= lane_at, source[pl.ds(row, count), :], source[pl.ds(row + 1, count), :]
    )
    return pltpu.roll(mixed, lax.rem(LANES - lane_at, LANES), 1)


def put_tile(target, row, block):
    count, width = block.shape
    step = width // LANES
    for j in range(step):
        piece = block[:, j * LANES : (j + 1) * LANES]
        if count == 1:
            target[row + j : row + j + 1, :] = piece
        else:
            target[pl.ds(row + j, count, stride=step), :] = piece


def front_tower(tower, ins, picked, last):
    x = ins[K.X, tower].get()[...]
    seq, caps, dim = x.shape
    total = seq * caps
    heads = dim // HEAD_DIM
    source = x.reshape(total, dim)
    unit, unused = standard(source.astype(F32))
    yield
    gain, bias = ins[K.GAIN, tower].get()[...], ins[K.BIAS, tower].get()[...]
    normed = (unit * gain + bias).astype(BF16)
    chosen, column, pick_at = picked_columns(caps, total, picked)
    last_at = pick_at
    if last is not picked:
        unused, unused, last_at = picked_columns(caps, total, last)
    pooled = dot(chosen, source)
    yield
    pooled_unit, unused = standard(pooled)
    pooled_normed = (pooled_unit * gain + bias).astype(BF16)
    w_ref = ins[K.W_QKV, tower].get()
    query = dot(pooled_normed, w_ref[0, :, :dim]).astype(BF16).astype(F32)
    yield
    through_keys = dot_nt(spread(query).astype(BF16), w_ref[0, :, dim : 2 * dim])
    yield
    scores = dot_nt(through_keys.astype(BF16), normed) * HEAD_DIM ** (-0.5)
    yield
    cap = lax.broadcasted_iota(jnp.int32, (caps, 1), 0)
    seen = jnp.where((lax.rem(column, caps) == cap) & (column <= last_at), 1.0, 0.0)
    seen = jnp.concatenate([seen] * heads, 0) > 0.5
    peak = jnp.max(jnp.where(seen, scores, MASKED), -1, keepdims=True)
    sums = jnp.sum(jnp.where(seen, jnp.exp(scores - peak), 0.0), -1, keepdims=True)
    probs = jnp.where(seen, jnp.exp(scores - (peak + jnp.log(sums))), 0.0)
    yield
    values = dot(probs.astype(BF16), normed)
    yield
    mixed = collect(dot(values.astype(BF16), w_ref[0, :, 2 * dim :]), caps).astype(BF16)
    return pooled, mixed, (normed, unit, probs, query, through_keys, values, chosen)


def attended_towers(ins):
    eot = ins[K.EOT].get()
    caps = eot.shape[0]
    seq = ins[K.X, 1].buf.shape[0]
    ends = [eot[b] for b in range(caps)]
    views = (ends, ends), ([0] * caps, [seq - 1] * caps)
    return run_together([front_tower(tower, ins, *views[tower]) for tower in range(2)])


def front_body(plan):
    def body(scalars, ins, outs, scratch):
        payload = []
        for pooled, mixed, unused in attended_towers(ins):
            payload += [pooled.astype(BF16), mixed]
        payload = jnp.concatenate(payload, 1)
        rows = outs[K.ROWS].ref

        @pl.loop(0, rows.shape[0])
        def _(chip):
            rows[chip] = payload

    return body


def pack_at(dim, hidden, caps):
    heads = dim // HEAD_DIM
    sizes = [heads * caps, heads * caps, caps, caps, caps, caps, caps, caps * hidden // dim]
    places, at = [], 0
    for size in sizes:
        places.append(slice(at, at + size))
        at += size
    return places, at


def weights_of(tower, ins):
    names = K.W_OUT, K.GAIN2, K.BIAS2, K.W_FC, K.W_FC_OUT, K.HEAD_GAIN, K.HEAD_BIAS, K.PROJ
    return [ins[name, tower] for name in names]


def side_body(plan):
    def body(scalars, ins, outs, scratch):
        dim, hidden = plan.dim, plan.hidden
        caps = ins[K.EOT].buf.shape[0]
        places, unused = pack_at(dim, hidden, caps)
        towers = attended_towers(ins)
        pack_windows(plan, outs[K.VALUES].ref, towers[0][2][5], towers[1][2][5], caps, None)
        outs[K.VALUES].push()
        kept = [], []
        for tower, (pooled, mixed, saved) in enumerate(towers):
            normed, unit, probs, query, through_keys, values, chosen = saved
            unit = unit.astype(BF16)
            for name, value in ((K.NORMED, normed), (K.UNIT, unit), (K.PROBS, probs)):
                outs[name, tower].ref[...] = value
                outs[name, tower].push()
            small = [through_keys, dot(probs.astype(BF16), unit), dot(chosen, unit), query]
            for place, value in zip(places, small):
                outs[K.PACK, tower].ref[place, :] = value
        run_together(
            [
                tower_forward(pooled, mixed, weights_of(tower, ins), kept[tower], None, None)
                for tower, (pooled, mixed, unused) in enumerate(towers)
            ]
        )
        for tower in range(2):
            pack = outs[K.PACK, tower]
            for place, value in zip(places[4:], kept[tower][:3]):
                pack.ref[place, :] = value
            for j in range(hidden // dim):
                at = places[7].start + j * caps
                pack.ref[at : at + caps, :] = kept[tower][3][:, j * dim : (j + 1) * dim]
            pack.push()

    return body


def run_together(steps):
    results = [None] * len(steps)
    live = list(range(len(steps)))
    while live:
        for index in list(live):
            try:
                next(steps[index])
            except StopIteration as stop:
                results[index] = stop.value
                live.remove(index)
    return results


def chunks(width):
    step = 512 if width % 512 == 0 else width
    return [slice(at, at + step) for at in range(0, width, step)]


def gate_slope(hidden):
    gate = jax.nn.sigmoid(1.702 * hidden)
    return gate + 1.702 * hidden * gate * (1.0 - gate)


def unit_rows_of(embed):
    length = lax.rsqrt(jnp.sum(embed * embed, -1, keepdims=True) + UNIT_EPS)
    return embed * length, length


def tower_forward(pooled, mixed, weights, kept, hidden_ref, active_ref):
    w_out, gain, bias, w_fc, w_fc_out, head_gain, head_bias, proj = weights
    middle = pooled + dot(mixed, w_out.get()[0])
    yield
    unit, unused = standard(middle)
    normed = (unit * gain.get()[...] + bias.get()[...]).astype(BF16)
    yield
    result = middle
    w_fc, w_fc_out = w_fc.get(), w_fc_out.get()
    every = []
    for cols in chunks(w_fc.shape[2]):
        hidden = dot(normed, w_fc[0, :, cols])
        active = (hidden * jax.nn.sigmoid(1.702 * hidden)).astype(BF16)
        every.append(hidden)
        if hidden_ref is not None:
            hidden_ref[:, cols] = hidden
            active_ref[:, cols] = active
        result = result + dot(active, w_fc_out[0, cols, :])
        yield
    head_unit, unused = standard(result)
    head_in = (head_unit * head_gain.get()[...][None] + head_bias.get()[...][None]).astype(BF16)
    embed = dot(head_in, proj.get()[...])
    yield
    if kept is not None:
        kept += [middle, result, embed]
        if hidden_ref is None:
            kept.append(jnp.concatenate(every, 1))
    return unit_rows_of(embed)[0].astype(BF16)


def log_sum(logits, axis):
    peak = jnp.max(logits, axis, keepdims=True)
    return peak + jnp.log(jnp.sum(jnp.exp(logits - peak), axis, keepdims=True))


def unit_gradient(multiplier, logits, own_total, other_total, matched, other):
    target = jnp.where(matched, 1.0, 0.0)
    own = 0.5 * multiplier * (jnp.exp(logits - own_total) - target)
    cross = 0.5 * multiplier * (jnp.exp(logits - other_total) - target)
    return dot(own.astype(BF16), other) + dot(cross.astype(BF16), other)


def embed_back(grad_unit, embed):
    unit_embed, length = unit_rows_of(embed)
    along = jnp.sum(unit_embed * grad_unit, -1, keepdims=True)
    return (length * (grad_unit - unit_embed * along)).astype(BF16)


def tower_backward(grad_embed, middle, result, hidden, weights, keep_hidden):
    w_out, gain, bias, w_fc, w_fc_out, head_gain, head_bias, proj = weights
    grad_head = dot_nt(grad_embed, proj.get()[...])
    yield
    head_unit, head_scale = standard(result)
    grad_result = norm_back(grad_head, head_unit, head_scale, head_gain.get()[...][None])
    grad_out = grad_result.astype(BF16)
    yield
    w_fc, w_fc_out = w_fc.get(), w_fc_out.get()
    grad_normed = 0.0
    for cols in chunks(w_fc.shape[2]):
        grad_active = dot_nt(grad_out, w_fc_out[0, cols, :])
        grad_hidden = (grad_active * gate_slope(hidden[:, cols])).astype(BF16)
        if keep_hidden is not None:
            keep_hidden[:, cols] = grad_hidden
        grad_normed = grad_normed + dot_nt(grad_hidden, w_fc[0, :, cols])
        yield
    unit, scale = standard(middle)
    grad_middle = grad_result + norm_back(grad_normed, unit, scale, gain.get()[...])
    yield
    grad_mixed = dot_nt(grad_middle.astype(BF16), w_out.get()[0]).astype(BF16)
    yield
    return grad_head, head_unit, grad_out, grad_normed, unit, grad_middle, grad_mixed


def own_steps(plan, tower, units, multiplier, own_at, ins, outs):
    mine, other = units[tower], units[1 - tower]
    own_out = outs[K.OWN, tower]
    caps, dim = own_out.ref.shape[1:]
    places, unused = pack_at(dim, plan.hidden, caps)
    other_total = log_sum(multiplier * dot_nt(mine, other), 0)
    yield
    pack = ins[K.PACK, tower].get()
    embed = pack[places[6], :]
    logits = multiplier * dot_nt(unit_rows_of(embed)[0].astype(BF16), other)
    matched = lax.broadcasted_iota(jnp.int32, logits.shape, 1) == own_at + lax.broadcasted_iota(
        jnp.int32, logits.shape, 0
    )
    grad_unit = unit_gradient(multiplier, logits, log_sum(logits, 1), other_total, matched, other)
    yield
    hidden_at = places[7].start
    hidden = jnp.concatenate(
        [pack[hidden_at + j * caps : hidden_at + (j + 1) * caps, :] for j in range(plan.hidden // dim)], 1
    )
    done = yield from tower_backward(
        embed_back(grad_unit, embed), pack[places[4], :], pack[places[5], :], hidden,
        weights_of(tower, ins), None,
    )
    grad_middle, grad_mixed = done[5], done[6].astype(F32)
    own_out.ref[0] = grad_mixed
    own_out.ref[1] = grad_middle
    own_out.push()
    w_ref = ins[K.W_QKV, tower].get()
    through_values = dot_nt(spread(grad_mixed).astype(BF16), w_ref[0, :, 2 * dim :])
    yield
    normed = ins[K.NORMED, tower].get()[...]
    grad_probs = dot_nt(through_values.astype(BF16), normed)
    yield
    probs = ins[K.PROBS, tower].get()[...]
    inner = jnp.sum(probs * grad_probs, -1, keepdims=True)
    grad_scores = (probs * (grad_probs - inner) * HEAD_DIM ** (-0.5)).astype(BF16)
    outs[K.SCORES, tower].ref[...] = grad_scores
    outs[K.SCORES, tower].push()
    yield
    spread_keys = dot(grad_scores, normed)
    yield
    grad_query = collect(dot(spread_keys.astype(BF16), w_ref[0, :, dim : 2 * dim]), caps).astype(BF16)
    outs[K.QUERY, tower].ref[...] = grad_query
    outs[K.QUERY, tower].push()
    yield
    units = pack[places[0], :] * dot(grad_scores, ins[K.UNIT, tower].get()[...])
    yield
    through_query = dot_nt(grad_query, w_ref[0, :, :dim])
    units = units + through_values * pack[places[1], :]
    gain_part = jnp.sum(units, 0, keepdims=True) + jnp.sum(
        through_query * pack[places[2], :], 0, keepdims=True
    )
    return spread_keys, grad_query, gain_part


def forward_pair(plan, rows, ins, kept, hidden, active):
    dim = plan.dim
    return run_together(
        [
            tower_forward(
                rows[:, 2 * tower * dim : (2 * tower + 1) * dim].astype(F32),
                rows[:, (2 * tower + 1) * dim : (2 * tower + 2) * dim],
                weights_of(tower, ins), kept[tower], hidden[tower], active[tower],
            )
            for tower in range(2)
        ]
    )


def middle_body(plan):
    def body(scalars, ins, outs, scratch):
        at_ref, scale_ref = scalars
        rows_ref, sems = scratch
        dim = plan.dim
        device = at_ref[0]
        caps, wide = rows_ref.shape[2:]
        copies = [
            pltpu.make_async_copy(ins[name].ref, rows_ref.at[:, core], sems.at[i])
            for i, (name, core) in enumerate(((K.MINE, device % 2), (K.OTHERS, 1 - device % 2)))
        ]
        for copy in copies:
            copy.start()
        for copy in copies:
            copy.wait()
        rows = rows_ref[...].reshape(plan.devices * caps, wide)
        outs[K.ROWS].ref[...] = rows
        outs[K.ROWS].push()
        units = forward_pair(plan, rows, ins, (None, None), (None, None), (None, None))
        multiplier = jnp.exp(jnp.full((1, 1), scale_ref[0], F32))
        own_at = device * caps
        parts = run_together(
            [own_steps(plan, tower, units, multiplier, own_at, ins, outs) for tower in range(2)]
        )
        (keys_t, query_t, gain_t), (keys_i, query_i, gain_i) = parts
        tiles = dim // LANES
        small = jnp.concatenate(
            [g[:, j * LANES : (j + 1) * LANES] for g in (gain_t, gain_i) for j in range(tiles)]
            + [jnp.zeros((caps - 2 * tiles, LANES), F32)],
            0,
        )
        common = [jnp.concatenate([query, small.astype(BF16)], 1) for query in (query_t, query_i)]
        pack_windows(plan, outs[K.SEND].ref, keys_t, keys_i, caps, common)

    return body


def tail_body(plan):
    def body(scalars, ins, outs, scratch):
        at_ref, scale_ref = scalars
        dim, hidden_dim = plan.dim, plan.hidden
        loss_ref, scale_grad_ref = outs[K.LOSS].ref, outs[K.SCALE].ref
        flat, flat_head, wide_t, wide_i, hidden_grad, small, hidden_t, hidden_i, active_t, active_i = scratch
        device = at_ref[0]
        eot = ins[K.EOT].get()
        caps = eot.shape[0]
        ends = [eot[b] for b in range(caps)]
        places, unused = pack_at(dim, hidden_dim, caps)
        multiplier = jnp.exp(jnp.full((1, 1), scale_ref[0], F32))

        def input_gradient(tower, picked, wide):
            names = K.X, K.GAIN, K.W_QKV, K.PROBS, K.PACK, K.OWN, K.SCORES, K.QUERY
            x, gain, w_ref, probs, pack, own, scores, query_grad = (
                ins[name, tower].get() for name in names
            )
            seq = x.shape[0]
            unit, scale = standard(x[...].reshape(seq * caps, dim).astype(F32))
            query = pack[places[3], :]
            grad_keys = dot_tn(scores[...], spread(query).astype(BF16)).astype(BF16)
            grad_values = dot_tn(probs[...].astype(BF16), spread(own[0]).astype(BF16)).astype(BF16)
            grad_normed = dot_nt(grad_keys, w_ref[0, :, dim : 2 * dim])
            grad_normed = grad_normed + dot_nt(grad_values, w_ref[0, :, 2 * dim :])
            through_query = dot_nt(query_grad[...], w_ref[0, :, :dim])
            wide[...] = grad_normed
            for b in range(caps):
                at = picked[b] * caps + b
                wide[pl.ds(at, 1), :] = wide[pl.ds(at, 1), :] + through_query[b : b + 1]
            wide[...] = norm_back(wide[...], unit, scale, gain[...])
            for b in range(caps):
                at = picked[b] * caps + b
                wide[pl.ds(at, 1), :] = wide[pl.ds(at, 1), :] + own[1][b : b + 1]
            outs[K.INPUT, tower].ref[...] = wide[...].reshape(seq, caps, dim)
            outs[K.INPUT, tower].push()

        input_gradient(0, ends, wide_t)
        input_gradient(1, [0] * caps, wide_i)

        rows = ins[K.ROWS].get()[...]
        count = rows.shape[0]
        kept = [], []
        hiddens, actives = (hidden_t, hidden_i), (active_t, active_i)
        units = forward_pair(plan, rows, ins, kept, hiddens, actives)
        embeds = [items[2] for items in kept]
        logits = multiplier * dot_nt(units[1], units[0])
        matched = lax.broadcasted_iota(jnp.int32, logits.shape, 1) == lax.broadcasted_iota(
            jnp.int32, logits.shape, 0
        )
        row_total, column_total = log_sum(logits, 1), log_sum(logits, 0)
        target = jnp.where(matched, 1.0, 0.0)
        by_row = 0.5 * (jnp.exp(logits - row_total) - target)
        by_column = 0.5 * (jnp.exp(logits - column_total) - target)
        total = jnp.sum(row_total) + jnp.sum(column_total) - 2.0 * jnp.sum(target * logits)
        loss_ref[0] = total / (2 * count)
        scale_grad_ref[0] = jnp.sum((by_row + by_column) * logits)
        by_row = (multiplier * by_row).astype(BF16)
        by_column = (multiplier * by_column).astype(BF16)
        grad_units = (
            dot_tn(by_row, units[1]) + dot_tn(by_column, units[1]),
            dot(by_row, units[0]) + dot(by_column, units[0]),
        )

        start, head_start = device * plan.share, device * plan.head_share
        front = plan.rows_out
        half = plan.head_total // 2
        for tower in range(2):
            weights = weights_of(tower, ins)
            gain, bias, head_gain, head_bias = (weights[j] for j in (1, 2, 5, 6))
            middle, result, unused = kept[tower]
            active = actives[tower]
            grad_embed = embed_back(grad_units[tower], embeds[tower])
            (done,) = run_together(
                [
                    tower_backward(
                        grad_embed, middle, result, hiddens[tower], weights, hidden_grad
                    )
                ]
            )
            grad_head, head_unit, grad_out, grad_normed, unit, grad_middle, grad_mixed = done
            outs[K.MIXED, tower].ref[...] = grad_mixed
            outs[K.MIXED, tower].push()
            middle_low = grad_middle.astype(BF16)
            normed = (unit * gain.get()[...] + bias.get()[...]).astype(BF16)
            head_in = head_unit * head_gain.get()[...][None] + head_bias.get()[...][None]
            head_in = head_in.astype(BF16)
            small[0:1, :] = jnp.sum(grad_normed * unit, 0, keepdims=True)
            small[1:2, :] = jnp.sum(grad_normed, 0, keepdims=True)
            small[2:3, :] = jnp.sum(grad_head * head_unit, 0, keepdims=True)
            small[3:4, :] = jnp.sum(grad_head, 0, keepdims=True)
            mixed = rows[:, (2 * tower + 1) * dim : (2 * tower + 2) * dim]

            def when_held(at, size, store):
                @pl.when((at < start + plan.share) & (at + size > start))
                def _():
                    store(front + (at - plan.out_at) // LANES)

            def when_kept(at, size, store):
                at = at + tower * half

                @pl.when((at < head_start + plan.head_share) & (at + size > head_start))
                def _():
                    store(at // LANES)

            def products(when, target, at, left, right):
                for t in range(left.shape[1] // LANES):
                    cols = slice(t * LANES, (t + 1) * LANES)
                    when(
                        at + t * LANES * right.shape[1],
                        LANES * right.shape[1],
                        lambda row: put_tile(target, row, dot_tn(left[:, cols], right[...])),
                    )

            def row_of(when, target, at, index):
                when(at, dim, lambda row: put_tile(target, row, small[index : index + 1, :]))

            products(when_held, flat, plan.out_at, mixed, middle_low)
            row_of(when_held, flat, plan.norm_at, 0)
            row_of(when_held, flat, plan.norm_at + dim, 1)
            products(when_held, flat, plan.fc_at, normed, hidden_grad)
            products(when_held, flat, plan.fc_out_at, active, grad_out)
            at = jnp.maximum(start - plan.out_at + front * LANES, 0)
            outs[K.PART, tower].ref[...] = take_rows(flat, at, plan.rows_out)
            outs[K.PART, tower].push()
            row_of(when_kept, flat_head, 0, 2)
            row_of(when_kept, flat_head, dim, 3)
            products(when_kept, flat_head, 2 * dim, head_in, grad_embed)

        outs[K.HEAD].ref[...] = take_rows(flat_head, head_start, plan.head_rows_out)
        outs[K.HEAD].push()

        for tower in range(2):
            bias = ins[K.BIAS, tower].get()

        @pl.when(device == 0)
        def _():
            for tower in range(2):
                w_ref = ins[K.W_QKV, tower].get()
                grads = dot_nt(outs[K.MIXED, tower].ref[...], w_ref[0, :, 2 * dim :])
                outs[K.BIAS].ref[tower : tower + 1, :] = jnp.sum(grads, 0, keepdims=True)

        @pl.when(device < plan.roots)
        def _():
            first = plan.column(device)
            lane = lax.broadcasted_iota(jnp.int32, (count, LANES), 1)
            picked_rows = []
            for tower in range(2):
                gain, bias, w_ref = (ins[name, tower].get() for name in (K.GAIN, K.BIAS, K.W_QKV))
                pooled = rows[:, 2 * tower * dim : (2 * tower + 1) * dim].astype(F32)
                unit, unused = standard(pooled)
                normed = unit * gain[...] + bias[...]
                outs[K.QUERIES].ref[:, tower * dim : (tower + 1) * dim] = dot(
                    normed.astype(BF16), w_ref[0, :, :dim]
                ).astype(BF16)
                shift = lax.rem(dim - first + tower * WINDOW, dim)
                picked_rows.append(pltpu.roll(normed, shift, 1)[:, :LANES])
            outs[K.WINDOWS].ref[...] = jnp.where(lane < WINDOW, picked_rows[0], picked_rows[1]).astype(BF16)

    return body


def last_body(plan):
    def body(scalars, ins, outs, scratch):
        (at_ref,) = scalars
        flat, wq, grad_query, sems = scratch
        dim = plan.dim
        heads = dim // HEAD_DIM
        tiles = dim // LANES
        device = at_ref[0]
        copies = [
            pltpu.make_async_copy(
                ins[K.W_QKV, tower].ref.at[0, :, pl.ds(0, dim)], wq.at[tower], sems.at[tower]
            )
            for tower in range(2)
        ]

        @pl.when(device == 0)
        def _():
            for copy in copies:
                copy.start()

        parts = [ins[K.PART, tower].get() for tower in range(2)]

        def store(tower, block):
            line = outs[K.SHARE, tower].ref
            line[...] = block.reshape(1, block.shape[0] * LANES)[:, : plan.share]

        @pl.when(device >= plan.roots)
        def _():
            for tower in range(2):
                store(tower, parts[tower][...])

        names = K.SENT, K.SWAPPED, K.VALUES, K.WINDOWS, K.QUERIES, K.BIAS, (K.MIXED, 0), (K.MIXED, 1)
        sent_ref, swapped, values_ref, windows, queries, bias, mixed_t, mixed_i = (
            ins[name].get() for name in names
        )

        @pl.when(device < plan.roots)
        def _():
            at_query = heads * LANES
            at_small = at_query + dim
            count = sent_ref.shape[0]
            for core in range(2):

                @pl.when(device % 2 == core)
                def _():
                    for tower, source in enumerate((sent_ref, swapped) if core == 0 else (swapped, sent_ref)):
                        grad_query[:, tower * dim : (tower + 1) * dim] = source[:, at_query:at_small]

            small = sent_ref[:, at_small:].astype(F32)
            small = jnp.sum(small.reshape(count // 8, 8, LANES), 0)
            query_part = dot_tn(windows[...], grad_query[...])
            lane = lax.broadcasted_iota(jnp.int32, (1, LANES), 1)
            halves = [(lane < HEAD_DIM).astype(F32), (lane >= HEAD_DIM).astype(F32)]
            for j in range(tiles):
                put = []
                cols = slice(j * LANES, (j + 1) * LANES)
                others = slice(dim + j * LANES, dim + (j + 1) * LANES)
                for source, factors in (
                    (sent_ref, (queries[:, cols], queries[:, others])),
                    (values_ref, (mixed_t[:, cols], mixed_i[:, cols])),
                ):
                    right = jnp.concatenate(factors, 1).astype(F32)
                    total = 0.0
                    for odd in range(2):
                        h = 2 * j + odd
                        left = source[:, h * LANES : (h + 1) * LANES]
                        mask = jnp.concatenate([halves[odd]] * 2, 1)
                        total = total + dot_tn(left, (right * mask).astype(BF16))
                    put.append(total)
                for tower in range(2):
                    rows = slice(tower * WINDOW, (tower + 1) * WINDOW)
                    own = slice(tower * LANES, (tower + 1) * LANES)
                    q_at = tower * dim + j * LANES
                    for part, block in enumerate(
                        (query_part[rows, q_at : q_at + LANES], put[0][rows, own], put[1][rows, own])
                    ):
                        flat[
                            tower,
                            pl.ds(2 * tiles + part * tiles + j, WINDOW, stride=3 * tiles),
                            :,
                        ] = block
            for tower in range(2):
                flat[tower, 0:tiles, :] = small[tower * tiles : (tower + 1) * tiles]

            @pl.when(device == 0)
            def _():
                for tower, copy in enumerate(copies):
                    copy.wait()
                    grads = grad_query[:, tower * dim : (tower + 1) * dim]
                    row = jnp.sum(dot_nt(grads, wq[tower]), 0, keepdims=True)
                    row = row + bias[tower : tower + 1, :]
                    for j in range(tiles):
                        flat[tower, tiles + j : tiles + j + 1, :] = row[
                            :, j * LANES : (j + 1) * LANES
                        ]

            start = device * plan.share
            at = start - plan.column(device) * plan.row
            shape = parts[0].shape
            index = (
                start
                + lax.broadcasted_iota(jnp.int32, shape, 0) * LANES
                + lax.broadcasted_iota(jnp.int32, shape, 1)
            )
            for tower in range(2):
                own = take_rows(flat.at[tower], at, plan.rows_out)
                store(tower, jnp.where(index < plan.out_at, own, parts[tower][...]))

    return body


class Fetch:
    def __init__(self, source, buf, sem, queue):
        self.ref, self.buf, self.queue, self.waited = source, buf, queue, False
        self.size = buf.dtype.itemsize
        for extent in buf.shape:
            self.size *= extent
        self.copy = pltpu.make_async_copy(source, buf, sem)

    def get(self):
        if not self.waited:
            self.queue.advance(self)
            self.copy.wait()
            self.waited = True
            self.queue.flying -= self.size
            self.queue.advance(None)
        return self.buf


class Queue:
    def __init__(self):
        self.waiting, self.flying = [], 0

    def advance(self, needed):
        while self.waiting and (
            needed in self.waiting or self.flying + self.waiting[0].size <= IN_FLIGHT
        ):
            fetch = self.waiting.pop(0)
            fetch.copy.start()
            self.flying += fetch.size


class Here:
    def __init__(self, ref):
        self.buf = self.ref = ref

    def get(self):
        return self.buf

    def push(self):
        pass


class Push:
    def __init__(self, ref, target, sem):
        self.ref, self.started = ref, False
        self.copy = pltpu.make_async_copy(ref, target, sem)

    def push(self):
        self.started = True
        self.copy.start()


def run(body, name, outs, scratch, scalars, arrays):
    smem = pl.BlockSpec(memory_space=pltpu.SMEM)
    hbm = pl.BlockSpec(memory_space=pltpu.HBM)
    vmem = pl.BlockSpec(memory_space=pltpu.VMEM)
    fetched = [(array, place) for array, place in arrays.values() if place in (Place.FAR, Place.FEW)]
    pushed = [(shape, kind) for shape, kind, place in outs.values() if place == Place.FAR]

    def kernel(*refs):
        at = 0

        def take(count):
            nonlocal at
            at += count
            return list(refs[at - count : at])

        scalar_refs, sources, targets = take(len(scalars)), take(len(arrays)), take(len(outs))
        in_bufs, out_bufs = take(len(fetched)), take(len(pushed))
        in_sems, out_sems = take(2)
        ins, results, fetches, pushes, queue = {}, {}, [], [], Queue()
        for source, (key, (unused, place)) in zip(sources, arrays.items()):
            if place in (Place.FAR, Place.FEW):
                sem = in_sems.at[len(fetches)]
                fetches.append(Fetch(source, in_bufs[len(fetches)], sem, queue))
                ins[key] = fetches[-1]
            else:
                ins[key] = Here(source)
        queue.waiting = list(fetches)
        queue.advance(None)
        for target, (key, (unused, unused, place)) in zip(targets, outs.items()):
            if place == Place.FAR:
                pushes.append(Push(out_bufs[len(pushes)], target, out_sems.at[len(pushes)]))
            results[key] = pushes[-1] if place == Place.FAR else Here(target)
        body(scalar_refs, ins, results, take(len(scratch)))
        for push in pushes:
            if not push.started:
                push.push()
        for fetch in fetches:
            fetch.get()
        for push in pushes:
            push.copy.wait()

    where = {Place.FAR: hbm, Place.FEW: hbm, Place.RAW: hbm, Place.AUTO: vmem, Place.SCALAR: smem}
    buffers = [
        (pltpu.SMEM if place == Place.FEW else pltpu.VMEM)(array.shape, array.dtype)
        for array, place in fetched
    ]
    buffers += [pltpu.VMEM(shape, kind) for shape, kind in pushed]
    buffers += [pltpu.SemaphoreType.DMA((max(len(group), 1),)) for group in (fetched, pushed)]
    pinned = [
        array if place == Place.AUTO else pltpu.with_memory_space_constraint(array, pltpu.HBM)
        for array, place in arrays.values()
    ]
    results = pl.pallas_call(
        kernel,
        name=name,
        out_shape=[
            (pltpu.HBM if place == Place.FAR else jax.ShapeDtypeStruct)(shape, kind)
            for shape, kind, place in outs.values()
        ],
        in_specs=[smem] * len(scalars) + [where[place] for unused, place in arrays.values()],
        out_specs=[where[place] for unused, unused, place in outs.values()],
        scratch_shapes=buffers + scratch,
        compiler_params=pltpu.CompilerParams(vmem_limit_bytes=LIMIT),
    )(*scalars, *pinned)
    return dict(zip(outs, results))


def exchange(array):
    return lax.all_to_all(array, "dp", split_axis=0, concat_axis=0, tiled=True)


def exchange_by_core(array, devices):
    groups = [list(range(core, devices, 2)) for core in range(2)]
    return lax.all_to_all(
        array, "dp", split_axis=0, concat_axis=0, tiled=True, axis_index_groups=groups
    )


def swap(array, devices):
    return lax.ppermute(array, "dp", [(i, i ^ 1) for i in range(devices)])


def compact(
    text_input, eot_index, image_input, ln1_gain, ln1_bias, w_qkv, w_attn_out, ln2_gain, ln2_bias,
    w_fc, w_fc_out, img_ln1_gain, img_ln1_bias, img_w_qkv, img_w_attn_out, img_ln2_gain,
    img_ln2_bias, img_w_fc, img_w_fc_out, final_gain, final_bias, text_proj, image_gain,
    image_bias, image_proj, logit_scale,
):
    caps, seq, dim = text_input.shape
    img_seq = image_input.shape[1]
    devices = lax.axis_size("dp")
    plan = Plan(dim, w_fc.shape[2], devices)
    heads = dim // HEAD_DIM
    count = devices * caps
    hidden = plan.hidden
    device = lax.axis_index("dp").astype(jnp.int32).reshape(1)
    text_input, image_input = text_input.swapaxes(0, 1), image_input.swapaxes(0, 1)
    totals = caps * seq, caps * img_seq
    chips = devices // 2
    width = heads * LANES

    first = {
        (K.X, 0): text_input, (K.X, 1): image_input,
        (K.GAIN, 0): ln1_gain, (K.BIAS, 0): ln1_bias,
        (K.GAIN, 1): img_ln1_gain, (K.BIAS, 1): img_ln1_bias,
        (K.W_QKV, 0): w_qkv, (K.W_QKV, 1): img_w_qkv,
    }
    second = {
        (K.W_OUT, 0): w_attn_out, (K.W_OUT, 1): img_w_attn_out,
        (K.GAIN2, 0): ln2_gain, (K.BIAS2, 0): ln2_bias,
        (K.GAIN2, 1): img_ln2_gain, (K.BIAS2, 1): img_ln2_bias,
        (K.W_FC, 0): w_fc, (K.W_FC_OUT, 0): w_fc_out,
        (K.W_FC, 1): img_w_fc, (K.W_FC_OUT, 1): img_w_fc_out,
        (K.HEAD_GAIN, 0): final_gain, (K.HEAD_BIAS, 0): final_bias,
        (K.HEAD_GAIN, 1): image_gain, (K.HEAD_BIAS, 1): image_bias,
        (K.PROJ, 0): text_proj, (K.PROJ, 1): image_proj,
    }

    def far(arrays):
        return {key: (array, Place.FAR) for key, array in arrays.items()}

    eot = {K.EOT: (eot_index, Place.FEW)}
    rows = run(
        front_body(plan),
        "front",
        {K.ROWS: ((chips, caps, 4 * dim), BF16, Place.AUTO)},
        [],
        [],
        eot | far(first),
    )[K.ROWS]
    mine = exchange_by_core(rows, devices)

    unused, pack_rows = pack_at(dim, hidden, caps)
    side_outs = {K.VALUES: ((devices, caps, width), BF16, Place.FAR)}
    middle_outs = {
        K.SEND: ((devices, caps, width + dim + LANES), BF16, Place.AUTO),
        K.ROWS: ((count, 4 * dim), BF16, Place.FAR),
    }
    for tower, total in enumerate(totals):
        side_outs |= {
            (K.NORMED, tower): ((total, dim), BF16, Place.FAR),
            (K.UNIT, tower): ((total, dim), BF16, Place.FAR),
            (K.PROBS, tower): ((heads * caps, total), F32, Place.FAR),
            (K.PACK, tower): ((pack_rows, dim), F32, Place.FAR),
        }
        middle_outs |= {
            (K.OWN, tower): ((2, caps, dim), F32, Place.FAR),
            (K.SCORES, tower): ((heads * caps, total), BF16, Place.FAR),
            (K.QUERY, tower): ((caps, dim), BF16, Place.FAR),
        }
    side = run(side_body(plan), "side", side_outs, [], [], eot | far(first) | far(second))
    values = exchange(side.pop(K.VALUES))
    mine, side[K.PACK, 0] = lax.optimization_barrier((mine, side[K.PACK, 0]))
    others = swap(mine, devices)

    late = {(K.W_QKV, 0): w_qkv, (K.W_QKV, 1): img_w_qkv}
    packs = {key: side[key] for key in ((K.PACK, 0), (K.PACK, 1))}
    middle = run(
        middle_body(plan),
        "middle",
        middle_outs,
        [pltpu.VMEM((chips, 2, caps, 4 * dim), BF16), pltpu.SemaphoreType.DMA((2,))],
        [device, logit_scale],
        {K.MINE: (mine, Place.AUTO), K.OTHERS: (others, Place.AUTO)}
        | far(second)
        | far(packs)
        | far(late)
        | far({(name, tower): side[name, tower] for name in (K.NORMED, K.PROBS, K.UNIT) for tower in (0, 1)}),
    )
    send, values = lax.optimization_barrier((middle[K.SEND], values))
    sent = exchange(send)

    share_rows = plan.rows_out
    region = (plan.total - plan.out_at) // LANES
    head_region = plan.head_total // LANES
    tail_ins = eot | far(first)
    tail_outs = {K.LOSS: ((1,), F32, Place.SCALAR), K.SCALE: ((1,), F32, Place.SCALAR)}
    for tower, length in enumerate((seq, img_seq)):
        for name, source in (
            (K.PROBS, side), (K.PACK, side), (K.OWN, middle), (K.SCORES, middle), (K.QUERY, middle)
        ):
            tail_ins |= far({(name, tower): source[name, tower]})
        tail_outs |= {
            (K.PART, tower): ((share_rows, LANES), F32, Place.FAR),
            (K.MIXED, tower): ((count, dim), BF16, Place.FAR),
            (K.INPUT, tower): ((length, caps, dim), F32, Place.FAR),
        }
    tail_outs |= {
        K.HEAD: ((plan.head_rows_out, LANES), F32, Place.FAR),
        K.WINDOWS: ((count, LANES), BF16, Place.FAR),
        K.QUERIES: ((count, 2 * dim), BF16, Place.FAR),
        K.BIAS: ((8, dim), F32, Place.FAR),
    }
    tail = run(
        tail_body(plan),
        "tail",
        tail_outs,
        [
            pltpu.VMEM((region + 2 * share_rows + 8, LANES), F32),
            pltpu.VMEM((head_region + plan.head_rows_out + 8, LANES), F32),
            pltpu.VMEM((totals[0], dim), F32),
            pltpu.VMEM((totals[1], dim), F32),
            pltpu.VMEM((count, hidden), BF16),
            pltpu.VMEM((8, dim), F32),
            pltpu.VMEM((count, hidden), F32),
            pltpu.VMEM((count, hidden), F32),
            pltpu.VMEM((count, hidden), BF16),
            pltpu.VMEM((count, hidden), BF16),
        ],
        [device, logit_scale],
        tail_ins | far({K.ROWS: middle[K.ROWS]} | second),
    )
    sent, tail[K.BIAS] = lax.optimization_barrier((sent, tail[K.BIAS]))
    swapped = swap(sent, devices)
    flat_rows = 2 * dim // LANES + max(WINDOW * plan.row, 2 * plan.row + share_rows * LANES) // LANES
    names = [(K.PART, 0), (K.PART, 1), K.WINDOWS, K.QUERIES, K.BIAS, (K.MIXED, 0), (K.MIXED, 1)]
    shares = run(
        last_body(plan),
        "last",
        {(K.SHARE, tower): ((1, plan.share), F32, Place.FAR) for tower in (0, 1)},
        [
            pltpu.VMEM((2, flat_rows // 8 * 8 + 16, LANES), F32),
            pltpu.VMEM((2, dim, dim), BF16),
            pltpu.VMEM((count, 2 * dim), BF16),
            pltpu.SemaphoreType.DMA((2,)),
        ],
        [device],
        far({name: tail[name] for name in names} | {K.VALUES: values.reshape(count, width)})
        | {key: (array.reshape(count, -1), Place.AUTO) for key, array in ((K.SENT, sent), (K.SWAPPED, swapped))}
        | {key: (array, Place.RAW) for key, array in late.items()},
    )

    def cut(array, size):
        return array.reshape(-1)[:size]

    return (
        tail[K.LOSS],
        tail[K.INPUT, 0].swapaxes(0, 1),
        tail[K.INPUT, 1].swapaxes(0, 1),
        shares[K.SHARE, 0],
        shares[K.SHARE, 1],
        cut(tail[K.HEAD], plan.head_share),
        tail[K.SCALE],
    )


def norm_apply(values, gain, bias):
    center = values - jnp.mean(values, -1, keepdims=True)
    spread = jnp.mean(center * center, -1, keepdims=True)
    return center * lax.rsqrt(spread + EPS) * gain + bias


def quick_gelu(values):
    return values * jax.nn.sigmoid(1.702 * values)


def unit_rows(values):
    return values * lax.rsqrt(jnp.sum(values * values, -1, keepdims=True) + UNIT_EPS)


def causal_mask(seq_len):
    row_pos = lax.broadcasted_iota(jnp.int32, (seq_len, seq_len), 0)
    col_pos = lax.broadcasted_iota(jnp.int32, (seq_len, seq_len), 1)
    return col_pos <= row_pos


def matmul(left, right):
    return jnp.dot(left, right, preferred_element_type=jnp.float32)


def inner_rows(left, right):
    return lax.dot_general(
        left, right, (((0,), (0,)), ((), ())), preferred_element_type=jnp.float32
    )


def outer_cols(left, right):
    return lax.dot_general(
        left, right, (((1,), (1,)), ((), ())), preferred_element_type=jnp.float32
    )


def layer_forward(stream, weights, causal):
    gain_one, bias_one, w_qkv, w_out, gain_two, bias_two, w_fc, w_fc_out = weights
    num_caps, seq_len, feat_dim = stream.shape
    num_heads = feat_dim // HEAD_DIM
    num_rows = num_caps * seq_len
    normed_one = (
        norm_apply(stream, gain_one, bias_one).astype(jnp.bfloat16).reshape(num_rows, feat_dim)
    )
    packed = (
        matmul(normed_one, w_qkv)
        .astype(jnp.bfloat16)
        .reshape(num_caps, seq_len, 3, num_heads, HEAD_DIM)
    )
    queries = packed[:, :, 0]
    key_rows = packed[:, :, 1]
    value_rows = packed[:, :, 2]
    raw_score = jnp.einsum("bqhd,bkhd->bhqk", queries, key_rows, preferred_element_type=jnp.float32)
    scores = raw_score * HEAD_DIM ** (-0.5)
    if causal:
        scores = jnp.where(causal_mask(seq_len), scores, MASKED)
    row_peak = jnp.max(scores, -1, keepdims=True)
    log_total = row_peak + jnp.log(jnp.sum(jnp.exp(scores - row_peak), -1, keepdims=True))
    attn_probs = jnp.exp(scores - log_total)
    probs_low = attn_probs.astype(jnp.bfloat16)
    mixed_rows = jnp.einsum(
        "bhqk,bkhd->bqhd", probs_low, value_rows, preferred_element_type=jnp.float32
    )
    mixed_rows = mixed_rows.astype(jnp.bfloat16).reshape(num_rows, feat_dim)
    middle = stream + matmul(mixed_rows, w_out).reshape(num_caps, seq_len, feat_dim)
    normed_two = (
        norm_apply(middle, gain_two, bias_two).astype(jnp.bfloat16).reshape(num_rows, feat_dim)
    )
    hidden = matmul(normed_two, w_fc)
    active = quick_gelu(hidden).astype(jnp.bfloat16)
    result = middle + matmul(active, w_fc_out).reshape(num_caps, seq_len, feat_dim)
    return (
        result,
        (normed_one, packed, attn_probs, probs_low, mixed_rows, middle, normed_two, hidden, active),
    )


def layer_backward(stream, weights, grad_out, causal):
    gain_one, bias_one, w_qkv, w_out, gain_two, bias_two, w_fc, w_fc_out = weights
    num_caps, seq_len, feat_dim = stream.shape
    num_heads = feat_dim // HEAD_DIM
    num_rows = num_caps * seq_len
    unused, kept = layer_forward(stream, weights, causal)
    normed_one, packed, attn_probs, probs_low, mixed_rows, middle, normed_two, hidden, active = kept
    grad_low = grad_out.reshape(num_rows, feat_dim).astype(jnp.bfloat16)
    grad_fc_out = inner_rows(active, grad_low)
    grad_active = outer_cols(grad_low, w_fc_out)
    unused_gelu, gelu_back = jax.vjp(quick_gelu, hidden)
    grad_hidden = gelu_back(grad_active)[0].astype(jnp.bfloat16)
    grad_fc = inner_rows(normed_two, grad_hidden)
    grad_normed_two = outer_cols(grad_hidden, w_fc)
    unused_two, norm_back_two = jax.vjp(norm_apply, middle, gain_two, bias_two)
    grad_mid_norm, grad_gain_two, grad_bias_two = norm_back_two(
        grad_normed_two.reshape(num_caps, seq_len, feat_dim)
    )
    grad_middle = grad_out + grad_mid_norm
    middle_low = grad_middle.reshape(num_rows, feat_dim).astype(jnp.bfloat16)
    grad_w_out = inner_rows(mixed_rows, middle_low)
    grad_mixed = (
        outer_cols(middle_low, w_out)
        .astype(jnp.bfloat16)
        .reshape(num_caps, seq_len, num_heads, HEAD_DIM)
    )
    queries = packed[:, :, 0]
    key_rows = packed[:, :, 1]
    value_rows = packed[:, :, 2]
    grad_values = jnp.einsum(
        "bhqk,bqhd->bkhd", probs_low, grad_mixed, preferred_element_type=jnp.float32
    )
    grad_probs = jnp.einsum(
        "bqhd,bkhd->bhqk", grad_mixed, value_rows, preferred_element_type=jnp.float32
    )
    row_inner = jnp.sum(attn_probs * grad_probs, -1, keepdims=True)
    grad_raw = (attn_probs * (grad_probs - row_inner) * HEAD_DIM ** (-0.5)).astype(jnp.bfloat16)
    grad_queries = jnp.einsum(
        "bhqk,bkhd->bqhd", grad_raw, key_rows, preferred_element_type=jnp.float32
    )
    grad_keys = jnp.einsum("bhqk,bqhd->bkhd", grad_raw, queries, preferred_element_type=jnp.float32)
    grad_packed = (
        jnp.stack([grad_queries, grad_keys, grad_values], 2)
        .astype(jnp.bfloat16)
        .reshape(num_rows, 3 * feat_dim)
    )
    grad_qkv = inner_rows(normed_one, grad_packed)
    grad_normed_one = outer_cols(grad_packed, w_qkv)
    unused_one, norm_back_one = jax.vjp(norm_apply, stream, gain_one, bias_one)
    grad_in_norm, grad_gain_one, grad_bias_one = norm_back_one(
        grad_normed_one.reshape(num_caps, seq_len, feat_dim)
    )
    grads_here = [
        grad_gain_one,
        grad_bias_one,
        grad_qkv,
        grad_w_out,
        grad_gain_two,
        grad_bias_two,
        grad_fc,
        grad_fc_out,
    ]
    return (grad_middle + grad_in_norm, grads_here)


def head_forward(features, gain, bias, proj):
    normed = norm_apply(features, gain, bias).astype(jnp.bfloat16)
    embedded = matmul(normed, proj)
    return (unit_rows(embedded), (normed, embedded))


def head_backward(features, gain, bias, proj, kept, grad_unit):
    normed, embedded = kept
    unused_unit, unit_back = jax.vjp(unit_rows, embedded)
    grad_embed = unit_back(grad_unit)[0].astype(jnp.bfloat16)
    grad_proj = inner_rows(normed, grad_embed)
    grad_normed = outer_cols(grad_embed, proj)
    unused_norm, norm_back = jax.vjp(norm_apply, features, gain, bias)
    grad_feat, grad_gain, grad_bias = norm_back(grad_normed)
    return (grad_feat, [grad_gain, grad_bias, grad_proj])


def plain_contrast(own_rows, other_rows, multiplier, start):
    logits = multiplier * outer_cols(own_rows, other_rows)
    row_peak = jnp.max(logits, -1, keepdims=True)
    log_total = row_peak + jnp.log(jnp.sum(jnp.exp(logits - row_peak), -1, keepdims=True))
    col_pos = lax.broadcasted_iota(jnp.int32, logits.shape, 1)
    target_pos = lax.broadcasted_iota(jnp.int32, logits.shape, 0) + start
    matched = (col_pos == target_pos).astype(jnp.float32)
    loss_sum = jnp.sum(log_total) - jnp.sum(matched * logits)
    grad_logits = 0.5 * (jnp.exp(logits - log_total) - matched)
    scale_part = jnp.sum(grad_logits * logits)
    return (loss_sum, scale_part, (multiplier * grad_logits).astype(jnp.bfloat16), log_total[:, 0])


def pack_flat(arrays, devices):
    flat = jnp.concatenate([array.reshape(-1) for array in arrays])
    padding = -flat.shape[0] % devices
    return jnp.concatenate([flat, jnp.zeros((padding,), jnp.float32)])


def plain(
    text_input,
    eot_index,
    image_input,
    ln1_gain,
    ln1_bias,
    w_qkv,
    w_attn_out,
    ln2_gain,
    ln2_bias,
    w_fc,
    w_fc_out,
    img_ln1_gain,
    img_ln1_bias,
    img_w_qkv,
    img_w_attn_out,
    img_ln2_gain,
    img_ln2_bias,
    img_w_fc,
    img_w_fc_out,
    final_gain,
    final_bias,
    text_proj,
    image_gain,
    image_bias,
    image_proj,
    logit_scale,
):
    num_caps, seq_len, feat_dim = text_input.shape
    devices = lax.axis_size("dp")
    all_caps = num_caps * devices
    start = lax.axis_index("dp") * num_caps
    depth = ln1_gain.shape[0]
    text_stack = (ln1_gain, ln1_bias, w_qkv, w_attn_out, ln2_gain, ln2_bias, w_fc, w_fc_out)
    image_stack = (
        img_ln1_gain,
        img_ln1_bias,
        img_w_qkv,
        img_w_attn_out,
        img_ln2_gain,
        img_ln2_bias,
        img_w_fc,
        img_w_fc_out,
    )

    def text_weights(layer_num):
        return tuple((array[layer_num] for array in text_stack))

    def image_weights(layer_num):
        return tuple((array[layer_num] for array in image_stack))

    stream = text_input.astype(jnp.float32)
    layer_num = 0
    text_saved = [stream]
    stream, unused = layer_forward(stream, text_weights(layer_num), True)
    pooled = jnp.take_along_axis(stream, eot_index[:, None, None], axis=1)[:, 0]
    picture = image_input.astype(jnp.float32)
    layer_num = 0
    image_saved = [picture]
    picture, unused = layer_forward(picture, image_weights(layer_num), False)
    image_pooled = picture[:, 0]
    text_unit, text_kept = head_forward(pooled, final_gain, final_bias, text_proj)
    image_unit, image_kept = head_forward(image_pooled, image_gain, image_bias, image_proj)
    image_low = image_unit.astype(jnp.bfloat16)
    text_low = text_unit.astype(jnp.bfloat16)
    image_all, text_all = (
        lax.all_gather(image_low, "dp", axis=0, tiled=True),
        lax.all_gather(text_low, "dp", axis=0, tiled=True),
    )
    multiplier = jnp.exp(logit_scale[0])
    loss_image, scale_image, grad_raw_it, unused_it = plain_contrast(
        image_low, text_all, multiplier, start
    )
    loss_text, scale_text, grad_raw_ti, unused_ti = plain_contrast(text_low, image_all, multiplier, start)
    spread_text = inner_rows(grad_raw_it, image_low)
    spread_image = inner_rows(grad_raw_ti, text_low)
    back_text, back_image = (
        lax.psum_scatter(spread_text, "dp", scatter_dimension=0, tiled=True),
        lax.psum_scatter(spread_image, "dp", scatter_dimension=0, tiled=True),
    )
    total, grad_scale = lax.psum((loss_image + loss_text, scale_image + scale_text), "dp")
    grad_image_unit = matmul(grad_raw_it, text_all) + back_image
    grad_text_unit = matmul(grad_raw_ti, image_all) + back_text
    grad_pooled, text_head_grads = head_backward(
        pooled, final_gain, final_bias, text_proj, text_kept, grad_text_unit
    )
    grad_image_pooled, image_head_grads = head_backward(
        image_pooled, image_gain, image_bias, image_proj, image_kept, grad_image_unit
    )
    head_flat = pack_flat(text_head_grads + image_head_grads, devices)
    image_flat = [None] * depth
    img_seq = image_input.shape[1]
    img_dim = image_input.shape[2]
    grad_picture = jnp.concatenate(
        [grad_image_pooled[:, None, :], jnp.zeros((num_caps, img_seq - 1, img_dim), jnp.float32)], 1
    )
    for layer_num in reversed(range(depth)):
        grad_picture, grads_here = layer_backward(
            image_saved[layer_num], image_weights(layer_num), grad_picture, False
        )
        image_flat[layer_num] = pack_flat(grads_here, devices)
    text_flat = [None] * depth
    selected = (
        lax.broadcasted_iota(jnp.int32, (num_caps, seq_len), 1) == eot_index[:, None]
    ).astype(jnp.float32)
    grad_stream = selected[:, :, None] * grad_pooled[:, None, :]
    for layer_num in reversed(range(depth)):
        grad_stream, grads_here = layer_backward(
            text_saved[layer_num], text_weights(layer_num), grad_stream, True
        )
        text_flat[layer_num] = pack_flat(grads_here, devices)
    text_share, image_share, head_share = (
        lax.psum_scatter(jnp.stack(text_flat), "dp", scatter_dimension=1, tiled=True),
        lax.psum_scatter(jnp.stack(image_flat), "dp", scatter_dimension=1, tiled=True),
        lax.psum_scatter(head_flat, "dp", scatter_dimension=0, tiled=True),
    )
    loss = (total / (2 * all_caps)).reshape(1)
    return (
        loss,
        grad_stream,
        grad_picture,
        text_share,
        image_share,
        head_share,
        grad_scale.reshape(1),
    )


def shards(*args):
    caps = args[0].shape[0] * lax.axis_size("dp")
    return compact(*args) if caps <= 512 else plain(*args)


def solution(mesh):
    return jax.shard_map(
        shards,
        mesh=mesh,
        in_specs=(
            P("dp", None, None),
            P("dp"),
            P("dp", None, None),
            P(),
            P(),
            P(),
            P(),
            P(),
            P(),
            P(),
            P(),
            P(),
            P(),
            P(),
            P(),
            P(),
            P(),
            P(),
            P(),
            P(),
            P(),
            P(),
            P(),
            P(),
            P(),
            P(),
        ),
        out_specs=(
            P(),
            P("dp", None, None),
            P("dp", None, None),
            P(None, "dp"),
            P(None, "dp"),
            P("dp"),
            P(),
        ),
        check_vma=False,
    )
```

```python
import enum

import jax
import jax.numpy as jnp
from jax import lax
from jax.experimental import pallas as pl
from jax.experimental.pallas import tpu as pltpu
from jax.sharding import PartitionSpec as P

HEAD_DIM = 64
LANES = 128

EPS = 1e-05
UNIT_EPS = 1e-06
MASKED = -1000000000.0
LIMIT = 44 * 2**20
F32 = jnp.float32
BF16 = jnp.bfloat16


class Place(enum.Enum):
    FAR = enum.auto()
    FEW = enum.auto()
    RAW = enum.auto()
    AUTO = enum.auto()
    SCALAR = enum.auto()


class K(enum.Enum):
    BIAS = enum.auto()
    BIAS2 = enum.auto()
    EOT = enum.auto()
    GAIN = enum.auto()
    GAIN2 = enum.auto()
    HEAD = enum.auto()
    HEAD_BIAS = enum.auto()
    HEAD_GAIN = enum.auto()
    INPUT = enum.auto()
    LOSS = enum.auto()
    MINE = enum.auto()
    MIXED = enum.auto()
    NORMED = enum.auto()
    OTHERS = enum.auto()
    OWN = enum.auto()
    PACK = enum.auto()
    PART = enum.auto()
    PROBS = enum.auto()
    PROJ = enum.auto()
    QUERIES = enum.auto()
    ROWS = enum.auto()
    SCALE = enum.auto()
    SCORES = enum.auto()
    SEND = enum.auto()
    SENT = enum.auto()
    SWAPPED = enum.auto()
    SHARE = enum.auto()
    UNIT = enum.auto()
    VALUES = enum.auto()
    W_FC = enum.auto()
    W_FC_OUT = enum.auto()
    W_OUT = enum.auto()
    W_QKV = enum.auto()
    WINDOWS = enum.auto()
    X = enum.auto()


def dot(left, right):
    return jnp.dot(left, right, preferred_element_type=F32)


def dot_nt(left, right):
    return lax.dot_general(left, right, (((1,), (1,)), ((), ())), preferred_element_type=F32)


def dot_tn(left, right):
    return lax.dot_general(left, right, (((0,), (0,)), ((), ())), preferred_element_type=F32)


def standard(values):
    center = values - jnp.mean(values, -1, keepdims=True)
    scale = lax.rsqrt(jnp.mean(center * center, -1, keepdims=True) + EPS)
    return center * scale, scale


def norm_back(grad, unit, scale, gain):
    scaled = grad * gain
    return scale * (
        scaled
        - jnp.mean(scaled, -1, keepdims=True)
        - unit * jnp.mean(scaled * unit, -1, keepdims=True)
    )


def head_masks(width):
    lane = lax.broadcasted_iota(jnp.int32, (1, width), 1)
    return [
        ((lane >= h * HEAD_DIM) & (lane < (h + 1) * HEAD_DIM)).astype(F32)
        for h in range(width // HEAD_DIM)
    ]


def spread(rows):
    return jnp.concatenate([rows * mask for mask in head_masks(rows.shape[1])], 0)


def collect(rows, caps):
    masks = head_masks(rows.shape[1])
    return sum(rows[h * caps : (h + 1) * caps] * mask for h, mask in enumerate(masks))


def picked_columns(caps, total, ends):
    cap = lax.broadcasted_iota(jnp.int32, (caps, 1), 0)
    at = cap
    for b in range(caps):
        at = jnp.where(cap == b, ends[b] * caps + b, at)
    column = lax.broadcasted_iota(jnp.int32, (caps, total), 1)
    chosen = jnp.where(column == at, 1.0, 0.0).astype(BF16)
    return chosen, column, at


class Plan:
    def __init__(self, dim, hidden, devices):
        self.dim, self.hidden, self.devices = dim, hidden, devices
        self.row = 3 * dim
        self.qkv_at = 2 * dim
        self.out_at = self.qkv_at + dim * self.row
        self.norm_at = self.out_at + dim * dim
        self.fc_at = self.norm_at + 2 * dim
        self.fc_out_at = self.fc_at + dim * hidden
        self.total = self.fc_out_at + hidden * dim
        self.share = -(-self.total // devices)
        self.head_total = 2 * (2 * dim + dim * dim)
        self.head_share = -(-self.head_total // devices)
        self.roots = -(-self.out_at // self.share)
        self.rows_out = -(-(self.share // LANES + 2) // 8) * 8
        self.head_rows_out = -(-(self.head_share // LANES + 2) // 8) * 8
        self.window = self.share // self.row + 2
        self.pad = -(-self.window // 8) * 8
        self.used = self.pad + self.window
        self.piece = LANES - self.used
        assert self.piece > 0 and -(-self.used // self.piece) < dim // HEAD_DIM
        assert self.total % devices == 0 and self.head_total % devices == 0

    def column(self, device):
        if isinstance(device, int):
            return min(max(device * self.share - self.qkv_at, 0) // self.row, self.dim - 1)
        return jnp.minimum(jnp.maximum(device * self.share - self.qkv_at, 0) // self.row, self.dim - 1)


def window_tiles(plan, text, image, device, caps):
    dim = text.shape[1]
    first = plan.column(device)
    lane = lax.broadcasted_iota(jnp.int32, (text.shape[0], LANES), 1)
    left = pltpu.roll(text, (dim - first) % dim, 1)[:, :LANES]
    right = pltpu.roll(image, (dim - first + plan.pad) % dim, 1)[:, :LANES]
    both = jnp.where(lane < plan.pad, left, right)
    heads = text.shape[0] // caps
    lane, last = lane[:caps], both[(heads - 1) * caps :]
    tiles = []
    for h in range(heads - 1):
        moved = pltpu.roll(last, (plan.used - h * plan.piece) % LANES, 1)
        tiles.append(jnp.where(lane < plan.used, both[h * caps : (h + 1) * caps], moved).astype(BF16))
    return jnp.concatenate(tiles, 1)


def last_head(plan, source, heads):
    lane = lax.broadcasted_iota(jnp.int32, (source.shape[0], LANES), 1)
    whole = jnp.zeros(lane.shape, F32)
    for h in range(-(-plan.used // plan.piece)):
        tile = source[:, h * LANES : (h + 1) * LANES].astype(F32)
        moved = pltpu.roll(tile, (LANES + h * plan.piece - plan.used) % LANES, 1)
        whole = jnp.where(lane >= h * plan.piece, moved, whole)
    return whole.astype(BF16)


def pack_windows(plan, target, text, image, caps, common):
    width = (text.shape[0] // caps - 1) * LANES
    held = plan.roots + plan.roots % 2

    def fill(device, core):
        target[device, :, :width] = window_tiles(plan, text, image, device, caps)
        if common is not None:
            target[device, :, width:] = common[core]

    if held <= 16:
        for device in range(held):
            fill(device, device % 2)
    else:

        @pl.loop(0, held // 2)
        def _(chip):
            for core in range(2):
                fill(2 * chip + core, core)


def clear_windows(plan, target):
    held = plan.roots + plan.roots % 2

    @pl.loop(held, target.shape[0])
    def _(device):
        target[device] = jnp.zeros(target.shape[1:], BF16)

    return slice(0, held), slice(held, target.shape[0])


def take_rows(source, at, count):
    row, lane_at = at // LANES, at % LANES
    lane = lax.broadcasted_iota(jnp.int32, (count, LANES), 1)
    mixed = jnp.where(
        lane >= lane_at, source[pl.ds(row, count), :], source[pl.ds(row + 1, count), :]
    )
    return pltpu.roll(mixed, lax.rem(LANES - lane_at, LANES), 1)


def put_tile(target, row, block):
    count, width = block.shape
    step = width // LANES
    for j in range(step):
        piece = block[:, j * LANES : (j + 1) * LANES]
        if count == 1:
            target[row + j : row + j + 1, :] = piece
        else:
            target[pl.ds(row + j, count, stride=step), :] = piece


def front_tower(tower, ins, picked, last):
    x = ins[K.X, tower].get()[...]
    seq, caps, dim = x.shape
    total = seq * caps
    heads = dim // HEAD_DIM
    source = x.reshape(total, dim)
    unit, unused = standard(source.astype(F32))
    yield
    gain, bias = ins[K.GAIN, tower].get()[...], ins[K.BIAS, tower].get()[...]
    normed = (unit * gain + bias).astype(BF16)
    chosen, column, pick_at = picked_columns(caps, total, picked)
    last_at = pick_at
    if last is not picked:
        unused, unused, last_at = picked_columns(caps, total, last)
    pooled = dot(chosen, source)
    yield
    pooled_unit, unused = standard(pooled)
    pooled_normed = (pooled_unit * gain + bias).astype(BF16)
    w_ref = ins[K.W_QKV, tower].get()
    query = dot(pooled_normed, w_ref[0, :, :dim]).astype(BF16).astype(F32)
    yield
    through_keys = dot_nt(spread(query).astype(BF16), w_ref[0, :, dim : 2 * dim])
    yield
    scores = dot_nt(through_keys.astype(BF16), normed) * HEAD_DIM ** (-0.5)
    yield
    cap = lax.broadcasted_iota(jnp.int32, (caps, 1), 0)
    seen = jnp.where((lax.rem(column, caps) == cap) & (column <= last_at), 1.0, 0.0)
    seen = jnp.concatenate([seen] * heads, 0) > 0.5
    peak = jnp.max(jnp.where(seen, scores, MASKED), -1, keepdims=True)
    sums = jnp.sum(jnp.where(seen, jnp.exp(scores - peak), 0.0), -1, keepdims=True)
    probs = jnp.where(seen, jnp.exp(scores - (peak + jnp.log(sums))), 0.0)
    yield
    values = dot(probs.astype(BF16), normed)
    yield
    mixed = collect(dot(values.astype(BF16), w_ref[0, :, 2 * dim :]), caps).astype(BF16)
    return pooled, mixed, (normed, unit, probs, query, through_keys, values, chosen)


def attended_towers(ins):
    eot = ins[K.EOT].get()
    caps = eot.shape[0]
    seq = ins[K.X, 1].buf.shape[0]
    ends = [eot[b] for b in range(caps)]
    views = (ends, ends), ([0] * caps, [seq - 1] * caps)
    return run_together([front_tower(tower, ins, *views[tower]) for tower in range(2)])


def front_body(plan):
    def body(scalars, ins, outs, scratch):
        payload = []
        for pooled, mixed, unused in attended_towers(ins):
            payload += [pooled.astype(BF16), mixed]
        payload = jnp.concatenate(payload, 1)
        rows = outs[K.ROWS].ref

        @pl.loop(0, rows.shape[0])
        def _(chip):
            rows[chip] = payload

    return body


def pack_at(dim, hidden, caps):
    heads = dim // HEAD_DIM
    sizes = [heads * caps, heads * caps, caps, caps, caps, caps, caps, caps * hidden // dim]
    places, at = [], 0
    for size in sizes:
        places.append(slice(at, at + size))
        at += size
    return places, at


def weights_of(tower, ins):
    names = K.W_OUT, K.GAIN2, K.BIAS2, K.W_FC, K.W_FC_OUT, K.HEAD_GAIN, K.HEAD_BIAS, K.PROJ
    return [ins[name, tower] for name in names]


def side_body(plan):
    def body(scalars, ins, outs, scratch):
        dim, hidden = plan.dim, plan.hidden
        caps = ins[K.EOT].buf.shape[0]
        places, unused = pack_at(dim, hidden, caps)
        towers = attended_towers(ins)
        clear_windows(plan, outs[K.VALUES].ref)
        pack_windows(plan, outs[K.VALUES].ref, towers[0][2][5], towers[1][2][5], caps, None)
        outs[K.VALUES].push()
        kept = [], []
        for tower, (pooled, mixed, saved) in enumerate(towers):
            normed, unit, probs, query, through_keys, values, chosen = saved
            unit = unit.astype(BF16)
            for name, value in ((K.NORMED, normed), (K.UNIT, unit), (K.PROBS, probs)):
                outs[name, tower].ref[...] = value
                outs[name, tower].push()
            small = [through_keys, dot(probs.astype(BF16), unit), dot(chosen, unit), query]
            for place, value in zip(places, small):
                outs[K.PACK, tower].ref[place, :] = value
        run_together(
            [
                tower_forward(pooled, mixed, weights_of(tower, ins), kept[tower], None, None)
                for tower, (pooled, mixed, unused) in enumerate(towers)
            ]
        )
        for tower in range(2):
            pack = outs[K.PACK, tower]
            for place, value in zip(places[4:], kept[tower][:3]):
                pack.ref[place, :] = value
            for j in range(hidden // dim):
                at = places[7].start + j * caps
                pack.ref[at : at + caps, :] = kept[tower][3][:, j * dim : (j + 1) * dim]
            pack.push()

    return body


def run_together(steps):
    results = [None] * len(steps)
    live = list(range(len(steps)))
    while live:
        for index in list(live):
            try:
                next(steps[index])
            except StopIteration as stop:
                results[index] = stop.value
                live.remove(index)
    return results


def chunks(width):
    step = 512 if width % 512 == 0 else width
    return [slice(at, at + step) for at in range(0, width, step)]


def gate_slope(hidden):
    gate = jax.nn.sigmoid(1.702 * hidden)
    return gate + 1.702 * hidden * gate * (1.0 - gate)


def unit_rows_of(embed):
    length = lax.rsqrt(jnp.sum(embed * embed, -1, keepdims=True) + UNIT_EPS)
    return embed * length, length


def tower_forward(pooled, mixed, weights, kept, hidden_ref, active_ref):
    w_out, gain, bias, w_fc, w_fc_out, head_gain, head_bias, proj = weights
    middle = pooled + dot(mixed, w_out.get()[0])
    yield
    unit, unused = standard(middle)
    normed = (unit * gain.get()[...] + bias.get()[...]).astype(BF16)
    yield
    result = middle
    w_fc = w_fc.get()
    every = []
    for cols in chunks(w_fc.shape[2]):
        hidden = dot(normed, w_fc[0, :, cols])
        active = (hidden * jax.nn.sigmoid(1.702 * hidden)).astype(BF16)
        every.append(hidden)
        if hidden_ref is not None:
            hidden_ref[:, cols] = hidden
            active_ref[:, cols] = active
        result = result + dot(active, w_fc_out.get()[0, cols, :])
        yield
    head_unit, unused = standard(result)
    head_in = (head_unit * head_gain.get()[...][None] + head_bias.get()[...][None]).astype(BF16)
    embed = dot(head_in, proj.get()[...])
    yield
    if kept is not None:
        kept += [middle, result, embed]
        if hidden_ref is None:
            kept.append(jnp.concatenate(every, 1))
    return unit_rows_of(embed)[0].astype(BF16)


def log_sum(logits, axis):
    peak = jnp.max(logits, axis, keepdims=True)
    return peak + jnp.log(jnp.sum(jnp.exp(logits - peak), axis, keepdims=True))


def unit_gradient(multiplier, logits, own_total, other_total, matched, other):
    target = jnp.where(matched, 1.0, 0.0)
    own = 0.5 * multiplier * (jnp.exp(logits - own_total) - target)
    cross = 0.5 * multiplier * (jnp.exp(logits - other_total) - target)
    return dot(own.astype(BF16), other) + dot(cross.astype(BF16), other)


def embed_back(grad_unit, embed):
    unit_embed, length = unit_rows_of(embed)
    along = jnp.sum(unit_embed * grad_unit, -1, keepdims=True)
    return (length * (grad_unit - unit_embed * along)).astype(BF16)


def tower_backward(grad_embed, middle, result, hidden, weights, keep_hidden):
    w_out, gain, bias, w_fc, w_fc_out, head_gain, head_bias, proj = weights
    grad_head = dot_nt(grad_embed, proj.get()[...])
    yield
    head_unit, head_scale = standard(result)
    grad_result = norm_back(grad_head, head_unit, head_scale, head_gain.get()[...][None])
    grad_out = grad_result.astype(BF16)
    yield
    w_fc, w_fc_out = w_fc.get(), w_fc_out.get()
    grad_normed = 0.0
    for cols in chunks(w_fc.shape[2]):
        grad_active = dot_nt(grad_out, w_fc_out[0, cols, :])
        grad_hidden = (grad_active * gate_slope(hidden[:, cols])).astype(BF16)
        if keep_hidden is not None:
            keep_hidden[:, cols] = grad_hidden
        grad_normed = grad_normed + dot_nt(grad_hidden, w_fc[0, :, cols])
        yield
    unit, scale = standard(middle)
    grad_middle = grad_result + norm_back(grad_normed, unit, scale, gain.get()[...])
    yield
    grad_mixed = dot_nt(grad_middle.astype(BF16), w_out.get()[0]).astype(BF16)
    yield
    return grad_head, head_unit, grad_out, grad_normed, unit, grad_middle, grad_mixed


def own_steps(plan, tower, units, multiplier, own_at, ins, outs):
    mine, other = units[tower], units[1 - tower]
    own_out, scores_out = outs[K.OWN, tower], outs[K.SCORES, tower]
    dim = plan.dim
    caps = scores_out.ref.shape[0] * HEAD_DIM // dim
    places, unused = pack_at(dim, plan.hidden, caps)
    other_total = log_sum(multiplier * dot_nt(mine, other), 0)
    yield
    pack = ins[K.PACK, tower].get()
    embed = pack[places[6], :]
    logits = multiplier * dot_nt(unit_rows_of(embed)[0].astype(BF16), other)
    matched = lax.broadcasted_iota(jnp.int32, logits.shape, 1) == own_at + lax.broadcasted_iota(
        jnp.int32, logits.shape, 0
    )
    grad_unit = unit_gradient(multiplier, logits, log_sum(logits, 1), other_total, matched, other)
    yield
    hidden_at = places[7].start
    hidden = jnp.concatenate(
        [pack[hidden_at + j * caps : hidden_at + (j + 1) * caps, :] for j in range(plan.hidden // dim)], 1
    )
    done = yield from tower_backward(
        embed_back(grad_unit, embed), pack[places[4], :], pack[places[5], :], hidden,
        weights_of(tower, ins), None,
    )
    grad_middle, grad_mixed = done[5], done[6].astype(F32)
    own_out.ref[:caps, :] = grad_middle
    w_ref = ins[K.W_QKV, tower].get()
    through_values = dot_nt(spread(grad_mixed).astype(BF16), w_ref[0, :, 2 * dim :])
    own_out.ref[2 * caps :, :] = through_values
    yield
    normed = ins[K.NORMED, tower].get()[...]
    grad_probs = dot_nt(through_values.astype(BF16), normed)
    yield
    probs = ins[K.PROBS, tower].get()[...]
    inner = jnp.sum(probs * grad_probs, -1, keepdims=True)
    grad_scores = (probs * (grad_probs - inner) * HEAD_DIM ** (-0.5)).astype(BF16)
    scores_out.ref[...] = grad_scores
    scores_out.push()
    yield
    spread_keys = dot(grad_scores, normed)
    yield
    grad_query = collect(dot(spread_keys.astype(BF16), w_ref[0, :, dim : 2 * dim]), caps).astype(BF16)
    yield
    units = pack[places[0], :] * dot(grad_scores, ins[K.UNIT, tower].get()[...])
    yield
    through_query = dot_nt(grad_query, w_ref[0, :, :dim])
    own_out.ref[caps : 2 * caps, :] = through_query
    own_out.push()
    units = units + through_values * pack[places[1], :]
    gain_part = jnp.sum(units, 0, keepdims=True) + jnp.sum(
        through_query * pack[places[2], :], 0, keepdims=True
    )
    bias_part = jnp.sum(through_values, 0, keepdims=True) + jnp.sum(through_query, 0, keepdims=True)
    return spread_keys, grad_query, (gain_part, bias_part)


def forward_pair(plan, rows, ins, kept, hidden, active):
    dim = plan.dim
    return run_together(
        [
            tower_forward(
                rows[:, 2 * tower * dim : (2 * tower + 1) * dim].astype(F32),
                rows[:, (2 * tower + 1) * dim : (2 * tower + 2) * dim],
                weights_of(tower, ins), kept[tower], hidden[tower], active[tower],
            )
            for tower in range(2)
        ]
    )


def row_copies(scalars, ins, scratch):
    core = scalars[0][0] % 2
    return [
        pltpu.make_async_copy(ins[name].ref, scratch[0].at[:, at], scratch[1].at[i])
        for i, (name, at) in enumerate(((K.MINE, core), (K.OTHERS, 1 - core)))
    ]


def join_rows(scalars, ins, scratch):
    for copy in row_copies(scalars, ins, scratch):
        copy.start()


def middle_body(plan):
    def body(scalars, ins, outs, scratch):
        at_ref, scale_ref = scalars
        rows_ref, sems = scratch
        dim = plan.dim
        device = at_ref[0]
        caps, wide = rows_ref.shape[2:]
        held, others = clear_windows(plan, outs[K.SEND].ref)
        outs[K.SEND].push_part(others)
        for copy in row_copies(scalars, ins, scratch):
            copy.wait()
        rows = rows_ref[...].reshape(plan.devices * caps, wide)
        outs[K.ROWS].ref[...] = rows
        outs[K.ROWS].push()
        units = forward_pair(plan, rows, ins, (None, None), (None, None), (None, None))
        multiplier = jnp.exp(jnp.full((1, 1), scale_ref[0], F32))
        own_at = device * caps
        parts = run_together(
            [own_steps(plan, tower, units, multiplier, own_at, ins, outs) for tower in range(2)]
        )
        tiles = dim // LANES
        common = []
        for unused, query, sums in parts:
            small = [row[:, j * LANES : (j + 1) * LANES] for row in sums for j in range(tiles)]
            small.append(jnp.zeros((caps - 2 * tiles, LANES), F32))
            common.append(jnp.concatenate([query, jnp.concatenate(small, 0).astype(BF16)], 1))
        keys_t, keys_i = parts[0][0], parts[1][0]
        pack_windows(plan, outs[K.SEND].ref, keys_t, keys_i, caps, common)
        outs[K.SEND].push_part(held)

    return body


def late_weights(ins, scratch):
    parts, sems = scratch[-2:]
    dim = parts.shape[1]
    return [
        pltpu.make_async_copy(
            ins[K.W_QKV, tower].ref.at[0, :, pl.ds(0, dim)], parts.at[tower], sems.at[tower]
        )
        for tower in range(2)
    ]


def tail_ahead(plan):
    def ahead(scalars, ins, scratch):
        @pl.when(scalars[0][0] < plan.roots)
        def _():
            for copy in late_weights(ins, scratch):
                copy.start()

    return ahead


def tail_body(plan):
    def body(scalars, ins, outs, scratch):
        at_ref, scale_ref = scalars
        dim, hidden_dim = plan.dim, plan.hidden
        loss_ref, scale_grad_ref = outs[K.LOSS].ref, outs[K.SCALE].ref
        flat, flat_head, wide_t, wide_i, small, hiddens, actives, hidden_grads, late, unused = scratch
        device = at_ref[0]
        eot = ins[K.EOT].get()
        caps = eot.shape[0]
        ends = [eot[b] for b in range(caps)]
        places, unused = pack_at(dim, hidden_dim, caps)
        multiplier = jnp.exp(jnp.full((1, 1), scale_ref[0], F32))

        def input_gradient(tower, picked, wide):
            x, gain = ins[K.X, tower].get(), ins[K.GAIN, tower].get()
            seq = x.shape[0]
            unit, scale = standard(x[...].reshape(seq * caps, dim).astype(F32))
            yield
            probs, pack, own, scores = (
                ins[name, tower].get() for name in (K.PROBS, K.PACK, K.OWN, K.SCORES)
            )
            left = jnp.concatenate([scores[...], probs[...].astype(BF16)], 0)
            right = jnp.concatenate([pack[places[0], :], own[2 * caps :, :]], 0).astype(BF16)
            wide[...] = dot_tn(left, right)
            yield
            for b in range(caps):
                at = picked[b] * caps + b
                wide[pl.ds(at, 1), :] = wide[pl.ds(at, 1), :] + own[caps + b : caps + b + 1, :]
            wide[...] = norm_back(wide[...], unit, scale, gain[...])
            yield
            for b in range(caps):
                at = picked[b] * caps + b
                wide[pl.ds(at, 1), :] = wide[pl.ds(at, 1), :] + own[b : b + 1, :]
            outs[K.INPUT, tower].ref[...] = wide[...].reshape(seq, caps, dim)
            outs[K.INPUT, tower].push()

        run_together([input_gradient(0, ends, wide_t), input_gradient(1, [0] * caps, wide_i)])

        rows = ins[K.ROWS].get()[...]
        count = rows.shape[0]
        kept = [], []
        units = forward_pair(plan, rows, ins, kept, hiddens, actives)
        embeds = [items[2] for items in kept]
        logits = multiplier * dot_nt(units[1], units[0])
        matched = lax.broadcasted_iota(jnp.int32, logits.shape, 1) == lax.broadcasted_iota(
            jnp.int32, logits.shape, 0
        )
        row_total, column_total = log_sum(logits, 1), log_sum(logits, 0)
        target = jnp.where(matched, 1.0, 0.0)
        by_row = 0.5 * (jnp.exp(logits - row_total) - target)
        by_column = 0.5 * (jnp.exp(logits - column_total) - target)
        total = jnp.sum(row_total) + jnp.sum(column_total) - 2.0 * jnp.sum(target * logits)
        loss_ref[0] = total / (2 * count)
        scale_grad_ref[0] = jnp.sum((by_row + by_column) * logits)
        by_row = (multiplier * by_row).astype(BF16)
        by_column = (multiplier * by_column).astype(BF16)
        grad_units = (
            dot_tn(by_row, units[1]) + dot_tn(by_column, units[1]),
            dot(by_row, units[0]) + dot(by_column, units[0]),
        )

        grad_embeds = [embed_back(grad_units[tower], embeds[tower]) for tower in range(2)]
        backs = run_together(
            [
                tower_backward(
                    grad_embeds[tower], kept[tower][0], kept[tower][1], hiddens[tower],
                    weights_of(tower, ins), hidden_grads[tower],
                )
                for tower in range(2)
            ]
        )

        mixed_grads = []
        start, head_start = device * plan.share, device * plan.head_share
        front = plan.rows_out
        half = plan.head_total // 2
        for tower in range(2):
            weights = weights_of(tower, ins)
            gain, bias, head_gain, head_bias = (weights[j] for j in (1, 2, 5, 6))
            active, hidden_grad = actives[tower], hidden_grads[tower]
            grad_embed, done = grad_embeds[tower], backs[tower]
            grad_head, head_unit, grad_out, grad_normed, unit, grad_middle, grad_mixed = done
            mixed_grads.append(grad_mixed)
            middle_low = grad_middle.astype(BF16)
            normed = (unit * gain.get()[...] + bias.get()[...]).astype(BF16)
            head_in = head_unit * head_gain.get()[...][None] + head_bias.get()[...][None]
            head_in = head_in.astype(BF16)
            small[0:1, :] = jnp.sum(grad_normed * unit, 0, keepdims=True)
            small[1:2, :] = jnp.sum(grad_normed, 0, keepdims=True)
            small[2:3, :] = jnp.sum(grad_head * head_unit, 0, keepdims=True)
            small[3:4, :] = jnp.sum(grad_head, 0, keepdims=True)
            mixed = rows[:, (2 * tower + 1) * dim : (2 * tower + 2) * dim]

            def when_held(at, size, store):
                @pl.when((at < start + plan.share) & (at + size > start))
                def _():
                    store(front + (at - plan.out_at) // LANES)

            def when_kept(at, size, store):
                at = at + tower * half

                @pl.when((at < head_start + plan.head_share) & (at + size > head_start))
                def _():
                    store(at // LANES)

            def products(when, target, at, left, right):
                for t in range(left.shape[1] // LANES):
                    cols = slice(t * LANES, (t + 1) * LANES)
                    when(
                        at + t * LANES * right.shape[1],
                        LANES * right.shape[1],
                        lambda row: put_tile(target, row, dot_tn(left[:, cols], right[...])),
                    )

            def row_of(when, target, at, index):
                when(at, dim, lambda row: put_tile(target, row, small[index : index + 1, :]))

            products(when_held, flat, plan.out_at, mixed, middle_low)
            row_of(when_held, flat, plan.norm_at, 0)
            row_of(when_held, flat, plan.norm_at + dim, 1)
            products(when_held, flat, plan.fc_at, normed, hidden_grad)
            products(when_held, flat, plan.fc_out_at, active, grad_out)
            at = jnp.maximum(start - plan.out_at + front * LANES, 0)
            outs[K.PART, tower].ref[...] = take_rows(flat, at, plan.rows_out)
            outs[K.PART, tower].push()
            row_of(when_kept, flat_head, 0, 2)
            row_of(when_kept, flat_head, dim, 3)
            products(when_kept, flat_head, 2 * dim, head_in, grad_embed)

        outs[K.HEAD].ref[...] = take_rows(flat_head, head_start, plan.head_rows_out)
        outs[K.HEAD].push()

        query_t, query_i = late_weights(ins, scratch)
        values = ins[K.VALUES].get()

        @pl.when(device < plan.roots)
        def _():
            query_t.wait()
            query_i.wait()
            first = plan.column(device)
            lane = lax.broadcasted_iota(jnp.int32, (count, LANES), 1)
            picked_rows = []
            for tower in range(2):
                gain, bias = ins[K.GAIN, tower].get(), ins[K.BIAS, tower].get()
                pooled = rows[:, 2 * tower * dim : (2 * tower + 1) * dim].astype(F32)
                unit, unused = standard(pooled)
                normed = unit * gain[...] + bias[...]
                outs[K.QUERIES].ref[:, tower * dim : (tower + 1) * dim] = dot(
                    normed.astype(BF16), late[tower]
                ).astype(BF16)
                shift = lax.rem(dim - first + tower * plan.pad, dim)
                picked_rows.append(pltpu.roll(normed, shift, 1)[:, :LANES])
            end = last_head(plan, values, dim // HEAD_DIM)
            for j in range(dim // LANES):
                cols = slice(j * LANES, (j + 1) * LANES)
                block = window_product(plan, values, end, mixed_grads, (0, 0), j)
                for tower in range(2):
                    at = tower * plan.pad
                    outs[K.VALUES].ref[tower, :, cols] = block[
                        at : at + plan.pad, tower * LANES : (tower + 1) * LANES
                    ]
            outs[K.WINDOWS].ref[...] = jnp.where(lane < plan.pad, picked_rows[0], picked_rows[1]).astype(BF16)

    return body


def window_product(plan, source, end, factors, offsets, j):
    lane = lax.broadcasted_iota(jnp.int32, (1, 2 * LANES), 1) % LANES
    right = [factor[:, at + j * LANES : at + (j + 1) * LANES] for factor, at in zip(factors, offsets)]
    right = jnp.concatenate(right, 1).astype(F32)
    total = 0.0
    for h in (2 * j, 2 * j + 1):
        left = end if (h + 1) * HEAD_DIM == plan.dim else source[:, h * LANES : (h + 1) * LANES]
        mine = (lane // HEAD_DIM == h % 2).astype(F32)
        total = total + dot_tn(left, (right * mine).astype(BF16))
    return total


def last_body(plan):
    def body(scalars, ins, outs, scratch):
        (at_ref,) = scalars
        flat, grad_query = scratch
        dim = plan.dim
        heads = dim // HEAD_DIM
        tiles = dim // LANES
        device = at_ref[0]
        parts = [ins[K.PART, tower].get() for tower in range(2)]

        def store(tower, block):
            line = outs[K.SHARE, tower].ref
            line[...] = block.reshape(1, block.shape[0] * LANES)[:, : plan.share]

        @pl.when(device >= plan.roots)
        def _():
            for tower in range(2):
                store(tower, parts[tower][...])

        names = K.SENT, K.SWAPPED, K.WINDOWS, K.QUERIES, K.VALUES
        sent_ref, swapped, windows, queries, value_part = (
            ins[name].get() for name in names
        )

        @pl.when(device < plan.roots)
        def _():
            at_query = (heads - 1) * LANES
            count = sent_ref.shape[0]
            caps = count // plan.devices
            for core in range(2):

                @pl.when(device % 2 == core)
                def _():
                    received = sent_ref[:, at_query:], swapped[...]
                    for tower, values in enumerate(received if core == 0 else received[::-1]):
                        grad_query[:, tower * dim : (tower + 1) * dim] = values[:, :dim]
                        small = values[:, dim:].astype(F32).reshape(plan.devices, caps, LANES)
                        flat[tower, : 2 * tiles, :] = jnp.sum(small, 0)[: 2 * tiles]

            query_part = dot_tn(windows[...], grad_query[...])
            end = last_head(plan, sent_ref, heads)
            for j in range(tiles):
                put = window_product(plan, sent_ref, end, (queries, queries), (0, dim), j)
                for tower in range(2):
                    rows = slice(tower * plan.pad, (tower + 1) * plan.pad)
                    own = slice(tower * LANES, (tower + 1) * LANES)
                    q_at = tower * dim + j * LANES
                    for part, block in enumerate(
                        (
                            query_part[rows, q_at : q_at + LANES],
                            put[rows, own],
                            value_part[tower, :, j * LANES : (j + 1) * LANES],
                        )
                    ):
                        flat[
                            tower,
                            pl.ds(2 * tiles + part * tiles + j, plan.pad, stride=3 * tiles),
                            :,
                        ] = block
            start = device * plan.share
            at = start - plan.column(device) * plan.row
            shape = parts[0].shape
            index = (
                start
                + lax.broadcasted_iota(jnp.int32, shape, 0) * LANES
                + lax.broadcasted_iota(jnp.int32, shape, 1)
            )
            for tower in range(2):
                own = take_rows(flat.at[tower], at, plan.rows_out)
                store(tower, jnp.where(index < plan.out_at, own, parts[tower][...]))

    return body


class Fetch:
    def __init__(self, source, buf, sem, group):
        self.ref, self.buf, self.group = source, buf, group
        self.copy = pltpu.make_async_copy(source, buf, sem)
        group.members.append(self)

    def get(self):
        self.group.wait()
        return self.buf


class Group:
    def __init__(self):
        self.members, self.waited = [], False

    def wait(self):
        if not self.waited:
            self.waited = True
            for fetch in self.members:
                fetch.copy.wait()


class Here:
    def __init__(self, ref):
        self.buf = self.ref = ref

    def get(self):
        return self.buf

    def push(self):
        pass


class Push:
    def __init__(self, ref, target, sem):
        self.ref, self.target, self.sem, self.started = ref, target, sem, False
        self.copy = pltpu.make_async_copy(ref, target, sem)

    def push(self):
        self.started = True
        self.copy.start()

    def push_part(self, part):
        self.started = True
        pltpu.make_async_copy(self.ref.at[part], self.target.at[part], self.sem).start()


def run(body, name, outs, scratch, scalars, arrays, ahead=None):
    smem = pl.BlockSpec(memory_space=pltpu.SMEM)
    hbm = pl.BlockSpec(memory_space=pltpu.HBM)
    vmem = pl.BlockSpec(memory_space=pltpu.VMEM)
    groups = arrays
    arrays = {key: value for group in groups for key, value in group.items()}
    fetched = [(array, place) for array, place in arrays.values() if place in (Place.FAR, Place.FEW)]
    pushed = [(shape, kind) for shape, kind, place in outs.values() if place == Place.FAR]

    def kernel(*refs):
        at = 0

        def take(count):
            nonlocal at
            at += count
            return list(refs[at - count : at])

        scalar_refs, sources, targets = take(len(scalars)), take(len(arrays)), take(len(outs))
        in_bufs, out_bufs = take(len(fetched)), take(len(pushed))
        in_sems, out_sems = take(2)
        ins, results, fetches, pushes = {}, {}, [], []
        sources = iter(sources)
        chain = [Group() for unused in groups]
        for group, together in zip(groups, chain):
            for (key, (unused, place)), source in zip(group.items(), sources):
                if place in (Place.FAR, Place.FEW):
                    sem = in_sems.at[len(fetches)]
                    fetches.append(Fetch(source, in_bufs[len(fetches)], sem, together))
                    ins[key] = fetches[-1]
                else:
                    ins[key] = Here(source)
        for target, (key, (unused, unused, place)) in zip(targets, outs.items()):
            if place == Place.FAR:
                pushes.append(Push(out_bufs[len(pushes)], target, out_sems.at[len(pushes)]))
            results[key] = pushes[-1] if place == Place.FAR else Here(target)
        own_scratch = take(len(scratch))
        if ahead is not None:
            ahead(scalar_refs, ins, own_scratch)
        for fetch in fetches:
            fetch.copy.start()
        body(scalar_refs, ins, results, own_scratch)
        for push in pushes:
            if not push.started:
                push.push()
        for fetch in fetches:
            fetch.get()
        for push in pushes:
            push.copy.wait()

    where = {Place.FAR: hbm, Place.FEW: hbm, Place.RAW: hbm, Place.AUTO: vmem, Place.SCALAR: smem}
    buffers = [
        (pltpu.SMEM if place == Place.FEW else pltpu.VMEM)(array.shape, array.dtype)
        for array, place in fetched
    ]
    buffers += [pltpu.VMEM(shape, kind) for shape, kind in pushed]
    buffers += [pltpu.SemaphoreType.DMA((max(len(group), 1),)) for group in (fetched, pushed)]
    pinned = [
        array if place == Place.AUTO else pltpu.with_memory_space_constraint(array, pltpu.HBM)
        for array, place in arrays.values()
    ]
    results = pl.pallas_call(
        kernel,
        name=name,
        out_shape=[
            (pltpu.HBM if place == Place.FAR else jax.ShapeDtypeStruct)(shape, kind)
            for shape, kind, place in outs.values()
        ],
        in_specs=[smem] * len(scalars) + [where[place] for unused, place in arrays.values()],
        out_specs=[where[place] for unused, unused, place in outs.values()],
        scratch_shapes=buffers + list(scratch),
        compiler_params=pltpu.CompilerParams(vmem_limit_bytes=LIMIT),
    )(*scalars, *pinned)
    return dict(zip(outs, results))


def exchange(array):
    return lax.all_to_all(array, "dp", split_axis=0, concat_axis=0, tiled=True)


def exchange_by_core(array, devices):
    groups = [list(range(core, devices, 2)) for core in range(2)]
    return lax.all_to_all(
        array, "dp", split_axis=0, concat_axis=0, tiled=True, axis_index_groups=groups
    )


def swap(array, devices):
    return lax.ppermute(array, "dp", [(i, i ^ 1) for i in range(devices)])


def compact(
    text_input, eot_index, image_input, ln1_gain, ln1_bias, w_qkv, w_attn_out, ln2_gain, ln2_bias,
    w_fc, w_fc_out, img_ln1_gain, img_ln1_bias, img_w_qkv, img_w_attn_out, img_ln2_gain,
    img_ln2_bias, img_w_fc, img_w_fc_out, final_gain, final_bias, text_proj, image_gain,
    image_bias, image_proj, logit_scale,
):
    caps, seq, dim = text_input.shape
    img_seq = image_input.shape[1]
    devices = lax.axis_size("dp")
    plan = Plan(dim, w_fc.shape[2], devices)
    heads = dim // HEAD_DIM
    count = devices * caps
    hidden = plan.hidden
    device = lax.axis_index("dp").astype(jnp.int32).reshape(1)
    text_input, image_input = text_input.swapaxes(0, 1), image_input.swapaxes(0, 1)
    totals = caps * seq, caps * img_seq
    chips = devices // 2
    width = (heads - 1) * LANES

    first = {
        (K.X, 0): text_input, (K.X, 1): image_input,
        (K.GAIN, 0): ln1_gain, (K.BIAS, 0): ln1_bias,
        (K.GAIN, 1): img_ln1_gain, (K.BIAS, 1): img_ln1_bias,
    }
    late = {(K.W_QKV, 0): w_qkv, (K.W_QKV, 1): img_w_qkv}
    second = {
        (K.W_OUT, 0): w_attn_out, (K.W_OUT, 1): img_w_attn_out,
        (K.GAIN2, 0): ln2_gain, (K.BIAS2, 0): ln2_bias,
        (K.GAIN2, 1): img_ln2_gain, (K.BIAS2, 1): img_ln2_bias,
    }
    hidden_in = {(K.W_FC, 0): w_fc, (K.W_FC, 1): img_w_fc}
    third = {
        (K.W_FC_OUT, 0): w_fc_out, (K.W_FC_OUT, 1): img_w_fc_out,
        (K.HEAD_GAIN, 0): final_gain, (K.HEAD_BIAS, 0): final_bias,
        (K.HEAD_GAIN, 1): image_gain, (K.HEAD_BIAS, 1): image_bias,
        (K.PROJ, 0): text_proj, (K.PROJ, 1): image_proj,
    }

    def far(arrays):
        return {key: (array, Place.FAR) for key, array in arrays.items()}

    eot = {K.EOT: (eot_index, Place.FEW)}
    rows = run(
        front_body(plan),
        "front",
        {K.ROWS: ((chips, caps, 4 * dim), BF16, Place.AUTO)},
        [],
        [],
        [eot | far(first), far(late)],
    )[K.ROWS]
    mine = exchange_by_core(rows, devices)

    unused, pack_rows = pack_at(dim, hidden, caps)
    side_outs = {K.VALUES: ((devices, caps, width), BF16, Place.FAR)}
    middle_outs = {
        K.SEND: ((devices, caps, width + dim + LANES), BF16, Place.FAR),
        K.ROWS: ((count, 4 * dim), BF16, Place.FAR),
    }
    for tower, total in enumerate(totals):
        side_outs |= {
            (K.NORMED, tower): ((total, dim), BF16, Place.FAR),
            (K.UNIT, tower): ((total, dim), BF16, Place.FAR),
            (K.PROBS, tower): ((heads * caps, total), F32, Place.FAR),
            (K.PACK, tower): ((pack_rows, dim), F32, Place.FAR),
        }
        middle_outs |= {
            (K.OWN, tower): (((2 + heads) * caps, dim), F32, Place.FAR),
            (K.SCORES, tower): ((heads * caps, total), BF16, Place.FAR),
        }
    side = run(side_body(plan), "side", side_outs, [], [], [eot | far(first), far(late), far(second | hidden_in | third)])
    values = exchange(side.pop(K.VALUES))
    mine, side[K.PACK, 0] = lax.optimization_barrier((mine, side[K.PACK, 0]))
    others = swap(mine, devices)

    packs = {key: side[key] for key in ((K.PACK, 0), (K.PACK, 1))}
    middle = run(
        middle_body(plan),
        "middle",
        middle_outs,
        [pltpu.VMEM((chips, 2, caps, 4 * dim), BF16), pltpu.SemaphoreType.DMA((2,))],
        [device, logit_scale],
        [
            {K.MINE: (mine, Place.AUTO), K.OTHERS: (others, Place.AUTO)} | far(second),
            far(hidden_in),
            far(third | packs),
            far(late)
            | far({(name, tower): side[name, tower] for name in (K.NORMED, K.PROBS, K.UNIT) for tower in (0, 1)}),
        ],
        join_rows,
    )
    send, values = lax.optimization_barrier((middle[K.SEND], values))
    sent = exchange(send)

    share_rows = plan.rows_out
    region = (plan.total - plan.out_at) // LANES
    head_region = plan.head_total // LANES
    attended = {}
    tail_outs = {K.LOSS: ((1,), F32, Place.SCALAR), K.SCALE: ((1,), F32, Place.SCALAR)}
    for tower, length in enumerate((seq, img_seq)):
        for name, source in ((K.PROBS, side), (K.PACK, side), (K.OWN, middle), (K.SCORES, middle)):
            attended[name, tower] = source[name, tower]
        tail_outs |= {
            (K.PART, tower): ((share_rows, LANES), F32, Place.FAR),
            (K.INPUT, tower): ((length, caps, dim), F32, Place.FAR),
        }
    tail_outs |= {
        K.HEAD: ((plan.head_rows_out, LANES), F32, Place.FAR),
        K.WINDOWS: ((count, LANES), BF16, Place.FAR),
        K.QUERIES: ((count, 2 * dim), BF16, Place.FAR),
        K.VALUES: ((2, plan.pad, dim), F32, Place.FAR),
    }
    tail = run(
        tail_body(plan),
        "tail",
        tail_outs,
        [
            pltpu.VMEM((region + 2 * share_rows + 8, LANES), F32),
            pltpu.VMEM((head_region + plan.head_rows_out + 8, LANES), F32),
            pltpu.VMEM((totals[0], dim), F32),
            pltpu.VMEM((totals[1], dim), F32),
            pltpu.VMEM((8, dim), F32),
            [pltpu.VMEM((count, hidden), F32)] * 2,
            [pltpu.VMEM((count, hidden), BF16)] * 2,
            [pltpu.VMEM((count, hidden), BF16)] * 2,
            pltpu.VMEM((2, dim, dim), BF16),
            pltpu.SemaphoreType.DMA((2,)),
        ],
        [device, logit_scale],
        [
            eot | far(first),
            far(attended),
            far({K.ROWS: middle[K.ROWS]} | second | hidden_in),
            far(third),
            far({K.VALUES: values.reshape(count, width)})
            | {key: (array, Place.RAW) for key, array in late.items()},
        ],
        tail_ahead(plan),
    )
    sent, tail[K.WINDOWS] = lax.optimization_barrier((sent, tail[K.WINDOWS]))
    swapped = swap(sent[:, :, width:], devices)
    flat_rows = max(2 * dim + plan.pad * plan.row, 2 * dim + 2 * plan.row + share_rows * LANES) // LANES
    names = [(K.PART, 0), (K.PART, 1), K.WINDOWS, K.QUERIES, K.VALUES]
    shares = run(
        last_body(plan),
        "last",
        {(K.SHARE, tower): ((1, plan.share), F32, Place.FAR) for tower in (0, 1)},
        [
            pltpu.VMEM((2, flat_rows // 8 * 8 + 16, LANES), F32),
            pltpu.VMEM((count, 2 * dim), BF16),
        ],
        [device],
        [
            far({name: tail[name] for name in names})
            | {K.SENT: (sent.reshape(count, -1), Place.AUTO)}
            | {K.SWAPPED: (swapped.reshape(count, -1), Place.AUTO)},
        ],
    )

    def cut(array, size):
        return array.reshape(-1)[:size]

    return (
        tail[K.LOSS],
        tail[K.INPUT, 0].swapaxes(0, 1),
        tail[K.INPUT, 1].swapaxes(0, 1),
        shares[K.SHARE, 0],
        shares[K.SHARE, 1],
        cut(tail[K.HEAD], plan.head_share),
        tail[K.SCALE],
    )


def norm_apply(values, gain, bias):
    center = values - jnp.mean(values, -1, keepdims=True)
    spread = jnp.mean(center * center, -1, keepdims=True)
    return center * lax.rsqrt(spread + EPS) * gain + bias


def quick_gelu(values):
    return values * jax.nn.sigmoid(1.702 * values)


def unit_rows(values):
    return values * lax.rsqrt(jnp.sum(values * values, -1, keepdims=True) + UNIT_EPS)


def causal_mask(seq_len):
    row_pos = lax.broadcasted_iota(jnp.int32, (seq_len, seq_len), 0)
    col_pos = lax.broadcasted_iota(jnp.int32, (seq_len, seq_len), 1)
    return col_pos <= row_pos


def matmul(left, right):
    return jnp.dot(left, right, preferred_element_type=jnp.float32)


def inner_rows(left, right):
    return lax.dot_general(
        left, right, (((0,), (0,)), ((), ())), preferred_element_type=jnp.float32
    )


def outer_cols(left, right):
    return lax.dot_general(
        left, right, (((1,), (1,)), ((), ())), preferred_element_type=jnp.float32
    )


def layer_forward(stream, weights, causal):
    gain_one, bias_one, w_qkv, w_out, gain_two, bias_two, w_fc, w_fc_out = weights
    num_caps, seq_len, feat_dim = stream.shape
    num_heads = feat_dim // HEAD_DIM
    num_rows = num_caps * seq_len
    normed_one = (
        norm_apply(stream, gain_one, bias_one).astype(jnp.bfloat16).reshape(num_rows, feat_dim)
    )
    packed = (
        matmul(normed_one, w_qkv)
        .astype(jnp.bfloat16)
        .reshape(num_caps, seq_len, 3, num_heads, HEAD_DIM)
    )
    queries = packed[:, :, 0]
    key_rows = packed[:, :, 1]
    value_rows = packed[:, :, 2]
    raw_score = jnp.einsum("bqhd,bkhd->bhqk", queries, key_rows, preferred_element_type=jnp.float32)
    scores = raw_score * HEAD_DIM ** (-0.5)
    if causal:
        scores = jnp.where(causal_mask(seq_len), scores, MASKED)
    row_peak = jnp.max(scores, -1, keepdims=True)
    log_total = row_peak + jnp.log(jnp.sum(jnp.exp(scores - row_peak), -1, keepdims=True))
    attn_probs = jnp.exp(scores - log_total)
    probs_low = attn_probs.astype(jnp.bfloat16)
    mixed_rows = jnp.einsum(
        "bhqk,bkhd->bqhd", probs_low, value_rows, preferred_element_type=jnp.float32
    )
    mixed_rows = mixed_rows.astype(jnp.bfloat16).reshape(num_rows, feat_dim)
    middle = stream + matmul(mixed_rows, w_out).reshape(num_caps, seq_len, feat_dim)
    normed_two = (
        norm_apply(middle, gain_two, bias_two).astype(jnp.bfloat16).reshape(num_rows, feat_dim)
    )
    hidden = matmul(normed_two, w_fc)
    active = quick_gelu(hidden).astype(jnp.bfloat16)
    result = middle + matmul(active, w_fc_out).reshape(num_caps, seq_len, feat_dim)
    return (
        result,
        (normed_one, packed, attn_probs, probs_low, mixed_rows, middle, normed_two, hidden, active),
    )


def layer_backward(stream, weights, grad_out, causal):
    gain_one, bias_one, w_qkv, w_out, gain_two, bias_two, w_fc, w_fc_out = weights
    num_caps, seq_len, feat_dim = stream.shape
    num_heads = feat_dim // HEAD_DIM
    num_rows = num_caps * seq_len
    unused, kept = layer_forward(stream, weights, causal)
    normed_one, packed, attn_probs, probs_low, mixed_rows, middle, normed_two, hidden, active = kept
    grad_low = grad_out.reshape(num_rows, feat_dim).astype(jnp.bfloat16)
    grad_fc_out = inner_rows(active, grad_low)
    grad_active = outer_cols(grad_low, w_fc_out)
    unused_gelu, gelu_back = jax.vjp(quick_gelu, hidden)
    grad_hidden = gelu_back(grad_active)[0].astype(jnp.bfloat16)
    grad_fc = inner_rows(normed_two, grad_hidden)
    grad_normed_two = outer_cols(grad_hidden, w_fc)
    unused_two, norm_back_two = jax.vjp(norm_apply, middle, gain_two, bias_two)
    grad_mid_norm, grad_gain_two, grad_bias_two = norm_back_two(
        grad_normed_two.reshape(num_caps, seq_len, feat_dim)
    )
    grad_middle = grad_out + grad_mid_norm
    middle_low = grad_middle.reshape(num_rows, feat_dim).astype(jnp.bfloat16)
    grad_w_out = inner_rows(mixed_rows, middle_low)
    grad_mixed = (
        outer_cols(middle_low, w_out)
        .astype(jnp.bfloat16)
        .reshape(num_caps, seq_len, num_heads, HEAD_DIM)
    )
    queries = packed[:, :, 0]
    key_rows = packed[:, :, 1]
    value_rows = packed[:, :, 2]
    grad_values = jnp.einsum(
        "bhqk,bqhd->bkhd", probs_low, grad_mixed, preferred_element_type=jnp.float32
    )
    grad_probs = jnp.einsum(
        "bqhd,bkhd->bhqk", grad_mixed, value_rows, preferred_element_type=jnp.float32
    )
    row_inner = jnp.sum(attn_probs * grad_probs, -1, keepdims=True)
    grad_raw = (attn_probs * (grad_probs - row_inner) * HEAD_DIM ** (-0.5)).astype(jnp.bfloat16)
    grad_queries = jnp.einsum(
        "bhqk,bkhd->bqhd", grad_raw, key_rows, preferred_element_type=jnp.float32
    )
    grad_keys = jnp.einsum("bhqk,bqhd->bkhd", grad_raw, queries, preferred_element_type=jnp.float32)
    grad_packed = (
        jnp.stack([grad_queries, grad_keys, grad_values], 2)
        .astype(jnp.bfloat16)
        .reshape(num_rows, 3 * feat_dim)
    )
    grad_qkv = inner_rows(normed_one, grad_packed)
    grad_normed_one = outer_cols(grad_packed, w_qkv)
    unused_one, norm_back_one = jax.vjp(norm_apply, stream, gain_one, bias_one)
    grad_in_norm, grad_gain_one, grad_bias_one = norm_back_one(
        grad_normed_one.reshape(num_caps, seq_len, feat_dim)
    )
    grads_here = [
        grad_gain_one,
        grad_bias_one,
        grad_qkv,
        grad_w_out,
        grad_gain_two,
        grad_bias_two,
        grad_fc,
        grad_fc_out,
    ]
    return (grad_middle + grad_in_norm, grads_here)


def head_forward(features, gain, bias, proj):
    normed = norm_apply(features, gain, bias).astype(jnp.bfloat16)
    embedded = matmul(normed, proj)
    return (unit_rows(embedded), (normed, embedded))


def head_backward(features, gain, bias, proj, kept, grad_unit):
    normed, embedded = kept
    unused_unit, unit_back = jax.vjp(unit_rows, embedded)
    grad_embed = unit_back(grad_unit)[0].astype(jnp.bfloat16)
    grad_proj = inner_rows(normed, grad_embed)
    grad_normed = outer_cols(grad_embed, proj)
    unused_norm, norm_back = jax.vjp(norm_apply, features, gain, bias)
    grad_feat, grad_gain, grad_bias = norm_back(grad_normed)
    return (grad_feat, [grad_gain, grad_bias, grad_proj])


def plain_contrast(own_rows, other_rows, multiplier, start):
    logits = multiplier * outer_cols(own_rows, other_rows)
    row_peak = jnp.max(logits, -1, keepdims=True)
    log_total = row_peak + jnp.log(jnp.sum(jnp.exp(logits - row_peak), -1, keepdims=True))
    col_pos = lax.broadcasted_iota(jnp.int32, logits.shape, 1)
    target_pos = lax.broadcasted_iota(jnp.int32, logits.shape, 0) + start
    matched = (col_pos == target_pos).astype(jnp.float32)
    loss_sum = jnp.sum(log_total) - jnp.sum(matched * logits)
    grad_logits = 0.5 * (jnp.exp(logits - log_total) - matched)
    scale_part = jnp.sum(grad_logits * logits)
    return (loss_sum, scale_part, (multiplier * grad_logits).astype(jnp.bfloat16), log_total[:, 0])


def pack_flat(arrays, devices):
    flat = jnp.concatenate([array.reshape(-1) for array in arrays])
    padding = -flat.shape[0] % devices
    return jnp.concatenate([flat, jnp.zeros((padding,), jnp.float32)])


def plain(
    text_input,
    eot_index,
    image_input,
    ln1_gain,
    ln1_bias,
    w_qkv,
    w_attn_out,
    ln2_gain,
    ln2_bias,
    w_fc,
    w_fc_out,
    img_ln1_gain,
    img_ln1_bias,
    img_w_qkv,
    img_w_attn_out,
    img_ln2_gain,
    img_ln2_bias,
    img_w_fc,
    img_w_fc_out,
    final_gain,
    final_bias,
    text_proj,
    image_gain,
    image_bias,
    image_proj,
    logit_scale,
):
    num_caps, seq_len, feat_dim = text_input.shape
    devices = lax.axis_size("dp")
    all_caps = num_caps * devices
    start = lax.axis_index("dp") * num_caps
    depth = ln1_gain.shape[0]
    text_stack = (ln1_gain, ln1_bias, w_qkv, w_attn_out, ln2_gain, ln2_bias, w_fc, w_fc_out)
    image_stack = (
        img_ln1_gain,
        img_ln1_bias,
        img_w_qkv,
        img_w_attn_out,
        img_ln2_gain,
        img_ln2_bias,
        img_w_fc,
        img_w_fc_out,
    )

    def text_weights(layer_num):
        return tuple((array[layer_num] for array in text_stack))

    def image_weights(layer_num):
        return tuple((array[layer_num] for array in image_stack))

    stream = text_input.astype(jnp.float32)
    layer_num = 0
    text_saved = [stream]
    stream, unused = layer_forward(stream, text_weights(layer_num), True)
    pooled = jnp.take_along_axis(stream, eot_index[:, None, None], axis=1)[:, 0]
    picture = image_input.astype(jnp.float32)
    layer_num = 0
    image_saved = [picture]
    picture, unused = layer_forward(picture, image_weights(layer_num), False)
    image_pooled = picture[:, 0]
    text_unit, text_kept = head_forward(pooled, final_gain, final_bias, text_proj)
    image_unit, image_kept = head_forward(image_pooled, image_gain, image_bias, image_proj)
    image_low = image_unit.astype(jnp.bfloat16)
    text_low = text_unit.astype(jnp.bfloat16)
    image_all, text_all = (
        lax.all_gather(image_low, "dp", axis=0, tiled=True),
        lax.all_gather(text_low, "dp", axis=0, tiled=True),
    )
    multiplier = jnp.exp(logit_scale[0])
    loss_image, scale_image, grad_raw_it, unused_it = plain_contrast(
        image_low, text_all, multiplier, start
    )
    loss_text, scale_text, grad_raw_ti, unused_ti = plain_contrast(text_low, image_all, multiplier, start)
    spread_text = inner_rows(grad_raw_it, image_low)
    spread_image = inner_rows(grad_raw_ti, text_low)
    back_text, back_image = (
        lax.psum_scatter(spread_text, "dp", scatter_dimension=0, tiled=True),
        lax.psum_scatter(spread_image, "dp", scatter_dimension=0, tiled=True),
    )
    total, grad_scale = lax.psum((loss_image + loss_text, scale_image + scale_text), "dp")
    grad_image_unit = matmul(grad_raw_it, text_all) + back_image
    grad_text_unit = matmul(grad_raw_ti, image_all) + back_text
    grad_pooled, text_head_grads = head_backward(
        pooled, final_gain, final_bias, text_proj, text_kept, grad_text_unit
    )
    grad_image_pooled, image_head_grads = head_backward(
        image_pooled, image_gain, image_bias, image_proj, image_kept, grad_image_unit
    )
    head_flat = pack_flat(text_head_grads + image_head_grads, devices)
    image_flat = [None] * depth
    img_seq = image_input.shape[1]
    img_dim = image_input.shape[2]
    grad_picture = jnp.concatenate(
        [grad_image_pooled[:, None, :], jnp.zeros((num_caps, img_seq - 1, img_dim), jnp.float32)], 1
    )
    for layer_num in reversed(range(depth)):
        grad_picture, grads_here = layer_backward(
            image_saved[layer_num], image_weights(layer_num), grad_picture, False
        )
        image_flat[layer_num] = pack_flat(grads_here, devices)
    text_flat = [None] * depth
    selected = (
        lax.broadcasted_iota(jnp.int32, (num_caps, seq_len), 1) == eot_index[:, None]
    ).astype(jnp.float32)
    grad_stream = selected[:, :, None] * grad_pooled[:, None, :]
    for layer_num in reversed(range(depth)):
        grad_stream, grads_here = layer_backward(
            text_saved[layer_num], text_weights(layer_num), grad_stream, True
        )
        text_flat[layer_num] = pack_flat(grads_here, devices)
    text_share, image_share, head_share = (
        lax.psum_scatter(jnp.stack(text_flat), "dp", scatter_dimension=1, tiled=True),
        lax.psum_scatter(jnp.stack(image_flat), "dp", scatter_dimension=1, tiled=True),
        lax.psum_scatter(head_flat, "dp", scatter_dimension=0, tiled=True),
    )
    loss = (total / (2 * all_caps)).reshape(1)
    return (
        loss,
        grad_stream,
        grad_picture,
        text_share,
        image_share,
        head_share,
        grad_scale.reshape(1),
    )


def shards(*args):
    caps = args[0].shape[0] * lax.axis_size("dp")
    return compact(*args) if caps <= 512 else plain(*args)


def solution(mesh):
    return jax.shard_map(
        shards,
        mesh=mesh,
        in_specs=(
            P("dp", None, None),
            P("dp"),
            P("dp", None, None),
            P(),
            P(),
            P(),
            P(),
            P(),
            P(),
            P(),
            P(),
            P(),
            P(),
            P(),
            P(),
            P(),
            P(),
            P(),
            P(),
            P(),
            P(),
            P(),
            P(),
            P(),
            P(),
            P(),
        ),
        out_specs=(
            P(),
            P("dp", None, None),
            P("dp", None, None),
            P(None, "dp"),
            P(None, "dp"),
            P("dp"),
            P(),
        ),
        check_vma=False,
    )
```

```python
import enum

import jax
import jax.numpy as jnp
from jax import lax
from jax.experimental import pallas as pl
from jax.experimental.pallas import tpu as pltpu
from jax.sharding import PartitionSpec as P

HEAD_DIM = 64
LANES = 128

EPS = 1e-05
UNIT_EPS = 1e-06
MASKED = -1000000000.0
LIMIT = 44 * 2**20
F32 = jnp.float32
BF16 = jnp.bfloat16


class Place(enum.Enum):
    FAR = enum.auto()
    FEW = enum.auto()
    RAW = enum.auto()
    AUTO = enum.auto()
    NEAR = enum.auto()
    SCALAR = enum.auto()


class K(enum.Enum):
    BIAS = enum.auto()
    BIAS2 = enum.auto()
    EOT = enum.auto()
    GAIN = enum.auto()
    GAIN2 = enum.auto()
    HEAD = enum.auto()
    HEAD_BIAS = enum.auto()
    HEAD_GAIN = enum.auto()
    INPUT = enum.auto()
    LOSS = enum.auto()
    MINE = enum.auto()
    MIXED = enum.auto()
    NORMED = enum.auto()
    OTHERS = enum.auto()
    OWN = enum.auto()
    PACK = enum.auto()
    PART = enum.auto()
    PROBS = enum.auto()
    PROJ = enum.auto()
    QUERIES = enum.auto()
    ROWS = enum.auto()
    SCALE = enum.auto()
    SCORES = enum.auto()
    SEND = enum.auto()
    SENT = enum.auto()
    SWAPPED = enum.auto()
    SHARE = enum.auto()
    UNIT = enum.auto()
    VALUES = enum.auto()
    W_FC = enum.auto()
    W_FC_OUT = enum.auto()
    W_OUT = enum.auto()
    W_QKV = enum.auto()
    WINDOWS = enum.auto()
    X = enum.auto()


def dot(left, right):
    return jnp.dot(left, right, preferred_element_type=F32)


def dot_nt(left, right):
    return lax.dot_general(left, right, (((1,), (1,)), ((), ())), preferred_element_type=F32)


def dot_tn(left, right):
    return lax.dot_general(left, right, (((0,), (0,)), ((), ())), preferred_element_type=F32)


def standard(values):
    center = values - jnp.mean(values, -1, keepdims=True)
    scale = lax.rsqrt(jnp.mean(center * center, -1, keepdims=True) + EPS)
    return center * scale, scale


def norm_back(grad, unit, scale, gain):
    scaled = grad * gain
    return scale * (
        scaled
        - jnp.mean(scaled, -1, keepdims=True)
        - unit * jnp.mean(scaled * unit, -1, keepdims=True)
    )


def head_masks(width):
    lane = lax.broadcasted_iota(jnp.int32, (1, width), 1)
    return [
        ((lane >= h * HEAD_DIM) & (lane < (h + 1) * HEAD_DIM)).astype(F32)
        for h in range(width // HEAD_DIM)
    ]


def spread(rows):
    return jnp.concatenate([rows * mask for mask in head_masks(rows.shape[1])], 0)


def collect(rows, caps):
    masks = head_masks(rows.shape[1])
    return sum(rows[h * caps : (h + 1) * caps] * mask for h, mask in enumerate(masks))


def picked_columns(caps, total, ends):
    cap = lax.broadcasted_iota(jnp.int32, (caps, 1), 0)
    at = cap
    for b in range(caps):
        at = jnp.where(cap == b, ends[b] * caps + b, at)
    column = lax.broadcasted_iota(jnp.int32, (caps, total), 1)
    chosen = jnp.where(column == at, 1.0, 0.0).astype(BF16)
    return chosen, column, at


class Plan:
    def __init__(self, dim, hidden, devices):
        self.dim, self.hidden, self.devices = dim, hidden, devices
        self.row = 3 * dim
        self.qkv_at = 2 * dim
        self.out_at = self.qkv_at + dim * self.row
        self.norm_at = self.out_at + dim * dim
        self.fc_at = self.norm_at + 2 * dim
        self.fc_out_at = self.fc_at + dim * hidden
        self.total = self.fc_out_at + hidden * dim
        self.share = -(-self.total // devices)
        self.head_total = 2 * (2 * dim + dim * dim)
        self.head_share = -(-self.head_total // devices)
        self.roots = -(-self.out_at // self.share)
        self.rows_out = -(-(self.share // LANES + 2) // 8) * 8
        self.head_rows_out = -(-(self.head_share // LANES + 2) // 8) * 8
        self.window = self.share // self.row + 2
        self.pad = -(-self.window // 8) * 8
        self.used = self.pad + self.window
        self.piece = LANES - self.used
        assert self.piece > 0 and -(-self.used // self.piece) < dim // HEAD_DIM
        assert self.total % devices == 0 and self.head_total % devices == 0

    def column(self, device):
        if isinstance(device, int):
            return min(max(device * self.share - self.qkv_at, 0) // self.row, self.dim - 1)
        return jnp.minimum(jnp.maximum(device * self.share - self.qkv_at, 0) // self.row, self.dim - 1)


def window_tiles(plan, text, image, device, caps):
    dim = text.shape[1]
    first = plan.column(device)
    lane = lax.broadcasted_iota(jnp.int32, (text.shape[0], LANES), 1)
    left = pltpu.roll(text, (dim - first) % dim, 1)[:, :LANES]
    right = pltpu.roll(image, (dim - first + plan.pad) % dim, 1)[:, :LANES]
    both = jnp.where(lane < plan.pad, left, right)
    heads = text.shape[0] // caps
    lane, last = lane[:caps], both[(heads - 1) * caps :]
    tiles = []
    for h in range(heads - 1):
        moved = pltpu.roll(last, (plan.used - h * plan.piece) % LANES, 1)
        tiles.append(jnp.where(lane < plan.used, both[h * caps : (h + 1) * caps], moved).astype(BF16))
    return jnp.concatenate(tiles, 1)


def last_head(plan, source, heads):
    lane = lax.broadcasted_iota(jnp.int32, (source.shape[0], LANES), 1)
    whole = jnp.zeros(lane.shape, F32)
    for h in range(-(-plan.used // plan.piece)):
        tile = source[:, h * LANES : (h + 1) * LANES].astype(F32)
        moved = pltpu.roll(tile, (LANES + h * plan.piece - plan.used) % LANES, 1)
        whole = jnp.where(lane >= h * plan.piece, moved, whole)
    return whole.astype(BF16)


def pack_windows(plan, target, text, image, caps, common):
    width = (text.shape[0] // caps - 1) * LANES
    held = plan.roots + plan.roots % 2

    def fill(device, core):
        target[device, :, :width] = window_tiles(plan, text, image, device, caps)
        if common is not None:
            target[device, :, width:] = common[core]

    if held <= 16:
        for device in range(held):
            fill(device, device % 2)
    else:

        @pl.loop(0, held // 2)
        def _(chip):
            for core in range(2):
                fill(2 * chip + core, core)


def clear_windows(plan, target):
    held = plan.roots + plan.roots % 2

    @pl.loop(held, target.shape[0])
    def _(device):
        target[device] = jnp.zeros(target.shape[1:], BF16)

    return slice(0, held), slice(held, target.shape[0])


def take_rows(source, at, count):
    row, lane_at = at // LANES, at % LANES
    lane = lax.broadcasted_iota(jnp.int32, (count, LANES), 1)
    mixed = jnp.where(
        lane >= lane_at, source[pl.ds(row, count), :], source[pl.ds(row + 1, count), :]
    )
    return pltpu.roll(mixed, lax.rem(LANES - lane_at, LANES), 1)


def put_tile(target, row, block):
    count, width = block.shape
    step = width // LANES
    for j in range(step):
        piece = block[:, j * LANES : (j + 1) * LANES]
        if count == 1:
            target[row + j : row + j + 1, :] = piece
        else:
            target[pl.ds(row + j, count, stride=step), :] = piece


def front_tower(tower, ins, picked, last):
    x = ins[K.X, tower].get()[...]
    seq, caps, dim = x.shape
    total = seq * caps
    heads = dim // HEAD_DIM
    source = x.reshape(total, dim)
    unit, unused = standard(source.astype(F32))
    yield
    gain, bias = ins[K.GAIN, tower].get()[...], ins[K.BIAS, tower].get()[...]
    normed = (unit * gain + bias).astype(BF16)
    chosen, column, pick_at = picked_columns(caps, total, picked)
    last_at = pick_at
    if last is not picked:
        unused, unused, last_at = picked_columns(caps, total, last)
    pooled = dot(chosen, source)
    yield
    pooled_unit, unused = standard(pooled)
    pooled_normed = (pooled_unit * gain + bias).astype(BF16)
    w_ref = ins[K.W_QKV, tower].get()
    query = dot(pooled_normed, w_ref[0, :, :dim]).astype(BF16).astype(F32)
    yield
    through_keys = dot_nt(spread(query).astype(BF16), w_ref[0, :, dim : 2 * dim])
    yield
    scores = dot_nt(through_keys.astype(BF16), normed) * HEAD_DIM ** (-0.5)
    yield
    cap = lax.broadcasted_iota(jnp.int32, (caps, 1), 0)
    seen = jnp.where((lax.rem(column, caps) == cap) & (column <= last_at), 1.0, 0.0)
    seen = jnp.concatenate([seen] * heads, 0) > 0.5
    peak = jnp.max(jnp.where(seen, scores, MASKED), -1, keepdims=True)
    sums = jnp.sum(jnp.where(seen, jnp.exp(scores - peak), 0.0), -1, keepdims=True)
    probs = jnp.where(seen, jnp.exp(scores - (peak + jnp.log(sums))), 0.0)
    yield
    values = dot(probs.astype(BF16), normed)
    yield
    mixed = collect(dot(values.astype(BF16), w_ref[0, :, 2 * dim :]), caps).astype(BF16)
    return pooled, mixed, (normed, unit, probs, query, through_keys, values, chosen)


def attended_towers(ins):
    eot = ins[K.EOT].get()
    caps = eot.shape[0]
    seq = ins[K.X, 1].buf.shape[0]
    ends = [eot[b] for b in range(caps)]
    views = (ends, ends), ([0] * caps, [seq - 1] * caps)
    return run_together([front_tower(tower, ins, *views[tower]) for tower in range(2)])


def front_body(plan):
    def body(scalars, ins, outs, scratch):
        payload = []
        for pooled, mixed, unused in attended_towers(ins):
            payload += [pooled.astype(BF16), mixed]
        payload = jnp.concatenate(payload, 1)
        rows = outs[K.ROWS].ref

        @pl.loop(0, rows.shape[0])
        def _(chip):
            rows[chip] = payload

    return body


def pack_at(dim, hidden, caps):
    heads = dim // HEAD_DIM
    sizes = [heads * caps] * 2 + [caps] * 8 + [caps * hidden // dim]
    places, at = [], 0
    for size in sizes:
        places.append(slice(at, at + size))
        at += size
    return places, at


def weights_of(tower, ins):
    names = K.W_OUT, K.GAIN2, K.BIAS2, K.W_FC, K.W_FC_OUT, K.HEAD_GAIN, K.HEAD_BIAS, K.PROJ
    return [ins[name, tower] for name in names]


def side_body(plan):
    def body(scalars, ins, outs, scratch):
        dim, hidden = plan.dim, plan.hidden
        caps = ins[K.EOT].buf.shape[0]
        places, unused = pack_at(dim, hidden, caps)
        towers = attended_towers(ins)
        clear_windows(plan, outs[K.VALUES].ref)
        pack_windows(plan, outs[K.VALUES].ref, towers[0][2][5], towers[1][2][5], caps, None)
        outs[K.VALUES].push()
        kept, hiddens = ([], []), scratch[0]
        for tower, (pooled, mixed, saved) in enumerate(towers):
            normed, unit, probs, query, through_keys, values, chosen = saved
            unit = unit.astype(BF16)
            for name, value in ((K.NORMED, normed), (K.UNIT, unit), (K.PROBS, probs)):
                outs[name, tower].ref[...] = value
                outs[name, tower].push()
            small = [through_keys, dot(probs.astype(BF16), unit), dot(chosen, unit), query]
            for place, value in zip(places, small):
                outs[K.PACK, tower].ref[place, :] = value
        run_together(
            [
                tower_forward(
                    pooled, mixed, weights_of(tower, ins), kept[tower], hiddens[tower], None
                )
                for tower, (pooled, mixed, unused) in enumerate(towers)
            ]
        )
        for tower in range(2):
            pack = outs[K.PACK, tower]
            for place, value in zip(places[4:10], kept[tower]):
                pack.ref[place, :] = jnp.broadcast_to(value, (caps, dim))
            for j in range(hidden // dim):
                at = places[10].start + j * caps
                pack.ref[at : at + caps, :] = gate_slope(hiddens[tower][:, j * dim : (j + 1) * dim])
            pack.push()

    return body


def run_together(steps):
    results = [None] * len(steps)
    live = list(range(len(steps)))
    while live:
        for index in list(live):
            try:
                next(steps[index])
            except StopIteration as stop:
                results[index] = stop.value
                live.remove(index)
    return results


def chunks(width):
    step = 512 if width % 512 == 0 else width
    return [slice(at, at + step) for at in range(0, width, step)]


def gate_slope(hidden):
    gate = jax.nn.sigmoid(1.702 * hidden)
    return gate + 1.702 * hidden * gate * (1.0 - gate)


def unit_rows_of(embed):
    length = lax.rsqrt(jnp.sum(embed * embed, -1, keepdims=True) + UNIT_EPS)
    return embed * length, length


def tower_forward(pooled, mixed, weights, kept, hidden_ref, active_ref):
    w_out, gain, bias, w_fc, w_fc_out, head_gain, head_bias, proj = weights
    middle = pooled + dot(mixed, w_out.get()[0])
    yield
    unit, scale = standard(middle)
    normed = (unit * gain.get()[...] + bias.get()[...]).astype(BF16)
    yield
    result = middle
    w_fc = w_fc.get()
    for cols in chunks(w_fc.shape[2]):
        hidden = dot(normed, w_fc[0, :, cols])
        active = (hidden * jax.nn.sigmoid(1.702 * hidden)).astype(BF16)
        if hidden_ref is not None:
            hidden_ref[:, cols] = hidden
        if active_ref is not None:
            active_ref[:, cols] = active
        result = result + dot(active, w_fc_out.get()[0, cols, :])
        yield
    head_unit, head_scale = standard(result)
    head_in = (head_unit * head_gain.get()[...][None] + head_bias.get()[...][None]).astype(BF16)
    embed = dot(head_in, proj.get()[...])
    yield
    unit_embed, length = unit_rows_of(embed)
    if kept is not None:
        kept += [unit, scale, head_unit, head_scale, unit_embed, length]
    return unit_embed.astype(BF16)


def log_sum(logits, axis):
    peak = jnp.max(logits, axis, keepdims=True)
    return peak + jnp.log(jnp.sum(jnp.exp(logits - peak), axis, keepdims=True))


def unit_gradient(multiplier, logits, own_total, other_total, matched, other):
    target = jnp.where(matched, 1.0, 0.0)
    own = 0.5 * multiplier * (jnp.exp(logits - own_total) - target)
    cross = 0.5 * multiplier * (jnp.exp(logits - other_total) - target)
    return dot(own.astype(BF16), other) + dot(cross.astype(BF16), other)


def embed_back(grad_unit, unit_embed, length):
    along = jnp.sum(unit_embed * grad_unit, -1, keepdims=True)
    return (length * (grad_unit - unit_embed * along)).astype(BF16)


def tower_backward(grad_embed, kept, slope, weights, keep_hidden):
    unit, scale, head_unit, head_scale = kept
    w_out, gain, bias, w_fc, w_fc_out, head_gain, head_bias, proj = weights
    grad_head = dot_nt(grad_embed, proj.get()[...])
    yield
    grad_result = norm_back(grad_head, head_unit, head_scale, head_gain.get()[...][None])
    grad_out = grad_result.astype(BF16)
    yield
    w_fc, w_fc_out = w_fc.get(), w_fc_out.get()
    grad_normed = 0.0
    for cols in chunks(w_fc.shape[2]):
        grad_active = dot_nt(grad_out, w_fc_out[0, cols, :])
        grad_hidden = (grad_active * slope(cols)).astype(BF16)
        if keep_hidden is not None:
            keep_hidden[:, cols] = grad_hidden
        grad_normed = grad_normed + dot_nt(grad_hidden, w_fc[0, :, cols])
        yield
    grad_middle = grad_result + norm_back(grad_normed, unit, scale, gain.get()[...])
    yield
    grad_mixed = dot_nt(grad_middle.astype(BF16), w_out.get()[0]).astype(BF16)
    yield
    return grad_head, grad_out, grad_normed, grad_middle, grad_mixed


def own_steps(plan, tower, units, multiplier, own_at, ins, outs):
    mine, other = units[tower], units[1 - tower]
    own_out, scores_out = outs[K.OWN, tower], outs[K.SCORES, tower]
    dim = plan.dim
    caps = scores_out.ref.shape[0] * HEAD_DIM // dim
    places, unused = pack_at(dim, plan.hidden, caps)
    other_total = log_sum(multiplier * dot_nt(mine, other), 0)
    yield
    pack = ins[K.PACK, tower].get()
    unit, scale, head_unit, head_scale, unit_embed, length = (pack[places[j], :] for j in range(4, 10))
    logits = multiplier * dot_nt(unit_embed.astype(BF16), other)
    matched = lax.broadcasted_iota(jnp.int32, logits.shape, 1) == own_at + lax.broadcasted_iota(
        jnp.int32, logits.shape, 0
    )
    grad_unit = unit_gradient(multiplier, logits, log_sum(logits, 1), other_total, matched, other)
    yield
    slope_at = places[10].start
    slopes = [pack[slope_at + j * caps : slope_at + (j + 1) * caps, :] for j in range(plan.hidden // dim)]
    slopes = jnp.concatenate(slopes, 1)
    done = yield from tower_backward(
        embed_back(grad_unit, unit_embed, length), (unit, scale, head_unit, head_scale),
        lambda cols: slopes[:, cols], weights_of(tower, ins), None,
    )
    grad_middle, grad_mixed = done[3], done[4].astype(F32)
    own_out.ref[:caps, :] = grad_middle
    w_ref = ins[K.W_QKV, tower].get()
    through_values = dot_nt(spread(grad_mixed).astype(BF16), w_ref[0, :, 2 * dim :])
    own_out.ref[2 * caps :, :] = through_values
    yield
    normed = ins[K.NORMED, tower].get()[...]
    grad_probs = dot_nt(through_values.astype(BF16), normed)
    yield
    probs = ins[K.PROBS, tower].get()[...]
    inner = jnp.sum(probs * grad_probs, -1, keepdims=True)
    grad_scores = (probs * (grad_probs - inner) * HEAD_DIM ** (-0.5)).astype(BF16)
    scores_out.ref[...] = grad_scores
    scores_out.push()
    yield
    spread_keys = dot(grad_scores, normed)
    yield
    grad_query = collect(dot(spread_keys.astype(BF16), w_ref[0, :, dim : 2 * dim]), caps).astype(BF16)
    yield
    units = pack[places[0], :] * dot(grad_scores, ins[K.UNIT, tower].get()[...])
    yield
    through_query = dot_nt(grad_query, w_ref[0, :, :dim])
    own_out.ref[caps : 2 * caps, :] = through_query
    own_out.push()
    units = units + through_values * pack[places[1], :]
    gain_part = jnp.sum(units, 0, keepdims=True) + jnp.sum(
        through_query * pack[places[2], :], 0, keepdims=True
    )
    bias_part = jnp.sum(through_values, 0, keepdims=True) + jnp.sum(through_query, 0, keepdims=True)
    return spread_keys, grad_query, (gain_part, bias_part)


def forward_pair(plan, rows, ins, kept, hidden, active):
    dim = plan.dim
    return run_together(
        [
            tower_forward(
                rows[:, 2 * tower * dim : (2 * tower + 1) * dim].astype(F32),
                rows[:, (2 * tower + 1) * dim : (2 * tower + 2) * dim],
                weights_of(tower, ins), kept[tower], hidden[tower], active[tower],
            )
            for tower in range(2)
        ]
    )


def row_copies(scalars, ins, scratch):
    core = scalars[0][0] % 2
    return [
        pltpu.make_async_copy(ins[name].ref, scratch[0].at[:, at], scratch[1].at[i])
        for i, (name, at) in enumerate(((K.MINE, core), (K.OTHERS, 1 - core)))
    ]


def join_rows(scalars, ins, scratch):
    for copy in row_copies(scalars, ins, scratch):
        copy.start()


def middle_body(plan):
    def body(scalars, ins, outs, scratch):
        at_ref, scale_ref = scalars
        rows_ref, sems = scratch
        dim = plan.dim
        device = at_ref[0]
        caps, wide = rows_ref.shape[2:]
        held, others = clear_windows(plan, outs[K.SEND].ref)
        outs[K.SEND].push_part(others)
        for copy in row_copies(scalars, ins, scratch):
            copy.wait()
        rows = rows_ref[...].reshape(plan.devices * caps, wide)
        outs[K.ROWS].ref[...] = rows
        outs[K.ROWS].push()
        units = forward_pair(plan, rows, ins, (None, None), (None, None), (None, None))
        multiplier = jnp.exp(jnp.full((1, 1), scale_ref[0], F32))
        own_at = device * caps
        parts = run_together(
            [own_steps(plan, tower, units, multiplier, own_at, ins, outs) for tower in range(2)]
        )
        tiles = dim // LANES
        common = []
        for unused, query, sums in parts:
            small = [row[:, j * LANES : (j + 1) * LANES] for row in sums for j in range(tiles)]
            small.append(jnp.zeros((caps - 2 * tiles, LANES), F32))
            common.append(jnp.concatenate([query, jnp.concatenate(small, 0).astype(BF16)], 1))
        keys_t, keys_i = parts[0][0], parts[1][0]
        pack_windows(plan, outs[K.SEND].ref, keys_t, keys_i, caps, common)
        outs[K.SEND].push_part(held)

    return body


def late_weights(ins, scratch):
    parts, sems = scratch[-2:]
    dim = parts.shape[1]
    return [
        pltpu.make_async_copy(
            ins[K.W_QKV, tower].ref.at[0, :, pl.ds(0, dim)], parts.at[tower], sems.at[tower]
        )
        for tower in range(2)
    ]


def tail_ahead(plan):
    def ahead(scalars, ins, scratch):
        @pl.when(scalars[0][0] < plan.roots)
        def _():
            for copy in late_weights(ins, scratch):
                copy.start()

    return ahead


def tail_body(plan):
    def body(scalars, ins, outs, scratch):
        at_ref, scale_ref = scalars
        dim, hidden_dim = plan.dim, plan.hidden
        loss_ref, scale_grad_ref = outs[K.LOSS].ref, outs[K.SCALE].ref
        flat, flat_head, wide_t, wide_i, small, hiddens, actives, hidden_grads, late, unused = scratch
        device = at_ref[0]
        eot = ins[K.EOT].get()
        caps = eot.shape[0]
        ends = [eot[b] for b in range(caps)]
        places, unused = pack_at(dim, hidden_dim, caps)
        multiplier = jnp.exp(jnp.full((1, 1), scale_ref[0], F32))

        def input_gradient(tower, picked, wide):
            x, gain = ins[K.X, tower].get(), ins[K.GAIN, tower].get()
            seq = x.shape[0]
            unit, scale = standard(x[...].reshape(seq * caps, dim).astype(F32))
            yield
            probs, pack, own, scores = (
                ins[name, tower].get() for name in (K.PROBS, K.PACK, K.OWN, K.SCORES)
            )
            left = jnp.concatenate([scores[...], probs[...].astype(BF16)], 0)
            right = jnp.concatenate([pack[places[0], :], own[2 * caps :, :]], 0).astype(BF16)
            wide[...] = dot_tn(left, right)
            yield
            for b in range(caps):
                at = picked[b] * caps + b
                wide[pl.ds(at, 1), :] = wide[pl.ds(at, 1), :] + own[caps + b : caps + b + 1, :]
            wide[...] = norm_back(wide[...], unit, scale, gain[...])
            yield
            for b in range(caps):
                at = picked[b] * caps + b
                wide[pl.ds(at, 1), :] = wide[pl.ds(at, 1), :] + own[b : b + 1, :]
            outs[K.INPUT, tower].ref[...] = wide[...].reshape(seq, caps, dim)
            outs[K.INPUT, tower].push()

        run_together([input_gradient(0, ends, wide_t), input_gradient(1, [0] * caps, wide_i)])

        rows = ins[K.ROWS].get()[...]
        count = rows.shape[0]
        kept = [], []
        units = forward_pair(plan, rows, ins, kept, hiddens, actives)
        logits = multiplier * dot_nt(units[1], units[0])
        matched = lax.broadcasted_iota(jnp.int32, logits.shape, 1) == lax.broadcasted_iota(
            jnp.int32, logits.shape, 0
        )
        row_total, column_total = log_sum(logits, 1), log_sum(logits, 0)
        target = jnp.where(matched, 1.0, 0.0)
        by_row = 0.5 * (jnp.exp(logits - row_total) - target)
        by_column = 0.5 * (jnp.exp(logits - column_total) - target)
        total = jnp.sum(row_total) + jnp.sum(column_total) - 2.0 * jnp.sum(target * logits)
        loss_ref[0] = total / (2 * count)
        scale_grad_ref[0] = jnp.sum((by_row + by_column) * logits)
        by_row = (multiplier * by_row).astype(BF16)
        by_column = (multiplier * by_column).astype(BF16)
        grad_units = (
            dot_tn(by_row, units[1]) + dot_tn(by_column, units[1]),
            dot(by_row, units[0]) + dot(by_column, units[0]),
        )

        grad_embeds = [embed_back(grad_units[tower], *kept[tower][4:]) for tower in range(2)]
        backs = run_together(
            [
                tower_backward(
                    grad_embeds[tower], kept[tower][:4],
                    lambda cols, hidden=hiddens[tower]: gate_slope(hidden[:, cols]),
                    weights_of(tower, ins), hidden_grads[tower],
                )
                for tower in range(2)
            ]
        )

        mixed_grads = []
        start, head_start = device * plan.share, device * plan.head_share
        front = plan.rows_out
        half = plan.head_total // 2
        for tower in range(2):
            weights = weights_of(tower, ins)
            gain, bias, head_gain, head_bias = (weights[j] for j in (1, 2, 5, 6))
            active, hidden_grad = actives[tower], hidden_grads[tower]
            grad_embed, done = grad_embeds[tower], backs[tower]
            grad_head, grad_out, grad_normed, grad_middle, grad_mixed = done
            unit, unused, head_unit = kept[tower][:3]
            mixed_grads.append(grad_mixed)
            middle_low = grad_middle.astype(BF16)
            normed = (unit * gain.get()[...] + bias.get()[...]).astype(BF16)
            head_in = head_unit * head_gain.get()[...][None] + head_bias.get()[...][None]
            head_in = head_in.astype(BF16)
            small[0:1, :] = jnp.sum(grad_normed * unit, 0, keepdims=True)
            small[1:2, :] = jnp.sum(grad_normed, 0, keepdims=True)
            small[2:3, :] = jnp.sum(grad_head * head_unit, 0, keepdims=True)
            small[3:4, :] = jnp.sum(grad_head, 0, keepdims=True)
            mixed = rows[:, (2 * tower + 1) * dim : (2 * tower + 2) * dim]

            def when_held(at, size, store):
                @pl.when((at < start + plan.share) & (at + size > start))
                def _():
                    store(front + (at - plan.out_at) // LANES)

            def when_kept(at, size, store):
                at = at + tower * half

                @pl.when((at < head_start + plan.head_share) & (at + size > head_start))
                def _():
                    store(at // LANES)

            def products(when, target, at, left, right):
                for t in range(left.shape[1] // LANES):
                    cols = slice(t * LANES, (t + 1) * LANES)
                    when(
                        at + t * LANES * right.shape[1],
                        LANES * right.shape[1],
                        lambda row: put_tile(target, row, dot_tn(left[:, cols], right[...])),
                    )

            def row_of(when, target, at, index):
                when(at, dim, lambda row: put_tile(target, row, small[index : index + 1, :]))

            products(when_held, flat, plan.out_at, mixed, middle_low)
            row_of(when_held, flat, plan.norm_at, 0)
            row_of(when_held, flat, plan.norm_at + dim, 1)
            products(when_held, flat, plan.fc_at, normed, hidden_grad)
            products(when_held, flat, plan.fc_out_at, active, grad_out)
            at = jnp.maximum(start - plan.out_at + front * LANES, 0)
            outs[K.PART, tower].ref[...] = take_rows(flat, at, plan.rows_out)
            outs[K.PART, tower].push()
            row_of(when_kept, flat_head, 0, 2)
            row_of(when_kept, flat_head, dim, 3)
            products(when_kept, flat_head, 2 * dim, head_in, grad_embed)

        outs[K.HEAD].ref[...] = take_rows(flat_head, head_start, plan.head_rows_out)
        outs[K.HEAD].push()

        query_t, query_i = late_weights(ins, scratch)
        values = ins[K.VALUES].get()

        @pl.when(device < plan.roots)
        def _():
            query_t.wait()
            query_i.wait()
            first = plan.column(device)
            lane = lax.broadcasted_iota(jnp.int32, (count, LANES), 1)
            picked_rows = []
            for tower in range(2):
                gain, bias = ins[K.GAIN, tower].get(), ins[K.BIAS, tower].get()
                pooled = rows[:, 2 * tower * dim : (2 * tower + 1) * dim].astype(F32)
                unit, unused = standard(pooled)
                normed = unit * gain[...] + bias[...]
                outs[K.QUERIES].ref[:, tower * dim : (tower + 1) * dim] = dot(
                    normed.astype(BF16), late[tower]
                ).astype(BF16)
                shift = lax.rem(dim - first + tower * plan.pad, dim)
                picked_rows.append(pltpu.roll(normed, shift, 1)[:, :LANES])
            end = last_head(plan, values, dim // HEAD_DIM)
            for j in range(dim // LANES):
                cols = slice(j * LANES, (j + 1) * LANES)
                block = window_product(plan, values, end, mixed_grads, (0, 0), j)
                for tower in range(2):
                    at = tower * plan.pad
                    outs[K.VALUES].ref[tower, :, cols] = block[
                        at : at + plan.pad, tower * LANES : (tower + 1) * LANES
                    ]
            outs[K.WINDOWS].ref[...] = jnp.where(lane < plan.pad, picked_rows[0], picked_rows[1]).astype(BF16)

    return body


def window_product(plan, source, end, factors, offsets, j):
    lane = lax.broadcasted_iota(jnp.int32, (1, 2 * LANES), 1) % LANES
    right = [factor[:, at + j * LANES : at + (j + 1) * LANES] for factor, at in zip(factors, offsets)]
    right = jnp.concatenate(right, 1).astype(F32)
    total = 0.0
    for h in (2 * j, 2 * j + 1):
        left = end if (h + 1) * HEAD_DIM == plan.dim else source[:, h * LANES : (h + 1) * LANES]
        mine = (lane // HEAD_DIM == h % 2).astype(F32)
        total = total + dot_tn(left, (right * mine).astype(BF16))
    return total


def last_body(plan):
    def body(scalars, ins, outs, scratch):
        (at_ref,) = scalars
        flat, grad_query = scratch
        dim = plan.dim
        heads = dim // HEAD_DIM
        tiles = dim // LANES
        device = at_ref[0]
        parts = [ins[K.PART, tower].get() for tower in range(2)]

        def store(tower, block):
            line = outs[K.SHARE, tower].ref
            line[...] = block.reshape(1, block.shape[0] * LANES)[:, : plan.share]

        @pl.when(device >= plan.roots)
        def _():
            for tower in range(2):
                store(tower, parts[tower][...])

        names = K.SENT, K.SWAPPED, K.WINDOWS, K.QUERIES, K.VALUES
        sent_ref, swapped, windows, queries, value_part = (
            ins[name].get() for name in names
        )

        @pl.when(device < plan.roots)
        def _():
            at_query = (heads - 1) * LANES
            count = sent_ref.shape[0]
            caps = count // plan.devices
            for core in range(2):

                @pl.when(device % 2 == core)
                def _():
                    received = sent_ref[:, at_query:], swapped[...]
                    for tower, values in enumerate(received if core == 0 else received[::-1]):
                        grad_query[:, tower * dim : (tower + 1) * dim] = values[:, :dim]
                        small = values[:, dim:].astype(F32).reshape(plan.devices, caps, LANES)
                        flat[tower, : 2 * tiles, :] = jnp.sum(small, 0)[: 2 * tiles]

            query_part = dot_tn(windows[...], grad_query[...])
            end = last_head(plan, sent_ref, heads)
            for j in range(tiles):
                put = window_product(plan, sent_ref, end, (queries, queries), (0, dim), j)
                for tower in range(2):
                    rows = slice(tower * plan.pad, (tower + 1) * plan.pad)
                    own = slice(tower * LANES, (tower + 1) * LANES)
                    q_at = tower * dim + j * LANES
                    for part, block in enumerate(
                        (
                            query_part[rows, q_at : q_at + LANES],
                            put[rows, own],
                            value_part[tower, :, j * LANES : (j + 1) * LANES],
                        )
                    ):
                        flat[
                            tower,
                            pl.ds(2 * tiles + part * tiles + j, plan.pad, stride=3 * tiles),
                            :,
                        ] = block
            start = device * plan.share
            at = start - plan.column(device) * plan.row
            shape = parts[0].shape
            index = (
                start
                + lax.broadcasted_iota(jnp.int32, shape, 0) * LANES
                + lax.broadcasted_iota(jnp.int32, shape, 1)
            )
            for tower in range(2):
                own = take_rows(flat.at[tower], at, plan.rows_out)
                store(tower, jnp.where(index < plan.out_at, own, parts[tower][...]))

    return body


class Fetch:
    def __init__(self, source, buf, sem, group):
        self.ref, self.buf, self.group = source, buf, group
        self.copy = pltpu.make_async_copy(source, buf, sem)
        group.members.append(self)

    def get(self):
        self.group.wait()
        return self.buf


class Group:
    def __init__(self):
        self.members, self.waited = [], False

    def wait(self):
        if not self.waited:
            self.waited = True
            for fetch in self.members:
                fetch.copy.wait()


class Here:
    def __init__(self, ref):
        self.buf = self.ref = ref

    def get(self):
        return self.buf

    def push(self):
        pass


class Push:
    def __init__(self, ref, target, sem):
        self.ref, self.target, self.sem, self.started = ref, target, sem, False
        self.copy = pltpu.make_async_copy(ref, target, sem)

    def push(self):
        self.started = True
        self.copy.start()

    def push_part(self, part):
        self.started = True
        pltpu.make_async_copy(self.ref.at[part], self.target.at[part], self.sem).start()


def run(body, name, outs, scratch, scalars, arrays, ahead=None):
    smem = pl.BlockSpec(memory_space=pltpu.SMEM)
    hbm = pl.BlockSpec(memory_space=pltpu.HBM)
    vmem = pl.BlockSpec(memory_space=pltpu.VMEM)
    groups = arrays
    arrays = {key: value for group in groups for key, value in group.items()}
    fetched = [(array, place) for array, place in arrays.values() if place in (Place.FAR, Place.FEW)]
    pushed = [(shape, kind) for shape, kind, place in outs.values() if place == Place.FAR]

    def kernel(*refs):
        at = 0

        def take(count):
            nonlocal at
            at += count
            return list(refs[at - count : at])

        scalar_refs, sources, targets = take(len(scalars)), take(len(arrays)), take(len(outs))
        in_bufs, out_bufs = take(len(fetched)), take(len(pushed))
        in_sems, out_sems = take(2)
        ins, results, fetches, pushes = {}, {}, [], []
        sources = iter(sources)
        chain = [Group() for unused in groups]
        for group, together in zip(groups, chain):
            for (key, (unused, place)), source in zip(group.items(), sources):
                if place in (Place.FAR, Place.FEW):
                    sem = in_sems.at[len(fetches)]
                    fetches.append(Fetch(source, in_bufs[len(fetches)], sem, together))
                    ins[key] = fetches[-1]
                else:
                    ins[key] = Here(source)
        for target, (key, (unused, unused, place)) in zip(targets, outs.items()):
            if place == Place.FAR:
                pushes.append(Push(out_bufs[len(pushes)], target, out_sems.at[len(pushes)]))
            results[key] = pushes[-1] if place == Place.FAR else Here(target)
        own_scratch = take(len(scratch))
        if ahead is not None:
            ahead(scalar_refs, ins, own_scratch)
        for fetch in fetches:
            fetch.copy.start()
        body(scalar_refs, ins, results, own_scratch)
        for push in pushes:
            if not push.started:
                push.push()
        for fetch in fetches:
            fetch.get()
        for push in pushes:
            push.copy.wait()

    where = {Place.FAR: hbm, Place.FEW: hbm, Place.RAW: hbm, Place.AUTO: vmem, Place.NEAR: vmem, Place.SCALAR: smem}
    buffers = [
        (pltpu.SMEM if place == Place.FEW else pltpu.VMEM)(array.shape, array.dtype)
        for array, place in fetched
    ]
    buffers += [pltpu.VMEM(shape, kind) for shape, kind in pushed]
    buffers += [pltpu.SemaphoreType.DMA((max(len(group), 1),)) for group in (fetched, pushed)]
    pinned = [
        array if place == Place.AUTO else pltpu.with_memory_space_constraint(array, pltpu.HBM)
        for array, place in arrays.values()
    ]
    results = pl.pallas_call(
        kernel,
        name=name,
        out_shape=[
            {Place.FAR: pltpu.HBM, Place.NEAR: pltpu.VMEM}.get(place, jax.ShapeDtypeStruct)(shape, kind)
            for shape, kind, place in outs.values()
        ],
        in_specs=[smem] * len(scalars) + [where[place] for unused, place in arrays.values()],
        out_specs=[where[place] for unused, unused, place in outs.values()],
        scratch_shapes=buffers + list(scratch),
        compiler_params=pltpu.CompilerParams(vmem_limit_bytes=LIMIT),
    )(*scalars, *pinned)
    return dict(zip(outs, results))


def exchange(array):
    return lax.all_to_all(array, "dp", split_axis=0, concat_axis=0, tiled=True)


def exchange_by_core(array, devices):
    groups = [list(range(core, devices, 2)) for core in range(2)]
    return lax.all_to_all(
        array, "dp", split_axis=0, concat_axis=0, tiled=True, axis_index_groups=groups
    )


def swap(array, devices):
    return lax.ppermute(array, "dp", [(i, i ^ 1) for i in range(devices)])


def compact(
    text_input, eot_index, image_input, ln1_gain, ln1_bias, w_qkv, w_attn_out, ln2_gain, ln2_bias,
    w_fc, w_fc_out, img_ln1_gain, img_ln1_bias, img_w_qkv, img_w_attn_out, img_ln2_gain,
    img_ln2_bias, img_w_fc, img_w_fc_out, final_gain, final_bias, text_proj, image_gain,
    image_bias, image_proj, logit_scale,
):
    caps, seq, dim = text_input.shape
    img_seq = image_input.shape[1]
    devices = lax.axis_size("dp")
    plan = Plan(dim, w_fc.shape[2], devices)
    heads = dim // HEAD_DIM
    count = devices * caps
    hidden = plan.hidden
    device = lax.axis_index("dp").astype(jnp.int32).reshape(1)
    text_input, image_input = text_input.swapaxes(0, 1), image_input.swapaxes(0, 1)
    totals = caps * seq, caps * img_seq
    chips = devices // 2
    width = (heads - 1) * LANES

    first = {
        (K.X, 0): text_input, (K.X, 1): image_input,
        (K.GAIN, 0): ln1_gain, (K.BIAS, 0): ln1_bias,
        (K.GAIN, 1): img_ln1_gain, (K.BIAS, 1): img_ln1_bias,
    }
    late = {(K.W_QKV, 0): w_qkv, (K.W_QKV, 1): img_w_qkv}
    outputs_in = {(K.W_OUT, 0): w_attn_out, (K.W_OUT, 1): img_w_attn_out}
    second = {
        (K.GAIN2, 0): ln2_gain, (K.BIAS2, 0): ln2_bias,
        (K.GAIN2, 1): img_ln2_gain, (K.BIAS2, 1): img_ln2_bias,
    }
    hidden_in = {(K.W_FC, 0): w_fc, (K.W_FC, 1): img_w_fc}
    third = {
        (K.W_FC_OUT, 0): w_fc_out, (K.W_FC_OUT, 1): img_w_fc_out,
        (K.HEAD_GAIN, 0): final_gain, (K.HEAD_BIAS, 0): final_bias,
        (K.HEAD_GAIN, 1): image_gain, (K.HEAD_BIAS, 1): image_bias,
        (K.PROJ, 0): text_proj, (K.PROJ, 1): image_proj,
    }

    def far(arrays):
        return {key: (array, Place.FAR) for key, array in arrays.items()}

    eot = {K.EOT: (eot_index, Place.FEW)}
    rows = run(
        front_body(plan),
        "front",
        {K.ROWS: ((chips, caps, 4 * dim), BF16, Place.NEAR)},
        [],
        [],
        [eot | far(first), far(late)],
    )[K.ROWS]
    mine = exchange_by_core(rows, devices)

    unused, pack_rows = pack_at(dim, hidden, caps)
    side_outs = {K.VALUES: ((devices, caps, width), BF16, Place.FAR)}
    middle_outs = {
        K.SEND: ((devices, caps, width + dim + LANES), BF16, Place.FAR),
        K.ROWS: ((count, 4 * dim), BF16, Place.FAR),
    }
    for tower, total in enumerate(totals):
        side_outs |= {
            (K.NORMED, tower): ((total, dim), BF16, Place.FAR),
            (K.UNIT, tower): ((total, dim), BF16, Place.FAR),
            (K.PROBS, tower): ((heads * caps, total), F32, Place.FAR),
            (K.PACK, tower): ((pack_rows, dim), F32, Place.FAR),
        }
        middle_outs |= {
            (K.OWN, tower): (((2 + heads) * caps, dim), F32, Place.FAR),
            (K.SCORES, tower): ((heads * caps, total), BF16, Place.FAR),
        }
    side = run(side_body(plan), "side", side_outs, [[pltpu.VMEM((caps, hidden), F32)] * 2], [], [eot | far(first), far(late), far(outputs_in | second | hidden_in | third)])
    values = exchange(side.pop(K.VALUES))
    mine, side[K.PACK, 0] = lax.optimization_barrier((mine, side[K.PACK, 0]))
    others = swap(mine, devices)

    packs = {key: side[key] for key in ((K.PACK, 0), (K.PACK, 1))}
    middle = run(
        middle_body(plan),
        "middle",
        middle_outs,
        [pltpu.VMEM((chips, 2, caps, 4 * dim), BF16), pltpu.SemaphoreType.DMA((2,))],
        [device, logit_scale],
        [
            {K.MINE: (mine, Place.AUTO), K.OTHERS: (others, Place.AUTO)}
            | {key: (array, Place.AUTO) for key, array in hidden_in.items()}
            | far(outputs_in | second),
            far(third | packs),
            far(late)
            | far({(name, tower): side[name, tower] for name in (K.NORMED, K.PROBS, K.UNIT) for tower in (0, 1)}),
        ],
        join_rows,
    )
    send, values = lax.optimization_barrier((middle[K.SEND], values))
    sent = exchange(send)

    share_rows = plan.rows_out
    region = (plan.total - plan.out_at) // LANES
    head_region = plan.head_total // LANES
    attended = {}
    tail_outs = {K.LOSS: ((1,), F32, Place.SCALAR), K.SCALE: ((1,), F32, Place.SCALAR)}
    for tower, length in enumerate((seq, img_seq)):
        for name, source in ((K.PROBS, side), (K.PACK, side), (K.OWN, middle), (K.SCORES, middle)):
            attended[name, tower] = source[name, tower]
        tail_outs |= {
            (K.PART, tower): ((share_rows, LANES), F32, Place.NEAR),
            (K.INPUT, tower): ((length, caps, dim), F32, Place.FAR),
        }
    tail_outs |= {
        K.HEAD: ((plan.head_rows_out, LANES), F32, Place.FAR),
        K.WINDOWS: ((count, LANES), BF16, Place.NEAR),
        K.QUERIES: ((count, 2 * dim), BF16, Place.NEAR),
        K.VALUES: ((2, plan.pad, dim), F32, Place.NEAR),
    }
    tail = run(
        tail_body(plan),
        "tail",
        tail_outs,
        [
            pltpu.VMEM((region + 2 * share_rows + 8, LANES), F32),
            pltpu.VMEM((head_region + plan.head_rows_out + 8, LANES), F32),
            pltpu.VMEM((totals[0], dim), F32),
            pltpu.VMEM((totals[1], dim), F32),
            pltpu.VMEM((8, dim), F32),
            [pltpu.VMEM((count, hidden), F32)] * 2,
            [pltpu.VMEM((count, hidden), BF16)] * 2,
            [pltpu.VMEM((count, hidden), BF16)] * 2,
            pltpu.VMEM((2, dim, dim), BF16),
            pltpu.SemaphoreType.DMA((2,)),
        ],
        [device, logit_scale],
        [
            eot | far(first),
            far(attended),
            far({K.ROWS: middle[K.ROWS]} | outputs_in | second | hidden_in),
            far(third),
            far({K.VALUES: values.reshape(count, width)})
            | {key: (array, Place.RAW) for key, array in late.items()},
        ],
        tail_ahead(plan),
    )
    sent, tail[K.WINDOWS] = lax.optimization_barrier((sent, tail[K.WINDOWS]))
    swapped = swap(sent[:, :, width:], devices)
    flat_rows = max(2 * dim + plan.pad * plan.row, 2 * dim + 2 * plan.row + share_rows * LANES) // LANES
    names = [(K.PART, 0), (K.PART, 1), K.WINDOWS, K.QUERIES, K.VALUES]
    shares = run(
        last_body(plan),
        "last",
        {(K.SHARE, tower): ((1, plan.share), F32, Place.FAR) for tower in (0, 1)},
        [
            pltpu.VMEM((2, flat_rows // 8 * 8 + 16, LANES), F32),
            pltpu.VMEM((count, 2 * dim), BF16),
        ],
        [device],
        [
            {name: (tail[name], Place.AUTO) for name in names}
            | {K.SENT: (sent.reshape(count, -1), Place.AUTO)}
            | {K.SWAPPED: (swapped.reshape(count, -1), Place.AUTO)},
        ],
    )

    def cut(array, size):
        return array.reshape(-1)[:size]

    return (
        tail[K.LOSS],
        tail[K.INPUT, 0].swapaxes(0, 1),
        tail[K.INPUT, 1].swapaxes(0, 1),
        shares[K.SHARE, 0],
        shares[K.SHARE, 1],
        cut(tail[K.HEAD], plan.head_share),
        tail[K.SCALE],
    )


def norm_apply(values, gain, bias):
    center = values - jnp.mean(values, -1, keepdims=True)
    spread = jnp.mean(center * center, -1, keepdims=True)
    return center * lax.rsqrt(spread + EPS) * gain + bias


def quick_gelu(values):
    return values * jax.nn.sigmoid(1.702 * values)


def unit_rows(values):
    return values * lax.rsqrt(jnp.sum(values * values, -1, keepdims=True) + UNIT_EPS)


def causal_mask(seq_len):
    row_pos = lax.broadcasted_iota(jnp.int32, (seq_len, seq_len), 0)
    col_pos = lax.broadcasted_iota(jnp.int32, (seq_len, seq_len), 1)
    return col_pos <= row_pos


def matmul(left, right):
    return jnp.dot(left, right, preferred_element_type=jnp.float32)


def inner_rows(left, right):
    return lax.dot_general(
        left, right, (((0,), (0,)), ((), ())), preferred_element_type=jnp.float32
    )


def outer_cols(left, right):
    return lax.dot_general(
        left, right, (((1,), (1,)), ((), ())), preferred_element_type=jnp.float32
    )


def layer_forward(stream, weights, causal):
    gain_one, bias_one, w_qkv, w_out, gain_two, bias_two, w_fc, w_fc_out = weights
    num_caps, seq_len, feat_dim = stream.shape
    num_heads = feat_dim // HEAD_DIM
    num_rows = num_caps * seq_len
    normed_one = (
        norm_apply(stream, gain_one, bias_one).astype(jnp.bfloat16).reshape(num_rows, feat_dim)
    )
    packed = (
        matmul(normed_one, w_qkv)
        .astype(jnp.bfloat16)
        .reshape(num_caps, seq_len, 3, num_heads, HEAD_DIM)
    )
    queries = packed[:, :, 0]
    key_rows = packed[:, :, 1]
    value_rows = packed[:, :, 2]
    raw_score = jnp.einsum("bqhd,bkhd->bhqk", queries, key_rows, preferred_element_type=jnp.float32)
    scores = raw_score * HEAD_DIM ** (-0.5)
    if causal:
        scores = jnp.where(causal_mask(seq_len), scores, MASKED)
    row_peak = jnp.max(scores, -1, keepdims=True)
    log_total = row_peak + jnp.log(jnp.sum(jnp.exp(scores - row_peak), -1, keepdims=True))
    attn_probs = jnp.exp(scores - log_total)
    probs_low = attn_probs.astype(jnp.bfloat16)
    mixed_rows = jnp.einsum(
        "bhqk,bkhd->bqhd", probs_low, value_rows, preferred_element_type=jnp.float32
    )
    mixed_rows = mixed_rows.astype(jnp.bfloat16).reshape(num_rows, feat_dim)
    middle = stream + matmul(mixed_rows, w_out).reshape(num_caps, seq_len, feat_dim)
    normed_two = (
        norm_apply(middle, gain_two, bias_two).astype(jnp.bfloat16).reshape(num_rows, feat_dim)
    )
    hidden = matmul(normed_two, w_fc)
    active = quick_gelu(hidden).astype(jnp.bfloat16)
    result = middle + matmul(active, w_fc_out).reshape(num_caps, seq_len, feat_dim)
    return (
        result,
        (normed_one, packed, attn_probs, probs_low, mixed_rows, middle, normed_two, hidden, active),
    )


def layer_backward(stream, weights, grad_out, causal):
    gain_one, bias_one, w_qkv, w_out, gain_two, bias_two, w_fc, w_fc_out = weights
    num_caps, seq_len, feat_dim = stream.shape
    num_heads = feat_dim // HEAD_DIM
    num_rows = num_caps * seq_len
    unused, kept = layer_forward(stream, weights, causal)
    normed_one, packed, attn_probs, probs_low, mixed_rows, middle, normed_two, hidden, active = kept
    grad_low = grad_out.reshape(num_rows, feat_dim).astype(jnp.bfloat16)
    grad_fc_out = inner_rows(active, grad_low)
    grad_active = outer_cols(grad_low, w_fc_out)
    unused_gelu, gelu_back = jax.vjp(quick_gelu, hidden)
    grad_hidden = gelu_back(grad_active)[0].astype(jnp.bfloat16)
    grad_fc = inner_rows(normed_two, grad_hidden)
    grad_normed_two = outer_cols(grad_hidden, w_fc)
    unused_two, norm_back_two = jax.vjp(norm_apply, middle, gain_two, bias_two)
    grad_mid_norm, grad_gain_two, grad_bias_two = norm_back_two(
        grad_normed_two.reshape(num_caps, seq_len, feat_dim)
    )
    grad_middle = grad_out + grad_mid_norm
    middle_low = grad_middle.reshape(num_rows, feat_dim).astype(jnp.bfloat16)
    grad_w_out = inner_rows(mixed_rows, middle_low)
    grad_mixed = (
        outer_cols(middle_low, w_out)
        .astype(jnp.bfloat16)
        .reshape(num_caps, seq_len, num_heads, HEAD_DIM)
    )
    queries = packed[:, :, 0]
    key_rows = packed[:, :, 1]
    value_rows = packed[:, :, 2]
    grad_values = jnp.einsum(
        "bhqk,bqhd->bkhd", probs_low, grad_mixed, preferred_element_type=jnp.float32
    )
    grad_probs = jnp.einsum(
        "bqhd,bkhd->bhqk", grad_mixed, value_rows, preferred_element_type=jnp.float32
    )
    row_inner = jnp.sum(attn_probs * grad_probs, -1, keepdims=True)
    grad_raw = (attn_probs * (grad_probs - row_inner) * HEAD_DIM ** (-0.5)).astype(jnp.bfloat16)
    grad_queries = jnp.einsum(
        "bhqk,bkhd->bqhd", grad_raw, key_rows, preferred_element_type=jnp.float32
    )
    grad_keys = jnp.einsum("bhqk,bqhd->bkhd", grad_raw, queries, preferred_element_type=jnp.float32)
    grad_packed = (
        jnp.stack([grad_queries, grad_keys, grad_values], 2)
        .astype(jnp.bfloat16)
        .reshape(num_rows, 3 * feat_dim)
    )
    grad_qkv = inner_rows(normed_one, grad_packed)
    grad_normed_one = outer_cols(grad_packed, w_qkv)
    unused_one, norm_back_one = jax.vjp(norm_apply, stream, gain_one, bias_one)
    grad_in_norm, grad_gain_one, grad_bias_one = norm_back_one(
        grad_normed_one.reshape(num_caps, seq_len, feat_dim)
    )
    grads_here = [
        grad_gain_one,
        grad_bias_one,
        grad_qkv,
        grad_w_out,
        grad_gain_two,
        grad_bias_two,
        grad_fc,
        grad_fc_out,
    ]
    return (grad_middle + grad_in_norm, grads_here)


def head_forward(features, gain, bias, proj):
    normed = norm_apply(features, gain, bias).astype(jnp.bfloat16)
    embedded = matmul(normed, proj)
    return (unit_rows(embedded), (normed, embedded))


def head_backward(features, gain, bias, proj, kept, grad_unit):
    normed, embedded = kept
    unused_unit, unit_back = jax.vjp(unit_rows, embedded)
    grad_embed = unit_back(grad_unit)[0].astype(jnp.bfloat16)
    grad_proj = inner_rows(normed, grad_embed)
    grad_normed = outer_cols(grad_embed, proj)
    unused_norm, norm_back = jax.vjp(norm_apply, features, gain, bias)
    grad_feat, grad_gain, grad_bias = norm_back(grad_normed)
    return (grad_feat, [grad_gain, grad_bias, grad_proj])


def plain_contrast(own_rows, other_rows, multiplier, start):
    logits = multiplier * outer_cols(own_rows, other_rows)
    row_peak = jnp.max(logits, -1, keepdims=True)
    log_total = row_peak + jnp.log(jnp.sum(jnp.exp(logits - row_peak), -1, keepdims=True))
    col_pos = lax.broadcasted_iota(jnp.int32, logits.shape, 1)
    target_pos = lax.broadcasted_iota(jnp.int32, logits.shape, 0) + start
    matched = (col_pos == target_pos).astype(jnp.float32)
    loss_sum = jnp.sum(log_total) - jnp.sum(matched * logits)
    grad_logits = 0.5 * (jnp.exp(logits - log_total) - matched)
    scale_part = jnp.sum(grad_logits * logits)
    return (loss_sum, scale_part, (multiplier * grad_logits).astype(jnp.bfloat16), log_total[:, 0])


def pack_flat(arrays, devices):
    flat = jnp.concatenate([array.reshape(-1) for array in arrays])
    padding = -flat.shape[0] % devices
    return jnp.concatenate([flat, jnp.zeros((padding,), jnp.float32)])


def plain(
    text_input,
    eot_index,
    image_input,
    ln1_gain,
    ln1_bias,
    w_qkv,
    w_attn_out,
    ln2_gain,
    ln2_bias,
    w_fc,
    w_fc_out,
    img_ln1_gain,
    img_ln1_bias,
    img_w_qkv,
    img_w_attn_out,
    img_ln2_gain,
    img_ln2_bias,
    img_w_fc,
    img_w_fc_out,
    final_gain,
    final_bias,
    text_proj,
    image_gain,
    image_bias,
    image_proj,
    logit_scale,
):
    num_caps, seq_len, feat_dim = text_input.shape
    devices = lax.axis_size("dp")
    all_caps = num_caps * devices
    start = lax.axis_index("dp") * num_caps
    depth = ln1_gain.shape[0]
    text_stack = (ln1_gain, ln1_bias, w_qkv, w_attn_out, ln2_gain, ln2_bias, w_fc, w_fc_out)
    image_stack = (
        img_ln1_gain,
        img_ln1_bias,
        img_w_qkv,
        img_w_attn_out,
        img_ln2_gain,
        img_ln2_bias,
        img_w_fc,
        img_w_fc_out,
    )

    def text_weights(layer_num):
        return tuple((array[layer_num] for array in text_stack))

    def image_weights(layer_num):
        return tuple((array[layer_num] for array in image_stack))

    stream = text_input.astype(jnp.float32)
    layer_num = 0
    text_saved = [stream]
    stream, unused = layer_forward(stream, text_weights(layer_num), True)
    pooled = jnp.take_along_axis(stream, eot_index[:, None, None], axis=1)[:, 0]
    picture = image_input.astype(jnp.float32)
    layer_num = 0
    image_saved = [picture]
    picture, unused = layer_forward(picture, image_weights(layer_num), False)
    image_pooled = picture[:, 0]
    text_unit, text_kept = head_forward(pooled, final_gain, final_bias, text_proj)
    image_unit, image_kept = head_forward(image_pooled, image_gain, image_bias, image_proj)
    image_low = image_unit.astype(jnp.bfloat16)
    text_low = text_unit.astype(jnp.bfloat16)
    image_all, text_all = (
        lax.all_gather(image_low, "dp", axis=0, tiled=True),
        lax.all_gather(text_low, "dp", axis=0, tiled=True),
    )
    multiplier = jnp.exp(logit_scale[0])
    loss_image, scale_image, grad_raw_it, unused_it = plain_contrast(
        image_low, text_all, multiplier, start
    )
    loss_text, scale_text, grad_raw_ti, unused_ti = plain_contrast(text_low, image_all, multiplier, start)
    spread_text = inner_rows(grad_raw_it, image_low)
    spread_image = inner_rows(grad_raw_ti, text_low)
    back_text, back_image = (
        lax.psum_scatter(spread_text, "dp", scatter_dimension=0, tiled=True),
        lax.psum_scatter(spread_image, "dp", scatter_dimension=0, tiled=True),
    )
    total, grad_scale = lax.psum((loss_image + loss_text, scale_image + scale_text), "dp")
    grad_image_unit = matmul(grad_raw_it, text_all) + back_image
    grad_text_unit = matmul(grad_raw_ti, image_all) + back_text
    grad_pooled, text_head_grads = head_backward(
        pooled, final_gain, final_bias, text_proj, text_kept, grad_text_unit
    )
    grad_image_pooled, image_head_grads = head_backward(
        image_pooled, image_gain, image_bias, image_proj, image_kept, grad_image_unit
    )
    head_flat = pack_flat(text_head_grads + image_head_grads, devices)
    image_flat = [None] * depth
    img_seq = image_input.shape[1]
    img_dim = image_input.shape[2]
    grad_picture = jnp.concatenate(
        [grad_image_pooled[:, None, :], jnp.zeros((num_caps, img_seq - 1, img_dim), jnp.float32)], 1
    )
    for layer_num in reversed(range(depth)):
        grad_picture, grads_here = layer_backward(
            image_saved[layer_num], image_weights(layer_num), grad_picture, False
        )
        image_flat[layer_num] = pack_flat(grads_here, devices)
    text_flat = [None] * depth
    selected = (
        lax.broadcasted_iota(jnp.int32, (num_caps, seq_len), 1) == eot_index[:, None]
    ).astype(jnp.float32)
    grad_stream = selected[:, :, None] * grad_pooled[:, None, :]
    for layer_num in reversed(range(depth)):
        grad_stream, grads_here = layer_backward(
            text_saved[layer_num], text_weights(layer_num), grad_stream, True
        )
        text_flat[layer_num] = pack_flat(grads_here, devices)
    text_share, image_share, head_share = (
        lax.psum_scatter(jnp.stack(text_flat), "dp", scatter_dimension=1, tiled=True),
        lax.psum_scatter(jnp.stack(image_flat), "dp", scatter_dimension=1, tiled=True),
        lax.psum_scatter(head_flat, "dp", scatter_dimension=0, tiled=True),
    )
    loss = (total / (2 * all_caps)).reshape(1)
    return (
        loss,
        grad_stream,
        grad_picture,
        text_share,
        image_share,
        head_share,
        grad_scale.reshape(1),
    )


def shards(*args):
    caps = args[0].shape[0] * lax.axis_size("dp")
    return compact(*args) if caps <= 512 else plain(*args)


def solution(mesh):
    return jax.shard_map(
        shards,
        mesh=mesh,
        in_specs=(
            P("dp", None, None),
            P("dp"),
            P("dp", None, None),
            P(),
            P(),
            P(),
            P(),
            P(),
            P(),
            P(),
            P(),
            P(),
            P(),
            P(),
            P(),
            P(),
            P(),
            P(),
            P(),
            P(),
            P(),
            P(),
            P(),
            P(),
            P(),
            P(),
        ),
        out_specs=(
            P(),
            P("dp", None, None),
            P("dp", None, None),
            P(None, "dp"),
            P(None, "dp"),
            P("dp"),
            P(),
        ),
        check_vma=False,
    )
```

```python
import enum

import jax
import jax.numpy as jnp
from jax import lax
from jax.experimental import pallas as pl
from jax.experimental.pallas import tpu as pltpu
from jax.sharding import PartitionSpec as P

HEAD_DIM = 64
LANES = 128

EPS = 1e-05
UNIT_EPS = 1e-06
MASKED = -1000000000.0
LIMIT = 44 * 2**20
F32 = jnp.float32
BF16 = jnp.bfloat16


class Place(enum.Enum):
    FAR = enum.auto()
    FEW = enum.auto()
    RAW = enum.auto()
    AUTO = enum.auto()
    NEAR = enum.auto()
    SCALAR = enum.auto()


class K(enum.Enum):
    BIAS = enum.auto()
    BIAS2 = enum.auto()
    EOT = enum.auto()
    GAIN = enum.auto()
    GAIN2 = enum.auto()
    HEAD = enum.auto()
    HEAD_BIAS = enum.auto()
    HEAD_GAIN = enum.auto()
    INPUT = enum.auto()
    LOSS = enum.auto()
    MINE = enum.auto()
    MIXED = enum.auto()
    NORMED = enum.auto()
    OTHERS = enum.auto()
    OWN = enum.auto()
    PACK = enum.auto()
    PART = enum.auto()
    PROBS = enum.auto()
    PROJ = enum.auto()
    QUERIES = enum.auto()
    ROWS = enum.auto()
    SCALE = enum.auto()
    SCORES = enum.auto()
    SEND = enum.auto()
    SENT = enum.auto()
    SWAPPED = enum.auto()
    SHARE = enum.auto()
    UNIT = enum.auto()
    VALUES = enum.auto()
    W_FC = enum.auto()
    W_FC_OUT = enum.auto()
    W_OUT = enum.auto()
    W_QKV = enum.auto()
    W_QUERY = enum.auto()
    WINDOWS = enum.auto()
    X = enum.auto()


def dot(left, right):
    return jnp.dot(left, right, preferred_element_type=F32)


def dot_nt(left, right):
    return lax.dot_general(left, right, (((1,), (1,)), ((), ())), preferred_element_type=F32)


def dot_tn(left, right):
    return lax.dot_general(left, right, (((0,), (0,)), ((), ())), preferred_element_type=F32)


def summed_through(rows, weights):
    total = dot(jnp.ones((8, rows.shape[0]), BF16), rows)
    high = total.astype(BF16)
    low = (total - high.astype(F32)).astype(BF16)
    both = dot_nt(jnp.concatenate([high, low], 0), weights)
    return both[:1] + both[8:9]


def standard(values):
    center = values - jnp.mean(values, -1, keepdims=True)
    scale = lax.rsqrt(jnp.mean(center * center, -1, keepdims=True) + EPS)
    return center * scale, scale


def norm_back(grad, unit, scale, gain):
    scaled = grad * gain
    return scale * (
        scaled
        - jnp.mean(scaled, -1, keepdims=True)
        - unit * jnp.mean(scaled * unit, -1, keepdims=True)
    )


def head_masks(width):
    lane = lax.broadcasted_iota(jnp.int32, (1, width), 1)
    return [
        ((lane >= h * HEAD_DIM) & (lane < (h + 1) * HEAD_DIM)).astype(F32)
        for h in range(width // HEAD_DIM)
    ]


def spread(rows):
    return jnp.concatenate([rows * mask for mask in head_masks(rows.shape[1])], 0)


def collect(rows, caps):
    masks = head_masks(rows.shape[1])
    return sum(rows[h * caps : (h + 1) * caps] * mask for h, mask in enumerate(masks))


def picked_columns(caps, total, ends):
    cap = lax.broadcasted_iota(jnp.int32, (caps, 1), 0)
    at = cap
    for b in range(caps):
        at = jnp.where(cap == b, ends[b] * caps + b, at)
    column = lax.broadcasted_iota(jnp.int32, (caps, total), 1)
    chosen = jnp.where(column == at, 1.0, 0.0).astype(BF16)
    return chosen, column, at


class Plan:
    def __init__(self, dim, hidden, devices, caps):
        self.dim, self.hidden, self.devices = dim, hidden, devices
        self.row = 3 * dim
        self.qkv_at = 2 * dim
        self.out_at = self.qkv_at + dim * self.row
        self.norm_at = self.out_at + dim * dim
        self.fc_at = self.norm_at + 2 * dim
        self.fc_out_at = self.fc_at + dim * hidden
        self.total = self.fc_out_at + hidden * dim
        self.share = -(-self.total // devices)
        self.head_total = 2 * (2 * dim + dim * dim)
        self.head_share = -(-self.head_total // devices)
        self.roots = -(-self.out_at // self.share)
        self.rows_out = -(-(self.share // LANES + 2) // 8) * 8
        self.head_rows_out = -(-(self.head_share // LANES + 2) // 8) * 8
        ends = [min((d + 1) * self.share - self.qkv_at, dim * self.row) for d in range(self.roots)]
        self.window = max((end - 1) // self.row + 1 - self.column(d) for d, end in enumerate(ends))
        self.used = 2 * self.window
        self.piece = LANES - self.used
        self.extra = dim // caps
        self.spare, at = [], 0
        for h in reversed(range(dim // HEAD_DIM - 1)):
            start = self.used + min(max(self.used - h * self.piece, 0), self.piece)
            size = min(LANES - start, self.extra - at)
            self.spare.append((h, start, size, at))
            at += size
        assert self.piece > 0 and -(-self.used // self.piece) < dim // HEAD_DIM
        assert at == self.extra <= LANES
        self.spare_from = min(h for h, unused, size, unused in self.spare if size > 0)

    def column(self, device):
        if isinstance(device, int):
            return min(max(device * self.share - self.qkv_at, 0) // self.row, self.dim - 1)
        return jnp.minimum(jnp.maximum(device * self.share - self.qkv_at, 0) // self.row, self.dim - 1)


def window_tiles(plan, text, image, device, caps, extra):
    dim = text.shape[1]
    first = plan.column(device)
    lane = lax.broadcasted_iota(jnp.int32, (text.shape[0], LANES), 1)
    left = pltpu.roll(text, (dim - first) % dim, 1)[:, :LANES]
    right = pltpu.roll(image, (dim - first + plan.window) % dim, 1)[:, :LANES]
    both = jnp.where(lane < plan.window, left, right)
    heads = text.shape[0] // caps
    lane, last = lane[:caps], both[(heads - 1) * caps :]
    tiles = []
    for h in range(heads - 1):
        moved = pltpu.roll(last, (plan.used - h * plan.piece) % LANES, 1)
        tile = jnp.where(lane < plan.used, both[h * caps : (h + 1) * caps], moved)
        for at, start, size, taken in plan.spare if extra is not None else ():
            if at == h and size > 0:
                moved = pltpu.roll(extra, (start - taken) % LANES, 1)
                tile = jnp.where((lane >= start) & (lane < start + size), moved, tile)
        tiles.append(tile.astype(BF16))
    return jnp.concatenate(tiles, 1)


def last_head(plan, source, heads):
    lane = lax.broadcasted_iota(jnp.int32, (source.shape[0], LANES), 1)
    whole = jnp.zeros(lane.shape, F32)
    for h in range(-(-plan.used // plan.piece)):
        tile = source[:, h * LANES : (h + 1) * LANES].astype(F32)
        moved = pltpu.roll(tile, (LANES + h * plan.piece - plan.used) % LANES, 1)
        whole = jnp.where(lane >= h * plan.piece, moved, whole)
    return whole.astype(BF16)


def fold_row(row, caps):
    dim = row.shape[1]
    step = dim // caps
    rows = [pltpu.roll(row, (dim - i * step) % dim, 1)[:, :LANES] for i in range(caps)]
    return jnp.concatenate(rows, 0)


def spare_row(plan, sums, first, dim):
    caps = sums.shape[0]
    lane = lax.broadcasted_iota(jnp.int32, (caps, LANES), 1)
    folded = jnp.zeros((caps, LANES), F32)
    for h, start, size, taken in plan.spare:
        if size > 0:
            tile = sums[:, (h - first) * LANES : (h - first + 1) * LANES]
            moved = pltpu.roll(tile, (taken - start) % LANES, 1)
            folded = jnp.where((lane >= taken) & (lane < taken + size), moved, folded)
    wide = jnp.concatenate([folded, jnp.zeros((caps, dim - LANES), F32)], 1)
    lane = lax.broadcasted_iota(jnp.int32, (1, dim), 1)
    row = jnp.zeros((1, dim), F32)
    for i in range(caps):
        moved = pltpu.roll(wide[i : i + 1], i * plan.extra, 1) if i else wide[:1]
        row = jnp.where((lane >= i * plan.extra) & (lane < (i + 1) * plan.extra), moved, row)
    return row


def pack_windows(plan, target, text, image, caps, common):
    width = (text.shape[0] // caps - 1) * LANES
    held = plan.roots + plan.roots % 2

    def fill(device, core):
        extra = None if common is None else common[core][1]
        target[device, :, :width] = window_tiles(plan, text, image, device, caps, extra)
        if common is not None:
            target[device, :, width:] = common[core][0]

    if held <= 16:
        for device in range(held):
            fill(device, device % 2)
    else:

        @pl.loop(0, held // 2)
        def _(chip):
            for core in range(2):
                fill(2 * chip + core, core)


def clear_windows(plan, target):
    held = plan.roots + plan.roots % 2

    @pl.loop(held, target.shape[0])
    def _(device):
        target[device] = jnp.zeros(target.shape[1:], BF16)

    return slice(0, held), slice(held, target.shape[0])


def take_rows(source, at, count):
    row, lane_at = at // LANES, at % LANES
    lane = lax.broadcasted_iota(jnp.int32, (count, LANES), 1)
    mixed = jnp.where(
        lane >= lane_at, source[pl.ds(row, count), :], source[pl.ds(row + 1, count), :]
    )
    return pltpu.roll(mixed, lax.rem(LANES - lane_at, LANES), 1)


def put_tile(target, row, block):
    count, width = block.shape
    step = width // LANES
    for j in range(step):
        piece = block[:, j * LANES : (j + 1) * LANES]
        if count == 1:
            target[row + j : row + j + 1, :] = piece
        else:
            target[pl.ds(row + j, count, stride=step), :] = piece


def front_tower(tower, ins, picked, last):
    x = ins[K.X, tower].get()[...]
    seq, caps, dim = x.shape
    total = seq * caps
    heads = dim // HEAD_DIM
    source = x.reshape(total, dim)
    chosen, column, pick_at = picked_columns(caps, total, picked)
    last_at = pick_at
    if last is not picked:
        unused, unused, last_at = picked_columns(caps, total, last)
    pooled = dot(chosen, source)
    unit, unused = standard(source.astype(F32))
    yield
    pooled_unit, unused = standard(pooled)
    gain, bias = ins[K.GAIN, tower].get()[...], ins[K.BIAS, tower].get()[...]
    pooled_normed = (pooled_unit * gain + bias).astype(BF16)
    normed = (unit * gain + bias).astype(BF16)
    yield
    w_ref = ins[K.W_QKV, tower].get()
    query = dot(pooled_normed, w_ref[0, :, :dim]).astype(BF16).astype(F32)
    yield
    through_keys = dot_nt(spread(query).astype(BF16), w_ref[0, :, dim : 2 * dim])
    yield
    scores = dot_nt(through_keys.astype(BF16), normed) * HEAD_DIM ** (-0.5)
    yield
    cap = lax.broadcasted_iota(jnp.int32, (caps, 1), 0)
    seen = jnp.where((lax.rem(column, caps) == cap) & (column <= last_at), 1.0, 0.0)
    seen = jnp.concatenate([seen] * heads, 0) > 0.5
    peak = jnp.max(jnp.where(seen, scores, MASKED), -1, keepdims=True)
    sums = jnp.sum(jnp.where(seen, jnp.exp(scores - peak), 0.0), -1, keepdims=True)
    probs = jnp.where(seen, jnp.exp(scores - (peak + jnp.log(sums))), 0.0)
    yield
    values = dot(probs.astype(BF16), normed)
    yield
    mixed = collect(dot(values.astype(BF16), w_ref[0, :, 2 * dim :]), caps).astype(BF16)
    return pooled, mixed, (normed, unit, probs, query, through_keys, values, chosen)


def attended_towers(ins):
    eot = ins[K.EOT].get()
    caps = eot.shape[0]
    seq = ins[K.X, 1].buf.shape[0]
    ends = [eot[b] for b in range(caps)]
    views = (ends, ends), ([0] * caps, [seq - 1] * caps)
    return run_together([front_tower(tower, ins, *views[tower]) for tower in range(2)])


def front_body(plan):
    def body(scalars, ins, outs, scratch):
        payload = []
        for pooled, mixed, unused in attended_towers(ins):
            payload += [pooled.astype(BF16), mixed]
        payload = jnp.concatenate(payload, 1)
        rows = outs[K.ROWS].ref

        @pl.loop(0, rows.shape[0])
        def _(chip):
            rows[chip] = payload

    return body


def pack_at(dim, hidden, caps):
    heads = dim // HEAD_DIM
    sizes = [heads * caps] * 2 + [caps] * 8 + [caps * hidden // dim]
    places, at = [], 0
    for size in sizes:
        places.append(slice(at, at + size))
        at += size
    return places, at


def weights_of(tower, ins):
    names = K.W_OUT, K.GAIN2, K.BIAS2, K.W_FC, K.W_FC_OUT, K.HEAD_GAIN, K.HEAD_BIAS, K.PROJ
    return [ins[name, tower] for name in names]


def side_body(plan):
    def body(scalars, ins, outs, scratch):
        dim, hidden = plan.dim, plan.hidden
        caps = ins[K.EOT].buf.shape[0]
        places, unused = pack_at(dim, hidden, caps)
        towers = attended_towers(ins)
        clear_windows(plan, outs[K.VALUES].ref)
        pack_windows(plan, outs[K.VALUES].ref, towers[0][2][5], towers[1][2][5], caps, None)
        outs[K.VALUES].push()
        kept, hiddens = ([], []), scratch[0]
        for tower, (pooled, mixed, saved) in enumerate(towers):
            normed, unit, probs, query, through_keys, values, chosen = saved
            unit = unit.astype(BF16)
            for name, value in ((K.NORMED, normed), (K.UNIT, unit), (K.PROBS, probs)):
                outs[name, tower].ref[...] = value
                outs[name, tower].push()
            small = [through_keys, dot(probs.astype(BF16), unit), dot(chosen, unit), query]
            for place, value in zip(places, small):
                outs[K.PACK, tower].ref[place, :] = value
        run_together(
            [
                tower_forward(
                    pooled, mixed, weights_of(tower, ins), kept[tower], hiddens[tower], None
                )
                for tower, (pooled, mixed, unused) in enumerate(towers)
            ]
        )
        for tower in range(2):
            pack = outs[K.PACK, tower]
            for place, value in zip(places[4:10], kept[tower]):
                pack.ref[place, :] = jnp.broadcast_to(value, (caps, dim))
            for j in range(hidden // dim):
                at = places[10].start + j * caps
                pack.ref[at : at + caps, :] = gate_slope(hiddens[tower][:, j * dim : (j + 1) * dim])
            pack.push()

    return body


def run_together(steps):
    results = [None] * len(steps)
    live = list(range(len(steps)))
    while live:
        for index in list(live):
            try:
                next(steps[index])
            except StopIteration as stop:
                results[index] = stop.value
                live.remove(index)
    return results


def chunks(width):
    step = 512 if width % 512 == 0 else width
    return [slice(at, at + step) for at in range(0, width, step)]


def gate_slope(hidden):
    gate = jax.nn.sigmoid(1.702 * hidden)
    return gate + 1.702 * hidden * gate * (1.0 - gate)


def unit_rows_of(embed):
    length = lax.rsqrt(jnp.sum(embed * embed, -1, keepdims=True) + UNIT_EPS)
    return embed * length, length


def tower_forward(pooled, mixed, weights, kept, hidden_ref, active_ref):
    w_out, gain, bias, w_fc, w_fc_out, head_gain, head_bias, proj = weights
    middle = pooled + dot(mixed, w_out.get()[0])
    yield
    unit, scale = standard(middle)
    normed = (unit * gain.get()[...] + bias.get()[...]).astype(BF16)
    yield
    result = middle
    w_fc = w_fc.get()
    for cols in chunks(w_fc.shape[2]):
        hidden = dot(normed, w_fc[0, :, cols])
        active = (hidden * jax.nn.sigmoid(1.702 * hidden)).astype(BF16)
        if hidden_ref is not None:
            hidden_ref[:, cols] = hidden
        if active_ref is not None:
            active_ref[:, cols] = active
        result = result + dot(active, w_fc_out.get()[0, cols, :])
        yield
    head_unit, head_scale = standard(result)
    head_in = (head_unit * head_gain.get()[...][None] + head_bias.get()[...][None]).astype(BF16)
    embed = dot(head_in, proj.get()[...])
    yield
    unit_embed, length = unit_rows_of(embed)
    if kept is not None:
        kept += [unit, scale, head_unit, head_scale, unit_embed, length]
    return unit_embed.astype(BF16)


def log_sum(logits, axis):
    peak = jnp.max(logits, axis, keepdims=True)
    return peak + jnp.log(jnp.sum(jnp.exp(logits - peak), axis, keepdims=True))


def unit_gradient(multiplier, logits, own_total, other_total, matched, other):
    target = jnp.where(matched, 1.0, 0.0)
    own = 0.5 * multiplier * (jnp.exp(logits - own_total) - target)
    cross = 0.5 * multiplier * (jnp.exp(logits - other_total) - target)
    return dot(own.astype(BF16), other) + dot(cross.astype(BF16), other)


def embed_back(grad_unit, unit_embed, length):
    along = jnp.sum(unit_embed * grad_unit, -1, keepdims=True)
    return (length * (grad_unit - unit_embed * along)).astype(BF16)


def tower_backward(grad_embed, kept, slope, weights, keep_hidden):
    unit, scale, head_unit, head_scale = kept
    w_out, gain, bias, w_fc, w_fc_out, head_gain, head_bias, proj = weights
    grad_head = dot_nt(grad_embed, proj.get()[...])
    yield
    grad_result = norm_back(grad_head, head_unit, head_scale, head_gain.get()[...][None])
    grad_out = grad_result.astype(BF16)
    yield
    w_fc, w_fc_out = w_fc.get(), w_fc_out.get()
    grad_normed = 0.0
    for cols in chunks(w_fc.shape[2]):
        grad_active = dot_nt(grad_out, w_fc_out[0, cols, :])
        grad_hidden = (grad_active * slope(cols)).astype(BF16)
        if keep_hidden is not None:
            keep_hidden[:, cols] = grad_hidden
        grad_normed = grad_normed + dot_nt(grad_hidden, w_fc[0, :, cols])
        yield
    grad_middle = grad_result + norm_back(grad_normed, unit, scale, gain.get()[...])
    yield
    grad_mixed = dot_nt(grad_middle.astype(BF16), w_out.get()[0]).astype(BF16)
    yield
    return grad_head, grad_out, grad_normed, grad_middle, grad_mixed


def own_steps(plan, tower, units, multiplier, own_at, ins, outs):
    mine, other = units[tower], units[1 - tower]
    own_out, scores_out = outs[K.OWN, tower], outs[K.SCORES, tower]
    dim = plan.dim
    caps = scores_out.ref.shape[0] * HEAD_DIM // dim
    places, unused = pack_at(dim, plan.hidden, caps)
    other_total = log_sum(multiplier * dot_nt(mine, other), 0)
    yield
    pack = ins[K.PACK, tower].get()
    unit, scale, head_unit, head_scale, unit_embed, length = (pack[places[j], :] for j in range(4, 10))
    logits = multiplier * dot_nt(unit_embed.astype(BF16), other)
    matched = lax.broadcasted_iota(jnp.int32, logits.shape, 1) == own_at + lax.broadcasted_iota(
        jnp.int32, logits.shape, 0
    )
    grad_unit = unit_gradient(multiplier, logits, log_sum(logits, 1), other_total, matched, other)
    yield
    slope_at = places[10].start
    slopes = [pack[slope_at + j * caps : slope_at + (j + 1) * caps, :] for j in range(plan.hidden // dim)]
    slopes = jnp.concatenate(slopes, 1)
    done = yield from tower_backward(
        embed_back(grad_unit, unit_embed, length), (unit, scale, head_unit, head_scale),
        lambda cols: slopes[:, cols], weights_of(tower, ins), None,
    )
    grad_middle, grad_mixed = done[3], done[4].astype(F32)
    own_out.ref[:caps, :] = grad_middle
    w_ref = ins[K.W_QKV, tower].get()
    through_values = dot_nt(spread(grad_mixed).astype(BF16), w_ref[0, :, 2 * dim :])
    own_out.ref[2 * caps :, :] = through_values
    yield
    normed = ins[K.NORMED, tower].get()[...]
    grad_probs = dot_nt(through_values.astype(BF16), normed)
    yield
    probs = ins[K.PROBS, tower].get()[...]
    inner = jnp.sum(probs * grad_probs, -1, keepdims=True)
    grad_scores = (probs * (grad_probs - inner) * HEAD_DIM ** (-0.5)).astype(BF16)
    scores_out.ref[...] = grad_scores
    scores_out.push()
    yield
    spread_keys = dot(grad_scores, normed)
    yield
    grad_query = collect(dot(spread_keys.astype(BF16), w_ref[0, :, dim : 2 * dim]), caps).astype(BF16)
    yield
    units = pack[places[0], :] * dot(grad_scores, ins[K.UNIT, tower].get()[...])
    yield
    through_query = dot_nt(grad_query, w_ref[0, :, :dim])
    own_out.ref[caps : 2 * caps, :] = through_query
    own_out.push()
    units = units + through_values * pack[places[1], :]
    gain_part = jnp.sum(units, 0, keepdims=True) + jnp.sum(
        through_query * pack[places[2], :], 0, keepdims=True
    )
    return spread_keys, grad_query, gain_part


def forward_pair(plan, rows, ins, kept, hidden, active):
    dim = plan.dim
    return run_together(
        [
            tower_forward(
                rows[:, 2 * tower * dim : (2 * tower + 1) * dim].astype(F32),
                rows[:, (2 * tower + 1) * dim : (2 * tower + 2) * dim],
                weights_of(tower, ins), kept[tower], hidden[tower], active[tower],
            )
            for tower in range(2)
        ]
    )


def row_copies(scalars, ins, scratch):
    core = scalars[0][0] % 2
    return [
        pltpu.make_async_copy(ins[name].ref, scratch[0].at[:, at], scratch[1].at[i])
        for i, (name, at) in enumerate(((K.MINE, core), (K.OTHERS, 1 - core)))
    ]


def join_rows(scalars, ins, outs, scratch):
    for copy in row_copies(scalars, ins, scratch):
        copy.start()


def middle_body(plan):
    def body(scalars, ins, outs, scratch):
        at_ref, scale_ref = scalars
        rows_ref, sems = scratch
        dim = plan.dim
        device = at_ref[0]
        caps, wide = rows_ref.shape[2:]
        held, others = clear_windows(plan, outs[K.SEND].ref)
        outs[K.SEND].push_part(others)
        for copy in row_copies(scalars, ins, scratch):
            copy.wait()
        rows = rows_ref[...].reshape(plan.devices * caps, wide)
        outs[K.ROWS].ref[...] = rows
        outs[K.ROWS].push()
        units = forward_pair(plan, rows, ins, (None, None), (None, None), (None, None))
        multiplier = jnp.exp(jnp.full((1, 1), scale_ref[0], F32))
        own_at = device * caps
        parts = run_together(
            [own_steps(plan, tower, units, multiplier, own_at, ins, outs) for tower in range(2)]
        )
        common = [(query, fold_row(gain_part, caps)) for unused, query, gain_part in parts]
        keys_t, keys_i = parts[0][0], parts[1][0]
        pack_windows(plan, outs[K.SEND].ref, keys_t, keys_i, caps, common)
        outs[K.SEND].push_part(held)

    return body


def late_weights(ins, outs, scratch):
    value, sems = scratch[-2:]
    dim = value.shape[1]
    return [
        pltpu.make_async_copy(
            ins[K.W_QKV, tower].ref.at[0, :, pl.ds(at, dim)], target.at[tower], sems.at[2 * part + tower]
        )
        for part, (at, target) in enumerate(((0, outs[K.W_QUERY].ref), (2 * dim, value)))
        for tower in range(2)
    ]


def tail_ahead(plan):
    def ahead(scalars, ins, outs, scratch):
        copies = late_weights(ins, outs, scratch)

        @pl.when(scalars[0][0] < plan.roots)
        def _():
            for copy in copies[:2]:
                copy.start()

        @pl.when(scalars[0][0] == 0)
        def _():
            for copy in copies[2:]:
                copy.start()

    return ahead


def tail_body(plan):
    def body(scalars, ins, outs, scratch):
        at_ref, scale_ref = scalars
        dim, hidden_dim = plan.dim, plan.hidden
        loss_ref, scale_grad_ref = outs[K.LOSS].ref, outs[K.SCALE].ref
        flat, flat_head, wide_t, wide_i, small, hiddens, actives, hidden_grads, late, unused = scratch
        device = at_ref[0]
        eot = ins[K.EOT].get()
        caps = eot.shape[0]
        ends = [eot[b] for b in range(caps)]
        places, unused = pack_at(dim, hidden_dim, caps)
        multiplier = jnp.exp(jnp.full((1, 1), scale_ref[0], F32))

        def input_gradient(tower, picked, wide):
            x, gain = ins[K.X, tower].get(), ins[K.GAIN, tower].get()
            seq = x.shape[0]
            unit, scale = standard(x[...].reshape(seq * caps, dim).astype(F32))
            yield
            probs, pack, own, scores = (
                ins[name, tower].get() for name in (K.PROBS, K.PACK, K.OWN, K.SCORES)
            )
            left = jnp.concatenate([scores[...], probs[...].astype(BF16)], 0)
            right = jnp.concatenate([pack[places[0], :], own[2 * caps :, :]], 0).astype(BF16)
            wide[...] = dot_tn(left, right)
            yield
            for b in range(caps):
                at = picked[b] * caps + b
                wide[pl.ds(at, 1), :] = wide[pl.ds(at, 1), :] + own[caps + b : caps + b + 1, :]
            wide[...] = norm_back(wide[...], unit, scale, gain[...])
            yield
            for b in range(caps):
                at = picked[b] * caps + b
                wide[pl.ds(at, 1), :] = wide[pl.ds(at, 1), :] + own[b : b + 1, :]
            outs[K.INPUT, tower].ref[...] = wide[...].reshape(seq, caps, dim)
            outs[K.INPUT, tower].push()

        run_together([input_gradient(0, ends, wide_t), input_gradient(1, [0] * caps, wide_i)])

        rows = ins[K.ROWS].get()[...]
        count = rows.shape[0]
        kept = [], []
        units = forward_pair(plan, rows, ins, kept, hiddens, actives)
        logits = multiplier * dot_nt(units[1], units[0])
        matched = lax.broadcasted_iota(jnp.int32, logits.shape, 1) == lax.broadcasted_iota(
            jnp.int32, logits.shape, 0
        )
        row_total, column_total = log_sum(logits, 1), log_sum(logits, 0)
        target = jnp.where(matched, 1.0, 0.0)
        by_row = 0.5 * (jnp.exp(logits - row_total) - target)
        by_column = 0.5 * (jnp.exp(logits - column_total) - target)
        total = jnp.sum(row_total) + jnp.sum(column_total) - 2.0 * jnp.sum(target * logits)
        loss_ref[0] = total / (2 * count)
        scale_grad_ref[0] = jnp.sum((by_row + by_column) * logits)
        by_row = (multiplier * by_row).astype(BF16)
        by_column = (multiplier * by_column).astype(BF16)
        grad_units = (
            dot_tn(by_row, units[1]) + dot_tn(by_column, units[1]),
            dot(by_row, units[0]) + dot(by_column, units[0]),
        )

        grad_embeds = [embed_back(grad_units[tower], *kept[tower][4:]) for tower in range(2)]
        backs = run_together(
            [
                tower_backward(
                    grad_embeds[tower], kept[tower][:4],
                    lambda cols, hidden=hiddens[tower]: gate_slope(hidden[:, cols]),
                    weights_of(tower, ins), hidden_grads[tower],
                )
                for tower in range(2)
            ]
        )

        mixed_grads = []
        start, head_start = device * plan.share, device * plan.head_share
        front = plan.rows_out
        half = plan.head_total // 2
        for tower in range(2):
            weights = weights_of(tower, ins)
            gain, bias, head_gain, head_bias = (weights[j] for j in (1, 2, 5, 6))
            active, hidden_grad = actives[tower], hidden_grads[tower]
            grad_embed, done = grad_embeds[tower], backs[tower]
            grad_head, grad_out, grad_normed, grad_middle, grad_mixed = done
            unit, unused, head_unit = kept[tower][:3]
            mixed_grads.append(grad_mixed)
            middle_low = grad_middle.astype(BF16)
            normed = (unit * gain.get()[...] + bias.get()[...]).astype(BF16)
            head_in = head_unit * head_gain.get()[...][None] + head_bias.get()[...][None]
            head_in = head_in.astype(BF16)
            small[0:1, :] = jnp.sum(grad_normed * unit, 0, keepdims=True)
            small[1:2, :] = jnp.sum(grad_normed, 0, keepdims=True)
            small[2:3, :] = jnp.sum(grad_head * head_unit, 0, keepdims=True)
            small[3:4, :] = jnp.sum(grad_head, 0, keepdims=True)
            mixed = rows[:, (2 * tower + 1) * dim : (2 * tower + 2) * dim]

            def when_held(at, size, store):
                @pl.when((at < start + plan.share) & (at + size > start))
                def _():
                    store(front + (at - plan.out_at) // LANES)

            def when_kept(at, size, store):
                at = at + tower * half

                @pl.when((at < head_start + plan.head_share) & (at + size > head_start))
                def _():
                    store(at // LANES)

            def products(when, target, at, left, right):
                for t in range(left.shape[1] // LANES):
                    cols = slice(t * LANES, (t + 1) * LANES)
                    when(
                        at + t * LANES * right.shape[1],
                        LANES * right.shape[1],
                        lambda row: put_tile(target, row, dot_tn(left[:, cols], right[...])),
                    )

            def row_of(when, target, at, index):
                when(at, dim, lambda row: put_tile(target, row, small[index : index + 1, :]))

            products(when_held, flat, plan.out_at, mixed, middle_low)
            row_of(when_held, flat, plan.norm_at, 0)
            row_of(when_held, flat, plan.norm_at + dim, 1)
            products(when_held, flat, plan.fc_at, normed, hidden_grad)
            products(when_held, flat, plan.fc_out_at, active, grad_out)
            at = jnp.maximum(start - plan.out_at + front * LANES, 0)
            outs[K.PART, tower].ref[...] = take_rows(flat, at, plan.rows_out)
            outs[K.PART, tower].push()
            row_of(when_kept, flat_head, 0, 2)
            row_of(when_kept, flat_head, dim, 3)
            products(when_kept, flat_head, 2 * dim, head_in, grad_embed)

        outs[K.HEAD].ref[...] = take_rows(flat_head, head_start, plan.head_rows_out)
        outs[K.HEAD].push()

        copies = late_weights(ins, outs, scratch)

        @pl.when(device == 0)
        def _():
            for tower in range(2):
                copies[2 + tower].wait()
                outs[K.BIAS].ref[tower : tower + 1, :] = summed_through(mixed_grads[tower], late[tower])

        values = ins[K.VALUES].get()

        @pl.when(device < plan.roots)
        def _():
            for copy in copies[:2]:
                copy.wait()
            first = plan.column(device)
            lane = lax.broadcasted_iota(jnp.int32, (count, LANES), 1)
            picked_rows = []
            for tower in range(2):
                gain, bias = ins[K.GAIN, tower].get(), ins[K.BIAS, tower].get()
                pooled = rows[:, 2 * tower * dim : (2 * tower + 1) * dim].astype(F32)
                unit, unused = standard(pooled)
                normed = unit * gain[...] + bias[...]
                outs[K.QUERIES].ref[:, tower * dim : (tower + 1) * dim] = dot(
                    normed.astype(BF16), outs[K.W_QUERY].ref[tower]
                ).astype(BF16)
                shift = lax.rem(dim - first + tower * plan.window, dim)
                picked_rows.append(pltpu.roll(normed, shift, 1)[:, :LANES])
            end = last_head(plan, values, dim // HEAD_DIM)
            for j in range(dim // LANES):
                cols = slice(j * LANES, (j + 1) * LANES)
                block = window_product(plan, values, end, mixed_grads, (0, 0), j)
                for tower in range(2):
                    at = tower * plan.window
                    outs[K.VALUES].ref[tower, :, cols] = block[
                        at : at + plan.window, tower * LANES : (tower + 1) * LANES
                    ]
            outs[K.WINDOWS].ref[...] = jnp.where(lane < plan.window, picked_rows[0], picked_rows[1]).astype(BF16)

    return body


def window_product(plan, source, end, factors, offsets, j):
    lane = lax.broadcasted_iota(jnp.int32, (1, 2 * LANES), 1) % LANES
    right = [factor[:, at + j * LANES : at + (j + 1) * LANES] for factor, at in zip(factors, offsets)]
    right = jnp.concatenate(right, 1).astype(F32)
    total = 0.0
    for h in (2 * j, 2 * j + 1):
        left = end if (h + 1) * HEAD_DIM == plan.dim else source[:, h * LANES : (h + 1) * LANES]
        mine = (lane // HEAD_DIM == h % 2).astype(F32)
        total = total + dot_tn(left, (right * mine).astype(BF16))
    return total


def last_body(plan):
    def body(scalars, ins, outs, scratch):
        (at_ref,) = scalars
        flat, grad_query = scratch
        dim = plan.dim
        heads = dim // HEAD_DIM
        tiles = dim // LANES
        device = at_ref[0]
        parts = [ins[K.PART, tower].get() for tower in range(2)]

        def store(tower, block):
            line = outs[K.SHARE, tower].ref
            line[...] = block.reshape(1, block.shape[0] * LANES)[:, : plan.share]

        @pl.when(device >= plan.roots)
        def _():
            for tower in range(2):
                store(tower, parts[tower][...])

        names = K.SENT, K.SWAPPED, K.WINDOWS, K.QUERIES, K.VALUES, K.W_QUERY, K.BIAS
        sent_ref, swapped, windows, queries, value_part, w_query, bias = (
            ins[name].get() for name in names
        )

        @pl.when(device < plan.roots)
        def _():
            count = sent_ref.shape[0]
            caps = count // plan.devices
            first = plan.spare_from
            for core in range(2):

                @pl.when(device % 2 == core)
                def _():
                    received = sent_ref[:, first * LANES :], swapped[...]
                    for tower, values in enumerate(received if core == 0 else received[::-1]):
                        grad_query[:, tower * dim : (tower + 1) * dim] = values[:, -dim:]

            @pl.when(device == 0)
            def _():
                for tower, values in enumerate((sent_ref[:, first * LANES :], swapped[...])):
                    sums = values[:, :-dim].astype(F32).reshape(plan.devices, caps, -1)
                    put_tile(flat.at[tower], 0, spare_row(plan, jnp.sum(sums, 0), first, dim))
                    grads = grad_query[:, tower * dim : (tower + 1) * dim]
                    row = summed_through(grads, w_query[tower])
                    put_tile(flat.at[tower], tiles, row + bias[tower : tower + 1, :])

            query_part = dot_tn(windows[...], grad_query[...])
            end = last_head(plan, sent_ref, heads)
            for j in range(tiles):
                put = window_product(plan, sent_ref, end, (queries, queries), (0, dim), j)
                for tower in range(2):
                    rows = slice(tower * plan.window, (tower + 1) * plan.window)
                    own = slice(tower * LANES, (tower + 1) * LANES)
                    q_at = tower * dim + j * LANES
                    for part, block in enumerate(
                        (
                            query_part[rows, q_at : q_at + LANES],
                            put[rows, own],
                            value_part[tower, :, j * LANES : (j + 1) * LANES],
                        )
                    ):
                        flat[
                            tower,
                            pl.ds(2 * tiles + part * tiles + j, plan.window, stride=3 * tiles),
                            :,
                        ] = block
            start = device * plan.share
            at = start - plan.column(device) * plan.row
            shape = parts[0].shape
            index = (
                start
                + lax.broadcasted_iota(jnp.int32, shape, 0) * LANES
                + lax.broadcasted_iota(jnp.int32, shape, 1)
            )
            for tower in range(2):
                own = take_rows(flat.at[tower], at, plan.rows_out)
                store(tower, jnp.where(index < plan.out_at, own, parts[tower][...]))

    return body


class Fetch:
    def __init__(self, source, buf, sem, group):
        self.ref, self.buf, self.group = source, buf, group
        self.copy = pltpu.make_async_copy(source, buf, sem)
        group.members.append(self)

    def get(self):
        self.group.wait()
        return self.buf


class Group:
    def __init__(self):
        self.members, self.waited = [], False

    def wait(self):
        if not self.waited:
            self.waited = True
            for fetch in self.members:
                fetch.copy.wait()


class Here:
    def __init__(self, ref):
        self.buf = self.ref = ref

    def get(self):
        return self.buf

    def push(self):
        pass


class Push:
    def __init__(self, ref, target, sem):
        self.ref, self.target, self.sem, self.started = ref, target, sem, False
        self.copy = pltpu.make_async_copy(ref, target, sem)

    def push(self):
        self.started = True
        self.copy.start()

    def push_part(self, part):
        self.started = True
        pltpu.make_async_copy(self.ref.at[part], self.target.at[part], self.sem).start()


def run(body, name, outs, scratch, scalars, arrays, ahead=None):
    smem = pl.BlockSpec(memory_space=pltpu.SMEM)
    hbm = pl.BlockSpec(memory_space=pltpu.HBM)
    vmem = pl.BlockSpec(memory_space=pltpu.VMEM)
    groups = arrays
    arrays = {key: value for group in groups for key, value in group.items()}
    fetched = [(array, place) for array, place in arrays.values() if place in (Place.FAR, Place.FEW)]
    pushed = [(shape, kind) for shape, kind, place in outs.values() if place == Place.FAR]

    def kernel(*refs):
        at = 0

        def take(count):
            nonlocal at
            at += count
            return list(refs[at - count : at])

        scalar_refs, sources, targets = take(len(scalars)), take(len(arrays)), take(len(outs))
        in_bufs, out_bufs = take(len(fetched)), take(len(pushed))
        in_sems, out_sems = take(2)
        ins, results, fetches, pushes = {}, {}, [], []
        sources = iter(sources)
        chain = [Group() for unused in groups]
        for group, together in zip(groups, chain):
            for (key, (unused, place)), source in zip(group.items(), sources):
                if place in (Place.FAR, Place.FEW):
                    sem = in_sems.at[len(fetches)]
                    fetches.append(Fetch(source, in_bufs[len(fetches)], sem, together))
                    ins[key] = fetches[-1]
                else:
                    ins[key] = Here(source)
        for target, (key, (unused, unused, place)) in zip(targets, outs.items()):
            if place == Place.FAR:
                pushes.append(Push(out_bufs[len(pushes)], target, out_sems.at[len(pushes)]))
            results[key] = pushes[-1] if place == Place.FAR else Here(target)
        own_scratch = take(len(scratch))
        if ahead is not None:
            ahead(scalar_refs, ins, results, own_scratch)
        for fetch in fetches:
            fetch.copy.start()
        body(scalar_refs, ins, results, own_scratch)
        for push in pushes:
            if not push.started:
                push.push()
        for fetch in fetches:
            fetch.get()
        for push in pushes:
            push.copy.wait()

    where = {Place.FAR: hbm, Place.FEW: hbm, Place.RAW: hbm, Place.AUTO: vmem, Place.NEAR: vmem, Place.SCALAR: smem}
    buffers = [
        (pltpu.SMEM if place == Place.FEW else pltpu.VMEM)(array.shape, array.dtype)
        for array, place in fetched
    ]
    buffers += [pltpu.VMEM(shape, kind) for shape, kind in pushed]
    buffers += [pltpu.SemaphoreType.DMA((max(len(group), 1),)) for group in (fetched, pushed)]
    pinned = [
        array if place == Place.AUTO else pltpu.with_memory_space_constraint(array, pltpu.HBM)
        for array, place in arrays.values()
    ]
    results = pl.pallas_call(
        kernel,
        name=name,
        out_shape=[
            {Place.FAR: pltpu.HBM, Place.NEAR: pltpu.VMEM}.get(place, jax.ShapeDtypeStruct)(shape, kind)
            for shape, kind, place in outs.values()
        ],
        in_specs=[smem] * len(scalars) + [where[place] for unused, place in arrays.values()],
        out_specs=[where[place] for unused, unused, place in outs.values()],
        scratch_shapes=buffers + list(scratch),
        compiler_params=pltpu.CompilerParams(vmem_limit_bytes=LIMIT),
    )(*scalars, *pinned)
    return dict(zip(outs, results))


def exchange(array):
    return lax.all_to_all(array, "dp", split_axis=0, concat_axis=0, tiled=True)


def exchange_by_core(array, devices):
    groups = [list(range(core, devices, 2)) for core in range(2)]
    return lax.all_to_all(
        array, "dp", split_axis=0, concat_axis=0, tiled=True, axis_index_groups=groups
    )


def swap(array, devices):
    return lax.ppermute(array, "dp", [(i, i ^ 1) for i in range(devices)])


def compact(
    text_input, eot_index, image_input, ln1_gain, ln1_bias, w_qkv, w_attn_out, ln2_gain, ln2_bias,
    w_fc, w_fc_out, img_ln1_gain, img_ln1_bias, img_w_qkv, img_w_attn_out, img_ln2_gain,
    img_ln2_bias, img_w_fc, img_w_fc_out, final_gain, final_bias, text_proj, image_gain,
    image_bias, image_proj, logit_scale,
):
    caps, seq, dim = text_input.shape
    img_seq = image_input.shape[1]
    devices = lax.axis_size("dp")
    plan = Plan(dim, w_fc.shape[2], devices, caps)
    heads = dim // HEAD_DIM
    count = devices * caps
    hidden = plan.hidden
    device = lax.axis_index("dp").astype(jnp.int32).reshape(1)
    text_input, image_input = text_input.swapaxes(0, 1), image_input.swapaxes(0, 1)
    totals = caps * seq, caps * img_seq
    chips = devices // 2
    width = (heads - 1) * LANES

    first = {
        (K.X, 0): text_input, (K.X, 1): image_input,
        (K.GAIN, 0): ln1_gain, (K.BIAS, 0): ln1_bias,
        (K.GAIN, 1): img_ln1_gain, (K.BIAS, 1): img_ln1_bias,
    }
    late = {(K.W_QKV, 0): w_qkv, (K.W_QKV, 1): img_w_qkv}
    outputs_in = {(K.W_OUT, 0): w_attn_out, (K.W_OUT, 1): img_w_attn_out}
    second = {
        (K.GAIN2, 0): ln2_gain, (K.BIAS2, 0): ln2_bias,
        (K.GAIN2, 1): img_ln2_gain, (K.BIAS2, 1): img_ln2_bias,
    }
    hidden_in = {(K.W_FC, 0): w_fc, (K.W_FC, 1): img_w_fc}
    third = {
        (K.W_FC_OUT, 0): w_fc_out, (K.W_FC_OUT, 1): img_w_fc_out,
        (K.HEAD_GAIN, 0): final_gain, (K.HEAD_BIAS, 0): final_bias,
        (K.HEAD_GAIN, 1): image_gain, (K.HEAD_BIAS, 1): image_bias,
        (K.PROJ, 0): text_proj, (K.PROJ, 1): image_proj,
    }

    def far(arrays):
        return {key: (array, Place.FAR) for key, array in arrays.items()}

    eot = {K.EOT: (eot_index, Place.FEW)}
    rows = run(
        front_body(plan),
        "front",
        {K.ROWS: ((chips, caps, 4 * dim), BF16, Place.NEAR)},
        [],
        [],
        [eot | far(first), far(late)],
    )[K.ROWS]
    mine = exchange_by_core(rows, devices)

    unused, pack_rows = pack_at(dim, hidden, caps)
    side_outs = {K.VALUES: ((devices, caps, width), BF16, Place.FAR)}
    middle_outs = {
        K.SEND: ((devices, caps, width + dim), BF16, Place.FAR),
        K.ROWS: ((count, 4 * dim), BF16, Place.FAR),
    }
    for tower, total in enumerate(totals):
        side_outs |= {
            (K.NORMED, tower): ((total, dim), BF16, Place.FAR),
            (K.UNIT, tower): ((total, dim), BF16, Place.FAR),
            (K.PROBS, tower): ((heads * caps, total), F32, Place.FAR),
            (K.PACK, tower): ((pack_rows, dim), F32, Place.FAR),
        }
        middle_outs |= {
            (K.OWN, tower): (((2 + heads) * caps, dim), F32, Place.FAR),
            (K.SCORES, tower): ((heads * caps, total), BF16, Place.FAR),
        }
    side = run(side_body(plan), "side", side_outs, [[pltpu.VMEM((caps, hidden), F32)] * 2], [], [eot | far(first), far(late), far(outputs_in | second | hidden_in | third)])
    values = exchange(side.pop(K.VALUES))
    mine, side[K.PACK, 0] = lax.optimization_barrier((mine, side[K.PACK, 0]))
    others = swap(mine, devices)

    packs = {key: side[key] for key in ((K.PACK, 0), (K.PACK, 1))}
    middle = run(
        middle_body(plan),
        "middle",
        middle_outs,
        [pltpu.VMEM((chips, 2, caps, 4 * dim), BF16), pltpu.SemaphoreType.DMA((2,))],
        [device, logit_scale],
        [
            {K.MINE: (mine, Place.AUTO), K.OTHERS: (others, Place.AUTO)}
            | {key: (array, Place.AUTO) for key, array in hidden_in.items()}
            | far(outputs_in | second),
            far(third | packs),
            far(late)
            | far({(name, tower): side[name, tower] for name in (K.NORMED, K.PROBS, K.UNIT) for tower in (0, 1)}),
        ],
        join_rows,
    )
    send, values = lax.optimization_barrier((middle[K.SEND], values))
    sent = exchange(send)

    share_rows = plan.rows_out
    region = (plan.total - plan.out_at) // LANES
    head_region = plan.head_total // LANES
    attended = {}
    tail_outs = {K.LOSS: ((1,), F32, Place.SCALAR), K.SCALE: ((1,), F32, Place.SCALAR)}
    for tower, length in enumerate((seq, img_seq)):
        for name, source in ((K.PROBS, side), (K.PACK, side), (K.OWN, middle), (K.SCORES, middle)):
            attended[name, tower] = source[name, tower]
        tail_outs |= {
            (K.PART, tower): ((share_rows, LANES), F32, Place.NEAR),
            (K.INPUT, tower): ((length, caps, dim), F32, Place.FAR),
        }
    tail_outs |= {
        K.HEAD: ((plan.head_rows_out, LANES), F32, Place.FAR),
        K.WINDOWS: ((count, LANES), BF16, Place.NEAR),
        K.QUERIES: ((count, 2 * dim), BF16, Place.NEAR),
        K.VALUES: ((2, plan.window, dim), F32, Place.NEAR),
        K.W_QUERY: ((2, dim, dim), BF16, Place.NEAR),
        K.BIAS: ((8, dim), F32, Place.NEAR),
    }
    tail = run(
        tail_body(plan),
        "tail",
        tail_outs,
        [
            pltpu.VMEM((region + 2 * share_rows + 8, LANES), F32),
            pltpu.VMEM((head_region + plan.head_rows_out + 8, LANES), F32),
            pltpu.VMEM((totals[0], dim), F32),
            pltpu.VMEM((totals[1], dim), F32),
            pltpu.VMEM((8, dim), F32),
            [pltpu.VMEM((count, hidden), F32)] * 2,
            [pltpu.VMEM((count, hidden), BF16)] * 2,
            [pltpu.VMEM((count, hidden), BF16)] * 2,
            pltpu.VMEM((2, dim, dim), BF16),
            pltpu.SemaphoreType.DMA((4,)),
        ],
        [device, logit_scale],
        [
            eot | far(first),
            far(attended),
            far({K.ROWS: middle[K.ROWS]} | outputs_in | second | hidden_in),
            far(third),
            far({K.VALUES: values.reshape(count, width)})
            | {key: (array, Place.RAW) for key, array in late.items()},
        ],
        tail_ahead(plan),
    )
    sent, tail[K.WINDOWS] = lax.optimization_barrier((sent, tail[K.WINDOWS]))
    swapped = swap(sent[:, :, plan.spare_from * LANES :], devices)
    flat_rows = max(2 * dim + plan.window * plan.row, 2 * dim + 2 * plan.row + share_rows * LANES) // LANES
    names = [(K.PART, 0), (K.PART, 1), K.WINDOWS, K.QUERIES, K.VALUES, K.W_QUERY, K.BIAS]
    shares = run(
        last_body(plan),
        "last",
        {(K.SHARE, tower): ((1, plan.share), F32, Place.FAR) for tower in (0, 1)},
        [
            pltpu.VMEM((2, flat_rows // 8 * 8 + 16, LANES), F32),
            pltpu.VMEM((count, 2 * dim), BF16),
        ],
        [device],
        [
            {name: (tail[name], Place.AUTO) for name in names}
            | {K.SENT: (sent.reshape(count, -1), Place.AUTO)}
            | {K.SWAPPED: (swapped.reshape(count, -1), Place.AUTO)},
        ],
    )

    def cut(array, size):
        return array.reshape(-1)[:size]

    return (
        tail[K.LOSS],
        tail[K.INPUT, 0].swapaxes(0, 1),
        tail[K.INPUT, 1].swapaxes(0, 1),
        shares[K.SHARE, 0],
        shares[K.SHARE, 1],
        cut(tail[K.HEAD], plan.head_share),
        tail[K.SCALE],
    )


def norm_apply(values, gain, bias):
    center = values - jnp.mean(values, -1, keepdims=True)
    spread = jnp.mean(center * center, -1, keepdims=True)
    return center * lax.rsqrt(spread + EPS) * gain + bias


def quick_gelu(values):
    return values * jax.nn.sigmoid(1.702 * values)


def unit_rows(values):
    return values * lax.rsqrt(jnp.sum(values * values, -1, keepdims=True) + UNIT_EPS)


def causal_mask(seq_len):
    row_pos = lax.broadcasted_iota(jnp.int32, (seq_len, seq_len), 0)
    col_pos = lax.broadcasted_iota(jnp.int32, (seq_len, seq_len), 1)
    return col_pos <= row_pos


def matmul(left, right):
    return jnp.dot(left, right, preferred_element_type=jnp.float32)


def inner_rows(left, right):
    return lax.dot_general(
        left, right, (((0,), (0,)), ((), ())), preferred_element_type=jnp.float32
    )


def outer_cols(left, right):
    return lax.dot_general(
        left, right, (((1,), (1,)), ((), ())), preferred_element_type=jnp.float32
    )


def layer_forward(stream, weights, causal):
    gain_one, bias_one, w_qkv, w_out, gain_two, bias_two, w_fc, w_fc_out = weights
    num_caps, seq_len, feat_dim = stream.shape
    num_heads = feat_dim // HEAD_DIM
    num_rows = num_caps * seq_len
    normed_one = (
        norm_apply(stream, gain_one, bias_one).astype(jnp.bfloat16).reshape(num_rows, feat_dim)
    )
    packed = (
        matmul(normed_one, w_qkv)
        .astype(jnp.bfloat16)
        .reshape(num_caps, seq_len, 3, num_heads, HEAD_DIM)
    )
    queries = packed[:, :, 0]
    key_rows = packed[:, :, 1]
    value_rows = packed[:, :, 2]
    raw_score = jnp.einsum("bqhd,bkhd->bhqk", queries, key_rows, preferred_element_type=jnp.float32)
    scores = raw_score * HEAD_DIM ** (-0.5)
    if causal:
        scores = jnp.where(causal_mask(seq_len), scores, MASKED)
    row_peak = jnp.max(scores, -1, keepdims=True)
    log_total = row_peak + jnp.log(jnp.sum(jnp.exp(scores - row_peak), -1, keepdims=True))
    attn_probs = jnp.exp(scores - log_total)
    probs_low = attn_probs.astype(jnp.bfloat16)
    mixed_rows = jnp.einsum(
        "bhqk,bkhd->bqhd", probs_low, value_rows, preferred_element_type=jnp.float32
    )
    mixed_rows = mixed_rows.astype(jnp.bfloat16).reshape(num_rows, feat_dim)
    middle = stream + matmul(mixed_rows, w_out).reshape(num_caps, seq_len, feat_dim)
    normed_two = (
        norm_apply(middle, gain_two, bias_two).astype(jnp.bfloat16).reshape(num_rows, feat_dim)
    )
    hidden = matmul(normed_two, w_fc)
    active = quick_gelu(hidden).astype(jnp.bfloat16)
    result = middle + matmul(active, w_fc_out).reshape(num_caps, seq_len, feat_dim)
    return (
        result,
        (normed_one, packed, attn_probs, probs_low, mixed_rows, middle, normed_two, hidden, active),
    )


def layer_backward(stream, weights, grad_out, causal):
    gain_one, bias_one, w_qkv, w_out, gain_two, bias_two, w_fc, w_fc_out = weights
    num_caps, seq_len, feat_dim = stream.shape
    num_heads = feat_dim // HEAD_DIM
    num_rows = num_caps * seq_len
    unused, kept = layer_forward(stream, weights, causal)
    normed_one, packed, attn_probs, probs_low, mixed_rows, middle, normed_two, hidden, active = kept
    grad_low = grad_out.reshape(num_rows, feat_dim).astype(jnp.bfloat16)
    grad_fc_out = inner_rows(active, grad_low)
    grad_active = outer_cols(grad_low, w_fc_out)
    unused_gelu, gelu_back = jax.vjp(quick_gelu, hidden)
    grad_hidden = gelu_back(grad_active)[0].astype(jnp.bfloat16)
    grad_fc = inner_rows(normed_two, grad_hidden)
    grad_normed_two = outer_cols(grad_hidden, w_fc)
    unused_two, norm_back_two = jax.vjp(norm_apply, middle, gain_two, bias_two)
    grad_mid_norm, grad_gain_two, grad_bias_two = norm_back_two(
        grad_normed_two.reshape(num_caps, seq_len, feat_dim)
    )
    grad_middle = grad_out + grad_mid_norm
    middle_low = grad_middle.reshape(num_rows, feat_dim).astype(jnp.bfloat16)
    grad_w_out = inner_rows(mixed_rows, middle_low)
    grad_mixed = (
        outer_cols(middle_low, w_out)
        .astype(jnp.bfloat16)
        .reshape(num_caps, seq_len, num_heads, HEAD_DIM)
    )
    queries = packed[:, :, 0]
    key_rows = packed[:, :, 1]
    value_rows = packed[:, :, 2]
    grad_values = jnp.einsum(
        "bhqk,bqhd->bkhd", probs_low, grad_mixed, preferred_element_type=jnp.float32
    )
    grad_probs = jnp.einsum(
        "bqhd,bkhd->bhqk", grad_mixed, value_rows, preferred_element_type=jnp.float32
    )
    row_inner = jnp.sum(attn_probs * grad_probs, -1, keepdims=True)
    grad_raw = (attn_probs * (grad_probs - row_inner) * HEAD_DIM ** (-0.5)).astype(jnp.bfloat16)
    grad_queries = jnp.einsum(
        "bhqk,bkhd->bqhd", grad_raw, key_rows, preferred_element_type=jnp.float32
    )
    grad_keys = jnp.einsum("bhqk,bqhd->bkhd", grad_raw, queries, preferred_element_type=jnp.float32)
    grad_packed = (
        jnp.stack([grad_queries, grad_keys, grad_values], 2)
        .astype(jnp.bfloat16)
        .reshape(num_rows, 3 * feat_dim)
    )
    grad_qkv = inner_rows(normed_one, grad_packed)
    grad_normed_one = outer_cols(grad_packed, w_qkv)
    unused_one, norm_back_one = jax.vjp(norm_apply, stream, gain_one, bias_one)
    grad_in_norm, grad_gain_one, grad_bias_one = norm_back_one(
        grad_normed_one.reshape(num_caps, seq_len, feat_dim)
    )
    grads_here = [
        grad_gain_one,
        grad_bias_one,
        grad_qkv,
        grad_w_out,
        grad_gain_two,
        grad_bias_two,
        grad_fc,
        grad_fc_out,
    ]
    return (grad_middle + grad_in_norm, grads_here)


def head_forward(features, gain, bias, proj):
    normed = norm_apply(features, gain, bias).astype(jnp.bfloat16)
    embedded = matmul(normed, proj)
    return (unit_rows(embedded), (normed, embedded))


def head_backward(features, gain, bias, proj, kept, grad_unit):
    normed, embedded = kept
    unused_unit, unit_back = jax.vjp(unit_rows, embedded)
    grad_embed = unit_back(grad_unit)[0].astype(jnp.bfloat16)
    grad_proj = inner_rows(normed, grad_embed)
    grad_normed = outer_cols(grad_embed, proj)
    unused_norm, norm_back = jax.vjp(norm_apply, features, gain, bias)
    grad_feat, grad_gain, grad_bias = norm_back(grad_normed)
    return (grad_feat, [grad_gain, grad_bias, grad_proj])


def plain_contrast(own_rows, other_rows, multiplier, start):
    logits = multiplier * outer_cols(own_rows, other_rows)
    row_peak = jnp.max(logits, -1, keepdims=True)
    log_total = row_peak + jnp.log(jnp.sum(jnp.exp(logits - row_peak), -1, keepdims=True))
    col_pos = lax.broadcasted_iota(jnp.int32, logits.shape, 1)
    target_pos = lax.broadcasted_iota(jnp.int32, logits.shape, 0) + start
    matched = (col_pos == target_pos).astype(jnp.float32)
    loss_sum = jnp.sum(log_total) - jnp.sum(matched * logits)
    grad_logits = 0.5 * (jnp.exp(logits - log_total) - matched)
    scale_part = jnp.sum(grad_logits * logits)
    return (loss_sum, scale_part, (multiplier * grad_logits).astype(jnp.bfloat16), log_total[:, 0])


def pack_flat(arrays, devices):
    flat = jnp.concatenate([array.reshape(-1) for array in arrays])
    padding = -flat.shape[0] % devices
    return jnp.concatenate([flat, jnp.zeros((padding,), jnp.float32)])


def plain(
    text_input,
    eot_index,
    image_input,
    ln1_gain,
    ln1_bias,
    w_qkv,
    w_attn_out,
    ln2_gain,
    ln2_bias,
    w_fc,
    w_fc_out,
    img_ln1_gain,
    img_ln1_bias,
    img_w_qkv,
    img_w_attn_out,
    img_ln2_gain,
    img_ln2_bias,
    img_w_fc,
    img_w_fc_out,
    final_gain,
    final_bias,
    text_proj,
    image_gain,
    image_bias,
    image_proj,
    logit_scale,
):
    num_caps, seq_len, feat_dim = text_input.shape
    devices = lax.axis_size("dp")
    all_caps = num_caps * devices
    start = lax.axis_index("dp") * num_caps
    depth = ln1_gain.shape[0]
    text_stack = (ln1_gain, ln1_bias, w_qkv, w_attn_out, ln2_gain, ln2_bias, w_fc, w_fc_out)
    image_stack = (
        img_ln1_gain,
        img_ln1_bias,
        img_w_qkv,
        img_w_attn_out,
        img_ln2_gain,
        img_ln2_bias,
        img_w_fc,
        img_w_fc_out,
    )

    def text_weights(layer_num):
        return tuple((array[layer_num] for array in text_stack))

    def image_weights(layer_num):
        return tuple((array[layer_num] for array in image_stack))

    stream = text_input.astype(jnp.float32)
    layer_num = 0
    text_saved = [stream]
    stream, unused = layer_forward(stream, text_weights(layer_num), True)
    pooled = jnp.take_along_axis(stream, eot_index[:, None, None], axis=1)[:, 0]
    picture = image_input.astype(jnp.float32)
    layer_num = 0
    image_saved = [picture]
    picture, unused = layer_forward(picture, image_weights(layer_num), False)
    image_pooled = picture[:, 0]
    text_unit, text_kept = head_forward(pooled, final_gain, final_bias, text_proj)
    image_unit, image_kept = head_forward(image_pooled, image_gain, image_bias, image_proj)
    image_low = image_unit.astype(jnp.bfloat16)
    text_low = text_unit.astype(jnp.bfloat16)
    image_all, text_all = (
        lax.all_gather(image_low, "dp", axis=0, tiled=True),
        lax.all_gather(text_low, "dp", axis=0, tiled=True),
    )
    multiplier = jnp.exp(logit_scale[0])
    loss_image, scale_image, grad_raw_it, unused_it = plain_contrast(
        image_low, text_all, multiplier, start
    )
    loss_text, scale_text, grad_raw_ti, unused_ti = plain_contrast(text_low, image_all, multiplier, start)
    spread_text = inner_rows(grad_raw_it, image_low)
    spread_image = inner_rows(grad_raw_ti, text_low)
    back_text, back_image = (
        lax.psum_scatter(spread_text, "dp", scatter_dimension=0, tiled=True),
        lax.psum_scatter(spread_image, "dp", scatter_dimension=0, tiled=True),
    )
    total, grad_scale = lax.psum((loss_image + loss_text, scale_image + scale_text), "dp")
    grad_image_unit = matmul(grad_raw_it, text_all) + back_image
    grad_text_unit = matmul(grad_raw_ti, image_all) + back_text
    grad_pooled, text_head_grads = head_backward(
        pooled, final_gain, final_bias, text_proj, text_kept, grad_text_unit
    )
    grad_image_pooled, image_head_grads = head_backward(
        image_pooled, image_gain, image_bias, image_proj, image_kept, grad_image_unit
    )
    head_flat = pack_flat(text_head_grads + image_head_grads, devices)
    image_flat = [None] * depth
    img_seq = image_input.shape[1]
    img_dim = image_input.shape[2]
    grad_picture = jnp.concatenate(
        [grad_image_pooled[:, None, :], jnp.zeros((num_caps, img_seq - 1, img_dim), jnp.float32)], 1
    )
    for layer_num in reversed(range(depth)):
        grad_picture, grads_here = layer_backward(
            image_saved[layer_num], image_weights(layer_num), grad_picture, False
        )
        image_flat[layer_num] = pack_flat(grads_here, devices)
    text_flat = [None] * depth
    selected = (
        lax.broadcasted_iota(jnp.int32, (num_caps, seq_len), 1) == eot_index[:, None]
    ).astype(jnp.float32)
    grad_stream = selected[:, :, None] * grad_pooled[:, None, :]
    for layer_num in reversed(range(depth)):
        grad_stream, grads_here = layer_backward(
            text_saved[layer_num], text_weights(layer_num), grad_stream, True
        )
        text_flat[layer_num] = pack_flat(grads_here, devices)
    text_share, image_share, head_share = (
        lax.psum_scatter(jnp.stack(text_flat), "dp", scatter_dimension=1, tiled=True),
        lax.psum_scatter(jnp.stack(image_flat), "dp", scatter_dimension=1, tiled=True),
        lax.psum_scatter(head_flat, "dp", scatter_dimension=0, tiled=True),
    )
    loss = (total / (2 * all_caps)).reshape(1)
    return (
        loss,
        grad_stream,
        grad_picture,
        text_share,
        image_share,
        head_share,
        grad_scale.reshape(1),
    )


def shards(*args):
    caps = args[0].shape[0] * lax.axis_size("dp")
    return compact(*args) if caps <= 512 else plain(*args)


def solution(mesh):
    return jax.shard_map(
        shards,
        mesh=mesh,
        in_specs=(
            P("dp", None, None),
            P("dp"),
            P("dp", None, None),
            P(),
            P(),
            P(),
            P(),
            P(),
            P(),
            P(),
            P(),
            P(),
            P(),
            P(),
            P(),
            P(),
            P(),
            P(),
            P(),
            P(),
            P(),
            P(),
            P(),
            P(),
            P(),
            P(),
        ),
        out_specs=(
            P(),
            P("dp", None, None),
            P("dp", None, None),
            P(None, "dp"),
            P(None, "dp"),
            P("dp"),
            P(),
        ),
        check_vma=False,
    )
```

```python
import enum

import jax
import jax.numpy as jnp
from jax import lax
from jax.experimental import pallas as pl
from jax.experimental.pallas import tpu as pltpu
from jax.sharding import PartitionSpec as P

HEAD_DIM = 64
LANES = 128

EPS = 1e-05
UNIT_EPS = 1e-06
MASKED = -1000000000.0
LIMIT = 44 * 2**20
F32 = jnp.float32
BF16 = jnp.bfloat16


class Place(enum.Enum):
    FAR = enum.auto()
    FEW = enum.auto()
    RAW = enum.auto()
    AUTO = enum.auto()
    NEAR = enum.auto()
    SCALAR = enum.auto()


class K(enum.Enum):
    BIAS = enum.auto()
    BIAS2 = enum.auto()
    EOT = enum.auto()
    GAIN = enum.auto()
    GAIN2 = enum.auto()
    HEAD = enum.auto()
    HEAD_BIAS = enum.auto()
    HEAD_GAIN = enum.auto()
    INPUT = enum.auto()
    LOSS = enum.auto()
    MINE = enum.auto()
    MIXED = enum.auto()
    NORMED = enum.auto()
    OTHERS = enum.auto()
    OWN = enum.auto()
    PACK = enum.auto()
    PART = enum.auto()
    PROBS = enum.auto()
    PROJ = enum.auto()
    QUERIES = enum.auto()
    ROWS = enum.auto()
    SCALE = enum.auto()
    SCORES = enum.auto()
    SEND = enum.auto()
    SENT = enum.auto()
    SWAPPED = enum.auto()
    SHARE = enum.auto()
    UNIT = enum.auto()
    VALUES = enum.auto()
    W_FC = enum.auto()
    W_FC_OUT = enum.auto()
    W_OUT = enum.auto()
    W_QKV = enum.auto()
    W_QUERY = enum.auto()
    WINDOWS = enum.auto()
    X = enum.auto()


def dot(left, right):
    return jnp.dot(left, right, preferred_element_type=F32)


def dot_nt(left, right):
    return lax.dot_general(left, right, (((1,), (1,)), ((), ())), preferred_element_type=F32)


def dot_tn(left, right):
    return lax.dot_general(left, right, (((0,), (0,)), ((), ())), preferred_element_type=F32)


def summed_through(rows, weights):
    total = dot(jnp.ones((8, rows.shape[0]), BF16), rows)
    high = total.astype(BF16)
    low = (total - high.astype(F32)).astype(BF16)
    both = dot_nt(jnp.concatenate([high, low], 0), weights)
    return both[:1] + both[8:9]


def standard(values):
    center = values - jnp.mean(values, -1, keepdims=True)
    scale = lax.rsqrt(jnp.mean(center * center, -1, keepdims=True) + EPS)
    return center * scale, scale


def norm_back(grad, unit, scale, gain):
    scaled = grad * gain
    return scale * (
        scaled
        - jnp.mean(scaled, -1, keepdims=True)
        - unit * jnp.mean(scaled * unit, -1, keepdims=True)
    )


def head_masks(width):
    lane = lax.broadcasted_iota(jnp.int32, (1, width), 1)
    return [
        ((lane >= h * HEAD_DIM) & (lane < (h + 1) * HEAD_DIM)).astype(F32)
        for h in range(width // HEAD_DIM)
    ]


def spread(rows):
    return jnp.concatenate([rows * mask for mask in head_masks(rows.shape[1])], 0)


def collect(rows, caps):
    masks = head_masks(rows.shape[1])
    return sum(rows[h * caps : (h + 1) * caps] * mask for h, mask in enumerate(masks))


def picked_columns(caps, total, ends):
    cap = lax.broadcasted_iota(jnp.int32, (caps, 1), 0)
    at = cap
    for b in range(caps):
        at = jnp.where(cap == b, ends[b] * caps + b, at)
    column = lax.broadcasted_iota(jnp.int32, (caps, total), 1)
    chosen = jnp.where(column == at, 1.0, 0.0).astype(BF16)
    return chosen, column, at


class Plan:
    def __init__(self, dim, hidden, devices, caps):
        self.dim, self.hidden, self.devices = dim, hidden, devices
        self.row = 3 * dim
        self.qkv_at = 2 * dim
        self.out_at = self.qkv_at + dim * self.row
        self.norm_at = self.out_at + dim * dim
        self.fc_at = self.norm_at + 2 * dim
        self.fc_out_at = self.fc_at + dim * hidden
        self.total = self.fc_out_at + hidden * dim
        self.share = -(-self.total // devices)
        self.head_total = 2 * (2 * dim + dim * dim)
        self.head_share = -(-self.head_total // devices)
        self.roots = -(-self.out_at // self.share)
        self.rows_out = -(-(self.share // LANES + 2) // 8) * 8
        self.head_rows_out = -(-(self.head_share // LANES + 2) // 8) * 8
        ends = [min((d + 1) * self.share - self.qkv_at, dim * self.row) for d in range(self.roots)]
        self.window = max((end - 1) // self.row + 1 - self.column(d) for d, end in enumerate(ends))
        self.used = 2 * self.window
        self.piece = LANES - self.used
        self.extra = dim // caps
        self.spare, at = [], 0
        for h in reversed(range(dim // HEAD_DIM - 1)):
            start = self.used + min(max(self.used - h * self.piece, 0), self.piece)
            size = min(LANES - start, self.extra - at)
            self.spare.append((h, start, size, at))
            at += size
        assert self.piece > 0 and -(-self.used // self.piece) < dim // HEAD_DIM
        assert at == self.extra <= LANES
        self.spare_from = min(h for h, unused, size, unused in self.spare if size > 0)

    def column(self, device):
        if isinstance(device, int):
            return min(max(device * self.share - self.qkv_at, 0) // self.row, self.dim - 1)
        return jnp.minimum(jnp.maximum(device * self.share - self.qkv_at, 0) // self.row, self.dim - 1)


def window_tiles(plan, text, image, device, caps, extra):
    dim = text.shape[1]
    first = plan.column(device)
    lane = lax.broadcasted_iota(jnp.int32, (text.shape[0], LANES), 1)
    left = pltpu.roll(text, (dim - first) % dim, 1)[:, :LANES]
    right = pltpu.roll(image, (dim - first + plan.window) % dim, 1)[:, :LANES]
    both = jnp.where(lane < plan.window, left, right)
    heads = text.shape[0] // caps
    lane, last = lane[:caps], both[(heads - 1) * caps :]
    tiles = []
    for h in range(heads - 1):
        moved = pltpu.roll(last, (plan.used - h * plan.piece) % LANES, 1)
        tile = jnp.where(lane < plan.used, both[h * caps : (h + 1) * caps], moved)
        for at, start, size, taken in plan.spare if extra is not None else ():
            if at == h and size > 0:
                moved = pltpu.roll(extra, (start - taken) % LANES, 1)
                tile = jnp.where((lane >= start) & (lane < start + size), moved, tile)
        tiles.append(tile.astype(BF16))
    return jnp.concatenate(tiles, 1)


def last_head(plan, source, heads):
    lane = lax.broadcasted_iota(jnp.int32, (source.shape[0], LANES), 1)
    whole = jnp.zeros(lane.shape, F32)
    for h in range(-(-plan.used // plan.piece)):
        tile = source[:, h * LANES : (h + 1) * LANES].astype(F32)
        moved = pltpu.roll(tile, (LANES + h * plan.piece - plan.used) % LANES, 1)
        whole = jnp.where(lane >= h * plan.piece, moved, whole)
    return whole.astype(BF16)


def fold_row(row, caps):
    dim = row.shape[1]
    step = dim // caps
    rows = [pltpu.roll(row, (dim - i * step) % dim, 1)[:, :LANES] for i in range(caps)]
    return jnp.concatenate(rows, 0)


def spare_row(plan, sums, first, dim):
    caps = sums.shape[0]
    lane = lax.broadcasted_iota(jnp.int32, (caps, LANES), 1)
    folded = jnp.zeros((caps, LANES), F32)
    for h, start, size, taken in plan.spare:
        if size > 0:
            tile = sums[:, (h - first) * LANES : (h - first + 1) * LANES]
            moved = pltpu.roll(tile, (taken - start) % LANES, 1)
            folded = jnp.where((lane >= taken) & (lane < taken + size), moved, folded)
    wide = jnp.concatenate([folded, jnp.zeros((caps, dim - LANES), F32)], 1)
    lane = lax.broadcasted_iota(jnp.int32, (1, dim), 1)
    row = jnp.zeros((1, dim), F32)
    for i in range(caps):
        moved = pltpu.roll(wide[i : i + 1], i * plan.extra, 1) if i else wide[:1]
        row = jnp.where((lane >= i * plan.extra) & (lane < (i + 1) * plan.extra), moved, row)
    return row


def pack_windows(plan, target, text, image, caps, common):
    width = (text.shape[0] // caps - 1) * LANES
    held = plan.roots + plan.roots % 2

    def fill(device, core):
        extra = None if common is None else common[core][1]
        target[device, :, :width] = window_tiles(plan, text, image, device, caps, extra)
        if common is not None:
            target[device, :, width:] = common[core][0]

    if held <= 16:
        for device in range(held):
            fill(device, device % 2)
    else:

        @pl.loop(0, held // 2)
        def _(chip):
            for core in range(2):
                fill(2 * chip + core, core)


def clear_windows(plan, target):
    held = plan.roots + plan.roots % 2

    @pl.loop(held, target.shape[0])
    def _(device):
        target[device] = jnp.zeros(target.shape[1:], BF16)

    return slice(0, held), slice(held, target.shape[0])


def take_rows(source, at, count):
    row, lane_at = at // LANES, at % LANES
    lane = lax.broadcasted_iota(jnp.int32, (count, LANES), 1)
    mixed = jnp.where(
        lane >= lane_at, source[pl.ds(row, count), :], source[pl.ds(row + 1, count), :]
    )
    return pltpu.roll(mixed, lax.rem(LANES - lane_at, LANES), 1)


def put_tile(target, row, block):
    count, width = block.shape
    step = width // LANES
    for j in range(step):
        piece = block[:, j * LANES : (j + 1) * LANES]
        if count == 1:
            target[row + j : row + j + 1, :] = piece
        else:
            target[pl.ds(row + j, count, stride=step), :] = piece


def front_tower(tower, ins, picked, last):
    x = ins[K.X, tower].get()[...]
    seq, caps, dim = x.shape
    total = seq * caps
    heads = dim // HEAD_DIM
    source = x.reshape(total, dim)
    chosen, column, pick_at = picked_columns(caps, total, picked)
    last_at = pick_at
    if last is not picked:
        unused, unused, last_at = picked_columns(caps, total, last)
    pooled = dot(chosen, source)
    unit, unused = standard(source.astype(F32))
    yield
    pooled_unit, unused = standard(pooled)
    gain, bias = ins[K.GAIN, tower].get()[...], ins[K.BIAS, tower].get()[...]
    pooled_normed = (pooled_unit * gain + bias).astype(BF16)
    normed = (unit * gain + bias).astype(BF16)
    yield
    w_ref = ins[K.W_QKV, tower].get()
    query = dot(pooled_normed, w_ref[0, :, :dim]).astype(BF16).astype(F32)
    yield
    through_keys = dot_nt(spread(query).astype(BF16), w_ref[0, :, dim : 2 * dim])
    yield
    scores = dot_nt(through_keys.astype(BF16), normed) * HEAD_DIM ** (-0.5)
    yield
    cap = lax.broadcasted_iota(jnp.int32, (caps, 1), 0)
    seen = jnp.where((lax.rem(column, caps) == cap) & (column <= last_at), 1.0, 0.0)
    seen = jnp.concatenate([seen] * heads, 0) > 0.5
    peak = jnp.max(jnp.where(seen, scores, MASKED), -1, keepdims=True)
    sums = jnp.sum(jnp.where(seen, jnp.exp(scores - peak), 0.0), -1, keepdims=True)
    probs = jnp.where(seen, jnp.exp(scores - (peak + jnp.log(sums))), 0.0)
    yield
    values = dot(probs.astype(BF16), normed)
    yield
    mixed = collect(dot(values.astype(BF16), w_ref[0, :, 2 * dim :]), caps).astype(BF16)
    return pooled, mixed, (normed, unit, probs, query, through_keys, values, chosen)


def attended_towers(ins):
    eot = ins[K.EOT].get()
    caps = eot.shape[0]
    seq = ins[K.X, 1].buf.shape[0]
    ends = [eot[b] for b in range(caps)]
    views = (ends, ends), ([0] * caps, [seq - 1] * caps)
    return run_together([front_tower(tower, ins, *views[tower]) for tower in range(2)])


def front_body(plan):
    def body(scalars, ins, outs, scratch):
        payload = [
            jnp.concatenate([pooled.astype(BF16), mixed], 1)
            for pooled, mixed, unused in attended_towers(ins)
        ]
        rows = outs[K.ROWS].ref

        @pl.loop(0, rows.shape[0] // 2)
        def _(chip):
            for core in range(2):
                rows[2 * chip + core] = payload[core]

    return body


def pack_at(dim, hidden, caps):
    heads = dim // HEAD_DIM
    sizes = [heads * caps] * 2 + [caps] * 8 + [caps * hidden // dim]
    places, at = [], 0
    for size in sizes:
        places.append(slice(at, at + size))
        at += size
    return places, at


def weights_of(tower, ins):
    names = K.W_OUT, K.GAIN2, K.BIAS2, K.W_FC, K.W_FC_OUT, K.HEAD_GAIN, K.HEAD_BIAS, K.PROJ
    return [ins[name, tower] for name in names]


def side_body(plan):
    def body(scalars, ins, outs, scratch):
        dim, hidden = plan.dim, plan.hidden
        caps = ins[K.EOT].buf.shape[0]
        places, unused = pack_at(dim, hidden, caps)
        towers = attended_towers(ins)
        clear_windows(plan, outs[K.VALUES].ref)
        pack_windows(plan, outs[K.VALUES].ref, towers[0][2][5], towers[1][2][5], caps, None)
        outs[K.VALUES].push()
        kept, hiddens = ([], []), scratch[0]
        for tower, (pooled, mixed, saved) in enumerate(towers):
            normed, unit, probs, query, through_keys, values, chosen = saved
            unit = unit.astype(BF16)
            for name, value in ((K.NORMED, normed), (K.UNIT, unit), (K.PROBS, probs)):
                outs[name, tower].ref[...] = value
                outs[name, tower].push()
            small = [through_keys, dot(probs.astype(BF16), unit), dot(chosen, unit), query]
            for place, value in zip(places, small):
                outs[K.PACK, tower].ref[place, :] = value
        run_together(
            [
                tower_forward(
                    pooled, mixed, weights_of(tower, ins), kept[tower], hiddens[tower], None
                )
                for tower, (pooled, mixed, unused) in enumerate(towers)
            ]
        )
        for tower in range(2):
            pack = outs[K.PACK, tower]
            for place, value in zip(places[4:10], kept[tower]):
                pack.ref[place, :] = jnp.broadcast_to(value, (caps, dim))
            for j in range(hidden // dim):
                at = places[10].start + j * caps
                pack.ref[at : at + caps, :] = gate_slope(hiddens[tower][:, j * dim : (j + 1) * dim])
            pack.push()

    return body


def run_together(steps):
    results = [None] * len(steps)
    live = list(range(len(steps)))
    while live:
        for index in list(live):
            try:
                next(steps[index])
            except StopIteration as stop:
                results[index] = stop.value
                live.remove(index)
    return results


def chunks(width):
    step = 512 if width % 512 == 0 else width
    return [slice(at, at + step) for at in range(0, width, step)]


def gate_slope(hidden):
    gate = jax.nn.sigmoid(1.702 * hidden)
    return gate + 1.702 * hidden * gate * (1.0 - gate)


def unit_rows_of(embed):
    length = lax.rsqrt(jnp.sum(embed * embed, -1, keepdims=True) + UNIT_EPS)
    return embed * length, length


def tower_forward(pooled, mixed, weights, kept, hidden_ref, active_ref):
    w_out, gain, bias, w_fc, w_fc_out, head_gain, head_bias, proj = weights
    middle = pooled + dot(mixed, w_out.get()[0])
    yield
    unit, scale = standard(middle)
    normed = (unit * gain.get()[...] + bias.get()[...]).astype(BF16)
    yield
    result = middle
    w_fc = w_fc.get()
    for cols in chunks(w_fc.shape[2]):
        hidden = dot(normed, w_fc[0, :, cols])
        active = (hidden * jax.nn.sigmoid(1.702 * hidden)).astype(BF16)
        if hidden_ref is not None:
            hidden_ref[:, cols] = hidden
        if active_ref is not None:
            active_ref[:, cols] = active
        result = result + dot(active, w_fc_out.get()[0, cols, :])
        yield
    head_unit, head_scale = standard(result)
    head_in = (head_unit * head_gain.get()[...][None] + head_bias.get()[...][None]).astype(BF16)
    embed = dot(head_in, proj.get()[...])
    yield
    unit_embed, length = unit_rows_of(embed)
    if kept is not None:
        kept += [unit, scale, head_unit, head_scale, unit_embed, length]
    return unit_embed.astype(BF16)


def log_sum(logits, axis):
    peak = jnp.max(logits, axis, keepdims=True)
    return peak + jnp.log(jnp.sum(jnp.exp(logits - peak), axis, keepdims=True))


def unit_gradient(multiplier, logits, own_total, other_total, matched, other):
    target = jnp.where(matched, 1.0, 0.0)
    own = 0.5 * multiplier * (jnp.exp(logits - own_total) - target)
    cross = 0.5 * multiplier * (jnp.exp(logits - other_total) - target)
    return dot(own.astype(BF16), other) + dot(cross.astype(BF16), other)


def embed_back(grad_unit, unit_embed, length):
    along = jnp.sum(unit_embed * grad_unit, -1, keepdims=True)
    return (length * (grad_unit - unit_embed * along)).astype(BF16)


def tower_backward(grad_embed, kept, slope, weights, keep_hidden):
    unit, scale, head_unit, head_scale = kept
    w_out, gain, bias, w_fc, w_fc_out, head_gain, head_bias, proj = weights
    grad_head = dot_nt(grad_embed, proj.get()[...])
    yield
    grad_result = norm_back(grad_head, head_unit, head_scale, head_gain.get()[...][None])
    grad_out = grad_result.astype(BF16)
    yield
    w_fc, w_fc_out = w_fc.get(), w_fc_out.get()
    grad_normed = 0.0
    for cols in chunks(w_fc.shape[2]):
        grad_active = dot_nt(grad_out, w_fc_out[0, cols, :])
        grad_hidden = (grad_active * slope(cols)).astype(BF16)
        if keep_hidden is not None:
            keep_hidden[:, cols] = grad_hidden
        grad_normed = grad_normed + dot_nt(grad_hidden, w_fc[0, :, cols])
        yield
    grad_middle = grad_result + norm_back(grad_normed, unit, scale, gain.get()[...])
    yield
    grad_mixed = dot_nt(grad_middle.astype(BF16), w_out.get()[0]).astype(BF16)
    yield
    return grad_head, grad_out, grad_normed, grad_middle, grad_mixed


def own_steps(plan, tower, units, multiplier, own_at, ins, outs):
    mine, other = units[tower], units[1 - tower]
    own_out, scores_out = outs[K.OWN, tower], outs[K.SCORES, tower]
    dim = plan.dim
    caps = scores_out.ref.shape[0] * HEAD_DIM // dim
    places, unused = pack_at(dim, plan.hidden, caps)
    other_total = log_sum(multiplier * dot_nt(mine, other), 0)
    yield
    pack = ins[K.PACK, tower].get()
    unit, scale, head_unit, head_scale, unit_embed, length = (pack[places[j], :] for j in range(4, 10))
    logits = multiplier * dot_nt(unit_embed.astype(BF16), other)
    matched = lax.broadcasted_iota(jnp.int32, logits.shape, 1) == own_at + lax.broadcasted_iota(
        jnp.int32, logits.shape, 0
    )
    grad_unit = unit_gradient(multiplier, logits, log_sum(logits, 1), other_total, matched, other)
    yield
    slope_at = places[10].start
    slopes = [pack[slope_at + j * caps : slope_at + (j + 1) * caps, :] for j in range(plan.hidden // dim)]
    slopes = jnp.concatenate(slopes, 1)
    done = yield from tower_backward(
        embed_back(grad_unit, unit_embed, length), (unit, scale, head_unit, head_scale),
        lambda cols: slopes[:, cols], weights_of(tower, ins), None,
    )
    grad_middle, grad_mixed = done[3], done[4].astype(F32)
    own_out.ref[:caps, :] = grad_middle
    w_ref = ins[K.W_QKV, tower].get()
    through_values = dot_nt(spread(grad_mixed).astype(BF16), w_ref[0, :, 2 * dim :])
    own_out.ref[2 * caps :, :] = through_values
    yield
    normed = ins[K.NORMED, tower].get()[...]
    grad_probs = dot_nt(through_values.astype(BF16), normed)
    yield
    probs = ins[K.PROBS, tower].get()[...]
    inner = jnp.sum(probs * grad_probs, -1, keepdims=True)
    grad_scores = (probs * (grad_probs - inner) * HEAD_DIM ** (-0.5)).astype(BF16)
    scores_out.ref[...] = grad_scores
    scores_out.push()
    yield
    spread_keys = dot(grad_scores, normed)
    yield
    grad_query = collect(dot(spread_keys.astype(BF16), w_ref[0, :, dim : 2 * dim]), caps).astype(BF16)
    yield
    units = pack[places[0], :] * dot(grad_scores, ins[K.UNIT, tower].get()[...])
    yield
    through_query = dot_nt(grad_query, w_ref[0, :, :dim])
    own_out.ref[caps : 2 * caps, :] = through_query
    own_out.push()
    units = units + through_values * pack[places[1], :]
    gain_part = jnp.sum(units, 0, keepdims=True) + jnp.sum(
        through_query * pack[places[2], :], 0, keepdims=True
    )
    return spread_keys, grad_query, gain_part


def forward_pair(plan, rows, ins, kept, hidden, active):
    dim = plan.dim
    return run_together(
        [
            tower_forward(
                rows[:, 2 * tower * dim : (2 * tower + 1) * dim].astype(F32),
                rows[:, (2 * tower + 1) * dim : (2 * tower + 2) * dim],
                weights_of(tower, ins), kept[tower], hidden[tower], active[tower],
            )
            for tower in range(2)
        ]
    )


def row_copies(scalars, ins, scratch):
    core = scalars[0][0] % 2
    wide = scratch[0].shape[1] // 2
    return [
        pltpu.make_async_copy(
            ins[name].ref,
            scratch[0].at[:, pl.ds(pl.multiple_of(tower * wide, LANES), wide)],
            scratch[1].at[i],
        )
        for i, (name, tower) in enumerate(((K.MINE, core), (K.OTHERS, 1 - core)))
    ]


def join_rows(scalars, ins, outs, scratch):
    for copy in row_copies(scalars, ins, scratch):
        copy.start()


def middle_body(plan):
    def body(scalars, ins, outs, scratch):
        at_ref, scale_ref = scalars
        rows_ref, sems = scratch
        dim = plan.dim
        device = at_ref[0]
        caps = rows_ref.shape[0] // plan.devices
        held, others = clear_windows(plan, outs[K.SEND].ref)
        outs[K.SEND].push_part(others)
        for copy in row_copies(scalars, ins, scratch):
            copy.wait()
        rows = rows_ref[...]
        outs[K.ROWS].ref[...] = rows
        outs[K.ROWS].push()
        units = forward_pair(plan, rows, ins, (None, None), (None, None), (None, None))
        multiplier = jnp.exp(jnp.full((1, 1), scale_ref[0], F32))
        own_at = device * caps
        parts = run_together(
            [own_steps(plan, tower, units, multiplier, own_at, ins, outs) for tower in range(2)]
        )
        common = [(query, fold_row(gain_part, caps)) for unused, query, gain_part in parts]
        keys_t, keys_i = parts[0][0], parts[1][0]
        pack_windows(plan, outs[K.SEND].ref, keys_t, keys_i, caps, common)
        outs[K.SEND].push_part(held)

    return body


def late_weights(ins, outs, scratch):
    value, sems = scratch[-2:]
    dim = value.shape[1]
    return [
        pltpu.make_async_copy(
            ins[K.W_QKV, tower].ref.at[0, :, pl.ds(at, dim)], target.at[tower], sems.at[2 * part + tower]
        )
        for part, (at, target) in enumerate(((0, outs[K.W_QUERY].ref), (2 * dim, value)))
        for tower in range(2)
    ]


def tail_ahead(plan):
    def ahead(scalars, ins, outs, scratch):
        copies = late_weights(ins, outs, scratch)

        @pl.when(scalars[0][0] < plan.roots)
        def _():
            for copy in copies[:2]:
                copy.start()

        @pl.when(scalars[0][0] == 0)
        def _():
            for copy in copies[2:]:
                copy.start()

    return ahead


def tail_body(plan):
    def body(scalars, ins, outs, scratch):
        at_ref, scale_ref = scalars
        dim, hidden_dim = plan.dim, plan.hidden
        loss_ref, scale_grad_ref = outs[K.LOSS].ref, outs[K.SCALE].ref
        flat, flat_head, wide_t, wide_i, small, hiddens, actives, hidden_grads, late, unused = scratch
        device = at_ref[0]
        eot = ins[K.EOT].get()
        caps = eot.shape[0]
        ends = [eot[b] for b in range(caps)]
        places, unused = pack_at(dim, hidden_dim, caps)
        multiplier = jnp.exp(jnp.full((1, 1), scale_ref[0], F32))

        def input_gradient(tower, picked, wide):
            x, gain = ins[K.X, tower].get(), ins[K.GAIN, tower].get()
            seq = x.shape[0]
            unit, scale = standard(x[...].reshape(seq * caps, dim).astype(F32))
            yield
            probs, pack, own, scores = (
                ins[name, tower].get() for name in (K.PROBS, K.PACK, K.OWN, K.SCORES)
            )
            left = jnp.concatenate([scores[...], probs[...].astype(BF16)], 0)
            right = jnp.concatenate([pack[places[0], :], own[2 * caps :, :]], 0).astype(BF16)
            wide[...] = dot_tn(left, right)
            yield
            for b in range(caps):
                at = picked[b] * caps + b
                wide[pl.ds(at, 1), :] = wide[pl.ds(at, 1), :] + own[caps + b : caps + b + 1, :]
            wide[...] = norm_back(wide[...], unit, scale, gain[...])
            yield
            for b in range(caps):
                at = picked[b] * caps + b
                wide[pl.ds(at, 1), :] = wide[pl.ds(at, 1), :] + own[b : b + 1, :]
            outs[K.INPUT, tower].ref[...] = wide[...].reshape(seq, caps, dim)
            outs[K.INPUT, tower].push()

        run_together([input_gradient(0, ends, wide_t), input_gradient(1, [0] * caps, wide_i)])

        rows = ins[K.ROWS].get()[...]
        count = rows.shape[0]
        kept = [], []
        units = forward_pair(plan, rows, ins, kept, hiddens, actives)
        logits = multiplier * dot_nt(units[1], units[0])
        matched = lax.broadcasted_iota(jnp.int32, logits.shape, 1) == lax.broadcasted_iota(
            jnp.int32, logits.shape, 0
        )
        row_total, column_total = log_sum(logits, 1), log_sum(logits, 0)
        target = jnp.where(matched, 1.0, 0.0)
        by_row = 0.5 * (jnp.exp(logits - row_total) - target)
        by_column = 0.5 * (jnp.exp(logits - column_total) - target)
        total = jnp.sum(row_total) + jnp.sum(column_total) - 2.0 * jnp.sum(target * logits)
        loss_ref[0] = total / (2 * count)
        scale_grad_ref[0] = jnp.sum((by_row + by_column) * logits)
        by_row = (multiplier * by_row).astype(BF16)
        by_column = (multiplier * by_column).astype(BF16)
        grad_units = (
            dot_tn(by_row, units[1]) + dot_tn(by_column, units[1]),
            dot(by_row, units[0]) + dot(by_column, units[0]),
        )

        grad_embeds = [embed_back(grad_units[tower], *kept[tower][4:]) for tower in range(2)]
        backs = run_together(
            [
                tower_backward(
                    grad_embeds[tower], kept[tower][:4],
                    lambda cols, hidden=hiddens[tower]: gate_slope(hidden[:, cols]),
                    weights_of(tower, ins), hidden_grads[tower],
                )
                for tower in range(2)
            ]
        )

        mixed_grads = []
        start, head_start = device * plan.share, device * plan.head_share
        front = plan.rows_out
        half = plan.head_total // 2
        for tower in range(2):
            weights = weights_of(tower, ins)
            gain, bias, head_gain, head_bias = (weights[j] for j in (1, 2, 5, 6))
            active, hidden_grad = actives[tower], hidden_grads[tower]
            grad_embed, done = grad_embeds[tower], backs[tower]
            grad_head, grad_out, grad_normed, grad_middle, grad_mixed = done
            unit, unused, head_unit = kept[tower][:3]
            mixed_grads.append(grad_mixed)
            middle_low = grad_middle.astype(BF16)
            normed = (unit * gain.get()[...] + bias.get()[...]).astype(BF16)
            head_in = head_unit * head_gain.get()[...][None] + head_bias.get()[...][None]
            head_in = head_in.astype(BF16)
            small[0:1, :] = jnp.sum(grad_normed * unit, 0, keepdims=True)
            small[1:2, :] = jnp.sum(grad_normed, 0, keepdims=True)
            small[2:3, :] = jnp.sum(grad_head * head_unit, 0, keepdims=True)
            small[3:4, :] = jnp.sum(grad_head, 0, keepdims=True)
            mixed = rows[:, (2 * tower + 1) * dim : (2 * tower + 2) * dim]

            def when_held(at, size, store):
                @pl.when((at < start + plan.share) & (at + size > start))
                def _():
                    store(front + (at - plan.out_at) // LANES)

            def when_kept(at, size, store):
                at = at + tower * half

                @pl.when((at < head_start + plan.head_share) & (at + size > head_start))
                def _():
                    store(at // LANES)

            def products(when, target, at, left, right):
                for t in range(left.shape[1] // LANES):
                    cols = slice(t * LANES, (t + 1) * LANES)
                    when(
                        at + t * LANES * right.shape[1],
                        LANES * right.shape[1],
                        lambda row: put_tile(target, row, dot_tn(left[:, cols], right[...])),
                    )

            def row_of(when, target, at, index):
                when(at, dim, lambda row: put_tile(target, row, small[index : index + 1, :]))

            products(when_held, flat, plan.out_at, mixed, middle_low)
            row_of(when_held, flat, plan.norm_at, 0)
            row_of(when_held, flat, plan.norm_at + dim, 1)
            products(when_held, flat, plan.fc_at, normed, hidden_grad)
            products(when_held, flat, plan.fc_out_at, active, grad_out)
            at = jnp.maximum(start - plan.out_at + front * LANES, 0)
            outs[K.PART, tower].ref[...] = take_rows(flat, at, plan.rows_out)
            outs[K.PART, tower].push()
            row_of(when_kept, flat_head, 0, 2)
            row_of(when_kept, flat_head, dim, 3)
            products(when_kept, flat_head, 2 * dim, head_in, grad_embed)

        outs[K.HEAD].ref[...] = take_rows(flat_head, head_start, plan.head_rows_out)
        outs[K.HEAD].push()

        copies = late_weights(ins, outs, scratch)

        @pl.when(device == 0)
        def _():
            for tower in range(2):
                copies[2 + tower].wait()
                outs[K.BIAS].ref[tower : tower + 1, :] = summed_through(mixed_grads[tower], late[tower])

        values = ins[K.VALUES].get()

        @pl.when(device < plan.roots)
        def _():
            for copy in copies[:2]:
                copy.wait()
            first = plan.column(device)
            lane = lax.broadcasted_iota(jnp.int32, (count, LANES), 1)
            picked_rows = []
            for tower in range(2):
                gain, bias = ins[K.GAIN, tower].get(), ins[K.BIAS, tower].get()
                pooled = rows[:, 2 * tower * dim : (2 * tower + 1) * dim].astype(F32)
                unit, unused = standard(pooled)
                normed = unit * gain[...] + bias[...]
                outs[K.QUERIES].ref[:, tower * dim : (tower + 1) * dim] = dot(
                    normed.astype(BF16), outs[K.W_QUERY].ref[tower]
                ).astype(BF16)
                shift = lax.rem(dim - first + tower * plan.window, dim)
                picked_rows.append(pltpu.roll(normed, shift, 1)[:, :LANES])
            end = last_head(plan, values, dim // HEAD_DIM)
            for j in range(dim // LANES):
                cols = slice(j * LANES, (j + 1) * LANES)
                block = window_product(plan, values, end, mixed_grads, (0, 0), j)
                for tower in range(2):
                    at = tower * plan.window
                    outs[K.VALUES].ref[tower, :, cols] = block[
                        at : at + plan.window, tower * LANES : (tower + 1) * LANES
                    ]
            outs[K.WINDOWS].ref[...] = jnp.where(lane < plan.window, picked_rows[0], picked_rows[1]).astype(BF16)

    return body


def window_product(plan, source, end, factors, offsets, j):
    lane = lax.broadcasted_iota(jnp.int32, (1, 2 * LANES), 1) % LANES
    right = [factor[:, at + j * LANES : at + (j + 1) * LANES] for factor, at in zip(factors, offsets)]
    right = jnp.concatenate(right, 1).astype(F32)
    total = 0.0
    for h in (2 * j, 2 * j + 1):
        left = end if (h + 1) * HEAD_DIM == plan.dim else source[:, h * LANES : (h + 1) * LANES]
        mine = (lane // HEAD_DIM == h % 2).astype(F32)
        total = total + dot_tn(left, (right * mine).astype(BF16))
    return total


def last_body(plan):
    def body(scalars, ins, outs, scratch):
        (at_ref,) = scalars
        flat, grad_query = scratch
        dim = plan.dim
        heads = dim // HEAD_DIM
        tiles = dim // LANES
        device = at_ref[0]
        parts = [ins[K.PART, tower].get() for tower in range(2)]

        def store(tower, block):
            line = outs[K.SHARE, tower].ref
            line[...] = block.reshape(1, block.shape[0] * LANES)[:, : plan.share]

        @pl.when(device >= plan.roots)
        def _():
            for tower in range(2):
                store(tower, parts[tower][...])

        names = K.SENT, K.SWAPPED, K.WINDOWS, K.QUERIES, K.VALUES, K.W_QUERY, K.BIAS
        sent_ref, swapped, windows, queries, value_part, w_query, bias = (
            ins[name].get() for name in names
        )

        @pl.when(device < plan.roots)
        def _():
            count = sent_ref.shape[0]
            caps = count // plan.devices
            first = plan.spare_from
            for core in range(2):

                @pl.when(device % 2 == core)
                def _():
                    received = sent_ref[:, first * LANES :], swapped[...]
                    for tower, values in enumerate(received if core == 0 else received[::-1]):
                        grad_query[:, tower * dim : (tower + 1) * dim] = values[:, -dim:]

            @pl.when(device == 0)
            def _():
                for tower, values in enumerate((sent_ref[:, first * LANES :], swapped[...])):
                    sums = values[:, :-dim].astype(F32).reshape(plan.devices, caps, -1)
                    put_tile(flat.at[tower], 0, spare_row(plan, jnp.sum(sums, 0), first, dim))
                    grads = grad_query[:, tower * dim : (tower + 1) * dim]
                    row = summed_through(grads, w_query[tower])
                    put_tile(flat.at[tower], tiles, row + bias[tower : tower + 1, :])

            query_part = dot_tn(windows[...], grad_query[...])
            end = last_head(plan, sent_ref, heads)
            for j in range(tiles):
                put = window_product(plan, sent_ref, end, (queries, queries), (0, dim), j)
                for tower in range(2):
                    rows = slice(tower * plan.window, (tower + 1) * plan.window)
                    own = slice(tower * LANES, (tower + 1) * LANES)
                    q_at = tower * dim + j * LANES
                    for part, block in enumerate(
                        (
                            query_part[rows, q_at : q_at + LANES],
                            put[rows, own],
                            value_part[tower, :, j * LANES : (j + 1) * LANES],
                        )
                    ):
                        flat[
                            tower,
                            pl.ds(2 * tiles + part * tiles + j, plan.window, stride=3 * tiles),
                            :,
                        ] = block
            start = device * plan.share
            at = start - plan.column(device) * plan.row
            shape = parts[0].shape
            index = (
                start
                + lax.broadcasted_iota(jnp.int32, shape, 0) * LANES
                + lax.broadcasted_iota(jnp.int32, shape, 1)
            )
            for tower in range(2):
                own = take_rows(flat.at[tower], at, plan.rows_out)
                store(tower, jnp.where(index < plan.out_at, own, parts[tower][...]))

    return body


class Fetch:
    def __init__(self, source, buf, sem, group):
        self.ref, self.buf, self.group = source, buf, group
        self.copy = pltpu.make_async_copy(source, buf, sem)
        group.members.append(self)

    def get(self):
        self.group.wait()
        return self.buf


class Group:
    def __init__(self):
        self.members, self.waited = [], False

    def wait(self):
        if not self.waited:
            self.waited = True
            for fetch in self.members:
                fetch.copy.wait()


class Here:
    def __init__(self, ref):
        self.buf = self.ref = ref

    def get(self):
        return self.buf

    def push(self):
        pass


class Push:
    def __init__(self, ref, target, sem):
        self.ref, self.target, self.sem, self.started = ref, target, sem, False
        self.copy = pltpu.make_async_copy(ref, target, sem)

    def push(self):
        self.started = True
        self.copy.start()

    def push_part(self, part):
        self.started = True
        pltpu.make_async_copy(self.ref.at[part], self.target.at[part], self.sem).start()


def run(body, name, outs, scratch, scalars, arrays, ahead=None):
    smem = pl.BlockSpec(memory_space=pltpu.SMEM)
    hbm = pl.BlockSpec(memory_space=pltpu.HBM)
    vmem = pl.BlockSpec(memory_space=pltpu.VMEM)
    groups = arrays
    arrays = {key: value for group in groups for key, value in group.items()}
    fetched = [(array, place) for array, place in arrays.values() if place in (Place.FAR, Place.FEW)]
    pushed = [(shape, kind) for shape, kind, place in outs.values() if place == Place.FAR]

    def kernel(*refs):
        at = 0

        def take(count):
            nonlocal at
            at += count
            return list(refs[at - count : at])

        scalar_refs, sources, targets = take(len(scalars)), take(len(arrays)), take(len(outs))
        in_bufs, out_bufs = take(len(fetched)), take(len(pushed))
        in_sems, out_sems = take(2)
        ins, results, fetches, pushes = {}, {}, [], []
        sources = iter(sources)
        chain = [Group() for unused in groups]
        for group, together in zip(groups, chain):
            for (key, (unused, place)), source in zip(group.items(), sources):
                if place in (Place.FAR, Place.FEW):
                    sem = in_sems.at[len(fetches)]
                    fetches.append(Fetch(source, in_bufs[len(fetches)], sem, together))
                    ins[key] = fetches[-1]
                else:
                    ins[key] = Here(source)
        for target, (key, (unused, unused, place)) in zip(targets, outs.items()):
            if place == Place.FAR:
                pushes.append(Push(out_bufs[len(pushes)], target, out_sems.at[len(pushes)]))
            results[key] = pushes[-1] if place == Place.FAR else Here(target)
        own_scratch = take(len(scratch))
        if ahead is not None:
            ahead(scalar_refs, ins, results, own_scratch)
        for fetch in fetches:
            fetch.copy.start()
        body(scalar_refs, ins, results, own_scratch)
        for push in pushes:
            if not push.started:
                push.push()
        for fetch in fetches:
            fetch.get()
        for push in pushes:
            push.copy.wait()

    where = {Place.FAR: hbm, Place.FEW: hbm, Place.RAW: hbm, Place.AUTO: vmem, Place.NEAR: vmem, Place.SCALAR: smem}
    buffers = [
        (pltpu.SMEM if place == Place.FEW else pltpu.VMEM)(array.shape, array.dtype)
        for array, place in fetched
    ]
    buffers += [pltpu.VMEM(shape, kind) for shape, kind in pushed]
    buffers += [pltpu.SemaphoreType.DMA((max(len(group), 1),)) for group in (fetched, pushed)]
    pinned = [
        array if place == Place.AUTO else pltpu.with_memory_space_constraint(array, pltpu.HBM)
        for array, place in arrays.values()
    ]
    results = pl.pallas_call(
        kernel,
        name=name,
        out_shape=[
            {Place.FAR: pltpu.HBM, Place.NEAR: pltpu.VMEM}.get(place, jax.ShapeDtypeStruct)(shape, kind)
            for shape, kind, place in outs.values()
        ],
        in_specs=[smem] * len(scalars) + [where[place] for unused, place in arrays.values()],
        out_specs=[where[place] for unused, unused, place in outs.values()],
        scratch_shapes=buffers + list(scratch),
        compiler_params=pltpu.CompilerParams(vmem_limit_bytes=LIMIT),
    )(*scalars, *pinned)
    return dict(zip(outs, results))


def exchange(array):
    return lax.all_to_all(array, "dp", split_axis=0, concat_axis=0, tiled=True)


def swap(array, devices):
    return lax.ppermute(array, "dp", [(i, i ^ 1) for i in range(devices)])


def compact(
    text_input, eot_index, image_input, ln1_gain, ln1_bias, w_qkv, w_attn_out, ln2_gain, ln2_bias,
    w_fc, w_fc_out, img_ln1_gain, img_ln1_bias, img_w_qkv, img_w_attn_out, img_ln2_gain,
    img_ln2_bias, img_w_fc, img_w_fc_out, final_gain, final_bias, text_proj, image_gain,
    image_bias, image_proj, logit_scale,
):
    caps, seq, dim = text_input.shape
    img_seq = image_input.shape[1]
    devices = lax.axis_size("dp")
    plan = Plan(dim, w_fc.shape[2], devices, caps)
    heads = dim // HEAD_DIM
    count = devices * caps
    hidden = plan.hidden
    device = lax.axis_index("dp").astype(jnp.int32).reshape(1)
    text_input, image_input = text_input.swapaxes(0, 1), image_input.swapaxes(0, 1)
    totals = caps * seq, caps * img_seq
    width = (heads - 1) * LANES

    first = {
        (K.X, 0): text_input, (K.X, 1): image_input,
        (K.GAIN, 0): ln1_gain, (K.BIAS, 0): ln1_bias,
        (K.GAIN, 1): img_ln1_gain, (K.BIAS, 1): img_ln1_bias,
    }
    late = {(K.W_QKV, 0): w_qkv, (K.W_QKV, 1): img_w_qkv}
    outputs_in = {(K.W_OUT, 0): w_attn_out, (K.W_OUT, 1): img_w_attn_out}
    second = {
        (K.GAIN2, 0): ln2_gain, (K.BIAS2, 0): ln2_bias,
        (K.GAIN2, 1): img_ln2_gain, (K.BIAS2, 1): img_ln2_bias,
    }
    hidden_in = {(K.W_FC, 0): w_fc, (K.W_FC, 1): img_w_fc}
    third = {
        (K.W_FC_OUT, 0): w_fc_out, (K.W_FC_OUT, 1): img_w_fc_out,
        (K.HEAD_GAIN, 0): final_gain, (K.HEAD_BIAS, 0): final_bias,
        (K.HEAD_GAIN, 1): image_gain, (K.HEAD_BIAS, 1): image_bias,
        (K.PROJ, 0): text_proj, (K.PROJ, 1): image_proj,
    }

    def far(arrays):
        return {key: (array, Place.FAR) for key, array in arrays.items()}

    eot = {K.EOT: (eot_index, Place.FEW)}
    rows = run(
        front_body(plan),
        "front",
        {K.ROWS: ((devices, caps, 2 * dim), BF16, Place.NEAR)},
        [],
        [],
        [eot | far(first), far(late)],
    )[K.ROWS]
    mine = exchange(rows).reshape(count, 2 * dim)

    unused, pack_rows = pack_at(dim, hidden, caps)
    side_outs = {K.VALUES: ((devices, caps, width), BF16, Place.FAR)}
    middle_outs = {
        K.SEND: ((devices, caps, width + dim), BF16, Place.FAR),
        K.ROWS: ((count, 4 * dim), BF16, Place.FAR),
    }
    for tower, total in enumerate(totals):
        side_outs |= {
            (K.NORMED, tower): ((total, dim), BF16, Place.FAR),
            (K.UNIT, tower): ((total, dim), BF16, Place.FAR),
            (K.PROBS, tower): ((heads * caps, total), F32, Place.FAR),
            (K.PACK, tower): ((pack_rows, dim), F32, Place.FAR),
        }
        middle_outs |= {
            (K.OWN, tower): (((2 + heads) * caps, dim), F32, Place.FAR),
            (K.SCORES, tower): ((heads * caps, total), BF16, Place.FAR),
        }
    side = run(side_body(plan), "side", side_outs, [[pltpu.VMEM((caps, hidden), F32)] * 2], [], [eot | far(first), far(late), far(outputs_in | second | hidden_in | third)])
    values = exchange(side.pop(K.VALUES))
    mine, side[K.PACK, 0] = lax.optimization_barrier((mine, side[K.PACK, 0]))
    others = swap(mine, devices)

    packs = {key: side[key] for key in ((K.PACK, 0), (K.PACK, 1))}
    middle = run(
        middle_body(plan),
        "middle",
        middle_outs,
        [pltpu.VMEM((count, 4 * dim), BF16), pltpu.SemaphoreType.DMA((2,))],
        [device, logit_scale],
        [
            {K.MINE: (mine, Place.AUTO), K.OTHERS: (others, Place.AUTO)}
            | {key: (array, Place.AUTO) for key, array in hidden_in.items()}
            | far(outputs_in | second),
            far(third | packs),
            far(late)
            | far({(name, tower): side[name, tower] for name in (K.NORMED, K.PROBS, K.UNIT) for tower in (0, 1)}),
        ],
        join_rows,
    )
    send, values = lax.optimization_barrier((middle[K.SEND], values))
    sent = exchange(send)

    share_rows = plan.rows_out
    region = (plan.total - plan.out_at) // LANES
    head_region = plan.head_total // LANES
    attended = {}
    tail_outs = {K.LOSS: ((1,), F32, Place.SCALAR), K.SCALE: ((1,), F32, Place.SCALAR)}
    for tower, length in enumerate((seq, img_seq)):
        for name, source in ((K.PROBS, side), (K.PACK, side), (K.OWN, middle), (K.SCORES, middle)):
            attended[name, tower] = source[name, tower]
        tail_outs |= {
            (K.PART, tower): ((share_rows, LANES), F32, Place.NEAR),
            (K.INPUT, tower): ((length, caps, dim), F32, Place.FAR),
        }
    tail_outs |= {
        K.HEAD: ((plan.head_rows_out, LANES), F32, Place.FAR),
        K.WINDOWS: ((count, LANES), BF16, Place.NEAR),
        K.QUERIES: ((count, 2 * dim), BF16, Place.NEAR),
        K.VALUES: ((2, plan.window, dim), F32, Place.NEAR),
        K.W_QUERY: ((2, dim, dim), BF16, Place.NEAR),
        K.BIAS: ((8, dim), F32, Place.NEAR),
    }
    tail = run(
        tail_body(plan),
        "tail",
        tail_outs,
        [
            pltpu.VMEM((region + 2 * share_rows + 8, LANES), F32),
            pltpu.VMEM((head_region + plan.head_rows_out + 8, LANES), F32),
            pltpu.VMEM((totals[0], dim), F32),
            pltpu.VMEM((totals[1], dim), F32),
            pltpu.VMEM((8, dim), F32),
            [pltpu.VMEM((count, hidden), F32)] * 2,
            [pltpu.VMEM((count, hidden), BF16)] * 2,
            [pltpu.VMEM((count, hidden), BF16)] * 2,
            pltpu.VMEM((2, dim, dim), BF16),
            pltpu.SemaphoreType.DMA((4,)),
        ],
        [device, logit_scale],
        [
            eot | far(first),
            far(attended),
            far({K.ROWS: middle[K.ROWS]} | outputs_in | second | hidden_in),
            far(third),
            far({K.VALUES: values.reshape(count, width)})
            | {key: (array, Place.RAW) for key, array in late.items()},
        ],
        tail_ahead(plan),
    )
    sent, tail[K.WINDOWS] = lax.optimization_barrier((sent, tail[K.WINDOWS]))
    swapped = swap(sent[:, :, plan.spare_from * LANES :], devices)
    flat_rows = max(2 * dim + plan.window * plan.row, 2 * dim + 2 * plan.row + share_rows * LANES) // LANES
    names = [(K.PART, 0), (K.PART, 1), K.WINDOWS, K.QUERIES, K.VALUES, K.W_QUERY, K.BIAS]
    shares = run(
        last_body(plan),
        "last",
        {(K.SHARE, tower): ((1, plan.share), F32, Place.FAR) for tower in (0, 1)},
        [
            pltpu.VMEM((2, flat_rows // 8 * 8 + 16, LANES), F32),
            pltpu.VMEM((count, 2 * dim), BF16),
        ],
        [device],
        [
            {name: (tail[name], Place.AUTO) for name in names}
            | {K.SENT: (sent.reshape(count, -1), Place.AUTO)}
            | {K.SWAPPED: (swapped.reshape(count, -1), Place.AUTO)},
        ],
    )

    def cut(array, size):
        return array.reshape(-1)[:size]

    return (
        tail[K.LOSS],
        tail[K.INPUT, 0].swapaxes(0, 1),
        tail[K.INPUT, 1].swapaxes(0, 1),
        shares[K.SHARE, 0],
        shares[K.SHARE, 1],
        cut(tail[K.HEAD], plan.head_share),
        tail[K.SCALE],
    )


def norm_apply(values, gain, bias):
    center = values - jnp.mean(values, -1, keepdims=True)
    spread = jnp.mean(center * center, -1, keepdims=True)
    return center * lax.rsqrt(spread + EPS) * gain + bias


def quick_gelu(values):
    return values * jax.nn.sigmoid(1.702 * values)


def unit_rows(values):
    return values * lax.rsqrt(jnp.sum(values * values, -1, keepdims=True) + UNIT_EPS)


def causal_mask(seq_len):
    row_pos = lax.broadcasted_iota(jnp.int32, (seq_len, seq_len), 0)
    col_pos = lax.broadcasted_iota(jnp.int32, (seq_len, seq_len), 1)
    return col_pos <= row_pos


def matmul(left, right):
    return jnp.dot(left, right, preferred_element_type=jnp.float32)


def inner_rows(left, right):
    return lax.dot_general(
        left, right, (((0,), (0,)), ((), ())), preferred_element_type=jnp.float32
    )


def outer_cols(left, right):
    return lax.dot_general(
        left, right, (((1,), (1,)), ((), ())), preferred_element_type=jnp.float32
    )


def layer_forward(stream, weights, causal):
    gain_one, bias_one, w_qkv, w_out, gain_two, bias_two, w_fc, w_fc_out = weights
    num_caps, seq_len, feat_dim = stream.shape
    num_heads = feat_dim // HEAD_DIM
    num_rows = num_caps * seq_len
    normed_one = (
        norm_apply(stream, gain_one, bias_one).astype(jnp.bfloat16).reshape(num_rows, feat_dim)
    )
    packed = (
        matmul(normed_one, w_qkv)
        .astype(jnp.bfloat16)
        .reshape(num_caps, seq_len, 3, num_heads, HEAD_DIM)
    )
    queries = packed[:, :, 0]
    key_rows = packed[:, :, 1]
    value_rows = packed[:, :, 2]
    raw_score = jnp.einsum("bqhd,bkhd->bhqk", queries, key_rows, preferred_element_type=jnp.float32)
    scores = raw_score * HEAD_DIM ** (-0.5)
    if causal:
        scores = jnp.where(causal_mask(seq_len), scores, MASKED)
    row_peak = jnp.max(scores, -1, keepdims=True)
    log_total = row_peak + jnp.log(jnp.sum(jnp.exp(scores - row_peak), -1, keepdims=True))
    attn_probs = jnp.exp(scores - log_total)
    probs_low = attn_probs.astype(jnp.bfloat16)
    mixed_rows = jnp.einsum(
        "bhqk,bkhd->bqhd", probs_low, value_rows, preferred_element_type=jnp.float32
    )
    mixed_rows = mixed_rows.astype(jnp.bfloat16).reshape(num_rows, feat_dim)
    middle = stream + matmul(mixed_rows, w_out).reshape(num_caps, seq_len, feat_dim)
    normed_two = (
        norm_apply(middle, gain_two, bias_two).astype(jnp.bfloat16).reshape(num_rows, feat_dim)
    )
    hidden = matmul(normed_two, w_fc)
    active = quick_gelu(hidden).astype(jnp.bfloat16)
    result = middle + matmul(active, w_fc_out).reshape(num_caps, seq_len, feat_dim)
    return (
        result,
        (normed_one, packed, attn_probs, probs_low, mixed_rows, middle, normed_two, hidden, active),
    )


def layer_backward(stream, weights, grad_out, causal):
    gain_one, bias_one, w_qkv, w_out, gain_two, bias_two, w_fc, w_fc_out = weights
    num_caps, seq_len, feat_dim = stream.shape
    num_heads = feat_dim // HEAD_DIM
    num_rows = num_caps * seq_len
    unused, kept = layer_forward(stream, weights, causal)
    normed_one, packed, attn_probs, probs_low, mixed_rows, middle, normed_two, hidden, active = kept
    grad_low = grad_out.reshape(num_rows, feat_dim).astype(jnp.bfloat16)
    grad_fc_out = inner_rows(active, grad_low)
    grad_active = outer_cols(grad_low, w_fc_out)
    unused_gelu, gelu_back = jax.vjp(quick_gelu, hidden)
    grad_hidden = gelu_back(grad_active)[0].astype(jnp.bfloat16)
    grad_fc = inner_rows(normed_two, grad_hidden)
    grad_normed_two = outer_cols(grad_hidden, w_fc)
    unused_two, norm_back_two = jax.vjp(norm_apply, middle, gain_two, bias_two)
    grad_mid_norm, grad_gain_two, grad_bias_two = norm_back_two(
        grad_normed_two.reshape(num_caps, seq_len, feat_dim)
    )
    grad_middle = grad_out + grad_mid_norm
    middle_low = grad_middle.reshape(num_rows, feat_dim).astype(jnp.bfloat16)
    grad_w_out = inner_rows(mixed_rows, middle_low)
    grad_mixed = (
        outer_cols(middle_low, w_out)
        .astype(jnp.bfloat16)
        .reshape(num_caps, seq_len, num_heads, HEAD_DIM)
    )
    queries = packed[:, :, 0]
    key_rows = packed[:, :, 1]
    value_rows = packed[:, :, 2]
    grad_values = jnp.einsum(
        "bhqk,bqhd->bkhd", probs_low, grad_mixed, preferred_element_type=jnp.float32
    )
    grad_probs = jnp.einsum(
        "bqhd,bkhd->bhqk", grad_mixed, value_rows, preferred_element_type=jnp.float32
    )
    row_inner = jnp.sum(attn_probs * grad_probs, -1, keepdims=True)
    grad_raw = (attn_probs * (grad_probs - row_inner) * HEAD_DIM ** (-0.5)).astype(jnp.bfloat16)
    grad_queries = jnp.einsum(
        "bhqk,bkhd->bqhd", grad_raw, key_rows, preferred_element_type=jnp.float32
    )
    grad_keys = jnp.einsum("bhqk,bqhd->bkhd", grad_raw, queries, preferred_element_type=jnp.float32)
    grad_packed = (
        jnp.stack([grad_queries, grad_keys, grad_values], 2)
        .astype(jnp.bfloat16)
        .reshape(num_rows, 3 * feat_dim)
    )
    grad_qkv = inner_rows(normed_one, grad_packed)
    grad_normed_one = outer_cols(grad_packed, w_qkv)
    unused_one, norm_back_one = jax.vjp(norm_apply, stream, gain_one, bias_one)
    grad_in_norm, grad_gain_one, grad_bias_one = norm_back_one(
        grad_normed_one.reshape(num_caps, seq_len, feat_dim)
    )
    grads_here = [
        grad_gain_one,
        grad_bias_one,
        grad_qkv,
        grad_w_out,
        grad_gain_two,
        grad_bias_two,
        grad_fc,
        grad_fc_out,
    ]
    return (grad_middle + grad_in_norm, grads_here)


def head_forward(features, gain, bias, proj):
    normed = norm_apply(features, gain, bias).astype(jnp.bfloat16)
    embedded = matmul(normed, proj)
    return (unit_rows(embedded), (normed, embedded))


def head_backward(features, gain, bias, proj, kept, grad_unit):
    normed, embedded = kept
    unused_unit, unit_back = jax.vjp(unit_rows, embedded)
    grad_embed = unit_back(grad_unit)[0].astype(jnp.bfloat16)
    grad_proj = inner_rows(normed, grad_embed)
    grad_normed = outer_cols(grad_embed, proj)
    unused_norm, norm_back = jax.vjp(norm_apply, features, gain, bias)
    grad_feat, grad_gain, grad_bias = norm_back(grad_normed)
    return (grad_feat, [grad_gain, grad_bias, grad_proj])


def plain_contrast(own_rows, other_rows, multiplier, start):
    logits = multiplier * outer_cols(own_rows, other_rows)
    row_peak = jnp.max(logits, -1, keepdims=True)
    log_total = row_peak + jnp.log(jnp.sum(jnp.exp(logits - row_peak), -1, keepdims=True))
    col_pos = lax.broadcasted_iota(jnp.int32, logits.shape, 1)
    target_pos = lax.broadcasted_iota(jnp.int32, logits.shape, 0) + start
    matched = (col_pos == target_pos).astype(jnp.float32)
    loss_sum = jnp.sum(log_total) - jnp.sum(matched * logits)
    grad_logits = 0.5 * (jnp.exp(logits - log_total) - matched)
    scale_part = jnp.sum(grad_logits * logits)
    return (loss_sum, scale_part, (multiplier * grad_logits).astype(jnp.bfloat16), log_total[:, 0])


def pack_flat(arrays, devices):
    flat = jnp.concatenate([array.reshape(-1) for array in arrays])
    padding = -flat.shape[0] % devices
    return jnp.concatenate([flat, jnp.zeros((padding,), jnp.float32)])


def plain(
    text_input,
    eot_index,
    image_input,
    ln1_gain,
    ln1_bias,
    w_qkv,
    w_attn_out,
    ln2_gain,
    ln2_bias,
    w_fc,
    w_fc_out,
    img_ln1_gain,
    img_ln1_bias,
    img_w_qkv,
    img_w_attn_out,
    img_ln2_gain,
    img_ln2_bias,
    img_w_fc,
    img_w_fc_out,
    final_gain,
    final_bias,
    text_proj,
    image_gain,
    image_bias,
    image_proj,
    logit_scale,
):
    num_caps, seq_len, feat_dim = text_input.shape
    devices = lax.axis_size("dp")
    all_caps = num_caps * devices
    start = lax.axis_index("dp") * num_caps
    depth = ln1_gain.shape[0]
    text_stack = (ln1_gain, ln1_bias, w_qkv, w_attn_out, ln2_gain, ln2_bias, w_fc, w_fc_out)
    image_stack = (
        img_ln1_gain,
        img_ln1_bias,
        img_w_qkv,
        img_w_attn_out,
        img_ln2_gain,
        img_ln2_bias,
        img_w_fc,
        img_w_fc_out,
    )

    def text_weights(layer_num):
        return tuple((array[layer_num] for array in text_stack))

    def image_weights(layer_num):
        return tuple((array[layer_num] for array in image_stack))

    stream = text_input.astype(jnp.float32)
    layer_num = 0
    text_saved = [stream]
    stream, unused = layer_forward(stream, text_weights(layer_num), True)
    pooled = jnp.take_along_axis(stream, eot_index[:, None, None], axis=1)[:, 0]
    picture = image_input.astype(jnp.float32)
    layer_num = 0
    image_saved = [picture]
    picture, unused = layer_forward(picture, image_weights(layer_num), False)
    image_pooled = picture[:, 0]
    text_unit, text_kept = head_forward(pooled, final_gain, final_bias, text_proj)
    image_unit, image_kept = head_forward(image_pooled, image_gain, image_bias, image_proj)
    image_low = image_unit.astype(jnp.bfloat16)
    text_low = text_unit.astype(jnp.bfloat16)
    image_all, text_all = (
        lax.all_gather(image_low, "dp", axis=0, tiled=True),
        lax.all_gather(text_low, "dp", axis=0, tiled=True),
    )
    multiplier = jnp.exp(logit_scale[0])
    loss_image, scale_image, grad_raw_it, unused_it = plain_contrast(
        image_low, text_all, multiplier, start
    )
    loss_text, scale_text, grad_raw_ti, unused_ti = plain_contrast(text_low, image_all, multiplier, start)
    spread_text = inner_rows(grad_raw_it, image_low)
    spread_image = inner_rows(grad_raw_ti, text_low)
    back_text, back_image = (
        lax.psum_scatter(spread_text, "dp", scatter_dimension=0, tiled=True),
        lax.psum_scatter(spread_image, "dp", scatter_dimension=0, tiled=True),
    )
    total, grad_scale = lax.psum((loss_image + loss_text, scale_image + scale_text), "dp")
    grad_image_unit = matmul(grad_raw_it, text_all) + back_image
    grad_text_unit = matmul(grad_raw_ti, image_all) + back_text
    grad_pooled, text_head_grads = head_backward(
        pooled, final_gain, final_bias, text_proj, text_kept, grad_text_unit
    )
    grad_image_pooled, image_head_grads = head_backward(
        image_pooled, image_gain, image_bias, image_proj, image_kept, grad_image_unit
    )
    head_flat = pack_flat(text_head_grads + image_head_grads, devices)
    image_flat = [None] * depth
    img_seq = image_input.shape[1]
    img_dim = image_input.shape[2]
    grad_picture = jnp.concatenate(
        [grad_image_pooled[:, None, :], jnp.zeros((num_caps, img_seq - 1, img_dim), jnp.float32)], 1
    )
    for layer_num in reversed(range(depth)):
        grad_picture, grads_here = layer_backward(
            image_saved[layer_num], image_weights(layer_num), grad_picture, False
        )
        image_flat[layer_num] = pack_flat(grads_here, devices)
    text_flat = [None] * depth
    selected = (
        lax.broadcasted_iota(jnp.int32, (num_caps, seq_len), 1) == eot_index[:, None]
    ).astype(jnp.float32)
    grad_stream = selected[:, :, None] * grad_pooled[:, None, :]
    for layer_num in reversed(range(depth)):
        grad_stream, grads_here = layer_backward(
            text_saved[layer_num], text_weights(layer_num), grad_stream, True
        )
        text_flat[layer_num] = pack_flat(grads_here, devices)
    text_share, image_share, head_share = (
        lax.psum_scatter(jnp.stack(text_flat), "dp", scatter_dimension=1, tiled=True),
        lax.psum_scatter(jnp.stack(image_flat), "dp", scatter_dimension=1, tiled=True),
        lax.psum_scatter(head_flat, "dp", scatter_dimension=0, tiled=True),
    )
    loss = (total / (2 * all_caps)).reshape(1)
    return (
        loss,
        grad_stream,
        grad_picture,
        text_share,
        image_share,
        head_share,
        grad_scale.reshape(1),
    )


def shards(*args):
    caps = args[0].shape[0] * lax.axis_size("dp")
    return compact(*args) if caps <= 512 else plain(*args)


def solution(mesh):
    return jax.shard_map(
        shards,
        mesh=mesh,
        in_specs=(
            P("dp", None, None),
            P("dp"),
            P("dp", None, None),
            P(),
            P(),
            P(),
            P(),
            P(),
            P(),
            P(),
            P(),
            P(),
            P(),
            P(),
            P(),
            P(),
            P(),
            P(),
            P(),
            P(),
            P(),
            P(),
            P(),
            P(),
            P(),
            P(),
        ),
        out_specs=(
            P(),
            P("dp", None, None),
            P("dp", None, None),
            P(None, "dp"),
            P(None, "dp"),
            P("dp"),
            P(),
        ),
        check_vma=False,
    )
```

```python
import enum

import jax
import jax.numpy as jnp
from jax import lax
from jax.experimental import pallas as pl
from jax.experimental.pallas import tpu as pltpu
from jax.sharding import PartitionSpec as P

HEAD_DIM = 64
LANES = 128

EPS = 1e-05
UNIT_EPS = 1e-06
MASKED = -1000000000.0
LIMIT = 44 * 2**20
F32 = jnp.float32
BF16 = jnp.bfloat16


class Place(enum.Enum):
    FAR = enum.auto()
    FEW = enum.auto()
    RAW = enum.auto()
    AUTO = enum.auto()
    NEAR = enum.auto()
    SCALAR = enum.auto()


class K(enum.Enum):
    BIAS = enum.auto()
    BIAS2 = enum.auto()
    EOT = enum.auto()
    GAIN = enum.auto()
    GAIN2 = enum.auto()
    HEAD = enum.auto()
    HEAD_BIAS = enum.auto()
    HEAD_GAIN = enum.auto()
    INPUT = enum.auto()
    LOSS = enum.auto()
    MINE = enum.auto()
    MIXED = enum.auto()
    NORMED = enum.auto()
    OTHERS = enum.auto()
    OWN = enum.auto()
    PACK = enum.auto()
    PART = enum.auto()
    PROBS = enum.auto()
    PROJ = enum.auto()
    QUERIES = enum.auto()
    ROWS = enum.auto()
    SCALE = enum.auto()
    SCORES = enum.auto()
    SEND = enum.auto()
    SENT = enum.auto()
    SWAPPED = enum.auto()
    SHARE = enum.auto()
    UNIT = enum.auto()
    VALUES = enum.auto()
    W_FC = enum.auto()
    W_FC_OUT = enum.auto()
    W_OUT = enum.auto()
    W_QKV = enum.auto()
    W_QUERY = enum.auto()
    WINDOWS = enum.auto()
    X = enum.auto()


def dot(left, right):
    return jnp.dot(left, right, preferred_element_type=F32)


def dot_nt(left, right):
    return lax.dot_general(left, right, (((1,), (1,)), ((), ())), preferred_element_type=F32)


def dot_tn(left, right):
    return lax.dot_general(left, right, (((0,), (0,)), ((), ())), preferred_element_type=F32)


def summed_through(rows, weights):
    total = dot(jnp.ones((8, rows.shape[0]), BF16), rows)
    high = total.astype(BF16)
    low = (total - high.astype(F32)).astype(BF16)
    both = dot_nt(jnp.concatenate([high, low], 0), weights)
    return both[:1] + both[8:9]


def standard(values):
    center = values - jnp.mean(values, -1, keepdims=True)
    scale = lax.rsqrt(jnp.mean(center * center, -1, keepdims=True) + EPS)
    return center * scale, scale


def norm_back(grad, unit, scale, gain):
    scaled = grad * gain
    return scale * (
        scaled
        - jnp.mean(scaled, -1, keepdims=True)
        - unit * jnp.mean(scaled * unit, -1, keepdims=True)
    )


def head_masks(width):
    lane = lax.broadcasted_iota(jnp.int32, (1, width), 1)
    return [
        ((lane >= h * HEAD_DIM) & (lane < (h + 1) * HEAD_DIM)).astype(F32)
        for h in range(width // HEAD_DIM)
    ]


def spread(rows):
    return jnp.concatenate([rows * mask for mask in head_masks(rows.shape[1])], 0)


def collect(rows, caps):
    masks = head_masks(rows.shape[1])
    return sum(rows[h * caps : (h + 1) * caps] * mask for h, mask in enumerate(masks))


def picked_columns(caps, total, ends):
    cap = lax.broadcasted_iota(jnp.int32, (caps, 1), 0)
    at = cap
    for b in range(caps):
        at = jnp.where(cap == b, ends[b] * caps + b, at)
    column = lax.broadcasted_iota(jnp.int32, (caps, total), 1)
    chosen = jnp.where(column == at, 1.0, 0.0).astype(BF16)
    return chosen, column, at


class Plan:
    def __init__(self, dim, hidden, devices, caps):
        self.dim, self.hidden, self.devices = dim, hidden, devices
        self.row = 3 * dim
        self.qkv_at = 2 * dim
        self.out_at = self.qkv_at + dim * self.row
        self.norm_at = self.out_at + dim * dim
        self.fc_at = self.norm_at + 2 * dim
        self.fc_out_at = self.fc_at + dim * hidden
        self.total = self.fc_out_at + hidden * dim
        self.share = -(-self.total // devices)
        self.head_total = 2 * (2 * dim + dim * dim)
        self.head_share = -(-self.head_total // devices)
        self.roots = -(-self.out_at // self.share)
        self.rows_out = -(-(self.share // LANES + 2) // 8) * 8
        self.head_rows_out = -(-(self.head_share // LANES + 2) // 8) * 8
        ends = [min((d + 1) * self.share - self.qkv_at, dim * self.row) for d in range(self.roots)]
        self.window = max((end - 1) // self.row + 1 - self.column(d) for d, end in enumerate(ends))
        self.used = 2 * self.window
        self.piece = LANES - self.used
        self.extra = dim // caps
        self.spare, at = [], 0
        for h in reversed(range(dim // HEAD_DIM - 1)):
            start = self.used + min(max(self.used - h * self.piece, 0), self.piece)
            size = min(LANES - start, self.extra - at)
            self.spare.append((h, start, size, at))
            at += size
        assert self.piece > 0 and -(-self.used // self.piece) < dim // HEAD_DIM
        assert at == self.extra <= LANES
        self.spare_from = min(h for h, unused, size, unused in self.spare if size > 0)

    def column(self, device):
        if isinstance(device, int):
            return min(max(device * self.share - self.qkv_at, 0) // self.row, self.dim - 1)
        return jnp.minimum(jnp.maximum(device * self.share - self.qkv_at, 0) // self.row, self.dim - 1)


def window_tiles(plan, text, image, device, caps, extra):
    dim = text.shape[1]
    first = plan.column(device)
    lane = lax.broadcasted_iota(jnp.int32, (text.shape[0], LANES), 1)
    left = pltpu.roll(text, (dim - first) % dim, 1)[:, :LANES]
    right = pltpu.roll(image, (dim - first + plan.window) % dim, 1)[:, :LANES]
    both = jnp.where(lane < plan.window, left, right)
    heads = text.shape[0] // caps
    lane, last = lane[:caps], both[(heads - 1) * caps :]
    tiles = []
    for h in range(heads - 1):
        moved = pltpu.roll(last, (plan.used - h * plan.piece) % LANES, 1)
        tile = jnp.where(lane < plan.used, both[h * caps : (h + 1) * caps], moved)
        for at, start, size, taken in plan.spare if extra is not None else ():
            if at == h and size > 0:
                moved = pltpu.roll(extra, (start - taken) % LANES, 1)
                tile = jnp.where((lane >= start) & (lane < start + size), moved, tile)
        tiles.append(tile.astype(BF16))
    return jnp.concatenate(tiles, 1)


def last_head(plan, source, heads):
    lane = lax.broadcasted_iota(jnp.int32, (source.shape[0], LANES), 1)
    whole = jnp.zeros(lane.shape, F32)
    for h in range(-(-plan.used // plan.piece)):
        tile = source[:, h * LANES : (h + 1) * LANES].astype(F32)
        moved = pltpu.roll(tile, (LANES + h * plan.piece - plan.used) % LANES, 1)
        whole = jnp.where(lane >= h * plan.piece, moved, whole)
    return whole.astype(BF16)


def fold_row(row, caps):
    dim = row.shape[1]
    step = dim // caps
    rows = [pltpu.roll(row, (dim - i * step) % dim, 1)[:, :LANES] for i in range(caps)]
    return jnp.concatenate(rows, 0)


def spare_row(plan, sums, first, dim):
    caps = sums.shape[0]
    lane = lax.broadcasted_iota(jnp.int32, (caps, LANES), 1)
    folded = jnp.zeros((caps, LANES), F32)
    for h, start, size, taken in plan.spare:
        if size > 0:
            tile = sums[:, (h - first) * LANES : (h - first + 1) * LANES]
            moved = pltpu.roll(tile, (taken - start) % LANES, 1)
            folded = jnp.where((lane >= taken) & (lane < taken + size), moved, folded)
    wide = jnp.concatenate([folded, jnp.zeros((caps, dim - LANES), F32)], 1)
    lane = lax.broadcasted_iota(jnp.int32, (1, dim), 1)
    row = jnp.zeros((1, dim), F32)
    for i in range(caps):
        moved = pltpu.roll(wide[i : i + 1], i * plan.extra, 1) if i else wide[:1]
        row = jnp.where((lane >= i * plan.extra) & (lane < (i + 1) * plan.extra), moved, row)
    return row


def pack_windows(plan, target, text, image, caps, common):
    width = (text.shape[0] // caps - 1) * LANES
    held = plan.roots + plan.roots % 2

    def fill(device, core):
        extra = None if common is None else common[core][1]
        target[device, :, :width] = window_tiles(plan, text, image, device, caps, extra)
        if common is not None:
            target[device, :, width:] = common[core][0]

    if held <= 16:
        for device in range(held):
            fill(device, device % 2)
    else:

        @pl.loop(0, held // 2)
        def _(chip):
            for core in range(2):
                fill(2 * chip + core, core)


def clear_windows(plan, target):
    held = plan.roots + plan.roots % 2

    @pl.loop(held, target.shape[0])
    def _(device):
        target[device] = jnp.zeros(target.shape[1:], BF16)

    return slice(0, held), slice(held, target.shape[0])


def take_rows(source, at, count):
    row, lane_at = at // LANES, at % LANES
    lane = lax.broadcasted_iota(jnp.int32, (count, LANES), 1)
    mixed = jnp.where(
        lane >= lane_at, source[pl.ds(row, count), :], source[pl.ds(row + 1, count), :]
    )
    return pltpu.roll(mixed, lax.rem(LANES - lane_at, LANES), 1)


def put_tile(target, row, block):
    count, width = block.shape
    step = width // LANES
    for j in range(step):
        piece = block[:, j * LANES : (j + 1) * LANES]
        if count == 1:
            target[row + j : row + j + 1, :] = piece
        else:
            target[pl.ds(row + j, count, stride=step), :] = piece


def front_tower(tower, ins, picked, last):
    x = ins[K.X, tower].get()[...]
    seq, caps, dim = x.shape
    total = seq * caps
    heads = dim // HEAD_DIM
    source = x.reshape(total, dim)
    chosen, column, pick_at = picked_columns(caps, total, picked)
    last_at = pick_at
    if last is not picked:
        unused, unused, last_at = picked_columns(caps, total, last)
    pooled = dot(chosen, source)
    unit, unused = standard(source.astype(F32))
    yield
    pooled_unit, unused = standard(pooled)
    gain, bias = ins[K.GAIN, tower].get()[...], ins[K.BIAS, tower].get()[...]
    pooled_normed = (pooled_unit * gain + bias).astype(BF16)
    normed = (unit * gain + bias).astype(BF16)
    yield
    w_ref = ins[K.W_QKV, tower].get()
    query = dot(pooled_normed, w_ref[0, :, :dim]).astype(BF16).astype(F32)
    yield
    through_keys = dot_nt(spread(query).astype(BF16), w_ref[0, :, dim : 2 * dim])
    yield
    scores = dot_nt(through_keys.astype(BF16), normed) * HEAD_DIM ** (-0.5)
    yield
    cap = lax.broadcasted_iota(jnp.int32, (caps, 1), 0)
    seen = jnp.where((lax.rem(column, caps) == cap) & (column <= last_at), 1.0, 0.0)
    seen = jnp.concatenate([seen] * heads, 0) > 0.5
    peak = jnp.max(jnp.where(seen, scores, MASKED), -1, keepdims=True)
    sums = jnp.sum(jnp.where(seen, jnp.exp(scores - peak), 0.0), -1, keepdims=True)
    probs = jnp.where(seen, jnp.exp(scores - (peak + jnp.log(sums))), 0.0)
    yield
    values = dot(probs.astype(BF16), normed)
    yield
    mixed = collect(dot(values.astype(BF16), w_ref[0, :, 2 * dim :]), caps).astype(BF16)
    return pooled, mixed, (normed, unit, probs, query, through_keys, values, chosen)


def attended_towers(ins):
    eot = ins[K.EOT].get()
    caps = eot.shape[0]
    seq = ins[K.X, 1].buf.shape[0]
    ends = [eot[b] for b in range(caps)]
    views = (ends, ends), ([0] * caps, [seq - 1] * caps)
    return run_together([front_tower(tower, ins, *views[tower]) for tower in range(2)])


def front_body(plan):
    def body(scalars, ins, outs, scratch):
        payload = [
            jnp.concatenate([pooled.astype(BF16), mixed], 1)
            for pooled, mixed, unused in attended_towers(ins)
        ]
        rows = outs[K.ROWS].ref

        @pl.loop(0, rows.shape[0] // 2)
        def _(chip):
            for core in range(2):
                rows[2 * chip + core] = payload[core]

    return body


def pack_at(dim, hidden, caps):
    heads = dim // HEAD_DIM
    sizes = [heads * caps] * 2 + [caps] * 8 + [caps * hidden // dim]
    places, at = [], 0
    for size in sizes:
        places.append(slice(at, at + size))
        at += size
    return places, at


def weights_of(tower, ins):
    names = K.W_OUT, K.GAIN2, K.BIAS2, K.W_FC, K.W_FC_OUT, K.HEAD_GAIN, K.HEAD_BIAS, K.PROJ
    return [ins[name, tower] for name in names]


def side_body(plan):
    def body(scalars, ins, outs, scratch):
        dim, hidden = plan.dim, plan.hidden
        caps = ins[K.EOT].buf.shape[0]
        places, unused = pack_at(dim, hidden, caps)
        towers = attended_towers(ins)
        clear_windows(plan, outs[K.VALUES].ref)
        pack_windows(plan, outs[K.VALUES].ref, towers[0][2][5], towers[1][2][5], caps, None)
        outs[K.VALUES].push()
        kept, hiddens = ([], []), scratch[0]
        for tower, (pooled, mixed, saved) in enumerate(towers):
            normed, unit, probs, query, through_keys, values, chosen = saved
            unit = unit.astype(BF16)
            for name, value in ((K.NORMED, normed), (K.UNIT, unit), (K.PROBS, probs)):
                outs[name, tower].ref[...] = value
                outs[name, tower].push()
            small = [through_keys, dot(probs.astype(BF16), unit), dot(chosen, unit), query]
            for place, value in zip(places, small):
                outs[K.PACK, tower].ref[place, :] = value
        run_together(
            [
                tower_forward(
                    pooled, mixed, weights_of(tower, ins), kept[tower], hiddens[tower], None
                )
                for tower, (pooled, mixed, unused) in enumerate(towers)
            ]
        )
        for tower in range(2):
            pack = outs[K.PACK, tower]
            for place, value in zip(places[4:10], kept[tower]):
                pack.ref[place, :] = jnp.broadcast_to(value, (caps, dim))
            for j in range(hidden // dim):
                at = places[10].start + j * caps
                pack.ref[at : at + caps, :] = gate_slope(hiddens[tower][:, j * dim : (j + 1) * dim])
            pack.push()

    return body


def run_together(steps):
    results = [None] * len(steps)
    live = list(range(len(steps)))
    while live:
        for index in list(live):
            try:
                next(steps[index])
            except StopIteration as stop:
                results[index] = stop.value
                live.remove(index)
    return results


def chunks(width):
    step = 512 if width % 512 == 0 else width
    return [slice(at, at + step) for at in range(0, width, step)]


def gate_slope(hidden):
    gate = jax.nn.sigmoid(1.702 * hidden)
    return gate + 1.702 * hidden * gate * (1.0 - gate)


def unit_rows_of(embed):
    length = lax.rsqrt(jnp.sum(embed * embed, -1, keepdims=True) + UNIT_EPS)
    return embed * length, length


def tower_forward(pooled, mixed, weights, kept, hidden_ref, active_ref):
    w_out, gain, bias, w_fc, w_fc_out, head_gain, head_bias, proj = weights
    middle = pooled + dot(mixed, w_out.get()[0])
    yield
    unit, scale = standard(middle)
    normed = (unit * gain.get()[...] + bias.get()[...]).astype(BF16)
    yield
    result = middle
    w_fc = w_fc.get()
    for cols in chunks(w_fc.shape[2]):
        hidden = dot(normed, w_fc[0, :, cols])
        active = (hidden * jax.nn.sigmoid(1.702 * hidden)).astype(BF16)
        if hidden_ref is not None:
            hidden_ref[:, cols] = hidden
        if active_ref is not None:
            active_ref[:, cols] = active
        result = result + dot(active, w_fc_out.get()[0, cols, :])
        yield
    head_unit, head_scale = standard(result)
    head_in = (head_unit * head_gain.get()[...][None] + head_bias.get()[...][None]).astype(BF16)
    embed = dot(head_in, proj.get()[...])
    yield
    unit_embed, length = unit_rows_of(embed)
    if kept is not None:
        kept += [unit, scale, head_unit, head_scale, unit_embed, length]
    return unit_embed.astype(BF16)


def log_sum(logits, axis):
    peak = jnp.max(logits, axis, keepdims=True)
    return peak + jnp.log(jnp.sum(jnp.exp(logits - peak), axis, keepdims=True))


def unit_gradient(multiplier, logits, own_total, other_total, matched, other):
    target = jnp.where(matched, 1.0, 0.0)
    own = 0.5 * multiplier * (jnp.exp(logits - own_total) - target)
    cross = 0.5 * multiplier * (jnp.exp(logits - other_total) - target)
    return dot(own.astype(BF16), other) + dot(cross.astype(BF16), other)


def embed_back(grad_unit, unit_embed, length):
    along = jnp.sum(unit_embed * grad_unit, -1, keepdims=True)
    return (length * (grad_unit - unit_embed * along)).astype(BF16)


def tower_backward(grad_embed, kept, slope, weights, keep_hidden):
    unit, scale, head_unit, head_scale = kept
    w_out, gain, bias, w_fc, w_fc_out, head_gain, head_bias, proj = weights
    grad_head = dot_nt(grad_embed, proj.get()[...])
    yield
    grad_result = norm_back(grad_head, head_unit, head_scale, head_gain.get()[...][None])
    grad_out = grad_result.astype(BF16)
    yield
    w_fc, w_fc_out = w_fc.get(), w_fc_out.get()
    grad_normed = 0.0
    for cols in chunks(w_fc.shape[2]):
        grad_active = dot_nt(grad_out, w_fc_out[0, cols, :])
        grad_hidden = (grad_active * slope(cols)).astype(BF16)
        if keep_hidden is not None:
            keep_hidden[:, cols] = grad_hidden
        grad_normed = grad_normed + dot_nt(grad_hidden, w_fc[0, :, cols])
        yield
    grad_middle = grad_result + norm_back(grad_normed, unit, scale, gain.get()[...])
    yield
    grad_mixed = dot_nt(grad_middle.astype(BF16), w_out.get()[0]).astype(BF16)
    yield
    return grad_head, grad_out, grad_normed, grad_middle, grad_mixed


def own_steps(plan, tower, units, multiplier, own_at, ins, outs):
    mine, other = units[tower], units[1 - tower]
    own_out, scores_out = outs[K.OWN, tower], outs[K.SCORES, tower]
    dim = plan.dim
    caps = scores_out.ref.shape[0] * HEAD_DIM // dim
    places, unused = pack_at(dim, plan.hidden, caps)
    other_total = log_sum(multiplier * dot_nt(mine, other), 0)
    yield
    pack = ins[K.PACK, tower].get()
    unit, scale, head_unit, head_scale, unit_embed, length = (pack[places[j], :] for j in range(4, 10))
    logits = multiplier * dot_nt(unit_embed.astype(BF16), other)
    matched = lax.broadcasted_iota(jnp.int32, logits.shape, 1) == own_at + lax.broadcasted_iota(
        jnp.int32, logits.shape, 0
    )
    grad_unit = unit_gradient(multiplier, logits, log_sum(logits, 1), other_total, matched, other)
    yield
    slope_at = places[10].start
    slopes = [pack[slope_at + j * caps : slope_at + (j + 1) * caps, :] for j in range(plan.hidden // dim)]
    slopes = jnp.concatenate(slopes, 1)
    done = yield from tower_backward(
        embed_back(grad_unit, unit_embed, length), (unit, scale, head_unit, head_scale),
        lambda cols: slopes[:, cols], weights_of(tower, ins), None,
    )
    grad_middle, grad_mixed = done[3], done[4].astype(F32)
    own_out.ref[:caps, :] = grad_middle
    w_ref = ins[K.W_QKV, tower].get()
    through_values = dot_nt(spread(grad_mixed).astype(BF16), w_ref[0, :, 2 * dim :])
    own_out.ref[2 * caps :, :] = through_values
    yield
    normed = ins[K.NORMED, tower].get()[...]
    grad_probs = dot_nt(through_values.astype(BF16), normed)
    yield
    probs = ins[K.PROBS, tower].get()[...]
    inner = jnp.sum(probs * grad_probs, -1, keepdims=True)
    grad_scores = (probs * (grad_probs - inner) * HEAD_DIM ** (-0.5)).astype(BF16)
    scores_out.ref[...] = grad_scores
    scores_out.push()
    yield
    spread_keys = dot(grad_scores, normed)
    yield
    grad_query = collect(dot(spread_keys.astype(BF16), w_ref[0, :, dim : 2 * dim]), caps).astype(BF16)
    yield
    units = pack[places[0], :] * dot(grad_scores, ins[K.UNIT, tower].get()[...])
    yield
    through_query = dot_nt(grad_query, w_ref[0, :, :dim])
    own_out.ref[caps : 2 * caps, :] = through_query
    own_out.push()
    units = units + through_values * pack[places[1], :]
    gain_part = jnp.sum(units, 0, keepdims=True) + jnp.sum(
        through_query * pack[places[2], :], 0, keepdims=True
    )
    return spread_keys, grad_query, gain_part


def forward_pair(plan, rows, ins, kept, hidden, active):
    dim = plan.dim
    return run_together(
        [
            tower_forward(
                rows[:, 2 * tower * dim : (2 * tower + 1) * dim].astype(F32),
                rows[:, (2 * tower + 1) * dim : (2 * tower + 2) * dim],
                weights_of(tower, ins), kept[tower], hidden[tower], active[tower],
            )
            for tower in range(2)
        ]
    )


def row_copies(scalars, ins, scratch):
    core = scalars[0][0] % 2
    wide = scratch[0].shape[1] // 2
    return [
        pltpu.make_async_copy(
            ins[name].ref,
            scratch[0].at[:, pl.ds(pl.multiple_of(tower * wide, LANES), wide)],
            scratch[1].at[i],
        )
        for i, (name, tower) in enumerate(((K.MINE, core), (K.OTHERS, 1 - core)))
    ]


def join_rows(scalars, ins, outs, scratch):
    for copy in row_copies(scalars, ins, scratch):
        copy.start()


def middle_body(plan):
    def body(scalars, ins, outs, scratch):
        at_ref, scale_ref = scalars
        rows_ref, sems = scratch
        dim = plan.dim
        device = at_ref[0]
        caps = rows_ref.shape[0] // plan.devices
        held, others = clear_windows(plan, outs[K.SEND].ref)
        outs[K.SEND].push_part(others)
        for copy in row_copies(scalars, ins, scratch):
            copy.wait()
        rows = rows_ref[...]
        outs[K.ROWS].ref[...] = rows
        outs[K.ROWS].push()
        units = forward_pair(plan, rows, ins, (None, None), (None, None), (None, None))
        multiplier = jnp.exp(jnp.full((1, 1), scale_ref[0], F32))
        own_at = device * caps
        parts = run_together(
            [own_steps(plan, tower, units, multiplier, own_at, ins, outs) for tower in range(2)]
        )
        common = [(query, fold_row(gain_part, caps)) for unused, query, gain_part in parts]
        keys_t, keys_i = parts[0][0], parts[1][0]
        pack_windows(plan, outs[K.SEND].ref, keys_t, keys_i, caps, common)
        outs[K.SEND].push_part(held)

    return body


def late_weights(ins, outs, scratch):
    value, sems = scratch[-2:]
    dim = value.shape[1]
    return [
        pltpu.make_async_copy(
            ins[K.W_QKV, tower].ref.at[0, :, pl.ds(at, dim)], target.at[tower], sems.at[2 * part + tower]
        )
        for part, (at, target) in enumerate(((0, outs[K.W_QUERY].ref), (2 * dim, value)))
        for tower in range(2)
    ]


def tail_ahead(plan):
    def ahead(scalars, ins, outs, scratch):
        copies = late_weights(ins, outs, scratch)

        @pl.when(scalars[0][0] < plan.roots)
        def _():
            for copy in copies[:2]:
                copy.start()

        @pl.when(scalars[0][0] == 0)
        def _():
            for copy in copies[2:]:
                copy.start()

    return ahead


def tail_body(plan):
    def body(scalars, ins, outs, scratch):
        at_ref, scale_ref = scalars
        dim, hidden_dim = plan.dim, plan.hidden
        loss_ref, scale_grad_ref = outs[K.LOSS].ref, outs[K.SCALE].ref
        flat, flat_head, wide_t, wide_i, small, hiddens, actives, hidden_grads, late, unused = scratch
        device = at_ref[0]
        eot = ins[K.EOT].get()
        caps = eot.shape[0]
        ends = [eot[b] for b in range(caps)]
        places, unused = pack_at(dim, hidden_dim, caps)
        multiplier = jnp.exp(jnp.full((1, 1), scale_ref[0], F32))

        def input_gradient(tower, picked, wide):
            x, gain = ins[K.X, tower].get(), ins[K.GAIN, tower].get()
            seq = x.shape[0]
            unit, scale = standard(x[...].reshape(seq * caps, dim).astype(F32))
            yield
            probs, pack, own, scores = (
                ins[name, tower].get() for name in (K.PROBS, K.PACK, K.OWN, K.SCORES)
            )
            left = jnp.concatenate([scores[...], probs[...].astype(BF16)], 0)
            right = jnp.concatenate([pack[places[0], :], own[2 * caps :, :]], 0).astype(BF16)
            wide[...] = dot_tn(left, right)
            yield
            for b in range(caps):
                at = picked[b] * caps + b
                wide[pl.ds(at, 1), :] = wide[pl.ds(at, 1), :] + own[caps + b : caps + b + 1, :]
            wide[...] = norm_back(wide[...], unit, scale, gain[...])
            yield
            for b in range(caps):
                at = picked[b] * caps + b
                wide[pl.ds(at, 1), :] = wide[pl.ds(at, 1), :] + own[b : b + 1, :]
            outs[K.INPUT, tower].ref[...] = wide[...].reshape(seq, caps, dim)
            outs[K.INPUT, tower].push()

        run_together([input_gradient(0, ends, wide_t), input_gradient(1, [0] * caps, wide_i)])

        rows = ins[K.ROWS].get()[...]
        count = rows.shape[0]
        kept = [], []
        units = forward_pair(plan, rows, ins, kept, hiddens, actives)
        logits = multiplier * dot_nt(units[1], units[0])
        matched = lax.broadcasted_iota(jnp.int32, logits.shape, 1) == lax.broadcasted_iota(
            jnp.int32, logits.shape, 0
        )
        row_total, column_total = log_sum(logits, 1), log_sum(logits, 0)
        target = jnp.where(matched, 1.0, 0.0)
        by_row = 0.5 * (jnp.exp(logits - row_total) - target)
        by_column = 0.5 * (jnp.exp(logits - column_total) - target)
        total = jnp.sum(row_total) + jnp.sum(column_total) - 2.0 * jnp.sum(target * logits)
        loss_ref[0] = total / (2 * count)
        scale_grad_ref[0] = jnp.sum((by_row + by_column) * logits)
        by_row = (multiplier * by_row).astype(BF16)
        by_column = (multiplier * by_column).astype(BF16)
        grad_units = (
            dot_tn(by_row, units[1]) + dot_tn(by_column, units[1]),
            dot(by_row, units[0]) + dot(by_column, units[0]),
        )

        grad_embeds = [embed_back(grad_units[tower], *kept[tower][4:]) for tower in range(2)]
        backs = run_together(
            [
                tower_backward(
                    grad_embeds[tower], kept[tower][:4],
                    lambda cols, hidden=hiddens[tower]: gate_slope(hidden[:, cols]),
                    weights_of(tower, ins), hidden_grads[tower],
                )
                for tower in range(2)
            ]
        )

        mixed_grads = []
        start, head_start = device * plan.share, device * plan.head_share
        front = plan.rows_out
        half = plan.head_total // 2
        for tower in range(2):
            weights = weights_of(tower, ins)
            gain, bias, head_gain, head_bias = (weights[j] for j in (1, 2, 5, 6))
            active, hidden_grad = actives[tower], hidden_grads[tower]
            grad_embed, done = grad_embeds[tower], backs[tower]
            grad_head, grad_out, grad_normed, grad_middle, grad_mixed = done
            unit, unused, head_unit = kept[tower][:3]
            mixed_grads.append(grad_mixed)
            middle_low = grad_middle.astype(BF16)
            normed = (unit * gain.get()[...] + bias.get()[...]).astype(BF16)
            head_in = head_unit * head_gain.get()[...][None] + head_bias.get()[...][None]
            head_in = head_in.astype(BF16)
            small[0:1, :] = jnp.sum(grad_normed * unit, 0, keepdims=True)
            small[1:2, :] = jnp.sum(grad_normed, 0, keepdims=True)
            small[2:3, :] = jnp.sum(grad_head * head_unit, 0, keepdims=True)
            small[3:4, :] = jnp.sum(grad_head, 0, keepdims=True)
            mixed = rows[:, (2 * tower + 1) * dim : (2 * tower + 2) * dim]

            def when_held(at, size, store):
                @pl.when((at < start + plan.share) & (at + size > start))
                def _():
                    store(front + (at - plan.out_at) // LANES)

            def when_kept(at, size, store):
                at = at + tower * half

                @pl.when((at < head_start + plan.head_share) & (at + size > head_start))
                def _():
                    store(at // LANES)

            def products(when, target, at, left, right):
                for t in range(left.shape[1] // LANES):
                    cols = slice(t * LANES, (t + 1) * LANES)
                    when(
                        at + t * LANES * right.shape[1],
                        LANES * right.shape[1],
                        lambda row: put_tile(target, row, dot_tn(left[:, cols], right[...])),
                    )

            def row_of(when, target, at, index):
                when(at, dim, lambda row: put_tile(target, row, small[index : index + 1, :]))

            products(when_held, flat, plan.out_at, mixed, middle_low)
            row_of(when_held, flat, plan.norm_at, 0)
            row_of(when_held, flat, plan.norm_at + dim, 1)
            products(when_held, flat, plan.fc_at, normed, hidden_grad)
            products(when_held, flat, plan.fc_out_at, active, grad_out)
            at = jnp.maximum(start - plan.out_at + front * LANES, 0)
            outs[K.PART, tower].ref[...] = take_rows(flat, at, plan.rows_out)
            outs[K.PART, tower].push()
            row_of(when_kept, flat_head, 0, 2)
            row_of(when_kept, flat_head, dim, 3)
            products(when_kept, flat_head, 2 * dim, head_in, grad_embed)

        outs[K.HEAD].ref[...] = take_rows(flat_head, head_start, plan.head_rows_out)
        outs[K.HEAD].push()

        copies = late_weights(ins, outs, scratch)

        @pl.when(device == 0)
        def _():
            for tower in range(2):
                copies[2 + tower].wait()
                outs[K.BIAS].ref[tower : tower + 1, :] = summed_through(mixed_grads[tower], late[tower])

        values = ins[K.VALUES].get()

        @pl.when(device < plan.roots)
        def _():
            for copy in copies[:2]:
                copy.wait()
            first = plan.column(device)
            lane = lax.broadcasted_iota(jnp.int32, (count, LANES), 1)
            picked_rows = []
            for tower in range(2):
                gain, bias = ins[K.GAIN, tower].get(), ins[K.BIAS, tower].get()
                pooled = rows[:, 2 * tower * dim : (2 * tower + 1) * dim].astype(F32)
                unit, unused = standard(pooled)
                normed = unit * gain[...] + bias[...]
                outs[K.QUERIES].ref[:, tower * dim : (tower + 1) * dim] = dot(
                    normed.astype(BF16), outs[K.W_QUERY].ref[tower]
                ).astype(BF16)
                shift = lax.rem(dim - first + tower * plan.window, dim)
                picked_rows.append(pltpu.roll(normed, shift, 1)[:, :LANES])
            end = last_head(plan, values, dim // HEAD_DIM)
            for j in range(dim // LANES):
                cols = slice(j * LANES, (j + 1) * LANES)
                block = window_product(plan, values, end, mixed_grads, (0, 0), j)
                for tower in range(2):
                    at = tower * plan.window
                    outs[K.VALUES].ref[tower, :, cols] = block[
                        at : at + plan.window, tower * LANES : (tower + 1) * LANES
                    ]
            outs[K.WINDOWS].ref[...] = jnp.where(lane < plan.window, picked_rows[0], picked_rows[1]).astype(BF16)

    return body


def window_product(plan, source, end, factors, offsets, j):
    lane = lax.broadcasted_iota(jnp.int32, (1, 2 * LANES), 1) % LANES
    right = [factor[:, at + j * LANES : at + (j + 1) * LANES] for factor, at in zip(factors, offsets)]
    right = jnp.concatenate(right, 1).astype(F32)
    total = 0.0
    for h in (2 * j, 2 * j + 1):
        left = end if (h + 1) * HEAD_DIM == plan.dim else source[:, h * LANES : (h + 1) * LANES]
        mine = (lane // HEAD_DIM == h % 2).astype(F32)
        total = total + dot_tn(left, (right * mine).astype(BF16))
    return total


def last_body(plan):
    def body(scalars, ins, outs, scratch):
        (at_ref,) = scalars
        flat, grad_query = scratch
        dim = plan.dim
        heads = dim // HEAD_DIM
        tiles = dim // LANES
        device = at_ref[0]
        parts = [ins[K.PART, tower].get() for tower in range(2)]

        def store(tower, block):
            line = outs[K.SHARE, tower].ref
            line[...] = block.reshape(1, block.shape[0] * LANES)[:, : plan.share]

        @pl.when(device >= plan.roots)
        def _():
            for tower in range(2):
                store(tower, parts[tower][...])

        names = K.SENT, K.SWAPPED, K.WINDOWS, K.QUERIES, K.VALUES, K.W_QUERY, K.BIAS
        sent_ref, swapped, windows, queries, value_part, w_query, bias = (
            ins[name].get() for name in names
        )

        @pl.when(device < plan.roots)
        def _():
            count = sent_ref.shape[0]
            caps = count // plan.devices
            first = plan.spare_from
            for core in range(2):

                @pl.when(device % 2 == core)
                def _():
                    received = sent_ref[:, first * LANES :], swapped[...]
                    for tower, values in enumerate(received if core == 0 else received[::-1]):
                        grad_query[:, tower * dim : (tower + 1) * dim] = values[:, -dim:]

            for tower, values in enumerate((sent_ref[:, first * LANES :], swapped[...])):
                sums = values[:, :-dim].astype(F32).reshape(plan.devices, caps, -1)
                put_tile(flat.at[tower], 0, spare_row(plan, jnp.sum(sums, 0), first, dim))
                grads = grad_query[:, tower * dim : (tower + 1) * dim]
                row = summed_through(grads, w_query[tower])
                put_tile(flat.at[tower], tiles, row + bias[tower : tower + 1, :])

            query_part = dot_tn(windows[...], grad_query[...])
            end = last_head(plan, sent_ref, heads)
            for j in range(tiles):
                put = window_product(plan, sent_ref, end, (queries, queries), (0, dim), j)
                for tower in range(2):
                    rows = slice(tower * plan.window, (tower + 1) * plan.window)
                    own = slice(tower * LANES, (tower + 1) * LANES)
                    q_at = tower * dim + j * LANES
                    for part, block in enumerate(
                        (
                            query_part[rows, q_at : q_at + LANES],
                            put[rows, own],
                            value_part[tower, :, j * LANES : (j + 1) * LANES],
                        )
                    ):
                        flat[
                            tower,
                            pl.ds(2 * tiles + part * tiles + j, plan.window, stride=3 * tiles),
                            :,
                        ] = block
            start = device * plan.share
            at = start - plan.column(device) * plan.row
            shape = parts[0].shape
            index = (
                start
                + lax.broadcasted_iota(jnp.int32, shape, 0) * LANES
                + lax.broadcasted_iota(jnp.int32, shape, 1)
            )
            for tower in range(2):
                own = take_rows(flat.at[tower], at, plan.rows_out)
                store(tower, jnp.where(index < plan.out_at, own, parts[tower][...]))

    return body


class Fetch:
    def __init__(self, source, buf, sem, group):
        self.ref, self.buf, self.group = source, buf, group
        self.copy = pltpu.make_async_copy(source, buf, sem)
        group.members.append(self)

    def get(self):
        self.group.wait()
        return self.buf


class Group:
    def __init__(self):
        self.members, self.waited = [], False

    def wait(self):
        if not self.waited:
            self.waited = True
            for fetch in self.members:
                fetch.copy.wait()


class Here:
    def __init__(self, ref):
        self.buf = self.ref = ref

    def get(self):
        return self.buf

    def push(self):
        pass


class Push:
    def __init__(self, ref, target, sem):
        self.ref, self.target, self.sem, self.started = ref, target, sem, False
        self.copy = pltpu.make_async_copy(ref, target, sem)

    def push(self):
        self.started = True
        self.copy.start()

    def push_part(self, part):
        self.started = True
        pltpu.make_async_copy(self.ref.at[part], self.target.at[part], self.sem).start()


def run(body, name, outs, scratch, scalars, arrays, ahead=None):
    smem = pl.BlockSpec(memory_space=pltpu.SMEM)
    hbm = pl.BlockSpec(memory_space=pltpu.HBM)
    vmem = pl.BlockSpec(memory_space=pltpu.VMEM)
    groups = arrays
    arrays = {key: value for group in groups for key, value in group.items()}
    fetched = [(array, place) for array, place in arrays.values() if place in (Place.FAR, Place.FEW)]
    pushed = [(shape, kind) for shape, kind, place in outs.values() if place == Place.FAR]

    def kernel(*refs):
        at = 0

        def take(count):
            nonlocal at
            at += count
            return list(refs[at - count : at])

        scalar_refs, sources, targets = take(len(scalars)), take(len(arrays)), take(len(outs))
        in_bufs, out_bufs = take(len(fetched)), take(len(pushed))
        in_sems, out_sems = take(2)
        ins, results, fetches, pushes = {}, {}, [], []
        sources = iter(sources)
        chain = [Group() for unused in groups]
        for group, together in zip(groups, chain):
            for (key, (unused, place)), source in zip(group.items(), sources):
                if place in (Place.FAR, Place.FEW):
                    sem = in_sems.at[len(fetches)]
                    fetches.append(Fetch(source, in_bufs[len(fetches)], sem, together))
                    ins[key] = fetches[-1]
                else:
                    ins[key] = Here(source)
        for target, (key, (unused, unused, place)) in zip(targets, outs.items()):
            if place == Place.FAR:
                pushes.append(Push(out_bufs[len(pushes)], target, out_sems.at[len(pushes)]))
            results[key] = pushes[-1] if place == Place.FAR else Here(target)
        own_scratch = take(len(scratch))
        if ahead is not None:
            ahead(scalar_refs, ins, results, own_scratch)
        for fetch in fetches:
            fetch.copy.start()
        body(scalar_refs, ins, results, own_scratch)
        for push in pushes:
            if not push.started:
                push.push()
        for fetch in fetches:
            fetch.get()
        for push in pushes:
            push.copy.wait()

    where = {Place.FAR: hbm, Place.FEW: hbm, Place.RAW: hbm, Place.AUTO: vmem, Place.NEAR: vmem, Place.SCALAR: smem}
    buffers = [
        (pltpu.SMEM if place == Place.FEW else pltpu.VMEM)(array.shape, array.dtype)
        for array, place in fetched
    ]
    buffers += [pltpu.VMEM(shape, kind) for shape, kind in pushed]
    buffers += [pltpu.SemaphoreType.DMA((max(len(group), 1),)) for group in (fetched, pushed)]
    pinned = [
        array if place == Place.AUTO else pltpu.with_memory_space_constraint(array, pltpu.HBM)
        for array, place in arrays.values()
    ]
    results = pl.pallas_call(
        kernel,
        name=name,
        out_shape=[
            {Place.FAR: pltpu.HBM, Place.NEAR: pltpu.VMEM}.get(place, jax.ShapeDtypeStruct)(shape, kind)
            for shape, kind, place in outs.values()
        ],
        in_specs=[smem] * len(scalars) + [where[place] for unused, place in arrays.values()],
        out_specs=[where[place] for unused, unused, place in outs.values()],
        scratch_shapes=buffers + list(scratch),
        compiler_params=pltpu.CompilerParams(vmem_limit_bytes=LIMIT),
    )(*scalars, *pinned)
    return dict(zip(outs, results))


def exchange(array):
    return lax.all_to_all(array, "dp", split_axis=0, concat_axis=0, tiled=True)


def swap(array, devices):
    return lax.ppermute(array, "dp", [(i, i ^ 1) for i in range(devices)])


def compact(
    text_input, eot_index, image_input, ln1_gain, ln1_bias, w_qkv, w_attn_out, ln2_gain, ln2_bias,
    w_fc, w_fc_out, img_ln1_gain, img_ln1_bias, img_w_qkv, img_w_attn_out, img_ln2_gain,
    img_ln2_bias, img_w_fc, img_w_fc_out, final_gain, final_bias, text_proj, image_gain,
    image_bias, image_proj, logit_scale,
):
    caps, seq, dim = text_input.shape
    img_seq = image_input.shape[1]
    devices = lax.axis_size("dp")
    plan = Plan(dim, w_fc.shape[2], devices, caps)
    heads = dim // HEAD_DIM
    count = devices * caps
    hidden = plan.hidden
    device = lax.axis_index("dp").astype(jnp.int32).reshape(1)
    text_input, image_input = text_input.swapaxes(0, 1), image_input.swapaxes(0, 1)
    totals = caps * seq, caps * img_seq
    width = (heads - 1) * LANES

    first = {
        (K.X, 0): text_input, (K.X, 1): image_input,
        (K.GAIN, 0): ln1_gain, (K.BIAS, 0): ln1_bias,
        (K.GAIN, 1): img_ln1_gain, (K.BIAS, 1): img_ln1_bias,
    }
    late = {(K.W_QKV, 0): w_qkv, (K.W_QKV, 1): img_w_qkv}
    outputs_in = {(K.W_OUT, 0): w_attn_out, (K.W_OUT, 1): img_w_attn_out}
    second = {
        (K.GAIN2, 0): ln2_gain, (K.BIAS2, 0): ln2_bias,
        (K.GAIN2, 1): img_ln2_gain, (K.BIAS2, 1): img_ln2_bias,
    }
    hidden_in = {(K.W_FC, 0): w_fc, (K.W_FC, 1): img_w_fc}
    third = {
        (K.W_FC_OUT, 0): w_fc_out, (K.W_FC_OUT, 1): img_w_fc_out,
        (K.HEAD_GAIN, 0): final_gain, (K.HEAD_BIAS, 0): final_bias,
        (K.HEAD_GAIN, 1): image_gain, (K.HEAD_BIAS, 1): image_bias,
        (K.PROJ, 0): text_proj, (K.PROJ, 1): image_proj,
    }

    def far(arrays):
        return {key: (array, Place.FAR) for key, array in arrays.items()}

    eot = {K.EOT: (eot_index, Place.FEW)}
    rows = run(
        front_body(plan),
        "front",
        {K.ROWS: ((devices, caps, 2 * dim), BF16, Place.NEAR)},
        [],
        [],
        [eot | far(first), far(late)],
    )[K.ROWS]
    mine = exchange(rows).reshape(count, 2 * dim)

    unused, pack_rows = pack_at(dim, hidden, caps)
    side_outs = {K.VALUES: ((devices, caps, width), BF16, Place.FAR)}
    middle_outs = {
        K.SEND: ((devices, caps, width + dim), BF16, Place.FAR),
        K.ROWS: ((count, 4 * dim), BF16, Place.FAR),
    }
    for tower, total in enumerate(totals):
        side_outs |= {
            (K.NORMED, tower): ((total, dim), BF16, Place.FAR),
            (K.UNIT, tower): ((total, dim), BF16, Place.FAR),
            (K.PROBS, tower): ((heads * caps, total), F32, Place.FAR),
            (K.PACK, tower): ((pack_rows, dim), F32, Place.FAR),
        }
        middle_outs |= {
            (K.OWN, tower): (((2 + heads) * caps, dim), F32, Place.FAR),
            (K.SCORES, tower): ((heads * caps, total), BF16, Place.FAR),
        }
    side = run(side_body(plan), "side", side_outs, [[pltpu.VMEM((caps, hidden), F32)] * 2], [], [eot | far(first), far(late), far(outputs_in | second | hidden_in | third)])
    values = exchange(side.pop(K.VALUES))
    mine, side[K.PACK, 0] = lax.optimization_barrier((mine, side[K.PACK, 0]))
    others = swap(mine, devices)

    packs = {key: side[key] for key in ((K.PACK, 0), (K.PACK, 1))}
    middle = run(
        middle_body(plan),
        "middle",
        middle_outs,
        [pltpu.VMEM((count, 4 * dim), BF16), pltpu.SemaphoreType.DMA((2,))],
        [device, logit_scale],
        [
            {K.MINE: (mine, Place.AUTO), K.OTHERS: (others, Place.AUTO)}
            | {key: (array, Place.AUTO) for key, array in hidden_in.items()}
            | far(outputs_in | second),
            far(third | packs),
            far(late)
            | far({(name, tower): side[name, tower] for name in (K.NORMED, K.PROBS, K.UNIT) for tower in (0, 1)}),
        ],
        join_rows,
    )
    send, values = lax.optimization_barrier((middle[K.SEND], values))
    sent = exchange(send)

    share_rows = plan.rows_out
    region = (plan.total - plan.out_at) // LANES
    head_region = plan.head_total // LANES
    attended = {}
    tail_outs = {K.LOSS: ((1,), F32, Place.SCALAR), K.SCALE: ((1,), F32, Place.SCALAR)}
    for tower, length in enumerate((seq, img_seq)):
        for name, source in ((K.PROBS, side), (K.PACK, side), (K.OWN, middle), (K.SCORES, middle)):
            attended[name, tower] = source[name, tower]
        tail_outs |= {
            (K.PART, tower): ((share_rows, LANES), F32, Place.NEAR),
            (K.INPUT, tower): ((length, caps, dim), F32, Place.FAR),
        }
    tail_outs |= {
        K.HEAD: ((plan.head_rows_out, LANES), F32, Place.FAR),
        K.WINDOWS: ((count, LANES), BF16, Place.NEAR),
        K.QUERIES: ((count, 2 * dim), BF16, Place.NEAR),
        K.VALUES: ((2, plan.window, dim), F32, Place.NEAR),
        K.W_QUERY: ((2, dim, dim), BF16, Place.NEAR),
        K.BIAS: ((8, dim), F32, Place.NEAR),
    }
    tail = run(
        tail_body(plan),
        "tail",
        tail_outs,
        [
            pltpu.VMEM((region + 2 * share_rows + 8, LANES), F32),
            pltpu.VMEM((head_region + plan.head_rows_out + 8, LANES), F32),
            pltpu.VMEM((totals[0], dim), F32),
            pltpu.VMEM((totals[1], dim), F32),
            pltpu.VMEM((8, dim), F32),
            [pltpu.VMEM((count, hidden), F32)] * 2,
            [pltpu.VMEM((count, hidden), BF16)] * 2,
            [pltpu.VMEM((count, hidden), BF16)] * 2,
            pltpu.VMEM((2, dim, dim), BF16),
            pltpu.SemaphoreType.DMA((4,)),
        ],
        [device, logit_scale],
        [
            eot | far(first),
            far(attended),
            far({K.ROWS: middle[K.ROWS]} | outputs_in | second | hidden_in),
            far(third),
            far({K.VALUES: values.reshape(count, width)})
            | {key: (array, Place.RAW) for key, array in late.items()},
        ],
        tail_ahead(plan),
    )
    sent, tail[K.WINDOWS] = lax.optimization_barrier((sent, tail[K.WINDOWS]))
    swapped = swap(sent[:, :, plan.spare_from * LANES :], devices)
    flat_rows = max(2 * dim + plan.window * plan.row, 2 * dim + 2 * plan.row + share_rows * LANES) // LANES
    names = [(K.PART, 0), (K.PART, 1), K.WINDOWS, K.QUERIES, K.VALUES, K.W_QUERY, K.BIAS]
    shares = run(
        last_body(plan),
        "last",
        {(K.SHARE, tower): ((1, plan.share), F32, Place.FAR) for tower in (0, 1)},
        [
            pltpu.VMEM((2, flat_rows // 8 * 8 + 16, LANES), F32),
            pltpu.VMEM((count, 2 * dim), BF16),
        ],
        [device],
        [
            {name: (tail[name], Place.AUTO) for name in names}
            | {K.SENT: (sent.reshape(count, -1), Place.AUTO)}
            | {K.SWAPPED: (swapped.reshape(count, -1), Place.AUTO)},
        ],
    )

    def cut(array, size):
        return array.reshape(-1)[:size]

    return (
        tail[K.LOSS],
        tail[K.INPUT, 0].swapaxes(0, 1),
        tail[K.INPUT, 1].swapaxes(0, 1),
        shares[K.SHARE, 0],
        shares[K.SHARE, 1],
        cut(tail[K.HEAD], plan.head_share),
        tail[K.SCALE],
    )


def norm_apply(values, gain, bias):
    center = values - jnp.mean(values, -1, keepdims=True)
    spread = jnp.mean(center * center, -1, keepdims=True)
    return center * lax.rsqrt(spread + EPS) * gain + bias


def quick_gelu(values):
    return values * jax.nn.sigmoid(1.702 * values)


def unit_rows(values):
    return values * lax.rsqrt(jnp.sum(values * values, -1, keepdims=True) + UNIT_EPS)


def causal_mask(seq_len):
    row_pos = lax.broadcasted_iota(jnp.int32, (seq_len, seq_len), 0)
    col_pos = lax.broadcasted_iota(jnp.int32, (seq_len, seq_len), 1)
    return col_pos <= row_pos


def matmul(left, right):
    return jnp.dot(left, right, preferred_element_type=jnp.float32)


def inner_rows(left, right):
    return lax.dot_general(
        left, right, (((0,), (0,)), ((), ())), preferred_element_type=jnp.float32
    )


def outer_cols(left, right):
    return lax.dot_general(
        left, right, (((1,), (1,)), ((), ())), preferred_element_type=jnp.float32
    )


def layer_forward(stream, weights, causal):
    gain_one, bias_one, w_qkv, w_out, gain_two, bias_two, w_fc, w_fc_out = weights
    num_caps, seq_len, feat_dim = stream.shape
    num_heads = feat_dim // HEAD_DIM
    num_rows = num_caps * seq_len
    normed_one = (
        norm_apply(stream, gain_one, bias_one).astype(jnp.bfloat16).reshape(num_rows, feat_dim)
    )
    packed = (
        matmul(normed_one, w_qkv)
        .astype(jnp.bfloat16)
        .reshape(num_caps, seq_len, 3, num_heads, HEAD_DIM)
    )
    queries = packed[:, :, 0]
    key_rows = packed[:, :, 1]
    value_rows = packed[:, :, 2]
    raw_score = jnp.einsum("bqhd,bkhd->bhqk", queries, key_rows, preferred_element_type=jnp.float32)
    scores = raw_score * HEAD_DIM ** (-0.5)
    if causal:
        scores = jnp.where(causal_mask(seq_len), scores, MASKED)
    row_peak = jnp.max(scores, -1, keepdims=True)
    log_total = row_peak + jnp.log(jnp.sum(jnp.exp(scores - row_peak), -1, keepdims=True))
    attn_probs = jnp.exp(scores - log_total)
    probs_low = attn_probs.astype(jnp.bfloat16)
    mixed_rows = jnp.einsum(
        "bhqk,bkhd->bqhd", probs_low, value_rows, preferred_element_type=jnp.float32
    )
    mixed_rows = mixed_rows.astype(jnp.bfloat16).reshape(num_rows, feat_dim)
    middle = stream + matmul(mixed_rows, w_out).reshape(num_caps, seq_len, feat_dim)
    normed_two = (
        norm_apply(middle, gain_two, bias_two).astype(jnp.bfloat16).reshape(num_rows, feat_dim)
    )
    hidden = matmul(normed_two, w_fc)
    active = quick_gelu(hidden).astype(jnp.bfloat16)
    result = middle + matmul(active, w_fc_out).reshape(num_caps, seq_len, feat_dim)
    return (
        result,
        (normed_one, packed, attn_probs, probs_low, mixed_rows, middle, normed_two, hidden, active),
    )


def layer_backward(stream, weights, grad_out, causal):
    gain_one, bias_one, w_qkv, w_out, gain_two, bias_two, w_fc, w_fc_out = weights
    num_caps, seq_len, feat_dim = stream.shape
    num_heads = feat_dim // HEAD_DIM
    num_rows = num_caps * seq_len
    unused, kept = layer_forward(stream, weights, causal)
    normed_one, packed, attn_probs, probs_low, mixed_rows, middle, normed_two, hidden, active = kept
    grad_low = grad_out.reshape(num_rows, feat_dim).astype(jnp.bfloat16)
    grad_fc_out = inner_rows(active, grad_low)
    grad_active = outer_cols(grad_low, w_fc_out)
    unused_gelu, gelu_back = jax.vjp(quick_gelu, hidden)
    grad_hidden = gelu_back(grad_active)[0].astype(jnp.bfloat16)
    grad_fc = inner_rows(normed_two, grad_hidden)
    grad_normed_two = outer_cols(grad_hidden, w_fc)
    unused_two, norm_back_two = jax.vjp(norm_apply, middle, gain_two, bias_two)
    grad_mid_norm, grad_gain_two, grad_bias_two = norm_back_two(
        grad_normed_two.reshape(num_caps, seq_len, feat_dim)
    )
    grad_middle = grad_out + grad_mid_norm
    middle_low = grad_middle.reshape(num_rows, feat_dim).astype(jnp.bfloat16)
    grad_w_out = inner_rows(mixed_rows, middle_low)
    grad_mixed = (
        outer_cols(middle_low, w_out)
        .astype(jnp.bfloat16)
        .reshape(num_caps, seq_len, num_heads, HEAD_DIM)
    )
    queries = packed[:, :, 0]
    key_rows = packed[:, :, 1]
    value_rows = packed[:, :, 2]
    grad_values = jnp.einsum(
        "bhqk,bqhd->bkhd", probs_low, grad_mixed, preferred_element_type=jnp.float32
    )
    grad_probs = jnp.einsum(
        "bqhd,bkhd->bhqk", grad_mixed, value_rows, preferred_element_type=jnp.float32
    )
    row_inner = jnp.sum(attn_probs * grad_probs, -1, keepdims=True)
    grad_raw = (attn_probs * (grad_probs - row_inner) * HEAD_DIM ** (-0.5)).astype(jnp.bfloat16)
    grad_queries = jnp.einsum(
        "bhqk,bkhd->bqhd", grad_raw, key_rows, preferred_element_type=jnp.float32
    )
    grad_keys = jnp.einsum("bhqk,bqhd->bkhd", grad_raw, queries, preferred_element_type=jnp.float32)
    grad_packed = (
        jnp.stack([grad_queries, grad_keys, grad_values], 2)
        .astype(jnp.bfloat16)
        .reshape(num_rows, 3 * feat_dim)
    )
    grad_qkv = inner_rows(normed_one, grad_packed)
    grad_normed_one = outer_cols(grad_packed, w_qkv)
    unused_one, norm_back_one = jax.vjp(norm_apply, stream, gain_one, bias_one)
    grad_in_norm, grad_gain_one, grad_bias_one = norm_back_one(
        grad_normed_one.reshape(num_caps, seq_len, feat_dim)
    )
    grads_here = [
        grad_gain_one,
        grad_bias_one,
        grad_qkv,
        grad_w_out,
        grad_gain_two,
        grad_bias_two,
        grad_fc,
        grad_fc_out,
    ]
    return (grad_middle + grad_in_norm, grads_here)


def head_forward(features, gain, bias, proj):
    normed = norm_apply(features, gain, bias).astype(jnp.bfloat16)
    embedded = matmul(normed, proj)
    return (unit_rows(embedded), (normed, embedded))


def head_backward(features, gain, bias, proj, kept, grad_unit):
    normed, embedded = kept
    unused_unit, unit_back = jax.vjp(unit_rows, embedded)
    grad_embed = unit_back(grad_unit)[0].astype(jnp.bfloat16)
    grad_proj = inner_rows(normed, grad_embed)
    grad_normed = outer_cols(grad_embed, proj)
    unused_norm, norm_back = jax.vjp(norm_apply, features, gain, bias)
    grad_feat, grad_gain, grad_bias = norm_back(grad_normed)
    return (grad_feat, [grad_gain, grad_bias, grad_proj])


def plain_contrast(own_rows, other_rows, multiplier, start):
    logits = multiplier * outer_cols(own_rows, other_rows)
    row_peak = jnp.max(logits, -1, keepdims=True)
    log_total = row_peak + jnp.log(jnp.sum(jnp.exp(logits - row_peak), -1, keepdims=True))
    col_pos = lax.broadcasted_iota(jnp.int32, logits.shape, 1)
    target_pos = lax.broadcasted_iota(jnp.int32, logits.shape, 0) + start
    matched = (col_pos == target_pos).astype(jnp.float32)
    loss_sum = jnp.sum(log_total) - jnp.sum(matched * logits)
    grad_logits = 0.5 * (jnp.exp(logits - log_total) - matched)
    scale_part = jnp.sum(grad_logits * logits)
    return (loss_sum, scale_part, (multiplier * grad_logits).astype(jnp.bfloat16), log_total[:, 0])


def pack_flat(arrays, devices):
    flat = jnp.concatenate([array.reshape(-1) for array in arrays])
    padding = -flat.shape[0] % devices
    return jnp.concatenate([flat, jnp.zeros((padding,), jnp.float32)])


def plain(
    text_input,
    eot_index,
    image_input,
    ln1_gain,
    ln1_bias,
    w_qkv,
    w_attn_out,
    ln2_gain,
    ln2_bias,
    w_fc,
    w_fc_out,
    img_ln1_gain,
    img_ln1_bias,
    img_w_qkv,
    img_w_attn_out,
    img_ln2_gain,
    img_ln2_bias,
    img_w_fc,
    img_w_fc_out,
    final_gain,
    final_bias,
    text_proj,
    image_gain,
    image_bias,
    image_proj,
    logit_scale,
):
    num_caps, seq_len, feat_dim = text_input.shape
    devices = lax.axis_size("dp")
    all_caps = num_caps * devices
    start = lax.axis_index("dp") * num_caps
    depth = ln1_gain.shape[0]
    text_stack = (ln1_gain, ln1_bias, w_qkv, w_attn_out, ln2_gain, ln2_bias, w_fc, w_fc_out)
    image_stack = (
        img_ln1_gain,
        img_ln1_bias,
        img_w_qkv,
        img_w_attn_out,
        img_ln2_gain,
        img_ln2_bias,
        img_w_fc,
        img_w_fc_out,
    )

    def text_weights(layer_num):
        return tuple((array[layer_num] for array in text_stack))

    def image_weights(layer_num):
        return tuple((array[layer_num] for array in image_stack))

    stream = text_input.astype(jnp.float32)
    layer_num = 0
    text_saved = [stream]
    stream, unused = layer_forward(stream, text_weights(layer_num), True)
    pooled = jnp.take_along_axis(stream, eot_index[:, None, None], axis=1)[:, 0]
    picture = image_input.astype(jnp.float32)
    layer_num = 0
    image_saved = [picture]
    picture, unused = layer_forward(picture, image_weights(layer_num), False)
    image_pooled = picture[:, 0]
    text_unit, text_kept = head_forward(pooled, final_gain, final_bias, text_proj)
    image_unit, image_kept = head_forward(image_pooled, image_gain, image_bias, image_proj)
    image_low = image_unit.astype(jnp.bfloat16)
    text_low = text_unit.astype(jnp.bfloat16)
    image_all, text_all = (
        lax.all_gather(image_low, "dp", axis=0, tiled=True),
        lax.all_gather(text_low, "dp", axis=0, tiled=True),
    )
    multiplier = jnp.exp(logit_scale[0])
    loss_image, scale_image, grad_raw_it, unused_it = plain_contrast(
        image_low, text_all, multiplier, start
    )
    loss_text, scale_text, grad_raw_ti, unused_ti = plain_contrast(text_low, image_all, multiplier, start)
    spread_text = inner_rows(grad_raw_it, image_low)
    spread_image = inner_rows(grad_raw_ti, text_low)
    back_text, back_image = (
        lax.psum_scatter(spread_text, "dp", scatter_dimension=0, tiled=True),
        lax.psum_scatter(spread_image, "dp", scatter_dimension=0, tiled=True),
    )
    total, grad_scale = lax.psum((loss_image + loss_text, scale_image + scale_text), "dp")
    grad_image_unit = matmul(grad_raw_it, text_all) + back_image
    grad_text_unit = matmul(grad_raw_ti, image_all) + back_text
    grad_pooled, text_head_grads = head_backward(
        pooled, final_gain, final_bias, text_proj, text_kept, grad_text_unit
    )
    grad_image_pooled, image_head_grads = head_backward(
        image_pooled, image_gain, image_bias, image_proj, image_kept, grad_image_unit
    )
    head_flat = pack_flat(text_head_grads + image_head_grads, devices)
    image_flat = [None] * depth
    img_seq = image_input.shape[1]
    img_dim = image_input.shape[2]
    grad_picture = jnp.concatenate(
        [grad_image_pooled[:, None, :], jnp.zeros((num_caps, img_seq - 1, img_dim), jnp.float32)], 1
    )
    for layer_num in reversed(range(depth)):
        grad_picture, grads_here = layer_backward(
            image_saved[layer_num], image_weights(layer_num), grad_picture, False
        )
        image_flat[layer_num] = pack_flat(grads_here, devices)
    text_flat = [None] * depth
    selected = (
        lax.broadcasted_iota(jnp.int32, (num_caps, seq_len), 1) == eot_index[:, None]
    ).astype(jnp.float32)
    grad_stream = selected[:, :, None] * grad_pooled[:, None, :]
    for layer_num in reversed(range(depth)):
        grad_stream, grads_here = layer_backward(
            text_saved[layer_num], text_weights(layer_num), grad_stream, True
        )
        text_flat[layer_num] = pack_flat(grads_here, devices)
    text_share, image_share, head_share = (
        lax.psum_scatter(jnp.stack(text_flat), "dp", scatter_dimension=1, tiled=True),
        lax.psum_scatter(jnp.stack(image_flat), "dp", scatter_dimension=1, tiled=True),
        lax.psum_scatter(head_flat, "dp", scatter_dimension=0, tiled=True),
    )
    loss = (total / (2 * all_caps)).reshape(1)
    return (
        loss,
        grad_stream,
        grad_picture,
        text_share,
        image_share,
        head_share,
        grad_scale.reshape(1),
    )


def shards(*args):
    caps = args[0].shape[0] * lax.axis_size("dp")
    return compact(*args) if caps <= 512 else plain(*args)


def solution(mesh):
    return jax.shard_map(
        shards,
        mesh=mesh,
        in_specs=(
            P("dp", None, None),
            P("dp"),
            P("dp", None, None),
            P(),
            P(),
            P(),
            P(),
            P(),
            P(),
            P(),
            P(),
            P(),
            P(),
            P(),
            P(),
            P(),
            P(),
            P(),
            P(),
            P(),
            P(),
            P(),
            P(),
            P(),
            P(),
            P(),
        ),
        out_specs=(
            P(),
            P("dp", None, None),
            P("dp", None, None),
            P(None, "dp"),
            P(None, "dp"),
            P("dp"),
            P(),
        ),
        check_vma=False,
    )
```

```python
import enum

import jax
import jax.numpy as jnp
from jax import lax
from jax.experimental import pallas as pl
from jax.experimental.pallas import tpu as pltpu
from jax.sharding import PartitionSpec as P

HEAD_DIM = 64
LANES = 128

EPS = 1e-05
UNIT_EPS = 1e-06
MASKED = -1000000000.0
LIMIT = 44 * 2**20
F32 = jnp.float32
BF16 = jnp.bfloat16


class Place(enum.Enum):
    FAR = enum.auto()
    FEW = enum.auto()
    RAW = enum.auto()
    AUTO = enum.auto()
    NEAR = enum.auto()
    SCALAR = enum.auto()


class K(enum.Enum):
    BIAS = enum.auto()
    BIAS2 = enum.auto()
    EOT = enum.auto()
    GAIN = enum.auto()
    GAIN2 = enum.auto()
    HEAD = enum.auto()
    HEAD_BIAS = enum.auto()
    HEAD_GAIN = enum.auto()
    INPUT = enum.auto()
    LOSS = enum.auto()
    MINE = enum.auto()
    MIXED = enum.auto()
    NORMED = enum.auto()
    OTHERS = enum.auto()
    OWN = enum.auto()
    PACK = enum.auto()
    PART = enum.auto()
    PROBS = enum.auto()
    PROJ = enum.auto()
    QUERIES = enum.auto()
    ROWS = enum.auto()
    SCALE = enum.auto()
    SCORES = enum.auto()
    SEND = enum.auto()
    SENT = enum.auto()
    SWAPPED = enum.auto()
    SHARE = enum.auto()
    UNIT = enum.auto()
    VALUES = enum.auto()
    W_FC = enum.auto()
    W_FC_OUT = enum.auto()
    W_OUT = enum.auto()
    W_QKV = enum.auto()
    W_QUERY = enum.auto()
    WINDOWS = enum.auto()
    X = enum.auto()


def dot(left, right):
    return jnp.dot(left, right, preferred_element_type=F32)


def dot_nt(left, right):
    return lax.dot_general(left, right, (((1,), (1,)), ((), ())), preferred_element_type=F32)


def dot_tn(left, right):
    return lax.dot_general(left, right, (((0,), (0,)), ((), ())), preferred_element_type=F32)


def summed_through(rows, weights):
    total = dot(jnp.ones((8, rows.shape[0]), BF16), rows)
    high = total.astype(BF16)
    low = (total - high.astype(F32)).astype(BF16)
    both = dot_nt(jnp.concatenate([high, low], 0), weights)
    return both[:1] + both[8:9]


def standard(values):
    center = values - jnp.mean(values, -1, keepdims=True)
    scale = lax.rsqrt(jnp.mean(center * center, -1, keepdims=True) + EPS)
    return center * scale, scale


def norm_back(grad, unit, scale, gain):
    scaled = grad * gain
    return scale * (
        scaled
        - jnp.mean(scaled, -1, keepdims=True)
        - unit * jnp.mean(scaled * unit, -1, keepdims=True)
    )


def head_masks(width):
    lane = lax.broadcasted_iota(jnp.int32, (1, width), 1)
    return [
        ((lane >= h * HEAD_DIM) & (lane < (h + 1) * HEAD_DIM)).astype(F32)
        for h in range(width // HEAD_DIM)
    ]


def spread(rows):
    return jnp.concatenate([rows * mask for mask in head_masks(rows.shape[1])], 0)


def collect(rows, caps):
    masks = head_masks(rows.shape[1])
    return sum(rows[h * caps : (h + 1) * caps] * mask for h, mask in enumerate(masks))


def picked_columns(caps, total, ends):
    cap = lax.broadcasted_iota(jnp.int32, (caps, 1), 0)
    at = cap
    for b in range(caps):
        at = jnp.where(cap == b, ends[b] * caps + b, at)
    column = lax.broadcasted_iota(jnp.int32, (caps, total), 1)
    chosen = jnp.where(column == at, 1.0, 0.0).astype(BF16)
    return chosen, column, at


class Plan:
    def __init__(self, dim, hidden, devices, caps):
        self.dim, self.hidden, self.devices = dim, hidden, devices
        self.row = 3 * dim
        self.qkv_at = 2 * dim
        self.out_at = self.qkv_at + dim * self.row
        self.norm_at = self.out_at + dim * dim
        self.fc_at = self.norm_at + 2 * dim
        self.fc_out_at = self.fc_at + dim * hidden
        self.total = self.fc_out_at + hidden * dim
        self.share = -(-self.total // devices)
        self.head_total = 2 * (2 * dim + dim * dim)
        self.head_share = -(-self.head_total // devices)
        self.roots = -(-self.out_at // self.share)
        self.rows_out = -(-(self.share // LANES + 2) // 8) * 8
        self.head_rows_out = -(-(self.head_share // LANES + 2) // 8) * 8
        ends = [min((d + 1) * self.share - self.qkv_at, dim * self.row) for d in range(self.roots)]
        self.window = max((end - 1) // self.row + 1 - self.column(d) for d, end in enumerate(ends))
        self.used = 2 * self.window
        self.piece = LANES - self.used
        self.extra = dim // caps
        self.spare, at = [], 0
        for h in reversed(range(dim // HEAD_DIM - 1)):
            start = self.used + min(max(self.used - h * self.piece, 0), self.piece)
            size = min(LANES - start, self.extra - at)
            self.spare.append((h, start, size, at))
            at += size
        assert self.piece > 0 and -(-self.used // self.piece) < dim // HEAD_DIM
        assert at == self.extra <= LANES
        self.spare_from = min(h for h, unused, size, unused in self.spare if size > 0)

    def column(self, device):
        if isinstance(device, int):
            return min(max(device * self.share - self.qkv_at, 0) // self.row, self.dim - 1)
        return jnp.minimum(jnp.maximum(device * self.share - self.qkv_at, 0) // self.row, self.dim - 1)


def window_tiles(plan, text, image, device, caps, extra):
    dim = text.shape[1]
    first = plan.column(device)
    lane = lax.broadcasted_iota(jnp.int32, (text.shape[0], LANES), 1)
    left = pltpu.roll(text, (dim - first) % dim, 1)[:, :LANES]
    right = pltpu.roll(image, (dim - first + plan.window) % dim, 1)[:, :LANES]
    both = jnp.where(lane < plan.window, left, right)
    heads = text.shape[0] // caps
    lane, last = lane[:caps], both[(heads - 1) * caps :]
    tiles = []
    for h in range(heads - 1):
        moved = pltpu.roll(last, (plan.used - h * plan.piece) % LANES, 1)
        tile = jnp.where(lane < plan.used, both[h * caps : (h + 1) * caps], moved)
        for at, start, size, taken in plan.spare if extra is not None else ():
            if at == h and size > 0:
                moved = pltpu.roll(extra, (start - taken) % LANES, 1)
                tile = jnp.where((lane >= start) & (lane < start + size), moved, tile)
        tiles.append(tile.astype(BF16))
    return jnp.concatenate(tiles, 1)


def last_head(plan, source, heads):
    lane = lax.broadcasted_iota(jnp.int32, (source.shape[0], LANES), 1)
    whole = jnp.zeros(lane.shape, F32)
    for h in range(-(-plan.used // plan.piece)):
        tile = source[:, h * LANES : (h + 1) * LANES].astype(F32)
        moved = pltpu.roll(tile, (LANES + h * plan.piece - plan.used) % LANES, 1)
        whole = jnp.where(lane >= h * plan.piece, moved, whole)
    return whole.astype(BF16)


def fold_row(row, caps):
    dim = row.shape[1]
    step = dim // caps
    rows = [pltpu.roll(row, (dim - i * step) % dim, 1)[:, :LANES] for i in range(caps)]
    return jnp.concatenate(rows, 0)


def spare_row(plan, sums, first, dim):
    caps = sums.shape[0]
    lane = lax.broadcasted_iota(jnp.int32, (caps, LANES), 1)
    folded = jnp.zeros((caps, LANES), F32)
    for h, start, size, taken in plan.spare:
        if size > 0:
            tile = sums[:, (h - first) * LANES : (h - first + 1) * LANES]
            moved = pltpu.roll(tile, (taken - start) % LANES, 1)
            folded = jnp.where((lane >= taken) & (lane < taken + size), moved, folded)
    wide = jnp.concatenate([folded, jnp.zeros((caps, dim - LANES), F32)], 1)
    lane = lax.broadcasted_iota(jnp.int32, (1, dim), 1)
    row = jnp.zeros((1, dim), F32)
    for i in range(caps):
        moved = pltpu.roll(wide[i : i + 1], i * plan.extra, 1) if i else wide[:1]
        row = jnp.where((lane >= i * plan.extra) & (lane < (i + 1) * plan.extra), moved, row)
    return row


def pack_windows(plan, target, text, image, caps, common):
    width = (text.shape[0] // caps - 1) * LANES
    held = plan.roots + plan.roots % 2

    def fill(device, core):
        extra = None if common is None else common[core][1]
        target[device, :, :width] = window_tiles(plan, text, image, device, caps, extra)
        if common is not None:
            target[device, :, width:] = common[core][0]

    if held <= 16:
        for device in range(held):
            fill(device, device % 2)
    else:

        @pl.loop(0, held // 2)
        def _(chip):
            for core in range(2):
                fill(2 * chip + core, core)


def clear_windows(plan, target):
    held = plan.roots + plan.roots % 2

    @pl.loop(held, target.shape[0])
    def _(device):
        target[device] = jnp.zeros(target.shape[1:], BF16)

    return slice(0, held), slice(held, target.shape[0])


def take_rows(source, at, count):
    row, lane_at = at // LANES, at % LANES
    lane = lax.broadcasted_iota(jnp.int32, (count, LANES), 1)
    mixed = jnp.where(
        lane >= lane_at, source[pl.ds(row, count), :], source[pl.ds(row + 1, count), :]
    )
    return pltpu.roll(mixed, lax.rem(LANES - lane_at, LANES), 1)


def put_tile(target, row, block):
    count, width = block.shape
    step = width // LANES
    for j in range(step):
        piece = block[:, j * LANES : (j + 1) * LANES]
        if count == 1:
            target[row + j : row + j + 1, :] = piece
        else:
            target[pl.ds(row + j, count, stride=step), :] = piece


def front_tower(tower, ins, picked, last):
    x = ins[K.X, tower].get()[...]
    seq, caps, dim = x.shape
    total = seq * caps
    heads = dim // HEAD_DIM
    source = x.reshape(total, dim)
    chosen, column, pick_at = picked_columns(caps, total, picked)
    last_at = pick_at
    if last is not picked:
        unused, unused, last_at = picked_columns(caps, total, last)
    pooled = dot(chosen, source)
    unit, unused = standard(source.astype(F32))
    yield
    pooled_unit, unused = standard(pooled)
    gain, bias = ins[K.GAIN, tower].get()[...], ins[K.BIAS, tower].get()[...]
    pooled_normed = (pooled_unit * gain + bias).astype(BF16)
    normed = (unit * gain + bias).astype(BF16)
    yield
    w_ref = ins[K.W_QKV, tower].get()
    query = dot(pooled_normed, w_ref[0, :, :dim]).astype(BF16).astype(F32)
    yield
    through_keys = dot_nt(spread(query).astype(BF16), w_ref[0, :, dim : 2 * dim])
    yield
    scores = dot_nt(through_keys.astype(BF16), normed) * HEAD_DIM ** (-0.5)
    yield
    cap = lax.broadcasted_iota(jnp.int32, (caps, 1), 0)
    seen = jnp.where((lax.rem(column, caps) == cap) & (column <= last_at), 1.0, 0.0)
    seen = jnp.concatenate([seen] * heads, 0) > 0.5
    peak = jnp.max(jnp.where(seen, scores, MASKED), -1, keepdims=True)
    sums = jnp.sum(jnp.where(seen, jnp.exp(scores - peak), 0.0), -1, keepdims=True)
    probs = jnp.where(seen, jnp.exp(scores - (peak + jnp.log(sums))), 0.0)
    yield
    values = dot(probs.astype(BF16), normed)
    yield
    mixed = collect(dot(values.astype(BF16), w_ref[0, :, 2 * dim :]), caps).astype(BF16)
    return pooled, mixed, (normed, unit, probs, query, through_keys, values, chosen)


def attended_towers(ins):
    eot = ins[K.EOT].get()
    caps = eot.shape[0]
    seq = ins[K.X, 1].buf.shape[0]
    ends = [eot[b] for b in range(caps)]
    views = (ends, ends), ([0] * caps, [seq - 1] * caps)
    return run_together([front_tower(tower, ins, *views[tower]) for tower in range(2)])


def front_body(plan):
    def body(scalars, ins, outs, scratch):
        payload = [
            jnp.concatenate([pooled.astype(BF16), mixed], 1)
            for pooled, mixed, unused in attended_towers(ins)
        ]
        rows = outs[K.ROWS].ref

        for device in range(rows.shape[0]):
            rows[device] = payload[device % 2]

    return body


def pack_at(dim, hidden, caps):
    heads = dim // HEAD_DIM
    sizes = [heads * caps] * 2 + [caps] * 8 + [caps * hidden // dim]
    places, at = [], 0
    for size in sizes:
        places.append(slice(at, at + size))
        at += size
    return places, at


def weights_of(tower, ins):
    names = K.W_OUT, K.GAIN2, K.BIAS2, K.W_FC, K.W_FC_OUT, K.HEAD_GAIN, K.HEAD_BIAS, K.PROJ
    return [ins[name, tower] for name in names]


def side_body(plan):
    def body(scalars, ins, outs, scratch):
        dim, hidden = plan.dim, plan.hidden
        caps = ins[K.EOT].buf.shape[0]
        places, unused = pack_at(dim, hidden, caps)
        towers = attended_towers(ins)
        clear_windows(plan, outs[K.VALUES].ref)
        pack_windows(plan, outs[K.VALUES].ref, towers[0][2][5], towers[1][2][5], caps, None)
        outs[K.VALUES].push()
        kept, hiddens = ([], []), scratch[0]
        for tower, (pooled, mixed, saved) in enumerate(towers):
            normed, unit, probs, query, through_keys, values, chosen = saved
            unit = unit.astype(BF16)
            for name, value in ((K.NORMED, normed), (K.UNIT, unit), (K.PROBS, probs)):
                outs[name, tower].ref[...] = value
                outs[name, tower].push()
            small = [through_keys, dot(probs.astype(BF16), unit), dot(chosen, unit), query]
            for place, value in zip(places, small):
                outs[K.PACK, tower].ref[place, :] = value
        run_together(
            [
                tower_forward(
                    pooled, mixed, weights_of(tower, ins), kept[tower], hiddens[tower], None
                )
                for tower, (pooled, mixed, unused) in enumerate(towers)
            ]
        )
        for tower in range(2):
            pack = outs[K.PACK, tower]
            for place, value in zip(places[4:10], kept[tower]):
                pack.ref[place, :] = jnp.broadcast_to(value, (caps, dim))
            for j in range(hidden // dim):
                at = places[10].start + j * caps
                pack.ref[at : at + caps, :] = gate_slope(hiddens[tower][:, j * dim : (j + 1) * dim])
            pack.push()

    return body


def run_together(steps):
    results = [None] * len(steps)
    live = list(range(len(steps)))
    while live:
        for index in list(live):
            try:
                next(steps[index])
            except StopIteration as stop:
                results[index] = stop.value
                live.remove(index)
    return results


def chunks(width):
    step = 512 if width % 512 == 0 else width
    return [slice(at, at + step) for at in range(0, width, step)]


def gate_slope(hidden):
    gate = jax.nn.sigmoid(1.702 * hidden)
    return gate + 1.702 * hidden * gate * (1.0 - gate)


def unit_rows_of(embed):
    length = lax.rsqrt(jnp.sum(embed * embed, -1, keepdims=True) + UNIT_EPS)
    return embed * length, length


def tower_forward(pooled, mixed, weights, kept, hidden_ref, active_ref):
    w_out, gain, bias, w_fc, w_fc_out, head_gain, head_bias, proj = weights
    middle = pooled + dot(mixed, w_out.get()[0])
    yield
    unit, scale = standard(middle)
    normed = (unit * gain.get()[...] + bias.get()[...]).astype(BF16)
    yield
    result = middle
    w_fc = w_fc.get()
    for cols in chunks(w_fc.shape[2]):
        hidden = dot(normed, w_fc[0, :, cols])
        active = (hidden * jax.nn.sigmoid(1.702 * hidden)).astype(BF16)
        if hidden_ref is not None:
            hidden_ref[:, cols] = hidden
        if active_ref is not None:
            active_ref[:, cols] = active
        result = result + dot(active, w_fc_out.get()[0, cols, :])
        yield
    head_unit, head_scale = standard(result)
    head_in = (head_unit * head_gain.get()[...][None] + head_bias.get()[...][None]).astype(BF16)
    embed = dot(head_in, proj.get()[...])
    yield
    unit_embed, length = unit_rows_of(embed)
    if kept is not None:
        kept += [unit, scale, head_unit, head_scale, unit_embed, length]
    return unit_embed.astype(BF16)


def log_sum(logits, axis):
    peak = jnp.max(logits, axis, keepdims=True)
    return peak + jnp.log(jnp.sum(jnp.exp(logits - peak), axis, keepdims=True))


def unit_gradient(multiplier, logits, own_total, other_total, matched, other):
    target = jnp.where(matched, 1.0, 0.0)
    own = 0.5 * multiplier * (jnp.exp(logits - own_total) - target)
    cross = 0.5 * multiplier * (jnp.exp(logits - other_total) - target)
    return dot(own.astype(BF16), other) + dot(cross.astype(BF16), other)


def embed_back(grad_unit, unit_embed, length):
    along = jnp.sum(unit_embed * grad_unit, -1, keepdims=True)
    return (length * (grad_unit - unit_embed * along)).astype(BF16)


def tower_backward(grad_embed, kept, slope, weights, keep_hidden):
    unit, scale, head_unit, head_scale = kept
    w_out, gain, bias, w_fc, w_fc_out, head_gain, head_bias, proj = weights
    grad_head = dot_nt(grad_embed, proj.get()[...])
    yield
    grad_result = norm_back(grad_head, head_unit, head_scale, head_gain.get()[...][None])
    grad_out = grad_result.astype(BF16)
    yield
    w_fc, w_fc_out = w_fc.get(), w_fc_out.get()
    grad_normed = 0.0
    for cols in chunks(w_fc.shape[2]):
        grad_active = dot_nt(grad_out, w_fc_out[0, cols, :])
        grad_hidden = (grad_active * slope(cols)).astype(BF16)
        if keep_hidden is not None:
            keep_hidden[:, cols] = grad_hidden
        grad_normed = grad_normed + dot_nt(grad_hidden, w_fc[0, :, cols])
        yield
    grad_middle = grad_result + norm_back(grad_normed, unit, scale, gain.get()[...])
    yield
    grad_mixed = dot_nt(grad_middle.astype(BF16), w_out.get()[0]).astype(BF16)
    yield
    return grad_head, grad_out, grad_normed, grad_middle, grad_mixed


def own_steps(plan, tower, units, multiplier, own_at, ins, outs):
    mine, other = units[tower], units[1 - tower]
    own_out, scores_out = outs[K.OWN, tower], outs[K.SCORES, tower]
    dim = plan.dim
    caps = scores_out.ref.shape[0] * HEAD_DIM // dim
    places, unused = pack_at(dim, plan.hidden, caps)
    other_total = log_sum(multiplier * dot_nt(mine, other), 0)
    yield
    pack = ins[K.PACK, tower].get()
    unit, scale, head_unit, head_scale, unit_embed, length = (pack[places[j], :] for j in range(4, 10))
    logits = multiplier * dot_nt(unit_embed.astype(BF16), other)
    matched = lax.broadcasted_iota(jnp.int32, logits.shape, 1) == own_at + lax.broadcasted_iota(
        jnp.int32, logits.shape, 0
    )
    grad_unit = unit_gradient(multiplier, logits, log_sum(logits, 1), other_total, matched, other)
    yield
    slope_at = places[10].start
    slopes = [pack[slope_at + j * caps : slope_at + (j + 1) * caps, :] for j in range(plan.hidden // dim)]
    slopes = jnp.concatenate(slopes, 1)
    done = yield from tower_backward(
        embed_back(grad_unit, unit_embed, length), (unit, scale, head_unit, head_scale),
        lambda cols: slopes[:, cols], weights_of(tower, ins), None,
    )
    grad_middle, grad_mixed = done[3], done[4].astype(F32)
    own_out.ref[:caps, :] = grad_middle
    w_ref = ins[K.W_QKV, tower].get()
    through_values = dot_nt(spread(grad_mixed).astype(BF16), w_ref[0, :, 2 * dim :])
    own_out.ref[2 * caps :, :] = through_values
    yield
    normed = ins[K.NORMED, tower].get()[...]
    grad_probs = dot_nt(through_values.astype(BF16), normed)
    yield
    probs = ins[K.PROBS, tower].get()[...]
    inner = jnp.sum(probs * grad_probs, -1, keepdims=True)
    grad_scores = (probs * (grad_probs - inner) * HEAD_DIM ** (-0.5)).astype(BF16)
    scores_out.ref[...] = grad_scores
    scores_out.push()
    yield
    spread_keys = dot(grad_scores, normed)
    yield
    grad_query = collect(dot(spread_keys.astype(BF16), w_ref[0, :, dim : 2 * dim]), caps).astype(BF16)
    yield
    units = pack[places[0], :] * dot(grad_scores, ins[K.UNIT, tower].get()[...])
    yield
    through_query = dot_nt(grad_query, w_ref[0, :, :dim])
    own_out.ref[caps : 2 * caps, :] = through_query
    own_out.push()
    units = units + through_values * pack[places[1], :]
    gain_part = jnp.sum(units, 0, keepdims=True) + jnp.sum(
        through_query * pack[places[2], :], 0, keepdims=True
    )
    return spread_keys, grad_query, gain_part


def forward_pair(plan, rows, ins, kept, hidden, active):
    dim = plan.dim
    return run_together(
        [
            tower_forward(
                rows[:, 2 * tower * dim : (2 * tower + 1) * dim].astype(F32),
                rows[:, (2 * tower + 1) * dim : (2 * tower + 2) * dim],
                weights_of(tower, ins), kept[tower], hidden[tower], active[tower],
            )
            for tower in range(2)
        ]
    )


def row_copies(scalars, ins, scratch):
    core = scalars[0][0] % 2
    wide = scratch[0].shape[1] // 2
    return [
        pltpu.make_async_copy(
            ins[name].ref,
            scratch[0].at[:, pl.ds(pl.multiple_of(tower * wide, LANES), wide)],
            scratch[1].at[i],
        )
        for i, (name, tower) in enumerate(((K.MINE, core), (K.OTHERS, 1 - core)))
    ]


def join_rows(scalars, ins, outs, scratch):
    for copy in row_copies(scalars, ins, scratch):
        copy.start()


def middle_body(plan):
    def body(scalars, ins, outs, scratch):
        at_ref, scale_ref = scalars
        rows_ref, sems = scratch
        dim = plan.dim
        device = at_ref[0]
        caps = rows_ref.shape[0] // plan.devices
        held, others = clear_windows(plan, outs[K.SEND].ref)
        outs[K.SEND].push_part(others)
        for copy in row_copies(scalars, ins, scratch):
            copy.wait()
        rows = rows_ref[...]
        outs[K.ROWS].ref[...] = rows
        outs[K.ROWS].push()
        units = forward_pair(plan, rows, ins, (None, None), (None, None), (None, None))
        multiplier = jnp.exp(jnp.full((1, 1), scale_ref[0], F32))
        own_at = device * caps
        parts = run_together(
            [own_steps(plan, tower, units, multiplier, own_at, ins, outs) for tower in range(2)]
        )
        common = [(query, fold_row(gain_part, caps)) for unused, query, gain_part in parts]
        keys_t, keys_i = parts[0][0], parts[1][0]
        pack_windows(plan, outs[K.SEND].ref, keys_t, keys_i, caps, common)
        outs[K.SEND].push_part(held)

    return body


def late_weights(ins, outs, scratch):
    value, sems = scratch[-2:]
    dim = value.shape[1]
    return [
        pltpu.make_async_copy(
            ins[K.W_QKV, tower].ref.at[0, :, pl.ds(at, dim)], target.at[tower], sems.at[2 * part + tower]
        )
        for part, (at, target) in enumerate(((0, outs[K.W_QUERY].ref), (2 * dim, value)))
        for tower in range(2)
    ]


def tail_ahead(plan):
    def ahead(scalars, ins, outs, scratch):
        copies = late_weights(ins, outs, scratch)

        @pl.when(scalars[0][0] < plan.roots)
        def _():
            for copy in copies[:2]:
                copy.start()

        @pl.when(scalars[0][0] == 0)
        def _():
            for copy in copies[2:]:
                copy.start()

    return ahead


def tail_body(plan):
    def body(scalars, ins, outs, scratch):
        at_ref, scale_ref = scalars
        dim, hidden_dim = plan.dim, plan.hidden
        loss_ref, scale_grad_ref = outs[K.LOSS].ref, outs[K.SCALE].ref
        flat, flat_head, wide_t, wide_i, small, hiddens, actives, hidden_grads, late, unused = scratch
        device = at_ref[0]
        eot = ins[K.EOT].get()
        caps = eot.shape[0]
        ends = [eot[b] for b in range(caps)]
        places, unused = pack_at(dim, hidden_dim, caps)
        multiplier = jnp.exp(jnp.full((1, 1), scale_ref[0], F32))

        def input_gradient(tower, picked, wide):
            x, gain = ins[K.X, tower].get(), ins[K.GAIN, tower].get()
            seq = x.shape[0]
            unit, scale = standard(x[...].reshape(seq * caps, dim).astype(F32))
            yield
            probs, pack, own, scores = (
                ins[name, tower].get() for name in (K.PROBS, K.PACK, K.OWN, K.SCORES)
            )
            left = jnp.concatenate([scores[...], probs[...].astype(BF16)], 0)
            right = jnp.concatenate([pack[places[0], :], own[2 * caps :, :]], 0).astype(BF16)
            wide[...] = dot_tn(left, right)
            yield
            for b in range(caps):
                at = picked[b] * caps + b
                wide[pl.ds(at, 1), :] = wide[pl.ds(at, 1), :] + own[caps + b : caps + b + 1, :]
            wide[...] = norm_back(wide[...], unit, scale, gain[...])
            yield
            for b in range(caps):
                at = picked[b] * caps + b
                wide[pl.ds(at, 1), :] = wide[pl.ds(at, 1), :] + own[b : b + 1, :]
            outs[K.INPUT, tower].ref[...] = wide[...].reshape(seq, caps, dim)
            outs[K.INPUT, tower].push()

        run_together([input_gradient(0, ends, wide_t), input_gradient(1, [0] * caps, wide_i)])

        rows = ins[K.ROWS].get()[...]
        count = rows.shape[0]
        kept = [], []
        units = forward_pair(plan, rows, ins, kept, hiddens, actives)
        logits = multiplier * dot_nt(units[1], units[0])
        matched = lax.broadcasted_iota(jnp.int32, logits.shape, 1) == lax.broadcasted_iota(
            jnp.int32, logits.shape, 0
        )
        row_total, column_total = log_sum(logits, 1), log_sum(logits, 0)
        target = jnp.where(matched, 1.0, 0.0)
        by_row = 0.5 * (jnp.exp(logits - row_total) - target)
        by_column = 0.5 * (jnp.exp(logits - column_total) - target)
        total = jnp.sum(row_total) + jnp.sum(column_total) - 2.0 * jnp.sum(target * logits)
        loss_ref[0] = total / (2 * count)
        scale_grad_ref[0] = jnp.sum((by_row + by_column) * logits)
        by_row = (multiplier * by_row).astype(BF16)
        by_column = (multiplier * by_column).astype(BF16)
        grad_units = (
            dot_tn(by_row, units[1]) + dot_tn(by_column, units[1]),
            dot(by_row, units[0]) + dot(by_column, units[0]),
        )

        grad_embeds = [embed_back(grad_units[tower], *kept[tower][4:]) for tower in range(2)]
        backs = run_together(
            [
                tower_backward(
                    grad_embeds[tower], kept[tower][:4],
                    lambda cols, hidden=hiddens[tower]: gate_slope(hidden[:, cols]),
                    weights_of(tower, ins), hidden_grads[tower],
                )
                for tower in range(2)
            ]
        )

        mixed_grads = []
        start, head_start = device * plan.share, device * plan.head_share
        front = plan.rows_out
        half = plan.head_total // 2
        for tower in range(2):
            weights = weights_of(tower, ins)
            gain, bias, head_gain, head_bias = (weights[j] for j in (1, 2, 5, 6))
            active, hidden_grad = actives[tower], hidden_grads[tower]
            grad_embed, done = grad_embeds[tower], backs[tower]
            grad_head, grad_out, grad_normed, grad_middle, grad_mixed = done
            unit, unused, head_unit = kept[tower][:3]
            mixed_grads.append(grad_mixed)
            middle_low = grad_middle.astype(BF16)
            normed = (unit * gain.get()[...] + bias.get()[...]).astype(BF16)
            head_in = head_unit * head_gain.get()[...][None] + head_bias.get()[...][None]
            head_in = head_in.astype(BF16)
            small[0:1, :] = jnp.sum(grad_normed * unit, 0, keepdims=True)
            small[1:2, :] = jnp.sum(grad_normed, 0, keepdims=True)
            small[2:3, :] = jnp.sum(grad_head * head_unit, 0, keepdims=True)
            small[3:4, :] = jnp.sum(grad_head, 0, keepdims=True)
            mixed = rows[:, (2 * tower + 1) * dim : (2 * tower + 2) * dim]

            def when_held(at, size, store):
                @pl.when((at < start + plan.share) & (at + size > start))
                def _():
                    store(front + (at - plan.out_at) // LANES)

            def when_kept(at, size, store):
                at = at + tower * half

                @pl.when((at < head_start + plan.head_share) & (at + size > head_start))
                def _():
                    store(at // LANES)

            def products(when, target, at, left, right):
                for t in range(left.shape[1] // LANES):
                    cols = slice(t * LANES, (t + 1) * LANES)
                    when(
                        at + t * LANES * right.shape[1],
                        LANES * right.shape[1],
                        lambda row: put_tile(target, row, dot_tn(left[:, cols], right[...])),
                    )

            def row_of(when, target, at, index):
                when(at, dim, lambda row: put_tile(target, row, small[index : index + 1, :]))

            products(when_held, flat, plan.out_at, mixed, middle_low)
            row_of(when_held, flat, plan.norm_at, 0)
            row_of(when_held, flat, plan.norm_at + dim, 1)
            products(when_held, flat, plan.fc_at, normed, hidden_grad)
            products(when_held, flat, plan.fc_out_at, active, grad_out)
            at = jnp.maximum(start - plan.out_at + front * LANES, 0)
            outs[K.PART, tower].ref[...] = take_rows(flat, at, plan.rows_out)
            outs[K.PART, tower].push()
            row_of(when_kept, flat_head, 0, 2)
            row_of(when_kept, flat_head, dim, 3)
            products(when_kept, flat_head, 2 * dim, head_in, grad_embed)

        outs[K.HEAD].ref[...] = take_rows(flat_head, head_start, plan.head_rows_out)
        outs[K.HEAD].push()

        copies = late_weights(ins, outs, scratch)

        @pl.when(device == 0)
        def _():
            for tower in range(2):
                copies[2 + tower].wait()
                outs[K.BIAS].ref[tower : tower + 1, :] = summed_through(mixed_grads[tower], late[tower])

        values = ins[K.VALUES].get()

        @pl.when(device < plan.roots)
        def _():
            for copy in copies[:2]:
                copy.wait()
            first = plan.column(device)
            lane = lax.broadcasted_iota(jnp.int32, (count, LANES), 1)
            picked_rows = []
            for tower in range(2):
                gain, bias = ins[K.GAIN, tower].get(), ins[K.BIAS, tower].get()
                pooled = rows[:, 2 * tower * dim : (2 * tower + 1) * dim].astype(F32)
                unit, unused = standard(pooled)
                normed = unit * gain[...] + bias[...]
                outs[K.QUERIES].ref[:, tower * dim : (tower + 1) * dim] = dot(
                    normed.astype(BF16), outs[K.W_QUERY].ref[tower]
                ).astype(BF16)
                shift = lax.rem(dim - first + tower * plan.window, dim)
                picked_rows.append(pltpu.roll(normed, shift, 1)[:, :LANES])
            end = last_head(plan, values, dim // HEAD_DIM)
            for j in range(dim // LANES):
                cols = slice(j * LANES, (j + 1) * LANES)
                block = window_product(plan, values, end, mixed_grads, (0, 0), j)
                for tower in range(2):
                    at = tower * plan.window
                    outs[K.VALUES].ref[tower, :, cols] = block[
                        at : at + plan.window, tower * LANES : (tower + 1) * LANES
                    ]
            outs[K.WINDOWS].ref[...] = jnp.where(lane < plan.window, picked_rows[0], picked_rows[1]).astype(BF16)

    return body


def window_product(plan, source, end, factors, offsets, j):
    lane = lax.broadcasted_iota(jnp.int32, (1, 2 * LANES), 1) % LANES
    right = [factor[:, at + j * LANES : at + (j + 1) * LANES] for factor, at in zip(factors, offsets)]
    right = jnp.concatenate(right, 1).astype(F32)
    total = 0.0
    for h in (2 * j, 2 * j + 1):
        left = end if (h + 1) * HEAD_DIM == plan.dim else source[:, h * LANES : (h + 1) * LANES]
        mine = (lane // HEAD_DIM == h % 2).astype(F32)
        total = total + dot_tn(left, (right * mine).astype(BF16))
    return total


def last_body(plan):
    def body(scalars, ins, outs, scratch):
        (at_ref,) = scalars
        flat, grad_query = scratch
        dim = plan.dim
        heads = dim // HEAD_DIM
        tiles = dim // LANES
        device = at_ref[0]
        parts = [ins[K.PART, tower].get() for tower in range(2)]

        def store(tower, block):
            line = outs[K.SHARE, tower].ref
            line[...] = block.reshape(1, block.shape[0] * LANES)[:, : plan.share]

        @pl.when(device >= plan.roots)
        def _():
            for tower in range(2):
                store(tower, parts[tower][...])

        names = K.SENT, K.SWAPPED, K.WINDOWS, K.QUERIES, K.VALUES, K.W_QUERY, K.BIAS
        sent_ref, swapped, windows, queries, value_part, w_query, bias = (
            ins[name].get() for name in names
        )

        @pl.when(device < plan.roots)
        def _():
            count = sent_ref.shape[0]
            caps = count // plan.devices
            first = plan.spare_from
            for core in range(2):

                @pl.when(device % 2 == core)
                def _():
                    received = sent_ref[:, first * LANES :], swapped[...]
                    for tower, values in enumerate(received if core == 0 else received[::-1]):
                        grad_query[:, tower * dim : (tower + 1) * dim] = values[:, -dim:]

            for tower, values in enumerate((sent_ref[:, first * LANES :], swapped[...])):
                sums = values[:, :-dim].astype(F32).reshape(plan.devices, caps, -1)
                put_tile(flat.at[tower], 0, spare_row(plan, jnp.sum(sums, 0), first, dim))
                grads = grad_query[:, tower * dim : (tower + 1) * dim]
                row = summed_through(grads, w_query[tower])
                put_tile(flat.at[tower], tiles, row + bias[tower : tower + 1, :])

            query_part = dot_tn(windows[...], grad_query[...])
            end = last_head(plan, sent_ref, heads)
            for j in range(tiles):
                put = window_product(plan, sent_ref, end, (queries, queries), (0, dim), j)
                for tower in range(2):
                    rows = slice(tower * plan.window, (tower + 1) * plan.window)
                    own = slice(tower * LANES, (tower + 1) * LANES)
                    q_at = tower * dim + j * LANES
                    for part, block in enumerate(
                        (
                            query_part[rows, q_at : q_at + LANES],
                            put[rows, own],
                            value_part[tower, :, j * LANES : (j + 1) * LANES],
                        )
                    ):
                        flat[
                            tower,
                            pl.ds(2 * tiles + part * tiles + j, plan.window, stride=3 * tiles),
                            :,
                        ] = block
            start = device * plan.share
            at = start - plan.column(device) * plan.row
            shape = parts[0].shape
            index = (
                start
                + lax.broadcasted_iota(jnp.int32, shape, 0) * LANES
                + lax.broadcasted_iota(jnp.int32, shape, 1)
            )
            for tower in range(2):
                own = take_rows(flat.at[tower], at, plan.rows_out)
                store(tower, jnp.where(index < plan.out_at, own, parts[tower][...]))

    return body


class Fetch:
    def __init__(self, source, buf, sem, group):
        self.ref, self.buf, self.group = source, buf, group
        self.copy = pltpu.make_async_copy(source, buf, sem)
        group.members.append(self)

    def get(self):
        self.group.wait()
        return self.buf


class Group:
    def __init__(self):
        self.members, self.waited = [], False

    def wait(self):
        if not self.waited:
            self.waited = True
            for fetch in self.members:
                fetch.copy.wait()


class Here:
    def __init__(self, ref):
        self.buf = self.ref = ref

    def get(self):
        return self.buf

    def push(self):
        pass


class Push:
    def __init__(self, ref, target, sem):
        self.ref, self.target, self.sem, self.started = ref, target, sem, False
        self.copy = pltpu.make_async_copy(ref, target, sem)

    def push(self):
        self.started = True
        self.copy.start()

    def push_part(self, part):
        self.started = True
        pltpu.make_async_copy(self.ref.at[part], self.target.at[part], self.sem).start()


def run(body, name, outs, scratch, scalars, arrays, ahead=None):
    smem = pl.BlockSpec(memory_space=pltpu.SMEM)
    hbm = pl.BlockSpec(memory_space=pltpu.HBM)
    vmem = pl.BlockSpec(memory_space=pltpu.VMEM)
    groups = arrays
    arrays = {key: value for group in groups for key, value in group.items()}
    fetched = [(array, place) for array, place in arrays.values() if place in (Place.FAR, Place.FEW)]
    pushed = [(shape, kind) for shape, kind, place in outs.values() if place == Place.FAR]

    def kernel(*refs):
        at = 0

        def take(count):
            nonlocal at
            at += count
            return list(refs[at - count : at])

        scalar_refs, sources, targets = take(len(scalars)), take(len(arrays)), take(len(outs))
        in_bufs, out_bufs = take(len(fetched)), take(len(pushed))
        in_sems, out_sems = take(2)
        ins, results, fetches, pushes = {}, {}, [], []
        sources = iter(sources)
        chain = [Group() for unused in groups]
        for group, together in zip(groups, chain):
            for (key, (unused, place)), source in zip(group.items(), sources):
                if place in (Place.FAR, Place.FEW):
                    sem = in_sems.at[len(fetches)]
                    fetches.append(Fetch(source, in_bufs[len(fetches)], sem, together))
                    ins[key] = fetches[-1]
                else:
                    ins[key] = Here(source)
        for target, (key, (unused, unused, place)) in zip(targets, outs.items()):
            if place == Place.FAR:
                pushes.append(Push(out_bufs[len(pushes)], target, out_sems.at[len(pushes)]))
            results[key] = pushes[-1] if place == Place.FAR else Here(target)
        own_scratch = take(len(scratch))
        if ahead is not None:
            ahead(scalar_refs, ins, results, own_scratch)
        for fetch in fetches:
            fetch.copy.start()
        body(scalar_refs, ins, results, own_scratch)
        for push in pushes:
            if not push.started:
                push.push()
        for fetch in fetches:
            fetch.get()
        for push in pushes:
            push.copy.wait()

    where = {Place.FAR: hbm, Place.FEW: hbm, Place.RAW: hbm, Place.AUTO: vmem, Place.NEAR: vmem, Place.SCALAR: smem}
    buffers = [
        (pltpu.SMEM if place == Place.FEW else pltpu.VMEM)(array.shape, array.dtype)
        for array, place in fetched
    ]
    buffers += [pltpu.VMEM(shape, kind) for shape, kind in pushed]
    buffers += [pltpu.SemaphoreType.DMA((max(len(group), 1),)) for group in (fetched, pushed)]
    pinned = [
        array if place == Place.AUTO else pltpu.with_memory_space_constraint(array, pltpu.HBM)
        for array, place in arrays.values()
    ]
    results = pl.pallas_call(
        kernel,
        name=name,
        out_shape=[
            {Place.FAR: pltpu.HBM, Place.NEAR: pltpu.VMEM}.get(place, jax.ShapeDtypeStruct)(shape, kind)
            for shape, kind, place in outs.values()
        ],
        in_specs=[smem] * len(scalars) + [where[place] for unused, place in arrays.values()],
        out_specs=[where[place] for unused, unused, place in outs.values()],
        scratch_shapes=buffers + list(scratch),
        compiler_params=pltpu.CompilerParams(vmem_limit_bytes=LIMIT),
    )(*scalars, *pinned)
    return dict(zip(outs, results))


def exchange(array):
    return lax.all_to_all(array, "dp", split_axis=0, concat_axis=0, tiled=True)


def swap(array, devices):
    return lax.ppermute(array, "dp", [(i, i ^ 1) for i in range(devices)])


def compact(
    text_input, eot_index, image_input, ln1_gain, ln1_bias, w_qkv, w_attn_out, ln2_gain, ln2_bias,
    w_fc, w_fc_out, img_ln1_gain, img_ln1_bias, img_w_qkv, img_w_attn_out, img_ln2_gain,
    img_ln2_bias, img_w_fc, img_w_fc_out, final_gain, final_bias, text_proj, image_gain,
    image_bias, image_proj, logit_scale,
):
    caps, seq, dim = text_input.shape
    img_seq = image_input.shape[1]
    devices = lax.axis_size("dp")
    plan = Plan(dim, w_fc.shape[2], devices, caps)
    heads = dim // HEAD_DIM
    count = devices * caps
    hidden = plan.hidden
    device = lax.axis_index("dp").astype(jnp.int32).reshape(1)
    text_input, image_input = text_input.swapaxes(0, 1), image_input.swapaxes(0, 1)
    totals = caps * seq, caps * img_seq
    width = (heads - 1) * LANES

    first = {
        (K.X, 0): text_input, (K.X, 1): image_input,
        (K.GAIN, 0): ln1_gain, (K.BIAS, 0): ln1_bias,
        (K.GAIN, 1): img_ln1_gain, (K.BIAS, 1): img_ln1_bias,
    }
    late = {(K.W_QKV, 0): w_qkv, (K.W_QKV, 1): img_w_qkv}
    outputs_in = {(K.W_OUT, 0): w_attn_out, (K.W_OUT, 1): img_w_attn_out}
    second = {
        (K.GAIN2, 0): ln2_gain, (K.BIAS2, 0): ln2_bias,
        (K.GAIN2, 1): img_ln2_gain, (K.BIAS2, 1): img_ln2_bias,
    }
    hidden_in = {(K.W_FC, 0): w_fc, (K.W_FC, 1): img_w_fc}
    third = {
        (K.W_FC_OUT, 0): w_fc_out, (K.W_FC_OUT, 1): img_w_fc_out,
        (K.HEAD_GAIN, 0): final_gain, (K.HEAD_BIAS, 0): final_bias,
        (K.HEAD_GAIN, 1): image_gain, (K.HEAD_BIAS, 1): image_bias,
        (K.PROJ, 0): text_proj, (K.PROJ, 1): image_proj,
    }

    def far(arrays):
        return {key: (array, Place.FAR) for key, array in arrays.items()}

    eot = {K.EOT: (eot_index, Place.FEW)}
    rows = run(
        front_body(plan),
        "front",
        {K.ROWS: ((devices, caps, 2 * dim), BF16, Place.NEAR)},
        [],
        [],
        [eot | far(first), far(late)],
    )[K.ROWS]
    mine = exchange(rows).reshape(count, 2 * dim)

    unused, pack_rows = pack_at(dim, hidden, caps)
    side_outs = {K.VALUES: ((devices, caps, width), BF16, Place.FAR)}
    middle_outs = {
        K.SEND: ((devices, caps, width + dim), BF16, Place.FAR),
        K.ROWS: ((count, 4 * dim), BF16, Place.FAR),
    }
    for tower, total in enumerate(totals):
        side_outs |= {
            (K.NORMED, tower): ((total, dim), BF16, Place.FAR),
            (K.UNIT, tower): ((total, dim), BF16, Place.FAR),
            (K.PROBS, tower): ((heads * caps, total), F32, Place.FAR),
            (K.PACK, tower): ((pack_rows, dim), F32, Place.FAR),
        }
        middle_outs |= {
            (K.OWN, tower): (((2 + heads) * caps, dim), F32, Place.FAR),
            (K.SCORES, tower): ((heads * caps, total), BF16, Place.FAR),
        }
    side = run(side_body(plan), "side", side_outs, [[pltpu.VMEM((caps, hidden), F32)] * 2], [], [eot | far(first), far(late), far(outputs_in | second | hidden_in | third)])
    values = exchange(side.pop(K.VALUES))
    mine, side[K.PACK, 0] = lax.optimization_barrier((mine, side[K.PACK, 0]))
    others = swap(mine, devices)

    packs = {key: side[key] for key in ((K.PACK, 0), (K.PACK, 1))}
    middle = run(
        middle_body(plan),
        "middle",
        middle_outs,
        [pltpu.VMEM((count, 4 * dim), BF16), pltpu.SemaphoreType.DMA((2,))],
        [device, logit_scale],
        [
            {K.MINE: (mine, Place.AUTO), K.OTHERS: (others, Place.AUTO)}
            | {key: (array, Place.AUTO) for key, array in hidden_in.items()}
            | far(outputs_in | second),
            far(third | packs),
            far(late)
            | far({(name, tower): side[name, tower] for name in (K.NORMED, K.PROBS, K.UNIT) for tower in (0, 1)}),
        ],
        join_rows,
    )
    send, values = lax.optimization_barrier((middle[K.SEND], values))
    sent = exchange(send)

    share_rows = plan.rows_out
    region = (plan.total - plan.out_at) // LANES
    head_region = plan.head_total // LANES
    attended = {}
    tail_outs = {K.LOSS: ((1,), F32, Place.SCALAR), K.SCALE: ((1,), F32, Place.SCALAR)}
    for tower, length in enumerate((seq, img_seq)):
        for name, source in ((K.PROBS, side), (K.PACK, side), (K.OWN, middle), (K.SCORES, middle)):
            attended[name, tower] = source[name, tower]
        tail_outs |= {
            (K.PART, tower): ((share_rows, LANES), F32, Place.NEAR),
            (K.INPUT, tower): ((length, caps, dim), F32, Place.FAR),
        }
    tail_outs |= {
        K.HEAD: ((plan.head_rows_out, LANES), F32, Place.FAR),
        K.WINDOWS: ((count, LANES), BF16, Place.NEAR),
        K.QUERIES: ((count, 2 * dim), BF16, Place.NEAR),
        K.VALUES: ((2, plan.window, dim), F32, Place.NEAR),
        K.W_QUERY: ((2, dim, dim), BF16, Place.NEAR),
        K.BIAS: ((8, dim), F32, Place.NEAR),
    }
    tail = run(
        tail_body(plan),
        "tail",
        tail_outs,
        [
            pltpu.VMEM((region + 2 * share_rows + 8, LANES), F32),
            pltpu.VMEM((head_region + plan.head_rows_out + 8, LANES), F32),
            pltpu.VMEM((totals[0], dim), F32),
            pltpu.VMEM((totals[1], dim), F32),
            pltpu.VMEM((8, dim), F32),
            [pltpu.VMEM((count, hidden), F32)] * 2,
            [pltpu.VMEM((count, hidden), BF16)] * 2,
            [pltpu.VMEM((count, hidden), BF16)] * 2,
            pltpu.VMEM((2, dim, dim), BF16),
            pltpu.SemaphoreType.DMA((4,)),
        ],
        [device, logit_scale],
        [
            eot | far(first),
            far(attended),
            far({K.ROWS: middle[K.ROWS]} | outputs_in | second | hidden_in),
            far(third),
            far({K.VALUES: values.reshape(count, width)})
            | {key: (array, Place.RAW) for key, array in late.items()},
        ],
        tail_ahead(plan),
    )
    sent, tail[K.WINDOWS] = lax.optimization_barrier((sent, tail[K.WINDOWS]))
    swapped = swap(sent[:, :, plan.spare_from * LANES :], devices)
    flat_rows = max(2 * dim + plan.window * plan.row, 2 * dim + 2 * plan.row + share_rows * LANES) // LANES
    names = [(K.PART, 0), (K.PART, 1), K.WINDOWS, K.QUERIES, K.VALUES, K.W_QUERY, K.BIAS]
    shares = run(
        last_body(plan),
        "last",
        {(K.SHARE, tower): ((1, plan.share), F32, Place.FAR) for tower in (0, 1)},
        [
            pltpu.VMEM((2, flat_rows // 8 * 8 + 16, LANES), F32),
            pltpu.VMEM((count, 2 * dim), BF16),
        ],
        [device],
        [
            {name: (tail[name], Place.AUTO) for name in names}
            | {K.SENT: (sent.reshape(count, -1), Place.AUTO)}
            | {K.SWAPPED: (swapped.reshape(count, -1), Place.AUTO)},
        ],
    )

    def cut(array, size):
        return array.reshape(-1)[:size]

    return (
        tail[K.LOSS],
        tail[K.INPUT, 0].swapaxes(0, 1),
        tail[K.INPUT, 1].swapaxes(0, 1),
        shares[K.SHARE, 0],
        shares[K.SHARE, 1],
        cut(tail[K.HEAD], plan.head_share),
        tail[K.SCALE],
    )


def norm_apply(values, gain, bias):
    center = values - jnp.mean(values, -1, keepdims=True)
    spread = jnp.mean(center * center, -1, keepdims=True)
    return center * lax.rsqrt(spread + EPS) * gain + bias


def quick_gelu(values):
    return values * jax.nn.sigmoid(1.702 * values)


def unit_rows(values):
    return values * lax.rsqrt(jnp.sum(values * values, -1, keepdims=True) + UNIT_EPS)


def causal_mask(seq_len):
    row_pos = lax.broadcasted_iota(jnp.int32, (seq_len, seq_len), 0)
    col_pos = lax.broadcasted_iota(jnp.int32, (seq_len, seq_len), 1)
    return col_pos <= row_pos


def matmul(left, right):
    return jnp.dot(left, right, preferred_element_type=jnp.float32)


def inner_rows(left, right):
    return lax.dot_general(
        left, right, (((0,), (0,)), ((), ())), preferred_element_type=jnp.float32
    )


def outer_cols(left, right):
    return lax.dot_general(
        left, right, (((1,), (1,)), ((), ())), preferred_element_type=jnp.float32
    )


def layer_forward(stream, weights, causal):
    gain_one, bias_one, w_qkv, w_out, gain_two, bias_two, w_fc, w_fc_out = weights
    num_caps, seq_len, feat_dim = stream.shape
    num_heads = feat_dim // HEAD_DIM
    num_rows = num_caps * seq_len
    normed_one = (
        norm_apply(stream, gain_one, bias_one).astype(jnp.bfloat16).reshape(num_rows, feat_dim)
    )
    packed = (
        matmul(normed_one, w_qkv)
        .astype(jnp.bfloat16)
        .reshape(num_caps, seq_len, 3, num_heads, HEAD_DIM)
    )
    queries = packed[:, :, 0]
    key_rows = packed[:, :, 1]
    value_rows = packed[:, :, 2]
    raw_score = jnp.einsum("bqhd,bkhd->bhqk", queries, key_rows, preferred_element_type=jnp.float32)
    scores = raw_score * HEAD_DIM ** (-0.5)
    if causal:
        scores = jnp.where(causal_mask(seq_len), scores, MASKED)
    row_peak = jnp.max(scores, -1, keepdims=True)
    log_total = row_peak + jnp.log(jnp.sum(jnp.exp(scores - row_peak), -1, keepdims=True))
    attn_probs = jnp.exp(scores - log_total)
    probs_low = attn_probs.astype(jnp.bfloat16)
    mixed_rows = jnp.einsum(
        "bhqk,bkhd->bqhd", probs_low, value_rows, preferred_element_type=jnp.float32
    )
    mixed_rows = mixed_rows.astype(jnp.bfloat16).reshape(num_rows, feat_dim)
    middle = stream + matmul(mixed_rows, w_out).reshape(num_caps, seq_len, feat_dim)
    normed_two = (
        norm_apply(middle, gain_two, bias_two).astype(jnp.bfloat16).reshape(num_rows, feat_dim)
    )
    hidden = matmul(normed_two, w_fc)
    active = quick_gelu(hidden).astype(jnp.bfloat16)
    result = middle + matmul(active, w_fc_out).reshape(num_caps, seq_len, feat_dim)
    return (
        result,
        (normed_one, packed, attn_probs, probs_low, mixed_rows, middle, normed_two, hidden, active),
    )


def layer_backward(stream, weights, grad_out, causal):
    gain_one, bias_one, w_qkv, w_out, gain_two, bias_two, w_fc, w_fc_out = weights
    num_caps, seq_len, feat_dim = stream.shape
    num_heads = feat_dim // HEAD_DIM
    num_rows = num_caps * seq_len
    unused, kept = layer_forward(stream, weights, causal)
    normed_one, packed, attn_probs, probs_low, mixed_rows, middle, normed_two, hidden, active = kept
    grad_low = grad_out.reshape(num_rows, feat_dim).astype(jnp.bfloat16)
    grad_fc_out = inner_rows(active, grad_low)
    grad_active = outer_cols(grad_low, w_fc_out)
    unused_gelu, gelu_back = jax.vjp(quick_gelu, hidden)
    grad_hidden = gelu_back(grad_active)[0].astype(jnp.bfloat16)
    grad_fc = inner_rows(normed_two, grad_hidden)
    grad_normed_two = outer_cols(grad_hidden, w_fc)
    unused_two, norm_back_two = jax.vjp(norm_apply, middle, gain_two, bias_two)
    grad_mid_norm, grad_gain_two, grad_bias_two = norm_back_two(
        grad_normed_two.reshape(num_caps, seq_len, feat_dim)
    )
    grad_middle = grad_out + grad_mid_norm
    middle_low = grad_middle.reshape(num_rows, feat_dim).astype(jnp.bfloat16)
    grad_w_out = inner_rows(mixed_rows, middle_low)
    grad_mixed = (
        outer_cols(middle_low, w_out)
        .astype(jnp.bfloat16)
        .reshape(num_caps, seq_len, num_heads, HEAD_DIM)
    )
    queries = packed[:, :, 0]
    key_rows = packed[:, :, 1]
    value_rows = packed[:, :, 2]
    grad_values = jnp.einsum(
        "bhqk,bqhd->bkhd", probs_low, grad_mixed, preferred_element_type=jnp.float32
    )
    grad_probs = jnp.einsum(
        "bqhd,bkhd->bhqk", grad_mixed, value_rows, preferred_element_type=jnp.float32
    )
    row_inner = jnp.sum(attn_probs * grad_probs, -1, keepdims=True)
    grad_raw = (attn_probs * (grad_probs - row_inner) * HEAD_DIM ** (-0.5)).astype(jnp.bfloat16)
    grad_queries = jnp.einsum(
        "bhqk,bkhd->bqhd", grad_raw, key_rows, preferred_element_type=jnp.float32
    )
    grad_keys = jnp.einsum("bhqk,bqhd->bkhd", grad_raw, queries, preferred_element_type=jnp.float32)
    grad_packed = (
        jnp.stack([grad_queries, grad_keys, grad_values], 2)
        .astype(jnp.bfloat16)
        .reshape(num_rows, 3 * feat_dim)
    )
    grad_qkv = inner_rows(normed_one, grad_packed)
    grad_normed_one = outer_cols(grad_packed, w_qkv)
    unused_one, norm_back_one = jax.vjp(norm_apply, stream, gain_one, bias_one)
    grad_in_norm, grad_gain_one, grad_bias_one = norm_back_one(
        grad_normed_one.reshape(num_caps, seq_len, feat_dim)
    )
    grads_here = [
        grad_gain_one,
        grad_bias_one,
        grad_qkv,
        grad_w_out,
        grad_gain_two,
        grad_bias_two,
        grad_fc,
        grad_fc_out,
    ]
    return (grad_middle + grad_in_norm, grads_here)


def head_forward(features, gain, bias, proj):
    normed = norm_apply(features, gain, bias).astype(jnp.bfloat16)
    embedded = matmul(normed, proj)
    return (unit_rows(embedded), (normed, embedded))


def head_backward(features, gain, bias, proj, kept, grad_unit):
    normed, embedded = kept
    unused_unit, unit_back = jax.vjp(unit_rows, embedded)
    grad_embed = unit_back(grad_unit)[0].astype(jnp.bfloat16)
    grad_proj = inner_rows(normed, grad_embed)
    grad_normed = outer_cols(grad_embed, proj)
    unused_norm, norm_back = jax.vjp(norm_apply, features, gain, bias)
    grad_feat, grad_gain, grad_bias = norm_back(grad_normed)
    return (grad_feat, [grad_gain, grad_bias, grad_proj])


def plain_contrast(own_rows, other_rows, multiplier, start):
    logits = multiplier * outer_cols(own_rows, other_rows)
    row_peak = jnp.max(logits, -1, keepdims=True)
    log_total = row_peak + jnp.log(jnp.sum(jnp.exp(logits - row_peak), -1, keepdims=True))
    col_pos = lax.broadcasted_iota(jnp.int32, logits.shape, 1)
    target_pos = lax.broadcasted_iota(jnp.int32, logits.shape, 0) + start
    matched = (col_pos == target_pos).astype(jnp.float32)
    loss_sum = jnp.sum(log_total) - jnp.sum(matched * logits)
    grad_logits = 0.5 * (jnp.exp(logits - log_total) - matched)
    scale_part = jnp.sum(grad_logits * logits)
    return (loss_sum, scale_part, (multiplier * grad_logits).astype(jnp.bfloat16), log_total[:, 0])


def pack_flat(arrays, devices):
    flat = jnp.concatenate([array.reshape(-1) for array in arrays])
    padding = -flat.shape[0] % devices
    return jnp.concatenate([flat, jnp.zeros((padding,), jnp.float32)])


def plain(
    text_input,
    eot_index,
    image_input,
    ln1_gain,
    ln1_bias,
    w_qkv,
    w_attn_out,
    ln2_gain,
    ln2_bias,
    w_fc,
    w_fc_out,
    img_ln1_gain,
    img_ln1_bias,
    img_w_qkv,
    img_w_attn_out,
    img_ln2_gain,
    img_ln2_bias,
    img_w_fc,
    img_w_fc_out,
    final_gain,
    final_bias,
    text_proj,
    image_gain,
    image_bias,
    image_proj,
    logit_scale,
):
    num_caps, seq_len, feat_dim = text_input.shape
    devices = lax.axis_size("dp")
    all_caps = num_caps * devices
    start = lax.axis_index("dp") * num_caps
    depth = ln1_gain.shape[0]
    text_stack = (ln1_gain, ln1_bias, w_qkv, w_attn_out, ln2_gain, ln2_bias, w_fc, w_fc_out)
    image_stack = (
        img_ln1_gain,
        img_ln1_bias,
        img_w_qkv,
        img_w_attn_out,
        img_ln2_gain,
        img_ln2_bias,
        img_w_fc,
        img_w_fc_out,
    )

    def text_weights(layer_num):
        return tuple((array[layer_num] for array in text_stack))

    def image_weights(layer_num):
        return tuple((array[layer_num] for array in image_stack))

    stream = text_input.astype(jnp.float32)
    layer_num = 0
    text_saved = [stream]
    stream, unused = layer_forward(stream, text_weights(layer_num), True)
    pooled = jnp.take_along_axis(stream, eot_index[:, None, None], axis=1)[:, 0]
    picture = image_input.astype(jnp.float32)
    layer_num = 0
    image_saved = [picture]
    picture, unused = layer_forward(picture, image_weights(layer_num), False)
    image_pooled = picture[:, 0]
    text_unit, text_kept = head_forward(pooled, final_gain, final_bias, text_proj)
    image_unit, image_kept = head_forward(image_pooled, image_gain, image_bias, image_proj)
    image_low = image_unit.astype(jnp.bfloat16)
    text_low = text_unit.astype(jnp.bfloat16)
    image_all, text_all = (
        lax.all_gather(image_low, "dp", axis=0, tiled=True),
        lax.all_gather(text_low, "dp", axis=0, tiled=True),
    )
    multiplier = jnp.exp(logit_scale[0])
    loss_image, scale_image, grad_raw_it, unused_it = plain_contrast(
        image_low, text_all, multiplier, start
    )
    loss_text, scale_text, grad_raw_ti, unused_ti = plain_contrast(text_low, image_all, multiplier, start)
    spread_text = inner_rows(grad_raw_it, image_low)
    spread_image = inner_rows(grad_raw_ti, text_low)
    back_text, back_image = (
        lax.psum_scatter(spread_text, "dp", scatter_dimension=0, tiled=True),
        lax.psum_scatter(spread_image, "dp", scatter_dimension=0, tiled=True),
    )
    total, grad_scale = lax.psum((loss_image + loss_text, scale_image + scale_text), "dp")
    grad_image_unit = matmul(grad_raw_it, text_all) + back_image
    grad_text_unit = matmul(grad_raw_ti, image_all) + back_text
    grad_pooled, text_head_grads = head_backward(
        pooled, final_gain, final_bias, text_proj, text_kept, grad_text_unit
    )
    grad_image_pooled, image_head_grads = head_backward(
        image_pooled, image_gain, image_bias, image_proj, image_kept, grad_image_unit
    )
    head_flat = pack_flat(text_head_grads + image_head_grads, devices)
    image_flat = [None] * depth
    img_seq = image_input.shape[1]
    img_dim = image_input.shape[2]
    grad_picture = jnp.concatenate(
        [grad_image_pooled[:, None, :], jnp.zeros((num_caps, img_seq - 1, img_dim), jnp.float32)], 1
    )
    for layer_num in reversed(range(depth)):
        grad_picture, grads_here = layer_backward(
            image_saved[layer_num], image_weights(layer_num), grad_picture, False
        )
        image_flat[layer_num] = pack_flat(grads_here, devices)
    text_flat = [None] * depth
    selected = (
        lax.broadcasted_iota(jnp.int32, (num_caps, seq_len), 1) == eot_index[:, None]
    ).astype(jnp.float32)
    grad_stream = selected[:, :, None] * grad_pooled[:, None, :]
    for layer_num in reversed(range(depth)):
        grad_stream, grads_here = layer_backward(
            text_saved[layer_num], text_weights(layer_num), grad_stream, True
        )
        text_flat[layer_num] = pack_flat(grads_here, devices)
    text_share, image_share, head_share = (
        lax.psum_scatter(jnp.stack(text_flat), "dp", scatter_dimension=1, tiled=True),
        lax.psum_scatter(jnp.stack(image_flat), "dp", scatter_dimension=1, tiled=True),
        lax.psum_scatter(head_flat, "dp", scatter_dimension=0, tiled=True),
    )
    loss = (total / (2 * all_caps)).reshape(1)
    return (
        loss,
        grad_stream,
        grad_picture,
        text_share,
        image_share,
        head_share,
        grad_scale.reshape(1),
    )


def shards(*args):
    caps = args[0].shape[0] * lax.axis_size("dp")
    return compact(*args) if caps <= 512 else plain(*args)


def solution(mesh):
    return jax.shard_map(
        shards,
        mesh=mesh,
        in_specs=(
            P("dp", None, None),
            P("dp"),
            P("dp", None, None),
            P(),
            P(),
            P(),
            P(),
            P(),
            P(),
            P(),
            P(),
            P(),
            P(),
            P(),
            P(),
            P(),
            P(),
            P(),
            P(),
            P(),
            P(),
            P(),
            P(),
            P(),
            P(),
            P(),
        ),
        out_specs=(
            P(),
            P("dp", None, None),
            P("dp", None, None),
            P(None, "dp"),
            P(None, "dp"),
            P("dp"),
            P(),
        ),
        check_vma=False,
    )
```
